32 devices in a mesh: ctx: 16 (over z, y, core), wt: 2 (over x).
Axes of the slice: x: 2, y: 2, z: 4, core: 2. Of those that a mesh axis runs over, the one named last changes fastest.
Arguments:
- block_in: bfloat16 [4, 4096, 512], P('wt', 'ctx'), may hold values from -6 to 6
- block_order: int32 [4, 32], P('wt'), may hold values from 0 to 31, as said below
- w_query: bfloat16 [512, 512], P('wt'), may hold values from -0.25 to 0.25
- b_query: bfloat16 [512], P('wt'), may hold values from -1.796875 to 1.796875
- w_key: bfloat16 [512, 512], P('wt'), may hold values from -0.25 to 0.25
- w_value: bfloat16 [512, 512], P('wt'), may hold values from -0.25 to 0.25
- b_value: bfloat16 [512], P('wt'), may hold values from -0.59765625 to 0.59765625
- w_out: bfloat16 [512, 512], P('wt'), may hold values from -1.5 to 1.5
- b_out: bfloat16 [512], P('wt'), may hold values from -1.796875 to 1.796875
- gain_one: bfloat16 [512], P('wt'), may hold values from 0.5 to 1.5
- shift_one: bfloat16 [512], P('wt'), may hold values from -1.796875 to 1.796875
- w_up: bfloat16 [512, 2048], P('wt'), may hold values from -0.25 to 0.25
- b_up: bfloat16 [2048], P('wt'), may hold values from -1.796875 to 1.796875
- w_down: bfloat16 [2048, 512], P('wt'), may hold values from -0.125 to 0.125
- b_down: bfloat16 [512], P('wt'), may hold values from -1.796875 to 1.796875
- gain_two: bfloat16 [512], P('wt'), may hold values from 0.5 to 1.5
- shift_two: bfloat16 [512], P('wt'), may hold values from -1.796875 to 1.796875
- cotangent: bfloat16 [4, 4096, 512], P('wt', 'ctx'), may hold values from -6 to 6
Outputs:
- block_out: bfloat16 [4, 4096, 512], P('wt', 'ctx')
- grad_in: bfloat16 [4, 4096, 512], P('wt', 'ctx')
- dw_query: float32 [512, 512], P('wt')
- db_query: float32 [512], P('wt')
- dw_key: float32 [512, 512], P('wt')
- dw_value: float32 [512, 512], P('wt')
- db_value: float32 [512], P('wt')
- dw_out: float32 [512, 512], P('wt')
- db_out: float32 [512], P('wt')
- dgain_one: float32 [512], P('wt')
- dshift_one: float32 [512], P('wt')
- dw_up: float32 [512, 2048], P('wt')
- db_up: float32 [2048], P('wt')
- dw_down: float32 [2048, 512], P('wt')
- db_down: float32 [512], P('wt')
- dgain_two: float32 [512], P('wt')
- dshift_two: float32 [512], P('wt')
The draws below stay inside these ranges and needn't reach their ends.
Inputs may be any that keep to these rules, and one draw needn't show every extreme that they name: `block_order`: each row lists the 32 blocks of a sequence in stored order and is a permutation; entries 2 i and 2 i + 1 of a row sum to 31.
All inputs are finite; a program needn't handle non-finite values.
Results may differ from the reference program's by a relative error of at most 0.024.
Values may be sent and summed in bfloat16 or wider, within the bound.
A program may use at most 192 MiB of HBM per device.

```python
import math
from functools import partial
import jax
import jax.numpy as jnp
from jax import lax

D = 512
HEADS = 8
HEAD_DIM = 64
FF = 2048
BLOCK = 128
SEQS = 4
NBLK = 32
SEQ_LEN = 4096


def draw_block_order(key, part):
    seq_keys = jax.random.split(key, SEQS)

    def one_sequence(seq_key):
        pair_key, flip_key = jax.random.split(seq_key)
        pairs = jax.random.permutation(pair_key, NBLK // 2).astype(jnp.int32)
        flips = jax.random.randint(flip_key, (NBLK // 2,), 0, 2).astype(jnp.int32)
        first = jnp.where(flips == 1, NBLK - 1 - pairs, pairs)
        second = NBLK - 1 - first
        return jnp.stack([first, second], axis=1).reshape(NBLK).astype(jnp.int32)
    return jax.vmap(one_sequence)(seq_keys)


def block_scale(key, dims, pieces, smallest, top_value):
    level = 1.0
    for position, parts in pieces:
        heights = jax.random.uniform(jax.random.fold_in(jax.random.fold_in(key, 6), position), (parts,), jnp.float32, smallest / len(pieces), top_value / len(pieces))
        level = level * jnp.repeat(jnp.exp(heights), dims[position] // parts).reshape((-1,) + (1,) * (len(dims) - 1 - position))
    return level


def noise(own_key, shape, scale, bound, cuts=(), kind=jnp.bfloat16):
    drawn = scale * jax.random.normal(own_key, shape, jnp.float32)
    if cuts:
        drawn = drawn * block_scale(own_key, shape, cuts, -0.22, 0.18)
    return jnp.clip(drawn, -bound, bound).astype(kind)


def setup_inputs(seed: int = 0) -> dict:
    key_list = jax.random.split(jax.random.key(seed), 19)
    block_in = noise(key_list[0], (SEQS, SEQ_LEN, D), 1.0, 6.0, ((0, 2), (1, 16)))
    block_order = draw_block_order(jax.random.fold_in(key_list[18], 71), 0)
    w_query = noise(key_list[2], (D, D), D ** -0.5, 0.25, ((0, 2),))
    b_query = noise(key_list[3], (D,), 0.3, 1.796875, ((0, 2),))
    w_key = noise(key_list[4], (D, D), D ** -0.5, 0.25, ((0, 2),))
    w_value = noise(key_list[5], (D, D), D ** -0.5, 0.25, ((0, 2),))
    b_value = noise(key_list[6], (D,), 0.1, 0.59765625, ((0, 2),))
    w_out = noise(key_list[7], (D, D), (max(1, D * 128 // SEQ_LEN)) ** -0.5, 1.5, ((0, 2),))
    b_out = noise(key_list[8], (D,), 0.3, 1.796875, ((0, 2),))
    gain_one = jnp.clip(1.0 + 0.1 * jax.random.normal(key_list[9], (D,), jnp.float32), 0.5, 1.5).astype(jnp.bfloat16)
    shift_one = noise(key_list[10], (D,), 0.3, 1.796875, ((0, 2),))
    w_up = noise(key_list[11], (D, FF), D ** -0.5, 0.25, ((0, 2),))
    b_up = noise(key_list[12], (FF,), 0.3, 1.796875, ((0, 2),))
    w_down = noise(key_list[13], (FF, D), FF ** -0.5, 0.125, ((0, 2),))
    b_down = noise(key_list[14], (D,), 0.3, 1.796875, ((0, 2),))
    gain_two = jnp.clip(1.0 + 0.1 * jax.random.normal(key_list[15], (D,), jnp.float32), 0.5, 1.5).astype(jnp.bfloat16)
    shift_two = noise(key_list[16], (D,), 0.3, 1.796875, ((0, 2),))
    cotangent = noise(key_list[17], (SEQS, SEQ_LEN, D), 1.0, 6.0, ((0, 2), (1, 16)))
    return dict(block_in=block_in, block_order=block_order, w_query=w_query, b_query=b_query, w_key=w_key, w_value=w_value, b_value=b_value, w_out=w_out, b_out=b_out, gain_one=gain_one, shift_one=shift_one, w_up=w_up, b_up=b_up, w_down=w_down, b_down=b_down, gain_two=gain_two, shift_two=shift_two, cotangent=cotangent)


masked_fill = -1e+30
norm_eps = 1e-05
highest = lax.Precision.HIGHEST

@jax.custom_vjp
def low(v):
    return lax.optimization_barrier(v.astype(jnp.bfloat16)).astype(jnp.float32)

@jax.custom_vjp
def low_back(v):
    return v

def low_keep(v):
    return (low(v), None)

def low_pass(kept, grad):
    return (grad,)

def back_keep(v):
    return (v, None)

def back_low(kept, grad):
    return (low(grad),)
low.defvjp(low_keep, low_pass)
low_back.defvjp(back_keep, back_low)

def smooth_gelu(values):
    inner = math.sqrt(2.0 / math.pi) * (values + 0.044715 * values * values * values)
    return 0.5 * values * (1.0 + jnp.tanh(inner))

def layer_norm(values, gain_vec, shift_vec):
    center = values - lax.optimization_barrier(jnp.mean(values, axis=-1, keepdims=True))
    spread = lax.optimization_barrier(jnp.mean(center * center, axis=-1, keepdims=True))
    return center * lax.rsqrt(spread + norm_eps) * gain_vec + shift_vec

def matmul(left, right):
    return jnp.dot(left, right, precision=highest, preferred_element_type=jnp.float32)

def row_softmax(scores):
    top = lax.optimization_barrier(jnp.max(scores, axis=-1, keepdims=True))
    powers = jnp.exp(scores - top)
    return powers / lax.optimization_barrier(jnp.sum(powers, axis=-1, keepdims=True))

def attend_sequence(operands):
    query_rows, key_rows, value_rows, positions = operands
    length = query_rows.shape[0]
    query_block = min(512, length)
    scale_factor = HEAD_DIM ** (-0.5)

    def one_block(block_ops):
        query_part, query_pos = block_ops
        scores = jnp.einsum('qhd,khd->hqk', query_part, key_rows, precision=highest) * scale_factor
        allowed = positions[None, :] <= query_pos[:, None]
        scores = jnp.where(allowed[None], scores, masked_fill)
        scores = low_back(scores)
        prob_rows = row_softmax(scores)
        return jnp.einsum('hqk,khd->qhd', low(prob_rows), value_rows, precision=highest)
    blocks = lax.map(jax.checkpoint(one_block), (query_rows.reshape(length // query_block, query_block, HEADS, HEAD_DIM), positions.reshape(length // query_block, query_block)))
    return blocks.reshape(length, HEADS * HEAD_DIM)

def forward(block_in, w_query, b_query, w_key, w_value, b_value, w_out, b_out, gain_one, shift_one, w_up, b_up, w_down, b_down, gain_two, shift_two, positions):
    seq_count, length, model_dim = block_in.shape
    tokens = block_in.reshape(seq_count * length, model_dim)
    queries = low(low_back(matmul(tokens, w_query) + b_query))
    key_rows = low(low_back(matmul(tokens, w_key)))
    value_rows = low(low_back(matmul(tokens, w_value) + b_value))
    head_shape = (seq_count, length, HEADS, HEAD_DIM)
    attended = lax.map(attend_sequence, (queries.reshape(head_shape), key_rows.reshape(head_shape), value_rows.reshape(head_shape), positions))
    attended = low(low_back(attended.reshape(seq_count * length, model_dim)))
    mixture = tokens + low_back(matmul(attended, w_out) + b_out)
    normed = layer_norm(mixture, gain_one, shift_one)
    pre_act = low_back(matmul(low(normed), w_up) + b_up)
    active = low(smooth_gelu(pre_act))
    ffn_out = low_back(matmul(active, w_down) + b_down)
    summed = ffn_out + normed + tokens
    return layer_norm(summed, gain_two, shift_two).reshape(seq_count, length, model_dim)

def reference(block_in, block_order, w_query, b_query, w_key, w_value, b_value, w_out, b_out, gain_one, shift_one, w_up, b_up, w_down, b_down, gain_two, shift_two, cotangent):
    seq_count = block_in.shape[0]
    positions = (block_order.astype(jnp.int32)[:, :, None] * BLOCK + jnp.arange(BLOCK, dtype=jnp.int32)[None, None, :]).reshape(seq_count, -1).astype(jnp.int32)
    params = [block_in, w_query, b_query, w_key, w_value, b_value, w_out, b_out, gain_one, shift_one, w_up, b_up, w_down, b_down, gain_two, shift_two]
    params = jax.tree.map(lambda tensor: tensor.astype(jnp.float32), params)
    outcome, pullback = jax.vjp(partial(forward, positions=positions), *params)
    gradients = pullback(cotangent.astype(jnp.float32))
    return (outcome.astype(jnp.bfloat16), gradients[0].astype(jnp.bfloat16), gradients[1], gradients[2], gradients[3], gradients[4], gradients[5], gradients[6], gradients[7], gradients[8], gradients[9], gradients[10], gradients[11], gradients[12], gradients[13], gradients[14], gradients[15])
```

```python
import functools
import math

import jax
import jax.numpy as jnp
from jax import lax
from jax.experimental import pallas as pl
from jax.experimental.pallas import tpu as pltpu
from jax.sharding import PartitionSpec as P

norm_eps = 1e-05

BLOCK = 128
LOG2E = 1.4426950408889634
bf16, f32 = jnp.bfloat16, jnp.float32
NT = (((1,), (1,)), ((), ()))
TN = (((0,), (0,)), ((), ()))

def dot(a, b, dims=(((1,), (0,)), ((), ()))):
    return lax.dot_general(a, b, dims, preferred_element_type=f32)

def fwd_kernel(nb, blk_ref, x_ref, wq_ref, wkv_ref, bq_ref, bkv_ref,
               o_ref, lse_ref, k_ref, v_ref, qt_ref, q_ref, vt_s, qs_s, acc_s, m_s, l_s, d_s):
    qs_s[...] = jnp.zeros_like(qs_s)
    d_s[...] = lax.broadcasted_iota(jnp.int32, d_s.shape, 0) - (lax.broadcasted_iota(jnp.int32, d_s.shape, 1) & 127)
    def proj(p, _):
        x = x_ref[pl.ds(pl.multiple_of(p * 256, 256), 256), :]
        kv = dot(x, wkv_ref[...])
        k = kv[:, :256].astype(bf16)
        v = (kv[:, 256:] + bkv_ref[...]).astype(bf16)
        for u in range(2):
            r = pl.ds(pl.multiple_of(blk_ref[2 * p + u] * BLOCK, BLOCK), BLOCK)
            k_ref[r, :] = k[u * BLOCK:(u + 1) * BLOCK]
            vb = v[u * BLOCK:(u + 1) * BLOCK]
            v_ref[r, :] = vb
            vt_s[:, r] = vb.astype(f32).T.astype(bf16)
        return 0
    lax.fori_loop(0, nb // 2, proj, 0)
    def projq(p, _):
        x = x_ref[pl.ds(pl.multiple_of(p * 256, 256), 256), :]
        q = (dot(x, wq_ref[...]) + bq_ref[...]) * (LOG2E / 8.0)
        q_ref[pl.ds(pl.multiple_of(p * 256, 256), 256), :] = q.astype(bf16)
        for u in range(2):
            qt = q[u * BLOCK:(u + 1) * BLOCK].T.astype(bf16)
            qt_ref[2 * p + u] = qt
            for h in range(4):
                qs_s[2 * p + u, 64 * h:64 * h + 64, 128 * h:128 * h + 128] = qt[64 * h:64 * h + 64]
        return 0
    lax.fori_loop(0, 4, projq, 0)

    def pair(p, _):
        b0 = blk_ref[2 * p]
        first_lo = b0 < nb // 2
        lo = jnp.where(first_lo, b0, nb - 1 - b0)
        hi = nb - 1 - lo
        u_lo = 2 * p + jnp.where(first_lo, 0, 1)
        u_hi = 2 * p + jnp.where(first_lo, 1, 0)
        n_lo = lax.div(lo, 2)
        n_hi = lax.div(hi, 2)
        def scores(kt, u):
            return dot(k_ref[pl.ds(pl.multiple_of(kt * 256, 256), 256), :], qs_s[u])
        def pv(kt, p16):
            c = pl.ds(pl.multiple_of(kt * 256, 256), 256)
            return jnp.concatenate([dot(vt_s[0:128, c], p16[:, 0:256]), dot(vt_s[128:256, c], p16[:, 256:512])], axis=1)
        for (s, kt, u, qp) in ((0, n_lo, u_lo, lo), (1, n_hi, u_hi, hi)):
            st = scores(kt, u)
            st = jnp.where(d_s[...] <= qp * 128 - kt * 256, st, -1e30)
            m = jnp.max(st, axis=0, keepdims=True)
            pr = jnp.exp2(st - m)
            m_s[s] = m
            l_s[s] = jnp.sum(pr, axis=0, keepdims=True)
            acc_s[s] = pv(kt, pr.astype(bf16))
        for t in range(nb // 2 - 1):
            is_lo = t < n_lo
            s = jnp.where(is_lo, 0, 1)
            kt = jnp.where(is_lo, t, t - n_lo)
            u = jnp.where(is_lo, u_lo, u_hi)
            st = scores(kt, u)
            m_old = m_s[s]
            m = jnp.maximum(m_old, jnp.max(st, axis=0, keepdims=True))
            pr = jnp.exp2(st - m)
            al = jnp.exp2(m_old - m)
            m_s[s] = m
            l_s[s] = l_s[s] * al + jnp.sum(pr, axis=0, keepdims=True)
            acc_s[s] = acc_s[s] * al + pv(kt, pr.astype(bf16))
        for (s, u) in ((0, u_lo), (1, u_hi)):
            l = l_s[s]
            lse_ref[u] = m_s[s] + jnp.log2(l)
            a = acc_s[s] * (1.0 / l)
            ot = jnp.concatenate([a[64 * (h % 2):64 * (h % 2) + 64, 128 * h:128 * h + 128] for h in range(4)], axis=0)
            o_ref[pl.ds(pl.multiple_of(u * 128, 128), 128), :] = ot.T
        return 0
    lax.fori_loop(0, 4, pair, 0)

def attn_fwd(blk, x, wq, wkv, bq, bkv):
    nb = blk.shape[0]
    V = pl.BlockSpec(memory_space=pltpu.VMEM)
    return pl.pallas_call(
        functools.partial(fwd_kernel, nb),
        out_shape=(jax.ShapeDtypeStruct((1024, 256), f32), jax.ShapeDtypeStruct((8, 1, 512), f32),
                   jax.ShapeDtypeStruct((nb * 128, 256), bf16), jax.ShapeDtypeStruct((nb * 128, 256), bf16),
                   jax.ShapeDtypeStruct((8, 256, 128), bf16), jax.ShapeDtypeStruct((1024, 256), bf16)),
        in_specs=[pl.BlockSpec(memory_space=pltpu.SMEM)] + [V] * 5, out_specs=(V,) * 6,
        scratch_shapes=[pltpu.VMEM((256, nb * 128), bf16), pltpu.VMEM((8, 256, 512), bf16), pltpu.VMEM((2, 128, 512), f32),
                        pltpu.VMEM((2, 1, 512), f32), pltpu.VMEM((2, 1, 512), f32), pltpu.VMEM((256, 512), jnp.int32)],
        compiler_params=pltpu.CompilerParams(vmem_limit_bytes=56 << 20),
        name="attn_fwd")(blk, x, wq, wkv, bq, bkv)

def bwd_kernel(nb, blk_ref, x_ref, k_ref, v_ref, qt_ref, q_ref, lse_ref, do_ref, of_ref, wq_ref, wkv_ref,
               dx_ref, dw_ref, db_ref, dxq_s, dqa_s, kt_s, qs_s, qn_s, dot_s, don_s, dl_s, dk_s, dv_s, dq_s, d_s):
    qs_s[...] = jnp.zeros_like(qs_s)
    qn_s[...] = jnp.zeros_like(qn_s)
    dot_s[...] = jnp.zeros_like(dot_s)
    don_s[...] = jnp.zeros_like(don_s)
    dk_s[...] = jnp.zeros_like(dk_s)
    dv_s[...] = jnp.zeros_like(dv_s)
    d_s[...] = lax.broadcasted_iota(jnp.int32, d_s.shape, 0) - (lax.broadcasted_iota(jnp.int32, d_s.shape, 1) & 127)
    def prep_k(j, _):
        r = pl.ds(pl.multiple_of(j * 256, 256), 256)
        kt_s[:, r] = k_ref[r, :].astype(f32).T.astype(bf16)
        return 0
    lax.fori_loop(0, nb // 2, prep_k, 0)
    def prep_q(u, s):
        r = pl.ds(pl.multiple_of(u * 128, 128), 128)
        do = do_ref[r, :]
        doT = do.astype(f32).T
        dlT = doT * of_ref[r, :].T
        q = q_ref[r, :]
        qt = qt_ref[u]
        for h in range(4):
            hs = slice(64 * h, 64 * h + 64)
            cs = slice(128 * h, 128 * h + 128)
            qs_s[s, hs, cs] = qt[hs]
            dot_s[s, hs, cs] = doT[hs].astype(bf16)
            dl_s[s, :, cs] = jnp.sum(dlT[hs], axis=0, keepdims=True)
            qn_s[s, cs, hs] = q[:, hs]
            don_s[s, cs, hs] = do[:, hs]
    def pair(p, _):
        b0 = blk_ref[2 * p]
        first_lo = b0 < nb // 2
        lo = jnp.where(first_lo, b0, nb - 1 - b0)
        hi = nb - 1 - lo
        u_lo = 2 * p + jnp.where(first_lo, 0, 1)
        u_hi = 2 * p + jnp.where(first_lo, 1, 0)
        n_lo = lax.div(lo, 2)
        n_hi = lax.div(hi, 2)
        prep_q(u_lo, 0)
        prep_q(u_hi, 1)
        def step(s, kt, u, qp, masked):
            r = pl.ds(pl.multiple_of(kt * 256, 256), 256)
            st = dot(k_ref[r, :], qs_s[s]) - lse_ref[u]
            if masked:
                st = jnp.where(d_s[...] <= qp * 128 - kt * 256, st, -1e30)
            pr = jnp.exp2(st)
            dp = dot(v_ref[r, :], dot_s[s]) - dl_s[s]
            ds = (pr * dp).astype(bf16)
            dv_s[r, :] += dot(pr.astype(bf16), don_s[s])
            dk_s[r, :] += dot(ds, qn_s[s])
            dq = jnp.concatenate([dot(kt_s[0:128, r], ds[:, 0:256]), dot(kt_s[128:256, r], ds[:, 256:512])], axis=1)
            if masked:
                dq_s[s] = dq
            else:
                dq_s[s] += dq
        step(0, n_lo, u_lo, lo, True)
        step(1, n_hi, u_hi, hi, True)
        for t in range(nb // 2 - 1):
            is_lo = t < n_lo
            step(jnp.where(is_lo, 0, 1), jnp.where(is_lo, t, t - n_lo), jnp.where(is_lo, u_lo, u_hi), 0, False)
        for (s, u) in ((0, u_lo), (1, u_hi)):
            a = dq_s[s] * 0.125
            dqT = jnp.concatenate([a[64 * (h % 2):64 * (h % 2) + 64, 128 * h:128 * h + 128] for h in range(4)], axis=0)
            dqa_s[pl.ds(pl.multiple_of(u * 128, 128), 128), :] = dqT.T.astype(bf16)
        return 0
    lax.fori_loop(0, 4, pair, 0)
    dw_ref[...] = jnp.zeros_like(dw_ref)
    db_ref[...] = jnp.zeros_like(db_ref)
    def fin_q(u, _):
        r = pl.ds(pl.multiple_of(u * 128, 128), 128)
        dq = dqa_s[r, :]
        dxq_s[r, :] = dot(dq, wq_ref[...], NT)
        dw_ref[:, 0:256] += dot(x_ref[r, :], dq, TN)
        db_ref[0:1, :] += jnp.sum(dq.astype(f32), axis=0, keepdims=True)
        return 0
    lax.fori_loop(0, 8, fin_q, 0)
    def fin_k(b, with_q):
        r = pl.ds(pl.multiple_of(b * 128, 128), 128)
        g = pl.ds(pl.multiple_of(blk_ref[b] * 128, 128), 128)
        dkv = jnp.concatenate([(dk_s[g, :] * (1.0 / LOG2E)).astype(bf16), dv_s[g, :].astype(bf16)], axis=1)
        d = dot(dkv, wkv_ref[...], NT)
        if with_q:
            d = d + dxq_s[r, :]
        dx_ref[r, :] = d.astype(bf16)
        dw_ref[:, 256:768] += dot(x_ref[r, :], dkv, TN)
        db_ref[1:2, :] += jnp.sum(dkv[:, 256:].astype(f32), axis=0, keepdims=True)
    def fin_a(b, _):
        fin_k(b, True)
        return 0
    def fin_b(b, _):
        fin_k(b, False)
        return 0
    lax.fori_loop(0, 8, fin_a, 0)
    lax.fori_loop(8, nb, fin_b, 0)

def attn_bwd(blk, x, k, v, qt, q, lse, do, of, wq, wkv):
    nb = blk.shape[0]
    V = pl.BlockSpec(memory_space=pltpu.VMEM)
    return pl.pallas_call(
        functools.partial(bwd_kernel, nb),
        out_shape=(jax.ShapeDtypeStruct((nb * 128, 512), bf16), jax.ShapeDtypeStruct((512, 768), f32),
                   jax.ShapeDtypeStruct((8, 256), f32)),
        in_specs=[pl.BlockSpec(memory_space=pltpu.SMEM)] + [V] * 10, out_specs=(V,) * 3,
        scratch_shapes=[pltpu.VMEM((1024, 512), f32), pltpu.VMEM((1024, 256), bf16), pltpu.VMEM((256, nb * 128), bf16), pltpu.VMEM((2, 256, 512), bf16), pltpu.VMEM((2, 512, 256), bf16),
                        pltpu.VMEM((2, 256, 512), bf16), pltpu.VMEM((2, 512, 256), bf16), pltpu.VMEM((2, 1, 512), f32),
                        pltpu.VMEM((nb * 128, 256), f32), pltpu.VMEM((nb * 128, 256), f32), pltpu.VMEM((2, 128, 512), f32),
                        pltpu.VMEM((256, 512), jnp.int32)],
        compiler_params=pltpu.CompilerParams(vmem_limit_bytes=60 << 20),
        name="attn_bwd")(blk, x, k, v, qt, q, lse, do, of, wq, wkv)


def dense_kernel(x_ref, cot_ref, att_ref, wo_ref, wu_ref, wd_ref, vec_ref, bup_ref,
                 out_ref, dsm_ref, do_ref, gw_ref, gv_ref, act_s, gp_s, norm_s, dpre_s):
    ff = wu_ref.shape[1]
    chunk = 512
    x = x_ref[...].astype(f32)
    vec = lambda i: vec_ref[i:i + 1, :]
    b_out, g1, s1, b_down, g2, s2 = (vec(i) for i in range(6))
    mean = lambda v: jnp.mean(v, axis=-1, keepdims=True)
    col = lambda v: jnp.sum(v, axis=0, keepdims=True)
    mix = x + dot(att_ref[...], wo_ref[...]) + b_out
    cen = mix - mean(mix)
    r1 = lax.rsqrt(mean(cen * cen) + norm_eps)
    n1 = cen * r1
    normed = n1 * g1 + s1
    nlow = normed.astype(bf16)
    norm_s[...] = nlow
    ffn = None
    for f in range(0, ff, chunk):
        fs = slice(f, f + chunk)
        pre = dot(nlow, wu_ref[:, fs]) + bup_ref[:, fs]
        c0 = math.sqrt(2.0 / math.pi)
        sq = pre * pre
        th = jnp.tanh(c0 * pre * (1.0 + 0.044715 * sq))
        half = 0.5 * (1.0 + th)
        act = (pre * half).astype(bf16)
        act_s[:, fs] = act
        gp_s[:, fs] = half + 0.5 * pre * (1.0 - th * th) * (c0 * (1.0 + 3 * 0.044715 * sq))
        part = dot(act, wd_ref[fs, :])
        ffn = part if ffn is None else ffn + part
    summed = ffn + b_down + normed + x
    cen = summed - mean(summed)
    r2 = lax.rsqrt(mean(cen * cen) + norm_eps)
    n2 = cen * r2
    out_ref[...] = (n2 * g2 + s2).astype(bf16)
    up = cot_ref[...].astype(f32)
    gv_ref[4:5, :] = col(up * n2)
    gv_ref[5:6, :] = col(up)
    dn = up * g2
    dsum = r2 * (dn - mean(dn) - n2 * mean(dn * n2))
    dffn = dsum.astype(bf16)
    gv_ref[3:4, :] = col(dffn.astype(f32))
    dnorm = dsum
    half_rows = wo_ref.shape[0] // 2
    half_ff = ff // 2
    def put(g, at, rows):
        gw_ref[0, at:at + rows, :] = g[:rows].astype(bf16)
        gw_ref[1, at:at + rows, :] = g[rows:].astype(bf16)
    for f in range(0, ff, chunk):
        fs = slice(f, f + chunk)
        dact = dot(dffn, wd_ref[fs, :], NT)
        dpre = (dact * gp_s[:, fs]).astype(bf16)
        gv_ref[8 + f // chunk:9 + f // chunk, :] = col(dpre.astype(f32))
        dnorm = dnorm + dot(dpre, wu_ref[:, fs], NT)
        put(dot(norm_s[...], dpre, TN), half_rows + (f // chunk) * half_rows, half_rows)
        gd = dot(act_s[:, fs], dffn, TN).astype(bf16)
        base = half_rows * (1 + ff // chunk)
        which, off = f // half_ff, f % half_ff
        gw_ref[which, base + off:base + off + chunk, :] = gd
    gv_ref[1:2, :] = col(dnorm * n1)
    gv_ref[2:3, :] = col(dnorm)
    dn = dnorm * g1
    dmix = r1 * (dn - mean(dn) - n1 * mean(dn * n1))
    dsm_ref[...] = dsum + dmix
    dbr = dmix.astype(bf16)
    gv_ref[0:1, :] = col(dbr.astype(f32))
    do_ref[...] = dot(dbr, wo_ref[...], NT).astype(bf16)
    put(dot(att_ref[...], dbr, TN), 0, half_rows)


def dense(x, cot, att, wo, wu, wd, vecs, bup):
    V = pl.BlockSpec(memory_space=pltpu.VMEM)
    tok, dim = x.shape
    ff = wu.shape[1]
    rows = (2 * dim * ff + dim * dim) // 2 // dim
    return pl.pallas_call(
        dense_kernel,
        out_shape=(jax.ShapeDtypeStruct((tok, dim), bf16), jax.ShapeDtypeStruct((tok, dim), f32),
                   jax.ShapeDtypeStruct((tok, dim), bf16), jax.ShapeDtypeStruct((2, rows, dim), bf16),
                   jax.ShapeDtypeStruct((16, dim), f32)),
        in_specs=[V] * 8, out_specs=(V,) * 5,
        scratch_shapes=[pltpu.VMEM((tok, ff), bf16), pltpu.VMEM((tok, ff), f32), pltpu.VMEM((tok, dim), bf16),
                        pltpu.VMEM((8, 128), f32)],
        compiler_params=pltpu.CompilerParams(vmem_limit_bytes=56 << 20),
        name="dense")(x, cot, att, wo, wu, wd, vecs, bup)


def body(block_in, block_order, w_query, b_query, w_key, w_value, b_value, w_out, b_out, gain_one, shift_one,
         w_up, b_up, w_down, b_down, gain_two, shift_two, cotangent, *, nc, nw):
    seqs, rows, dim = block_in.shape
    nz = nc // 4
    hb = rows // BLOCK
    half = dim // 2
    me = lax.axis_index("ctx")
    yy = (me // 2) % 2
    cc = me % 2
    zz = me // 4
    xor = lambda v: [(i, i ^ v) for i in range(nc)]
    ring = [(i, ((i // 4 + 1) % nz) * 4 + i % 4) for i in range(nc)]
    perm = lambda v, p: lax.ppermute(v, "ctx", p)
    gather = lambda v: lax.all_gather(v, "wt", axis=0, tiled=True)
    pick = lambda v, i: lax.dynamic_index_in_dim(v, i, 0, keepdims=False)

    cols = lambda w: lax.dynamic_slice_in_dim(w, cc * half, half, 1)
    wqkv = gather(jnp.concatenate([cols(w_query), cols(w_key), cols(w_value)], axis=1))
    wq, wkv = wqkv[:, :half], wqkv[:, half:]
    small = jnp.concatenate([v.reshape(-1, dim // nw) for v in (b_query, b_value, b_out, gain_one, shift_one, b_down, gain_two, shift_two, b_up)], axis=0)
    small = lax.all_gather(small, "wt", axis=0)
    ffr = b_up.shape[0] // (dim // nw)
    vecs = jnp.transpose(small[:, :8], (1, 0, 2)).reshape(8, dim).astype(f32)
    bup = small[:, 8:].reshape(1, -1).astype(f32)
    bq = lax.dynamic_slice_in_dim(vecs[0:1], cc * half, half, 1)
    bv = lax.dynamic_slice_in_dim(vecs[1:2], cc * half, half, 1)
    bkv = bv
    dvec = vecs[2:8]

    own = pick(block_in, yy)
    got = perm(pick(block_in, 1 - yy), xor(2))
    ring_x = jnp.concatenate([own, got], axis=0)
    pieces = []
    for r in range(nz):
        pieces += [ring_x, perm(ring_x, xor(1))]
        if r < nz - 1:
            ring_x = perm(ring_x, ring)
    x_all = jnp.concatenate(pieces, axis=0)
    r_ids = (zz - jnp.arange(nz, dtype=jnp.int32)) % nz
    quad = (me % 4) ^ jnp.array([0, 2, 1, 3], jnp.int32)
    order_row = pick(block_order, yy)
    slots = (r_ids[:, None, None] * 4 + quad[None, :, None]) * hb + jnp.arange(hb, dtype=jnp.int32)
    blk = order_row[slots.reshape(-1)]

    wo, wu, wd = gather(w_out), gather(w_up), gather(w_down)
    o, lse, k, v, qt, q = attn_fwd(blk, x_all, wq, wkv, bq, bkv)
    o16 = o.astype(bf16)
    o_self = o16[:rows]
    o_y = perm(o16[rows:2 * rows], xor(2))
    o_c = perm(o16[2 * rows:3 * rows], xor(1))
    o_yc = perm(o16[3 * rows:], xor(3))
    by_seq = lambda a, b: jnp.where(yy == 0, jnp.concatenate([a, b], 0), jnp.concatenate([b, a], 0))
    mine, other = by_seq(o_self, o_y), by_seq(o_c, o_yc)
    att = jnp.where(cc == 0, jnp.concatenate([mine, other], 1), jnp.concatenate([other, mine], 1))

    out, dsm, d_o, gw, gv = dense(block_in.reshape(-1, dim), cotangent.reshape(-1, dim), att, wo, wu, wd, dvec, bup)

    d_o = d_o.reshape(seqs, rows, dim)
    d_own, d_oth = pick(d_o, yy), pick(d_o, 1 - yy)
    fh = lambda v, c: lax.dynamic_slice_in_dim(v, c * half, half, 1)
    do_all = jnp.concatenate([fh(d_own, cc), perm(fh(d_oth, cc), xor(2)), perm(fh(d_own, 1 - cc), xor(1)), perm(fh(d_oth, 1 - cc), xor(3))], axis=0)
    dx, gq, gb = attn_bwd(blk, x_all, k, v, qt, q, lse, do_all, o, wq, wkv)
    dx = dx.reshape(nz, 2, 2 * rows, dim)
    part = lambda r: dx[r, 0].astype(f32) + perm(dx[r, 1], xor(1)).astype(f32)
    acc = None
    for r in list(range(1, nz)) + [0]:
        acc = part(r) if acc is None else perm(acc.astype(bf16), ring).astype(f32) + part(r)
    from_y = perm(acc[rows:].astype(bf16), xor(2)).astype(f32)
    dkv_sum = by_seq(acc[:rows], from_y)
    grad_in = (dsm + dkv_sum).astype(bf16).reshape(seqs, rows, dim)

    gvec = jnp.zeros((18, dim), f32).at[:16].set(gv)
    gvec = lax.dynamic_update_slice(gvec, gb[0:1], (16, cc * half))
    gvec = lax.dynamic_update_slice(gvec, gb[1:2], (17, cc * half))
    gvec = lax.psum(gvec, ("ctx", "wt"))
    wi = lax.axis_index("wt")
    def share(vv):
        n = vv.size // nw
        return lax.dynamic_slice_in_dim(vv.reshape(-1), wi * n, n, 0)
    rr = w_query.shape[0]
    ff = w_up.shape[1]
    hr = dim // 2
    g_out = gw[:, :hr].reshape(dim, dim)
    g_up = gw[:, hr:hr + (ff // dim) * hr].reshape(2, ff // dim, hr, dim).transpose(0, 2, 1, 3).reshape(dim, ff)
    g_down = gw[:, hr + (ff // dim) * hr:].reshape(ff, dim)
    zq = jnp.zeros((3, dim, dim), bf16)
    gq3 = gq.astype(bf16).reshape(dim, 3, half).transpose(1, 0, 2)
    g_qkv = lax.dynamic_update_slice(zq, gq3, (0, 0, cc * half))
    def total(g):
        s = lax.psum_scatter(g, "wt", scatter_dimension=0, tiled=True)
        return lax.psum(s, "ctx").astype(f32)
    gqkv = [total(g_qkv[i]) for i in range(3)]
    return (out.reshape(seqs, rows, dim), grad_in, gqkv[0], share(gvec[16]), gqkv[1], gqkv[2], share(gvec[17]), total(g_out), share(gvec[0]),
            share(gvec[1]), share(gvec[2]), total(g_up), share(gvec[8:8 + ff // dim]), total(g_down), share(gvec[3]), share(gvec[4]), share(gvec[5]))


def solution(mesh):
    seq, mat, vec = P("wt", "ctx", None), P("wt", None), P("wt")
    ins = (seq, mat, mat, vec, mat, mat, vec, mat, vec, vec, vec, mat, vec, mat, vec, vec, vec, seq)
    outs = (seq, seq, mat, vec, mat, mat, vec, mat, vec, vec, vec, mat, vec, mat, vec, vec, vec)
    run = functools.partial(body, nc=mesh.shape["ctx"], nw=mesh.shape["wt"])
    return jax.shard_map(run, mesh=mesh, in_specs=ins, out_specs=outs, check_vma=False)
```

```python
import functools
import math

import jax
import jax.numpy as jnp
from jax import lax
from jax.experimental import pallas as pl
from jax.experimental.pallas import tpu as pltpu
from jax.sharding import PartitionSpec as P

norm_eps = 1e-05

BLOCK = 128
LOG2E = 1.4426950408889634
bf16, f32 = jnp.bfloat16, jnp.float32
NT = (((1,), (1,)), ((), ()))
TN = (((0,), (0,)), ((), ()))

def dot(a, b, dims=(((1,), (0,)), ((), ()))):
    return lax.dot_general(a, b, dims, preferred_element_type=f32)

def fwd_kernel(nb, blk_ref, x_ref, wq_ref, wkv_ref, bq_ref, bkv_ref,
               o_ref, lse_ref, k_ref, v_ref, qt_ref, q_ref, vt_s, qs_s, acc_s, m_s, l_s, d_s):
    qs_s[...] = jnp.zeros_like(qs_s)
    d_s[...] = lax.broadcasted_iota(jnp.int32, d_s.shape, 0) - (lax.broadcasted_iota(jnp.int32, d_s.shape, 1) & 127)
    def proj(p, _):
        x = x_ref[pl.ds(pl.multiple_of(p * 256, 256), 256), :]
        kv = dot(x, wkv_ref[...])
        k = kv[:, :256].astype(bf16)
        v = (kv[:, 256:] + bkv_ref[...]).astype(bf16)
        for u in range(2):
            r = pl.ds(pl.multiple_of(blk_ref[2 * p + u] * BLOCK, BLOCK), BLOCK)
            k_ref[r, :] = k[u * BLOCK:(u + 1) * BLOCK]
            vb = v[u * BLOCK:(u + 1) * BLOCK]
            v_ref[r, :] = vb
            vt_s[:, r] = vb.astype(f32).T.astype(bf16)
        return 0
    lax.fori_loop(0, nb // 2, proj, 0)
    def projq(p, _):
        x = x_ref[pl.ds(pl.multiple_of(p * 256, 256), 256), :]
        q = (dot(x, wq_ref[...]) + bq_ref[...]) * (LOG2E / 8.0)
        q_ref[pl.ds(pl.multiple_of(p * 256, 256), 256), :] = q.astype(bf16)
        for u in range(2):
            qt = q[u * BLOCK:(u + 1) * BLOCK].T.astype(bf16)
            qt_ref[2 * p + u] = qt
            for h in range(4):
                qs_s[2 * p + u, 64 * h:64 * h + 64, 128 * h:128 * h + 128] = qt[64 * h:64 * h + 64]
        return 0
    lax.fori_loop(0, 4, projq, 0)

    def pair(p, _):
        b0 = blk_ref[2 * p]
        first_lo = b0 < nb // 2
        lo = jnp.where(first_lo, b0, nb - 1 - b0)
        hi = nb - 1 - lo
        u_lo = 2 * p + jnp.where(first_lo, 0, 1)
        u_hi = 2 * p + jnp.where(first_lo, 1, 0)
        n_lo = lax.div(lo, 2)
        n_hi = lax.div(hi, 2)
        def scores(kt, u):
            return dot(k_ref[pl.ds(pl.multiple_of(kt * 256, 256), 256), :], qs_s[u])
        def pv(kt, p16):
            c = pl.ds(pl.multiple_of(kt * 256, 256), 256)
            return jnp.concatenate([dot(vt_s[0:128, c], p16[:, 0:256]), dot(vt_s[128:256, c], p16[:, 256:512])], axis=1)
        for (s, kt, u, qp) in ((0, n_lo, u_lo, lo), (1, n_hi, u_hi, hi)):
            st = scores(kt, u)
            st = jnp.where(d_s[...] <= qp * 128 - kt * 256, st, -1e30)
            m = jnp.max(st, axis=0, keepdims=True)
            pr = jnp.exp2(st - m)
            m_s[s] = m
            l_s[s] = jnp.sum(pr, axis=0, keepdims=True)
            acc_s[s] = pv(kt, pr.astype(bf16))
        for t in range(nb // 2 - 1):
            is_lo = t < n_lo
            s = jnp.where(is_lo, 0, 1)
            kt = jnp.where(is_lo, t, t - n_lo)
            u = jnp.where(is_lo, u_lo, u_hi)
            st = scores(kt, u)
            m_old = m_s[s]
            m = jnp.maximum(m_old, jnp.max(st, axis=0, keepdims=True))
            pr = jnp.exp2(st - m)
            al = jnp.exp2(m_old - m)
            m_s[s] = m
            l_s[s] = l_s[s] * al + jnp.sum(pr, axis=0, keepdims=True)
            acc_s[s] = acc_s[s] * al + pv(kt, pr.astype(bf16))
        for (s, u) in ((0, u_lo), (1, u_hi)):
            l = l_s[s]
            lse_ref[u] = m_s[s] + jnp.log2(l)
            a = acc_s[s] * (1.0 / l)
            ot = jnp.concatenate([a[64 * (h % 2):64 * (h % 2) + 64, 128 * h:128 * h + 128] for h in range(4)], axis=0)
            o_ref[pl.ds(pl.multiple_of(u * 128, 128), 128), :] = ot.T
        return 0
    lax.fori_loop(0, 4, pair, 0)

def attn_fwd(blk, x, wq, wkv, bq, bkv):
    nb = blk.shape[0]
    V = pl.BlockSpec(memory_space=pltpu.VMEM)
    return pl.pallas_call(
        functools.partial(fwd_kernel, nb),
        out_shape=(jax.ShapeDtypeStruct((1024, 256), f32), jax.ShapeDtypeStruct((8, 1, 512), f32),
                   jax.ShapeDtypeStruct((nb * 128, 256), bf16), jax.ShapeDtypeStruct((nb * 128, 256), bf16),
                   jax.ShapeDtypeStruct((8, 256, 128), bf16), jax.ShapeDtypeStruct((1024, 256), bf16)),
        in_specs=[pl.BlockSpec(memory_space=pltpu.SMEM)] + [V] * 5, out_specs=(V,) * 6,
        scratch_shapes=[pltpu.VMEM((256, nb * 128), bf16), pltpu.VMEM((8, 256, 512), bf16), pltpu.VMEM((2, 128, 512), f32),
                        pltpu.VMEM((2, 1, 512), f32), pltpu.VMEM((2, 1, 512), f32), pltpu.VMEM((256, 512), jnp.int32)],
        compiler_params=pltpu.CompilerParams(vmem_limit_bytes=56 << 20),
        name="attn_fwd")(blk, x, wq, wkv, bq, bkv)

def bwd_kernel(nb, blk_ref, x_ref, k_ref, v_ref, qt_ref, q_ref, lse_ref, do_ref, of_ref, wq_ref, wkv_ref,
               dx_ref, gq_ref, db_ref, dw_ref, dxq_s, dqa_s, kt_s, qs_s, qn_s, dot_s, don_s, dl_s, dk_s, dv_s, dq_s, d_s):
    qs_s[...] = jnp.zeros_like(qs_s)
    qn_s[...] = jnp.zeros_like(qn_s)
    dot_s[...] = jnp.zeros_like(dot_s)
    don_s[...] = jnp.zeros_like(don_s)
    dk_s[...] = jnp.zeros_like(dk_s)
    dv_s[...] = jnp.zeros_like(dv_s)
    d_s[...] = lax.broadcasted_iota(jnp.int32, d_s.shape, 0) - (lax.broadcasted_iota(jnp.int32, d_s.shape, 1) & 127)
    def prep_k(j, _):
        r = pl.ds(pl.multiple_of(j * 256, 256), 256)
        kt_s[:, r] = k_ref[r, :].astype(f32).T.astype(bf16)
        return 0
    lax.fori_loop(0, nb // 2, prep_k, 0)
    def prep_q(u, s):
        r = pl.ds(pl.multiple_of(u * 128, 128), 128)
        do = do_ref[r, :]
        doT = do.astype(f32).T
        dlT = doT * of_ref[r, :].T
        q = q_ref[r, :]
        qt = qt_ref[u]
        for h in range(4):
            hs = slice(64 * h, 64 * h + 64)
            cs = slice(128 * h, 128 * h + 128)
            qs_s[s, hs, cs] = qt[hs]
            dot_s[s, hs, cs] = doT[hs].astype(bf16)
            dl_s[s, :, cs] = jnp.sum(dlT[hs], axis=0, keepdims=True)
            qn_s[s, cs, hs] = q[:, hs]
            don_s[s, cs, hs] = do[:, hs]
    def pair(p, _):
        b0 = blk_ref[2 * p]
        first_lo = b0 < nb // 2
        lo = jnp.where(first_lo, b0, nb - 1 - b0)
        hi = nb - 1 - lo
        u_lo = 2 * p + jnp.where(first_lo, 0, 1)
        u_hi = 2 * p + jnp.where(first_lo, 1, 0)
        n_lo = lax.div(lo, 2)
        n_hi = lax.div(hi, 2)
        prep_q(u_lo, 0)
        prep_q(u_hi, 1)
        def step(s, kt, u, qp, masked):
            r = pl.ds(pl.multiple_of(kt * 256, 256), 256)
            st = dot(k_ref[r, :], qs_s[s]) - lse_ref[u]
            if masked:
                st = jnp.where(d_s[...] <= qp * 128 - kt * 256, st, -1e30)
            pr = jnp.exp2(st)
            dp = dot(v_ref[r, :], dot_s[s]) - dl_s[s]
            ds = (pr * dp).astype(bf16)
            dv_s[r, :] += dot(pr.astype(bf16), don_s[s])
            dk_s[r, :] += dot(ds, qn_s[s])
            dq = jnp.concatenate([dot(kt_s[0:128, r], ds[:, 0:256]), dot(kt_s[128:256, r], ds[:, 256:512])], axis=1)
            if masked:
                dq_s[s] = dq
            else:
                dq_s[s] += dq
        step(0, n_lo, u_lo, lo, True)
        step(1, n_hi, u_hi, hi, True)
        for t in range(nb // 2 - 1):
            is_lo = t < n_lo
            step(jnp.where(is_lo, 0, 1), jnp.where(is_lo, t, t - n_lo), jnp.where(is_lo, u_lo, u_hi), 0, False)
        for (s, u) in ((0, u_lo), (1, u_hi)):
            a = dq_s[s] * 0.125
            dqT = jnp.concatenate([a[64 * (h % 2):64 * (h % 2) + 64, 128 * h:128 * h + 128] for h in range(4)], axis=0)
            dqa_s[pl.ds(pl.multiple_of(u * 128, 128), 128), :] = dqT.T.astype(bf16)
        return 0
    lax.fori_loop(0, 4, pair, 0)
    dw_ref[...] = jnp.zeros_like(dw_ref)
    db_ref[...] = jnp.zeros_like(db_ref)
    def fin_q(u, _):
        r = pl.ds(pl.multiple_of(u * 128, 128), 128)
        dq = dqa_s[r, :]
        dxq_s[r, :] = dot(dq, wq_ref[...], NT)
        dw_ref[:, 0:256] += dot(x_ref[r, :], dq, TN)
        db_ref[0:1, :] += jnp.sum(dq.astype(f32), axis=0, keepdims=True)
        return 0
    lax.fori_loop(0, 8, fin_q, 0)
    def fin_k(b, with_q):
        r = pl.ds(pl.multiple_of(b * 128, 128), 128)
        g = pl.ds(pl.multiple_of(blk_ref[b] * 128, 128), 128)
        dkv = jnp.concatenate([(dk_s[g, :] * (1.0 / LOG2E)).astype(bf16), dv_s[g, :].astype(bf16)], axis=1)
        d = dot(dkv, wkv_ref[...], NT)
        if with_q:
            d = d + dxq_s[r, :]
        dx_ref[r, :] = d.astype(bf16)
        dw_ref[:, 256:768] += dot(x_ref[r, :], dkv, TN)
        db_ref[1:2, :] += jnp.sum(dkv[:, 256:].astype(f32), axis=0, keepdims=True)
    def fin_a(b, _):
        fin_k(b, True)
        return 0
    def fin_b(b, _):
        fin_k(b, False)
        return 0
    lax.fori_loop(0, 8, fin_a, 0)
    lax.fori_loop(8, nb, fin_b, 0)
    for k in range(2):
        for m in range(3):
            gq_ref[k, m * 256:m * 256 + 256, :] = dw_ref[k * 256:k * 256 + 256, m * 256:m * 256 + 256].astype(bf16)

def attn_bwd(blk, x, k, v, qt, q, lse, do, of, wq, wkv):
    nb = blk.shape[0]
    V = pl.BlockSpec(memory_space=pltpu.VMEM)
    return pl.pallas_call(
        functools.partial(bwd_kernel, nb),
        out_shape=(jax.ShapeDtypeStruct((nb * 128, 512), bf16), jax.ShapeDtypeStruct((2, 768, 256), bf16),
                   jax.ShapeDtypeStruct((8, 256), f32)),
        in_specs=[pl.BlockSpec(memory_space=pltpu.SMEM)] + [V] * 10, out_specs=(V,) * 3,
        scratch_shapes=[pltpu.VMEM((512, 768), f32), pltpu.VMEM((1024, 512), f32), pltpu.VMEM((1024, 256), bf16), pltpu.VMEM((256, nb * 128), bf16), pltpu.VMEM((2, 256, 512), bf16), pltpu.VMEM((2, 512, 256), bf16),
                        pltpu.VMEM((2, 256, 512), bf16), pltpu.VMEM((2, 512, 256), bf16), pltpu.VMEM((2, 1, 512), f32),
                        pltpu.VMEM((nb * 128, 256), f32), pltpu.VMEM((nb * 128, 256), f32), pltpu.VMEM((2, 128, 512), f32),
                        pltpu.VMEM((256, 512), jnp.int32)],
        compiler_params=pltpu.CompilerParams(vmem_limit_bytes=60 << 20),
        name="attn_bwd")(blk, x, k, v, qt, q, lse, do, of, wq, wkv)


def dense_kernel(x_ref, cot_ref, att_ref, wo_ref, wu_ref, wd_ref, vec_ref, bup_ref,
                 out_ref, dsm_ref, do_ref, gw_ref, gv_ref, act_s, gp_s, norm_s, dpre_s):
    ff = wu_ref.shape[1]
    chunk = 512
    x = x_ref[...].astype(f32)
    vec = lambda i: vec_ref[i:i + 1, :]
    b_out, g1, s1, b_down, g2, s2 = (vec(i) for i in range(6))
    mean = lambda v: jnp.mean(v, axis=-1, keepdims=True)
    col = lambda v: jnp.sum(v, axis=0, keepdims=True)
    mix = x + dot(att_ref[...], wo_ref[...]) + b_out
    cen = mix - mean(mix)
    r1 = lax.rsqrt(mean(cen * cen) + norm_eps)
    n1 = cen * r1
    normed = n1 * g1 + s1
    nlow = normed.astype(bf16)
    norm_s[...] = nlow
    ffn = None
    for f in range(0, ff, chunk):
        fs = slice(f, f + chunk)
        pre = dot(nlow, wu_ref[:, fs]) + bup_ref[:, fs]
        c0 = math.sqrt(2.0 / math.pi)
        sq = pre * pre
        th = jnp.tanh(c0 * pre * (1.0 + 0.044715 * sq))
        half = 0.5 * (1.0 + th)
        act = (pre * half).astype(bf16)
        act_s[:, fs] = act
        gp_s[:, fs] = half + 0.5 * pre * (1.0 - th * th) * (c0 * (1.0 + 3 * 0.044715 * sq))
        part = dot(act, wd_ref[fs, :])
        ffn = part if ffn is None else ffn + part
    summed = ffn + b_down + normed + x
    cen = summed - mean(summed)
    r2 = lax.rsqrt(mean(cen * cen) + norm_eps)
    n2 = cen * r2
    out_ref[...] = (n2 * g2 + s2).astype(bf16)
    up = cot_ref[...].astype(f32)
    gv_ref[4:5, :] = col(up * n2)
    gv_ref[5:6, :] = col(up)
    dn = up * g2
    dsum = r2 * (dn - mean(dn) - n2 * mean(dn * n2))
    dffn = dsum.astype(bf16)
    gv_ref[3:4, :] = col(dffn.astype(f32))
    dnorm = dsum
    half_rows = wo_ref.shape[0] // 2
    half_ff = ff // 2
    def put(g, at, rows):
        gw_ref[0, at:at + rows, :] = g[:rows].astype(bf16)
        gw_ref[1, at:at + rows, :] = g[rows:].astype(bf16)
    for f in range(0, ff, chunk):
        fs = slice(f, f + chunk)
        dact = dot(dffn, wd_ref[fs, :], NT)
        dpre = (dact * gp_s[:, fs]).astype(bf16)
        gv_ref[8 + f // chunk:9 + f // chunk, :] = col(dpre.astype(f32))
        dnorm = dnorm + dot(dpre, wu_ref[:, fs], NT)
        put(dot(norm_s[...], dpre, TN), half_rows + (f // chunk) * half_rows, half_rows)
        gd = dot(act_s[:, fs], dffn, TN).astype(bf16)
        base = half_rows * (1 + ff // chunk)
        which, off = f // half_ff, f % half_ff
        gw_ref[which, base + off:base + off + chunk, :] = gd
    gv_ref[1:2, :] = col(dnorm * n1)
    gv_ref[2:3, :] = col(dnorm)
    dn = dnorm * g1
    dmix = r1 * (dn - mean(dn) - n1 * mean(dn * n1))
    dsm_ref[...] = dsum + dmix
    dbr = dmix.astype(bf16)
    gv_ref[0:1, :] = col(dbr.astype(f32))
    do_ref[...] = dot(dbr, wo_ref[...], NT).astype(bf16)
    put(dot(att_ref[...], dbr, TN), 0, half_rows)


def dense(x, cot, att, wo, wu, wd, vecs, bup):
    V = pl.BlockSpec(memory_space=pltpu.VMEM)
    tok, dim = x.shape
    ff = wu.shape[1]
    rows = (2 * dim * ff + dim * dim) // 2 // dim
    return pl.pallas_call(
        dense_kernel,
        out_shape=(jax.ShapeDtypeStruct((tok, dim), bf16), jax.ShapeDtypeStruct((tok, dim), f32),
                   jax.ShapeDtypeStruct((tok, dim), bf16), jax.ShapeDtypeStruct((2, rows, dim), bf16),
                   jax.ShapeDtypeStruct((16, dim), f32)),
        in_specs=[V] * 8, out_specs=(V,) * 5,
        scratch_shapes=[pltpu.VMEM((tok, ff), bf16), pltpu.VMEM((tok, ff), f32), pltpu.VMEM((tok, dim), bf16),
                        pltpu.VMEM((8, 128), f32)],
        compiler_params=pltpu.CompilerParams(vmem_limit_bytes=56 << 20),
        name="dense")(x, cot, att, wo, wu, wd, vecs, bup)


MESH = pl.DeviceIdType.MESH


def places(nz):
    me, wi = lax.axis_index("ctx"), lax.axis_index("wt")
    z, y, c = me // 4, lax.rem(me // 2, 2), lax.rem(me, 2)
    low = lax.rem(me, 4)
    at = lambda zz, ll: (zz * 4 + ll, wi)
    to = dict(up=at(lax.rem(z + 1, nz), low), down=at(lax.rem(z + nz - 1, nz), low), core=at(z, low + 1 - 2 * c), y=at(z, low + 2 - 4 * y),
              x=(me, 1 - wi))
    return me, wi, z, y, c, low, to


def meet(targets):
    bar = pltpu.get_barrier_semaphore()
    for t in targets:
        pl.semaphore_signal(bar, inc=1, device_id=t, device_id_type=MESH)
    pl.semaphore_wait(bar, len(targets))


class Wires:
    def __init__(self, send, recv):
        self.send, self.recv, self.n, self.live = send, recv, 0, []

    def make(self, src, dst, to):
        cp = pltpu.make_async_remote_copy(src, dst, self.send.at[self.n], self.recv.at[self.n], device_id=to, device_id_type=MESH)
        self.n += 1
        return cp

    def go(self, src, dst, to):
        cp = self.make(src, dst, to)
        cp.start()
        self.live.append(cp)
        return cp

    def drain(self):
        for cp in self.live:
            cp.wait_send()


def rows_of(start, size, mult=16):
    return pl.ds(pl.multiple_of(start, mult), size)


def gather_kernel(nz, with_w, *refs):
    if with_w:
        (x_ref, wq_ref, wk_ref, wv_ref, wo_ref, wu_ref, wd_ref, sm_ref,
         xall, wqkv, wo, wu, wd, sm, send, recv, lsem) = refs
    else:
        x_ref, xall, send, recv, lsem = refs
    me, wi, z, y, c, low, to = places(nz)
    rows = x_ref.shape[1]
    local = []

    def copy(src, dst):
        cp = pltpu.make_async_copy(src, dst, lsem.at[len(local)])
        cp.start()
        local.append(cp)

    copy(x_ref.at[y], xall.at[0, 0])
    if with_w:
        R, half = wq_ref.shape[0], wq_ref.shape[1] // 2
        for i, w in enumerate((wq_ref, wk_ref, wv_ref)):
            copy(w.at[:, rows_of(c * half, half, 128)], wqkv.at[rows_of(wi * R, R), pl.ds(i * half, half)])
        for w, full in ((wo_ref, wo), (wu_ref, wu), (wd_ref, wd)):
            n = w.shape[0]
            copy(w, full.at[rows_of(wi * n, n)])
        copy(sm_ref, sm.at[wi])
    near = [to["up"], to["down"], to["core"], to["y"]] + ([to["x"]] if with_w else [])
    meet(near)
    wires = Wires(send, recv)
    yx = wires.go(x_ref.at[1 - y], xall.at[0, 1], to["y"])
    ring = {(1, 0): wires.go(x_ref.at[y], xall.at[1, 0], to["up"])}
    core = {(0, 0): wires.go(x_ref.at[y], xall.at[0, 2], to["core"])}
    if with_w:
        xs = []
        for i, w in enumerate((wq_ref, wk_ref, wv_ref)):
            xs.append(wires.go(w.at[:, rows_of(c * half, half, 128)], wqkv.at[rows_of(wi * R, R), pl.ds(i * half, half)], to["x"]))
        xs.append(wires.go(sm_ref, sm.at[wi], to["x"]))
        big = []
        for w, full in ((wo_ref, wo), (wu_ref, wu), (wd_ref, wd)):
            n = w.shape[0]
            h = n // 2
            cp = wires.go(w.at[rows_of(c * h, h)], full.at[rows_of(wi * n + c * h, h)], to["x"])
            big.append((cp, full, rows_of((1 - wi) * n + c * h, h)))
    yx.wait_recv()
    ring[1, 1] = wires.go(xall.at[0, 1], xall.at[1, 1], to["up"])
    core[0, 1] = wires.go(xall.at[0, 1], xall.at[0, 3], to["core"])
    shared = []
    for r in range(1, nz):
        for s in range(2):
            ring[r, s].wait_recv()
            if r < nz - 1:
                ring[r + 1, s] = wires.go(xall.at[r, s], xall.at[r + 1, s], to["up"])
            core[r, s] = wires.go(xall.at[r, s], xall.at[r, 2 + s], to["core"])
        if with_w and r - 1 < len(big):
            cp, full, where = big[r - 1]
            cp.wait_recv()
            shared.append(wires.go(full.at[where], full.at[where], to["core"]))
    if with_w:
        for cp, full, where in big[nz - 1:]:
            cp.wait_recv()
            shared.append(wires.go(full.at[where], full.at[where], to["core"]))
        for cp in xs + shared:
            cp.wait_recv()
    for cp in core.values():
        cp.wait_recv()
    wires.drain()
    for cp in local:
        cp.wait()


def gather_all(nz, x, weights=None, small=None):
    A = pl.BlockSpec(memory_space=pl.ANY)
    sds = jax.ShapeDtypeStruct
    rows, dim = x.shape[1:]
    outs = [sds((nz, 4, rows, dim), bf16)]
    ins = [x]
    ncopy = 1 + 2 * (nz - 1) + 2 * nz
    if weights is not None:
        wq, wk, wv, wo, wu, wd = weights
        ins += list(weights) + [small]
        outs += [sds((dim, 3 * dim // 2), bf16)] + [sds((2 * w.shape[0], w.shape[1]), bf16) for w in (wo, wu, wd)] + [sds((2,) + small.shape, bf16)]
        ncopy += 10
    return pl.pallas_call(
        functools.partial(gather_kernel, nz, weights is not None),
        out_shape=tuple(outs), in_specs=[A] * len(ins), out_specs=(A,) * len(outs),
        scratch_shapes=[pltpu.SemaphoreType.DMA((ncopy,)), pltpu.SemaphoreType.DMA((ncopy,)), pltpu.SemaphoreType.DMA((8,))],
        compiler_params=pltpu.CompilerParams(collective_id=1, has_side_effects=True, vmem_limit_bytes=16 << 20),
        name="gather_all")(*ins)


def add_into(dst, parts, rows, step=64):
    def body(i, _):
        r = rows_of(i * step, step)
        total = parts[0](r)[...].astype(f32)
        for p in parts[1:]:
            total = total + p(r)[...].astype(f32)
        d = dst(r)
        d[...] = total.astype(bf16)
        return 0
    lax.fori_loop(0, rows // step, body, 0)


def offset(ref, lead, start):
    def view(r):
        at = pl.ds(pl.multiple_of(start + r.start, 16), r.size)
        return ref.at[lead + (at,)]
    return view


STREAMS = ((768, 512), (768, 512), (768, 512), (1536, 256))


def reduce_kernel(nz, dx_ref, gw_ref, gq_ref, gv_ref, dxo, go, gqo, gvo,
                  dx_core, dx_acc, dx_in, cr, cs, xr, xs_, yr, ys_, zr, cq, xrq, xsq, yrq, ysq, zrq, gvs, gvr, send, recv):
    me, wi, z, y, c, low, to = places(nz)
    zto = [(lax.rem(z + d, nz) * 4 + low, wi) for d in range(1, nz)]
    meet([to["core"], to["y"], to["x"]] + zto)
    w = Wires(send, recv)
    hrow = 256
    got = {}
    for s in range(3):
        got["c", s] = w.go(gw_ref.at[:, rows_of(s * 768 + (1 - c) * 384, 384)], cr.at[s], to["core"])
        r = s + 1
        got["d", r] = w.go(dx_ref.at[r, pl.ds(512, 512)], dx_core.at[r], to["core"])
    got["d", 0] = w.go(dx_ref.at[0, pl.ds(512, 512)], dx_core.at[0], to["core"])

    width = [384, 384, 384, 768]
    n_y = [v // 2 for v in width]
    n_z = [v // (2 * nz) for v in width]
    X_in = [xr.at[s] for s in range(3)] + [xrq]
    X_sum = [xs_.at[s] for s in range(3)] + [xsq]
    Y_in = [yr.at[s] for s in range(3)] + [yrq]
    Y_sum = [ys_.at[s] for s in range(3)] + [ysq]
    Z_in = [zr.at[s] for s in range(3)] + [zrq]
    out = [go.at[s] for s in range(3)] + [gqo]

    def x_send(s):
        if s < 3:
            got["c", s].wait_recv()
            for k in range(2):
                add_into(offset(cs, (s, k), 0), [offset(gw_ref, (k,), s * 768 + c * 384), offset(cr, (s, k), 0)], 384)
            got["x", s] = w.go(cs.at[s, 1 - wi], X_in[s], to["x"])
        else:
            got["x", s] = w.go(gq_ref.at[1 - wi], X_in[s], to["x"])

    def y_send(s):
        got["x", s].wait_recv()
        mine = offset(cs, (s, wi), 0) if s < 3 else offset(gq_ref, (wi,), 0)
        add_into(offset(X_sum[s], (), 0), [mine, offset(X_in[s], (), 0)], width[s])
        got["y", s] = w.go(X_sum[s].at[rows_of((1 - y) * n_y[s], n_y[s])], Y_in[s], to["y"])

    def z_send(s):
        got["y", s].wait_recv()
        add_into(offset(Y_sum[s], (), 0), [offset(X_sum[s], (), y * n_y[s]), offset(Y_in[s], (), 0)], n_y[s])
        for d in range(1, nz):
            zd = lax.rem(z + d, nz)
            got["z", s, d] = w.go(Y_sum[s].at[rows_of(zd * n_z[s], n_z[s])], Z_in[s].at[d - 1], zto[d - 1])

    def z_share(s):
        for d in range(1, nz):
            got["z", s, d].wait_recv()
        base = c * width[s] + y * n_y[s] + z * n_z[s]
        add_into(offset(out[s], (), base), [offset(Y_sum[s], (), z * n_z[s])] + [offset(Z_in[s], (d,), 0) for d in range(nz - 1)], n_z[s], 48)
        at = rows_of(base, n_z[s])
        for d in range(1, nz):
            got["zs", s, d] = w.go(out[s].at[at], out[s].at[at], zto[d - 1])

    def y_share(s):
        for d in range(1, nz):
            got["zs", s, d].wait_recv()
        at = rows_of(c * width[s] + y * n_y[s], n_y[s])
        got["ys", s] = w.go(out[s].at[at], out[s].at[at], to["y"])

    def c_share(s):
        got["ys", s].wait_recv()
        at = rows_of(c * width[s], width[s])
        got["cs", s] = w.go(out[s].at[at], out[s].at[at], to["core"])

    def fold(r):
        got["d", r].wait_recv()
        add_into(offset(dx_acc, (r,), 0), [offset(dx_ref, (r,), 0), offset(dx_core, (r,), 0)], 512)

    def hop(r, h):
        if r != 1:
            got["r", r, h].wait_recv()
            if r:
                add_into(offset(dx_acc, (r,), h * hrow), [offset(dx_acc, (r,), h * hrow), offset(dx_in, (r,), h * hrow)], hrow)
            else:
                dst = offset(dxo, (0,), 0) if h == 0 else offset(dx_acc, (0,), hrow)
                add_into(dst, [offset(dx_acc, (0,), h * hrow), offset(dx_in, (0,), h * hrow)], hrow)
        at = pl.ds(h * hrow, hrow)
        if r:
            n = (r + 1) % nz
            got["r", n, h] = w.go(dx_acc.at[r, at], dx_in.at[n, at], to["up"])
        elif h:
            got["dy"] = w.go(dx_acc.at[0, at], dxo.at[1], to["y"])

    vec_to = [to["core"], to["y"], to["x"]] + [(zz * 4 + low, wi) for zz in (z + 1 - 2 * lax.rem(z, 2), z + 2 - 4 * (z // 2))]

    def vec_send(k):
        if k == 0:
            gvs[0] = gv_ref[...]
        else:
            got["v", k - 1].wait_recv()
            gvs[k] = gvs[k - 1] + gvr[k - 1]
        if k < 5:
            got["v", k] = w.go(gvs.at[k], gvr.at[k], vec_to[k])
        else:
            gvo[...] = gvs[5]

    x_send(3)
    vec_send(0)
    fold(1)
    hop(1, 1)
    hop(1, 0)
    x_send(0)
    vec_send(1)
    x_send(1)
    fold(2)
    hop(2, 1)
    x_send(2)
    vec_send(2)
    fold(3)
    y_send(3)
    hop(2, 0)
    vec_send(3)
    fold(0)
    z_send(3)
    hop(3, 1)
    y_send(0)
    z_share(3)
    vec_send(4)
    hop(3, 0)
    z_send(0)
    vec_send(5)
    y_share(3)
    y_send(1)
    hop(0, 1)
    z_share(0)
    c_share(3)
    z_send(1)
    y_send(2)
    hop(0, 0)
    y_share(0)
    z_share(1)
    z_send(2)
    c_share(0)
    y_share(1)
    z_share(2)
    c_share(1)
    y_share(2)
    c_share(2)
    for s in range(4):
        got["cs", s].wait_recv()
    got["dy"].wait_recv()
    w.drain()


def reduce_all(nz, dx, gw, gq, gv):
    V = pl.BlockSpec(memory_space=pltpu.VMEM)
    sds = jax.ShapeDtypeStruct
    M = lambda *s: pltpu.VMEM(s, bf16)
    ncopy = 100
    return pl.pallas_call(
        functools.partial(reduce_kernel, nz),
        out_shape=(sds((2, 256, 512), bf16), sds((3, 768, 512), bf16), sds((1536, 256), bf16), sds(gv.shape, f32)),
        in_specs=[V] * 4, out_specs=(V,) * 4,
        scratch_shapes=[M(nz, 512, 512), M(nz, 512, 512), M(nz, 512, 512), M(3, 2, 384, 512), M(3, 2, 384, 512),
                        M(3, 384, 512), M(3, 384, 512), M(3, 192, 512), M(3, 192, 512), M(3, nz - 1, 48, 512),
                        M(8, 128), M(768, 256), M(768, 256), M(384, 256), M(384, 256), M(nz - 1, 96, 256),
                        pltpu.VMEM((6,) + gv.shape, f32), pltpu.VMEM((5,) + gv.shape, f32),
                        pltpu.SemaphoreType.DMA((ncopy,)), pltpu.SemaphoreType.DMA((ncopy,))],
        compiler_params=pltpu.CompilerParams(collective_id=2, has_side_effects=True, vmem_limit_bytes=60 << 20),
        name="reduce_all")(dx, gw, gq, gv)


def body(block_in, block_order, w_query, b_query, w_key, w_value, b_value, w_out, b_out, gain_one, shift_one,
         w_up, b_up, w_down, b_down, gain_two, shift_two, cotangent, *, nc, nw):
    seqs, rows, dim = block_in.shape
    nz = nc // 4
    hb = rows // BLOCK
    half = dim // 2
    me = lax.axis_index("ctx")
    yy = (me // 2) % 2
    cc = me % 2
    zz = me // 4
    xor = lambda v: [(i, i ^ v) for i in range(nc)]
    ring = [(i, ((i // 4 + 1) % nz) * 4 + i % 4) for i in range(nc)]
    perm = lambda v, p: lax.ppermute(v, "ctx", p)
    gather = lambda v: lax.all_gather(v, "wt", axis=0, tiled=True)
    pick = lambda v, i: lax.dynamic_index_in_dim(v, i, 0, keepdims=False)

    ours = nw == 2 and nz == 4
    small = jnp.concatenate([v.reshape(-1, dim // nw) for v in (b_query, b_value, b_out, gain_one, shift_one, b_down, gain_two, shift_two, b_up)], axis=0)
    if ours:
        small = jnp.pad(small, ((0, -small.shape[0] % 16), (0, 0)))
        x_all, wqkv, wo, wu, wd, small = gather_all(nz, block_in, (w_query, w_key, w_value, w_out, w_up, w_down), small)
    else:
        cols = lambda w: lax.dynamic_slice_in_dim(w, cc * half, half, 1)
        wqkv = gather(jnp.concatenate([cols(w_query), cols(w_key), cols(w_value)], axis=1))
        small = lax.all_gather(small, "wt", axis=0)
        wo, wu, wd = gather(w_out), gather(w_up), gather(w_down)
        x_all = gather_all(nz, block_in)[0]
    x_all = x_all.reshape(-1, dim)
    wq, wkv = wqkv[:, :half], wqkv[:, half:]
    vecs = jnp.transpose(small[:, :8], (1, 0, 2)).reshape(8, dim).astype(f32)
    bup = small[:, 8:8 + b_up.shape[0] // (dim // nw)].reshape(1, -1).astype(f32)
    bq = lax.dynamic_slice_in_dim(vecs[0:1], cc * half, half, 1)
    bkv = lax.dynamic_slice_in_dim(vecs[1:2], cc * half, half, 1)
    dvec = vecs[2:8]
    r_ids = (zz - jnp.arange(nz, dtype=jnp.int32)) % nz
    quad = (me % 4) ^ jnp.array([0, 2, 1, 3], jnp.int32)
    order_row = pick(block_order, yy)
    slots = (r_ids[:, None, None] * 4 + quad[None, :, None]) * hb + jnp.arange(hb, dtype=jnp.int32)
    blk = order_row[slots.reshape(-1)]

    o, lse, k, v, qt, q = attn_fwd(blk, x_all, wq, wkv, bq, bkv)
    o16 = o.astype(bf16)
    o_self = o16[:rows]
    o_y = perm(o16[rows:2 * rows], xor(2))
    o_c = perm(o16[2 * rows:3 * rows], xor(1))
    o_yc = perm(o16[3 * rows:], xor(3))
    by_seq = lambda a, b: jnp.where(yy == 0, jnp.concatenate([a, b], 0), jnp.concatenate([b, a], 0))
    mine, other = by_seq(o_self, o_y), by_seq(o_c, o_yc)
    att = jnp.where(cc == 0, jnp.concatenate([mine, other], 1), jnp.concatenate([other, mine], 1))

    out, dsm, d_o, gw, gv = dense(block_in.reshape(-1, dim), cotangent.reshape(-1, dim), att, wo, wu, wd, dvec, bup)

    d_o = d_o.reshape(seqs, rows, dim)
    d_own, d_oth = pick(d_o, yy), pick(d_o, 1 - yy)
    fh = lambda v, c: lax.dynamic_slice_in_dim(v, c * half, half, 1)
    do_all = jnp.concatenate([fh(d_own, cc), perm(fh(d_oth, cc), xor(2)), perm(fh(d_own, 1 - cc), xor(1)), perm(fh(d_oth, 1 - cc), xor(3))], axis=0)
    dx, gq, gb = attn_bwd(blk, x_all, k, v, qt, q, lse, do_all, o, wq, wkv)
    gvec = jnp.zeros((24, dim), f32).at[:16].set(gv)
    gvec = lax.dynamic_update_slice(gvec, gb[0:1], (16, cc * half))
    gvec = lax.dynamic_update_slice(gvec, gb[1:2], (17, cc * half))
    wi = lax.axis_index("wt")
    ff, hr = w_up.shape[1], dim // 2
    nu = ff // dim
    if ours:
        dxo, go, gqo, gvec = reduce_all(nz, dx.reshape(nz, 4 * rows, dim), gw, gq, gvec)
        go = go.reshape(-1, dim)
        t_out = go[:hr].astype(f32)
        t_up = go[hr:hr + nu * hr].astype(f32).reshape(nu, hr, dim).transpose(1, 0, 2).reshape(hr, ff)
        t_down = go[hr + nu * hr:].astype(f32)
        gqo = gqo.reshape(2, 3, hr, half).transpose(1, 2, 0, 3).reshape(3, hr, dim)
        t_qkv = [gqo[i].astype(f32) for i in range(3)]
        dkv_sum = by_seq(dxo[0], dxo[1]).astype(f32)
    else:
        dx = dx.reshape(nz, 2, 2 * rows, dim)
        part = lambda r: dx[r, 0].astype(f32) + perm(dx[r, 1], xor(1)).astype(f32)
        acc = None
        for r in list(range(1, nz)) + [0]:
            acc = part(r) if acc is None else perm(acc.astype(bf16), ring).astype(f32) + part(r)
        from_y = perm(acc[rows:].astype(bf16), xor(2)).astype(f32)
        dkv_sum = by_seq(acc[:rows], from_y)
        gvec = lax.psum(gvec, ("ctx", "wt"))
        g_out = gw[:, :hr].reshape(dim, dim)
        g_up = gw[:, hr:hr + nu * hr].reshape(2, nu, hr, dim).transpose(0, 2, 1, 3).reshape(dim, ff)
        g_down = gw[:, hr + nu * hr:].reshape(ff, dim)
        gq3 = gq.reshape(2, 3, hr, half).transpose(1, 0, 2, 3).reshape(3, dim, half)
        g_qkv = lax.dynamic_update_slice(jnp.zeros((3, dim, dim), bf16), gq3, (0, 0, cc * half))
        total = lambda g: lax.psum(lax.psum_scatter(g, "wt", scatter_dimension=0, tiled=True), "ctx").astype(f32)
        t_out, t_up, t_down = total(g_out), total(g_up), total(g_down)
        t_qkv = [total(g_qkv[i]) for i in range(3)]
    grad_in = (dsm + dkv_sum).astype(bf16).reshape(seqs, rows, dim)

    def share(vv):
        n = vv.size // nw
        return lax.dynamic_slice_in_dim(vv.reshape(-1), wi * n, n, 0)
    return (out.reshape(seqs, rows, dim), grad_in, t_qkv[0], share(gvec[16]), t_qkv[1], t_qkv[2], share(gvec[17]), t_out, share(gvec[0]),
            share(gvec[1]), share(gvec[2]), t_up, share(gvec[8:8 + nu]), t_down, share(gvec[3]), share(gvec[4]), share(gvec[5]))


def solution(mesh):
    seq, mat, vec = P("wt", "ctx", None), P("wt", None), P("wt")
    ins = (seq, mat, mat, vec, mat, mat, vec, mat, vec, vec, vec, mat, vec, mat, vec, vec, vec, seq)
    outs = (seq, seq, mat, vec, mat, mat, vec, mat, vec, vec, vec, mat, vec, mat, vec, vec, vec)
    run = functools.partial(body, nc=mesh.shape["ctx"], nw=mesh.shape["wt"])
    return jax.shard_map(run, mesh=mesh, in_specs=ins, out_specs=outs, check_vma=False)
```

```python
import functools
import math

import jax
import jax.numpy as jnp
from jax import lax
from jax.experimental import pallas as pl
from jax.experimental.pallas import tpu as pltpu
from jax.sharding import PartitionSpec as P

norm_eps = 1e-05

BLOCK = 128
HEADS_HERE = 4
LOG2E = 1.4426950408889634
FAR = -1e30
bf16, f32 = jnp.bfloat16, jnp.float32
NT = (((1,), (1,)), ((), ()))
TN = (((0,), (0,)), ((), ()))


def dot(a, b, dims=(((1,), (0,)), ((), ()))):
    return lax.dot_general(a, b, dims, preferred_element_type=f32)


def turned(v):
    return v.astype(f32).T.astype(bf16)


def head_slices():
    return [(slice(64 * h, 64 * h + 64), slice(128 * h, 128 * h + 128)) for h in range(HEADS_HERE)]


class Pairs:
    def __init__(self, nb, first):
        self.nb, self.first = nb, first

    def first_lo(self, n):
        return self.first(n) < self.nb // 2

    def lo(self, n):
        b = self.first(n)
        return jnp.where(b < self.nb // 2, b, self.nb - 1 - b)

    def ordered(self, n, v):
        a, b = v[:BLOCK], v[BLOCK:]
        first = self.first_lo(n)
        return jnp.where(first, a, b), jnp.where(first, b, a)


def project_chunk(pairs, r, x_ref, wkv_ref, wkvt_ref, bkv_ref, bkvt_ref, K, V, KT, VT):
    def piece(p, _):
        x = jnp.concatenate(pairs.ordered(r * 4 + p, x_ref[r, p]), axis=0)
        kv = dot(x, wkv_ref[...])
        k, v = kv[:, :256].astype(bf16), (kv[:, 256:] + bkv_ref[...]).astype(bf16)
        kvt = dot(wkvt_ref[...], x, NT)
        kt, vt = kvt[:256].astype(bf16), (kvt[256:] + bkvt_ref[...]).astype(bf16)
        at = pl.ds(pl.multiple_of(p * BLOCK, BLOCK), BLOCK)
        for u in range(2):
            rows = slice(u * BLOCK, (u + 1) * BLOCK)
            K[r, u, at, :] = k[rows]
            V[r, u, at, :] = v[rows]
            KT[r, u, :, at] = kt[:, rows]
            VT[r, u, :, at] = vt[:, rows]
        return 0
    lax.fori_loop(0, 4, piece, 0)


def project_queries(pairs, x_ref, wq_ref, bq_ref, qn, qt, qs):
    qs[...] = jnp.zeros_like(qs)

    def piece(p, _):
        x = jnp.concatenate(pairs.ordered(p, x_ref[0, p]), axis=0)
        q = (dot(x, wq_ref[...]) + bq_ref[...]) * (LOG2E / 8.0)
        for u in range(2):
            mine = q[u * BLOCK:(u + 1) * BLOCK]
            qn[p, u] = mine.astype(bf16)
            t = mine.T.astype(bf16)
            qt[p, u] = t
            for hs, cs in head_slices():
                qs[p, u, hs, cs] = t[hs]
        return 0
    lax.fori_loop(0, 4, piece, 0)


def by_pair(vt, p16):
    return jnp.concatenate([dot(vt[0:128], p16[:, 0:256]), dot(vt[128:256], p16[:, 256:512])], axis=1)


def unpair(a):
    return jnp.concatenate([a[64 * (h % 2):64 * (h % 2) + 64, 128 * h:128 * h + 128] for h in range(HEADS_HERE)], axis=0)


def fwd_step(pairs, r, i, own, K, VT, qs, m_s, l_s, acc, d_s, sb, pb):
    col = lambda v: jnp.max(v, axis=0, keepdims=True)
    tot = lambda v: jnp.sum(v, axis=0, keepdims=True)
    lo_i = pairs.lo(i)
    pick = [lo_i > pairs.lo(r * 4 + j) for j in range(4)]
    sa = dot(K[r, 0], qs[i, 1])
    for j in range(4):
        u = jnp.where(pick[j], 0, 1)
        s = dot(K[r, u, j * BLOCK:(j + 1) * BLOCK, :], qs[i, u])
        if own:
            s = jnp.where(d_s[...] <= jnp.where(i == j, 0, 2 * BLOCK), s, FAR)
        sb[j] = s
    tops = [col(sb[j]) for j in range(4)]
    m_hi, m_lo = col(sa), None
    for j in range(4):
        m_hi = jnp.maximum(m_hi, jnp.where(pick[j], FAR, tops[j]))
        t = jnp.where(pick[j], tops[j], FAR)
        m_lo = t if m_lo is None else jnp.maximum(m_lo, t)
    if own:
        rows = pl.ds(pl.multiple_of(i * BLOCK, BLOCK), BLOCK)
        sd = jnp.where(d_s[...] <= 0, dot(K[r, 0, rows, :], qs[i, 0]), FAR)
        m_lo = jnp.maximum(m_lo, col(sd))
    else:
        old_hi, old_lo = m_s[i, 1], m_s[i, 0]
        m_hi, m_lo = jnp.maximum(m_hi, old_hi), jnp.maximum(m_lo, old_lo)
    pa = jnp.exp2(sa - m_hi)
    l_hi, l_lo = tot(pa), jnp.zeros((1, 512), f32)
    for j in range(4):
        p = jnp.exp2(sb[j] - jnp.where(pick[j], m_lo, m_hi))
        t = tot(p)
        l_hi = l_hi + jnp.where(pick[j], 0.0, t)
        l_lo = l_lo + jnp.where(pick[j], t, 0.0)
        low = p.astype(bf16)
        rows = slice(j * BLOCK, (j + 1) * BLOCK)
        zero = jnp.zeros_like(low)
        pb[0, rows, :] = jnp.where(pick[j], low, zero)
        pb[1, rows, :] = jnp.where(pick[j], zero, low)
    o_hi = by_pair(VT[r, 0], pa.astype(bf16)) + by_pair(VT[r, 1], pb[1])
    o_lo = by_pair(VT[r, 0], pb[0])
    if own:
        p = jnp.exp2(sd - m_lo)
        l_lo = l_lo + tot(p)
        at = pl.ds(pl.multiple_of(i * BLOCK, BLOCK), BLOCK)
        o_lo = o_lo + by_pair(VT[r, 0, :, at], p.astype(bf16))
        l_s[i, 1], l_s[i, 0] = l_hi, l_lo
        acc[i, 1], acc[i, 0] = o_hi, o_lo
    else:
        f_hi, f_lo = jnp.exp2(old_hi - m_hi), jnp.exp2(old_lo - m_lo)
        l_s[i, 1] = l_s[i, 1] * f_hi + l_hi
        l_s[i, 0] = l_s[i, 0] * f_lo + l_lo
        acc[i, 1] = acc[i, 1] * f_hi + o_hi
        acc[i, 0] = acc[i, 0] * f_lo + o_lo
    m_s[i, 1], m_s[i, 0] = m_hi, m_lo


def fwd_finish(pairs, m_s, l_s, acc, lse, ot, o_ref):
    def pair(i, _):
        first = pairs.first_lo(i)
        out = []
        for u in range(2):
            l = l_s[i, u]
            lse[i, u] = m_s[i, u] + jnp.log2(l)
            t = unpair(acc[i, u] * (1.0 / l))
            ot[i, u] = t
            out.append(t.T.astype(bf16))
        o_ref[i, 0:BLOCK, :] = jnp.where(first, out[0], out[1])
        o_ref[i, BLOCK:2 * BLOCK, :] = jnp.where(first, out[1], out[0])
        return 0
    lax.fori_loop(0, 4, pair, 0)


def diagonal(d_s):
    d_s[...] = lax.broadcasted_iota(jnp.int32, d_s.shape, 0) - (lax.broadcasted_iota(jnp.int32, d_s.shape, 1) & (BLOCK - 1))


def fwd_local(nz, blk_ref, x_ref, wqkv_ref, bq_ref, bkv_ref, bkvt_ref, o_ref, ot, lse, K, V, KT, qn, qt, VT, qs, m_s, l_s, acc, d_s, sb, pb, wkvt):
    pairs = Pairs(nz * 8, lambda n: blk_ref[2 * n])
    diagonal(d_s)
    wkvt[...] = turned(wqkv_ref[:, 256:])
    project_queries(pairs, x_ref, wqkv_ref.at[:, 0:256], bq_ref, qn, qt, qs)
    for r in range(nz):
        project_chunk(pairs, r, x_ref, wqkv_ref.at[:, 256:768], wkvt, bkv_ref, bkvt_ref, K, V, KT, VT)
        def step(i, _):
            fwd_step(pairs, r, i, r == 0, K, VT, qs, m_s, l_s, acc, d_s, sb, pb)
            return 0
        lax.fori_loop(0, 4, step, 0)
    fwd_finish(pairs, m_s, l_s, acc, lse, ot, o_ref)


def fwd_outs(nz):
    sds = jax.ShapeDtypeStruct
    kv = sds((nz, 2, 512, 256), bf16)
    return (sds((4, 256, 256), bf16), sds((4, 2, 256, 128), f32), sds((4, 2, 1, 512), f32), kv, kv, sds((nz, 2, 256, 512), bf16),
            sds((4, 2, 128, 256), bf16), sds((4, 2, 256, 128), bf16))


def fwd_scratch(nz):
    M = pltpu.VMEM
    return [M((nz, 2, 256, 512), bf16), M((4, 2, 256, 512), bf16), M((4, 2, 1, 512), f32), M((4, 2, 1, 512), f32), M((4, 2, 128, 512), f32),
            M((128, 512), jnp.int32), M((4, 128, 512), f32), M((2, 512, 512), bf16), M((512, 512), bf16)]


def attn_fwd(nz, blk, x, wqkv, bq, bkv):
    V = pl.BlockSpec(memory_space=pltpu.VMEM)
    return pl.pallas_call(
        functools.partial(fwd_local, nz), out_shape=fwd_outs(nz),
        in_specs=[pl.BlockSpec(memory_space=pltpu.SMEM)] + [V] * 5, out_specs=(V,) * 8, scratch_shapes=fwd_scratch(nz),
        compiler_params=pltpu.CompilerParams(vmem_limit_bytes=58 << 20), name="attn_fwd")(blk, x, wqkv, bq, bkv, bkv.reshape(256, 1))


def bwd_queries(pairs, do_ref, ot, qn, qt, qs, dos, qns, dons, dl):
    for s in (qs, dos, qns, dons):
        s[...] = jnp.zeros_like(s)

    def piece(i, _):
        for u, do in enumerate(pairs.ordered(i, do_ref[i])):
            dot_t = do.astype(f32).T
            prod = dot_t * ot[i, u]
            low = dot_t.astype(bf16)
            q, t = qn[i, u], qt[i, u]
            for hs, cs in head_slices():
                qs[i, u, hs, cs] = t[hs]
                dos[i, u, hs, cs] = low[hs]
                qns[i, u, cs, hs] = q[:, hs]
                dons[i, u, cs, hs] = do[:, hs]
                dl[i, u, :, cs] = jnp.sum(prod[hs], axis=0, keepdims=True)
        return 0
    lax.fori_loop(0, 4, piece, 0)


def bwd_step(pairs, r, i, own, first, K, V, KT, qs, dos, qns, dons, lse, dl, dk, dv, dq, d_s, gb):
    lo_i = pairs.lo(i)
    pick = [lo_i > pairs.lo(r * 4 + j) for j in range(4)]

    def pieces(k, v, u, mask):
        s = dot(k, qs[i, u]) - lse[i, u]
        if mask is not None:
            s = jnp.where(d_s[...] <= mask, s, FAR)
        p = jnp.exp2(s)
        g = p * (dot(v, dos[i, u]) - dl[i, u])
        return p.astype(bf16), g.astype(bf16)

    p, g = pieces(K[r, 0], V[r, 0], 1, None)
    dv[0] += dot(p, dons[i, 1])
    dk[0] += dot(g, qns[i, 1])
    q_hi = by_pair(KT[r, 0], g)
    for j in range(4):
        u = jnp.where(pick[j], 0, 1)
        rows = slice(j * BLOCK, (j + 1) * BLOCK)
        p, g = pieces(K[r, u, rows, :], V[r, u, rows, :], u, jnp.where(i == j, 0, 2 * BLOCK) if own else None)
        gv, gk = dot(p, dons[i, u]), dot(g, qns[i, u])
        dv[0, rows, :] += jnp.where(pick[j], gv, 0.0)
        dv[1, rows, :] += jnp.where(pick[j], 0.0, gv)
        dk[0, rows, :] += jnp.where(pick[j], gk, 0.0)
        dk[1, rows, :] += jnp.where(pick[j], 0.0, gk)
        zero = jnp.zeros_like(g)
        gb[0, rows, :] = jnp.where(pick[j], g, zero)
        gb[1, rows, :] = jnp.where(pick[j], zero, g)
    q_hi = q_hi + by_pair(KT[r, 1], gb[1])
    q_lo = by_pair(KT[r, 0], gb[0])
    if own:
        rows = pl.ds(pl.multiple_of(i * BLOCK, BLOCK), BLOCK)
        p, g = pieces(K[r, 0, rows, :], V[r, 0, rows, :], 0, 0)
        dv[0, rows, :] += dot(p, dons[i, 0])
        dk[0, rows, :] += dot(g, qns[i, 0])
        q_lo = q_lo + by_pair(KT[r, 0, :, rows], g)
    if first:
        dq[i, 1], dq[i, 0] = q_hi, q_lo
    else:
        dq[i, 1] += q_hi
        dq[i, 0] += q_lo


def bwd_chunk_out(pairs, r, last, x_ref, wqkv_ref, dk, dv, dxq, dx, dw, db):
    def piece(p, _):
        at = pl.ds(pl.multiple_of(p * BLOCK, BLOCK), BLOCK)
        g = [jnp.concatenate([(dk[u, at, :] * (1.0 / LOG2E)).astype(bf16), dv[u, at, :].astype(bf16)], axis=1) for u in range(2)]
        first = pairs.first_lo(r * 4 + p)
        g = jnp.concatenate([jnp.where(first, g[0], g[1]), jnp.where(first, g[1], g[0])], axis=0)
        d = dot(g, wqkv_ref[:, 256:768], NT)
        if last:
            d = d + dxq[p]
        dx[r, pl.ds(pl.multiple_of(p * 256, 256), 256), :] = d.astype(bf16)
        dw[:, 256:768] += dot(x_ref[r, p], g, TN)
        db[1:2, :] += jnp.sum(g[:, 256:].astype(f32), axis=0, keepdims=True)
        return 0
    lax.fori_loop(0, 4, piece, 0)


def bwd_query_out(pairs, x_ref, wqkv_ref, dq, dxq, dw, db):
    def piece(i, _):
        t = [(unpair(dq[i, u]) * 0.125).T.astype(bf16) for u in range(2)]
        first = pairs.first_lo(i)
        g = jnp.concatenate([jnp.where(first, t[0], t[1]), jnp.where(first, t[1], t[0])], axis=0)
        dxq[i] = dot(g, wqkv_ref[:, 0:256], NT)
        dw[:, 0:256] += dot(x_ref[0, i], g, TN)
        db[0:1, :] += jnp.sum(g.astype(f32), axis=0, keepdims=True)
        return 0
    lax.fori_loop(0, 4, piece, 0)


def weight_rows(dw, gq):
    for k in range(2):
        for m in range(3):
            gq[k, m * 256:m * 256 + 256, :] = dw[k * 256:k * 256 + 256, m * 256:m * 256 + 256].astype(bf16)


def bwd_local(nz, blk_ref, x_ref, wqkv_ref, K, V, KT, qn, qt, ot, lse, do_ref, dx, gq, db, qs, dos, qns, dons, dl, dk, dv, dq, d_s, gb, dxq, dw):
    pairs = Pairs(nz * 8, lambda n: blk_ref[2 * n])
    diagonal(d_s)
    dw[...] = jnp.zeros_like(dw)
    db[...] = jnp.zeros_like(db)
    bwd_queries(pairs, do_ref, ot, qn, qt, qs, dos, qns, dons, dl)
    for r in list(range(1, nz)) + [0]:
        dk[...] = jnp.zeros_like(dk)
        dv[...] = jnp.zeros_like(dv)
        def step(i, _):
            bwd_step(pairs, r, i, r == 0, r == 1, K, V, KT, qs, dos, qns, dons, lse, dl, dk, dv, dq, d_s, gb)
            return 0
        lax.fori_loop(0, 4, step, 0)
        if r == 0:
            bwd_query_out(pairs, x_ref, wqkv_ref, dq, dxq, dw, db)
        bwd_chunk_out(pairs, r, r == 0, x_ref, wqkv_ref, dk, dv, dxq, dx, dw, db)
    weight_rows(dw, gq)


def bwd_scratch():
    M = pltpu.VMEM
    return [M((4, 2, 256, 512), bf16), M((4, 2, 256, 512), bf16), M((4, 2, 512, 256), bf16), M((4, 2, 512, 256), bf16), M((4, 2, 1, 512), f32),
            M((2, 512, 256), f32), M((2, 512, 256), f32), M((4, 2, 128, 512), f32), M((128, 512), jnp.int32), M((2, 512, 512), bf16),
            M((4, 256, 512), f32), M((512, 768), f32)]


def attn_bwd(nz, blk, x, wqkv, K, V, KT, qn, qt, ot, lse, do):
    S = pl.BlockSpec(memory_space=pltpu.VMEM)
    sds = jax.ShapeDtypeStruct
    return pl.pallas_call(
        functools.partial(bwd_local, nz), out_shape=(sds((nz, 1024, 512), bf16), sds((2, 768, 256), bf16), sds((8, 256), f32)),
        in_specs=[pl.BlockSpec(memory_space=pltpu.SMEM)] + [S] * 10, out_specs=(S,) * 3, scratch_shapes=bwd_scratch(),
        compiler_params=pltpu.CompilerParams(vmem_limit_bytes=58 << 20), name="attn_bwd")(blk, x, wqkv, K, V, KT, qn, qt, ot, lse, do)


def dense_kernel(x_ref, cot_ref, att_ref, wo_ref, wu_ref, wd_ref, sm_ref,
                 out_ref, dsm_ref, do_ref, gw_ref, gv_ref, act_s, gp_s, norm_s, dpre_s):
    ff = wu_ref.shape[1]
    chunk = 512
    x = x_ref[...].astype(f32)
    vec = lambda i: jnp.concatenate([sm_ref[0, i:i + 1, :], sm_ref[1, i:i + 1, :]], axis=1)
    b_out, g1, s1, b_down, g2, s2 = (vec(i) for i in range(2, 8))
    mean = lambda v: jnp.mean(v, axis=-1, keepdims=True)
    col = lambda v: jnp.sum(v, axis=0, keepdims=True)
    mix = x + dot(att_ref[...], wo_ref[...]) + b_out
    cen = mix - mean(mix)
    r1 = lax.rsqrt(mean(cen * cen) + norm_eps)
    n1 = cen * r1
    normed = n1 * g1 + s1
    nlow = normed.astype(bf16)
    norm_s[...] = nlow
    ffn = None
    for f in range(0, ff, chunk):
        fs = slice(f, f + chunk)
        at = 8 + f % (ff // 2) // 256
        b_up = jnp.concatenate([sm_ref[2 * f // ff, at + k:at + k + 1, :] for k in range(chunk // 256)], axis=1)
        pre = dot(nlow, wu_ref[:, fs]) + b_up
        c0 = math.sqrt(2.0 / math.pi)
        sq = pre * pre
        th = jnp.tanh(c0 * pre * (1.0 + 0.044715 * sq))
        half = 0.5 * (1.0 + th)
        act = (pre * half).astype(bf16)
        act_s[:, fs] = act
        gp_s[:, fs] = half + 0.5 * pre * (1.0 - th * th) * (c0 * (1.0 + 3 * 0.044715 * sq))
        part = dot(act, wd_ref[fs, :])
        ffn = part if ffn is None else ffn + part
    summed = ffn + b_down + normed + x
    cen = summed - mean(summed)
    r2 = lax.rsqrt(mean(cen * cen) + norm_eps)
    n2 = cen * r2
    out_ref[...] = (n2 * g2 + s2).astype(bf16)
    up = cot_ref[...].astype(f32)
    gv_ref[4:5, :] = col(up * n2)
    gv_ref[5:6, :] = col(up)
    dn = up * g2
    dsum = r2 * (dn - mean(dn) - n2 * mean(dn * n2))
    dffn = dsum.astype(bf16)
    gv_ref[3:4, :] = col(dffn.astype(f32))
    dnorm = dsum
    half_rows = wo_ref.shape[0] // 2
    half_ff = ff // 2
    def put(g, at, rows):
        gw_ref[0, at:at + rows, :] = g[:rows].astype(bf16)
        gw_ref[1, at:at + rows, :] = g[rows:].astype(bf16)
    for f in range(0, ff, chunk):
        fs = slice(f, f + chunk)
        dact = dot(dffn, wd_ref[fs, :], NT)
        dpre = (dact * gp_s[:, fs]).astype(bf16)
        gv_ref[8 + f // chunk:9 + f // chunk, :] = col(dpre.astype(f32))
        dnorm = dnorm + dot(dpre, wu_ref[:, fs], NT)
        put(dot(norm_s[...], dpre, TN), half_rows + (f // chunk) * half_rows, half_rows)
        gd = dot(act_s[:, fs], dffn, TN).astype(bf16)
        base = half_rows * (1 + ff // chunk)
        which, off = f // half_ff, f % half_ff
        gw_ref[which, base + off:base + off + chunk, :] = gd
    gv_ref[1:2, :] = col(dnorm * n1)
    gv_ref[2:3, :] = col(dnorm)
    dn = dnorm * g1
    dmix = r1 * (dn - mean(dn) - n1 * mean(dn * n1))
    dsm_ref[...] = dsum + dmix
    dbr = dmix.astype(bf16)
    gv_ref[0:1, :] = col(dbr.astype(f32))
    do_ref[...] = dot(dbr, wo_ref[...], NT).astype(bf16)
    put(dot(att_ref[...], dbr, TN), 0, half_rows)


def dense(x, cot, att, wo, wu, wd, sm):
    V = pl.BlockSpec(memory_space=pltpu.VMEM)
    tok, dim = x.shape
    ff = wu.shape[1]
    rows = (2 * dim * ff + dim * dim) // 2 // dim
    return pl.pallas_call(
        dense_kernel,
        out_shape=(jax.ShapeDtypeStruct((tok, dim), bf16), jax.ShapeDtypeStruct((tok, dim), f32),
                   jax.ShapeDtypeStruct((tok, dim), bf16), jax.ShapeDtypeStruct((2, rows, dim), bf16),
                   jax.ShapeDtypeStruct((16, dim), f32)),
        in_specs=[V] * 7, out_specs=(V,) * 5,
        scratch_shapes=[pltpu.VMEM((tok, ff), bf16), pltpu.VMEM((tok, ff), f32), pltpu.VMEM((tok, dim), bf16),
                        pltpu.VMEM((8, 128), f32)],
        compiler_params=pltpu.CompilerParams(vmem_limit_bytes=56 << 20),
        name="dense")(x, cot, att, wo, wu, wd, sm)


MESH = pl.DeviceIdType.MESH


def places(nz):
    me, wi = lax.axis_index("ctx"), lax.axis_index("wt")
    z, y, c = me // 4, lax.rem(me // 2, 2), lax.rem(me, 2)
    low = lax.rem(me, 4)
    at = lambda zz, ll: (zz * 4 + ll, wi)
    to = dict(up=at(lax.rem(z + 1, nz), low), down=at(lax.rem(z + nz - 1, nz), low), core=at(z, low + 1 - 2 * c), y=at(z, low + 2 - 4 * y),
              x=(me, 1 - wi))
    return me, wi, z, y, c, low, to


def meet(targets):
    bar = pltpu.get_barrier_semaphore()
    for t in targets:
        pl.semaphore_signal(bar, inc=1, device_id=t, device_id_type=MESH)
    pl.semaphore_wait(bar, len(targets))


class Wires:
    def __init__(self, send, recv):
        self.send, self.recv, self.n, self.live = send, recv, 0, []

    def make(self, src, dst, to):
        cp = pltpu.make_async_remote_copy(src, dst, self.send.at[self.n], self.recv.at[self.n], device_id=to, device_id_type=MESH)
        self.n += 1
        return cp

    def go(self, src, dst, to):
        cp = self.make(src, dst, to)
        cp.start()
        self.live.append(cp)
        return cp

    def drain(self):
        for cp in self.live:
            cp.wait_send()


def rows_of(start, size, mult=16):
    return pl.ds(pl.multiple_of(start, mult), size)


def gather_kernel(nz, with_w, *refs):
    if with_w:
        (x_ref, wq_ref, wk_ref, wv_ref, wo_ref, wu_ref, wd_ref, sm_ref,
         xall, wqkv, wo, wu, wd, sm, send, recv, lsem) = refs
    else:
        x_ref, xall, send, recv, lsem = refs
    me, wi, z, y, c, low, to = places(nz)
    rows = x_ref.shape[1]
    local = []

    def copy(src, dst):
        cp = pltpu.make_async_copy(src, dst, lsem.at[len(local)])
        cp.start()
        local.append(cp)

    copy(x_ref.at[y], xall.at[0, 0])
    if with_w:
        R, half = wq_ref.shape[0], wq_ref.shape[1] // 2
        for i, w in enumerate((wq_ref, wk_ref, wv_ref)):
            copy(w.at[:, rows_of(c * half, half, 128)], wqkv.at[rows_of(wi * R, R), pl.ds(i * half, half)])
        for w, full in ((wo_ref, wo), (wu_ref, wu), (wd_ref, wd)):
            n = w.shape[0]
            copy(w, full.at[rows_of(wi * n, n)])
        copy(sm_ref, sm.at[wi])
    near = [to["up"], to["down"], to["core"], to["y"]] + ([to["x"]] if with_w else [])
    meet(near)
    wires = Wires(send, recv)
    yx = wires.go(x_ref.at[1 - y], xall.at[0, 1], to["y"])
    ring = {(1, 0): wires.go(x_ref.at[y], xall.at[1, 0], to["up"])}
    core = {(0, 0): wires.go(x_ref.at[y], xall.at[0, 2], to["core"])}
    if with_w:
        xs = []
        for i, w in enumerate((wq_ref, wk_ref, wv_ref)):
            xs.append(wires.go(w.at[:, rows_of(c * half, half, 128)], wqkv.at[rows_of(wi * R, R), pl.ds(i * half, half)], to["x"]))
        xs.append(wires.go(sm_ref, sm.at[wi], to["x"]))
        big = []
        for w, full in ((wo_ref, wo), (wu_ref, wu), (wd_ref, wd)):
            n = w.shape[0]
            h = n // 2
            cp = wires.go(w.at[rows_of(c * h, h)], full.at[rows_of(wi * n + c * h, h)], to["x"])
            big.append((cp, full, rows_of((1 - wi) * n + c * h, h)))
    yx.wait_recv()
    ring[1, 1] = wires.go(xall.at[0, 1], xall.at[1, 1], to["up"])
    core[0, 1] = wires.go(xall.at[0, 1], xall.at[0, 3], to["core"])
    shared = []
    for r in range(1, nz):
        for s in range(2):
            ring[r, s].wait_recv()
            if r < nz - 1:
                ring[r + 1, s] = wires.go(xall.at[r, s], xall.at[r + 1, s], to["up"])
            core[r, s] = wires.go(xall.at[r, s], xall.at[r, 2 + s], to["core"])
        if with_w and r - 1 < len(big):
            cp, full, where = big[r - 1]
            cp.wait_recv()
            shared.append(wires.go(full.at[where], full.at[where], to["core"]))
    if with_w:
        for cp, full, where in big[nz - 1:]:
            cp.wait_recv()
            shared.append(wires.go(full.at[where], full.at[where], to["core"]))
        for cp in xs + shared:
            cp.wait_recv()
    for cp in core.values():
        cp.wait_recv()
    wires.drain()
    for cp in local:
        cp.wait()


def gather_all(nz, x, weights=None, small=None):
    A = pl.BlockSpec(memory_space=pl.ANY)
    sds = jax.ShapeDtypeStruct
    rows, dim = x.shape[1:]
    outs = [sds((nz, 4, rows, dim), bf16)]
    ins = [x]
    ncopy = 1 + 2 * (nz - 1) + 2 * nz
    if weights is not None:
        wq, wk, wv, wo, wu, wd = weights
        ins += list(weights) + [small]
        outs += [sds((dim, 3 * dim // 2), bf16)] + [sds((2 * w.shape[0], w.shape[1]), bf16) for w in (wo, wu, wd)] + [sds((2,) + small.shape, bf16)]
        ncopy += 10
    return pl.pallas_call(
        functools.partial(gather_kernel, nz, weights is not None),
        out_shape=tuple(outs), in_specs=[A] * len(ins), out_specs=(A,) * len(outs),
        scratch_shapes=[pltpu.SemaphoreType.DMA((ncopy,)), pltpu.SemaphoreType.DMA((ncopy,)), pltpu.SemaphoreType.DMA((8,))],
        compiler_params=pltpu.CompilerParams(collective_id=1, has_side_effects=True, vmem_limit_bytes=16 << 20),
        name="gather_all")(*ins)


def add_into(dst, parts, rows, step=64):
    def body(i, _):
        r = rows_of(i * step, step)
        total = parts[0](r)[...].astype(f32)
        for p in parts[1:]:
            total = total + p(r)[...].astype(f32)
        d = dst(r)
        d[...] = total.astype(bf16)
        return 0
    lax.fori_loop(0, rows // step, body, 0)


def offset(ref, lead, start):
    def view(r):
        at = pl.ds(pl.multiple_of(start + r.start, 16), r.size)
        return ref.at[lead + (at,)]
    return view


STREAMS = ((768, 512), (768, 512), (768, 512), (1536, 256))


def reduce_kernel(nz, dx_ref, gw_ref, gq_ref, gv_ref, dxo, go, gqo, gvo,
                  dx_core, dx_acc, dx_in, cr, cs, xr, xs_, yr, ys_, zr, cq, xrq, xsq, yrq, ysq, zrq, gvs, gvr, send, recv):
    me, wi, z, y, c, low, to = places(nz)
    zto = [(lax.rem(z + d, nz) * 4 + low, wi) for d in range(1, nz)]
    meet([to["core"], to["y"], to["x"]] + zto)
    w = Wires(send, recv)
    hrow = 256
    got = {}
    for s in range(3):
        got["c", s] = w.go(gw_ref.at[:, rows_of(s * 768 + (1 - c) * 384, 384)], cr.at[s], to["core"])
        r = s + 1
        got["d", r] = w.go(dx_ref.at[r, pl.ds(512, 512)], dx_core.at[r], to["core"])
    got["d", 0] = w.go(dx_ref.at[0, pl.ds(512, 512)], dx_core.at[0], to["core"])

    width = [384, 384, 384, 768]
    n_y = [v // 2 for v in width]
    n_z = [v // (2 * nz) for v in width]
    X_in = [xr.at[s] for s in range(3)] + [xrq]
    X_sum = [xs_.at[s] for s in range(3)] + [xsq]
    Y_in = [yr.at[s] for s in range(3)] + [yrq]
    Y_sum = [ys_.at[s] for s in range(3)] + [ysq]
    Z_in = [zr.at[s] for s in range(3)] + [zrq]
    out = [go.at[s] for s in range(3)] + [gqo]

    def x_send(s):
        if s < 3:
            got["c", s].wait_recv()
            for k in range(2):
                add_into(offset(cs, (s, k), 0), [offset(gw_ref, (k,), s * 768 + c * 384), offset(cr, (s, k), 0)], 384)
            got["x", s] = w.go(cs.at[s, 1 - wi], X_in[s], to["x"])
        else:
            got["x", s] = w.go(gq_ref.at[1 - wi], X_in[s], to["x"])

    def y_send(s):
        got["x", s].wait_recv()
        mine = offset(cs, (s, wi), 0) if s < 3 else offset(gq_ref, (wi,), 0)
        add_into(offset(X_sum[s], (), 0), [mine, offset(X_in[s], (), 0)], width[s])
        got["y", s] = w.go(X_sum[s].at[rows_of((1 - y) * n_y[s], n_y[s])], Y_in[s], to["y"])

    def z_send(s):
        got["y", s].wait_recv()
        add_into(offset(Y_sum[s], (), 0), [offset(X_sum[s], (), y * n_y[s]), offset(Y_in[s], (), 0)], n_y[s])
        for d in range(1, nz):
            zd = lax.rem(z + d, nz)
            got["z", s, d] = w.go(Y_sum[s].at[rows_of(zd * n_z[s], n_z[s])], Z_in[s].at[d - 1], zto[d - 1])

    def z_share(s):
        for d in range(1, nz):
            got["z", s, d].wait_recv()
        base = c * width[s] + y * n_y[s] + z * n_z[s]
        add_into(offset(out[s], (), base), [offset(Y_sum[s], (), z * n_z[s])] + [offset(Z_in[s], (d,), 0) for d in range(nz - 1)], n_z[s], 48)
        at = rows_of(base, n_z[s])
        for d in range(1, nz):
            got["zs", s, d] = w.go(out[s].at[at], out[s].at[at], zto[d - 1])

    def y_share(s):
        for d in range(1, nz):
            got["zs", s, d].wait_recv()
        at = rows_of(c * width[s] + y * n_y[s], n_y[s])
        got["ys", s] = w.go(out[s].at[at], out[s].at[at], to["y"])

    def c_share(s):
        got["ys", s].wait_recv()
        at = rows_of(c * width[s], width[s])
        got["cs", s] = w.go(out[s].at[at], out[s].at[at], to["core"])

    def fold(r):
        got["d", r].wait_recv()
        add_into(offset(dx_acc, (r,), 0), [offset(dx_ref, (r,), 0), offset(dx_core, (r,), 0)], 512)

    def hop(r, h):
        if r != 1:
            got["r", r, h].wait_recv()
            if r:
                add_into(offset(dx_acc, (r,), h * hrow), [offset(dx_acc, (r,), h * hrow), offset(dx_in, (r,), h * hrow)], hrow)
            else:
                dst = offset(dxo, (0,), 0) if h == 0 else offset(dx_acc, (0,), hrow)
                add_into(dst, [offset(dx_acc, (0,), h * hrow), offset(dx_in, (0,), h * hrow)], hrow)
        at = pl.ds(h * hrow, hrow)
        if r:
            n = (r + 1) % nz
            got["r", n, h] = w.go(dx_acc.at[r, at], dx_in.at[n, at], to["up"])
        elif h:
            got["dy"] = w.go(dx_acc.at[0, at], dxo.at[1], to["y"])

    vec_to = [to["core"], to["y"], to["x"]] + [(zz * 4 + low, wi) for zz in (z + 1 - 2 * lax.rem(z, 2), z + 2 - 4 * (z // 2))]

    def vec_send(k):
        if k == 0:
            gvs[0] = gv_ref[...]
        else:
            got["v", k - 1].wait_recv()
            gvs[k] = gvs[k - 1] + gvr[k - 1]
        if k < 5:
            got["v", k] = w.go(gvs.at[k], gvr.at[k], vec_to[k])
        else:
            gvo[...] = gvs[5]

    x_send(3)
    vec_send(0)
    fold(1)
    hop(1, 1)
    hop(1, 0)
    x_send(0)
    vec_send(1)
    x_send(1)
    fold(2)
    hop(2, 1)
    x_send(2)
    vec_send(2)
    fold(3)
    y_send(3)
    hop(2, 0)
    vec_send(3)
    fold(0)
    z_send(3)
    hop(3, 1)
    y_send(0)
    z_share(3)
    vec_send(4)
    hop(3, 0)
    z_send(0)
    vec_send(5)
    y_share(3)
    y_send(1)
    hop(0, 1)
    z_share(0)
    c_share(3)
    z_send(1)
    y_send(2)
    hop(0, 0)
    y_share(0)
    z_share(1)
    z_send(2)
    c_share(0)
    y_share(1)
    z_share(2)
    c_share(1)
    y_share(2)
    c_share(2)
    for s in range(4):
        got["cs", s].wait_recv()
    got["dy"].wait_recv()
    w.drain()


def reduce_all(nz, dx, gw, gq, gv):
    V = pl.BlockSpec(memory_space=pltpu.VMEM)
    sds = jax.ShapeDtypeStruct
    M = lambda *s: pltpu.VMEM(s, bf16)
    ncopy = 100
    return pl.pallas_call(
        functools.partial(reduce_kernel, nz),
        out_shape=(sds((2, 256, 512), bf16), sds((3, 768, 512), bf16), sds((1536, 256), bf16), sds(gv.shape, f32)),
        in_specs=[V] * 4, out_specs=(V,) * 4,
        scratch_shapes=[M(nz, 512, 512), M(nz, 512, 512), M(nz, 512, 512), M(3, 2, 384, 512), M(3, 2, 384, 512),
                        M(3, 384, 512), M(3, 384, 512), M(3, 192, 512), M(3, 192, 512), M(3, nz - 1, 48, 512),
                        M(8, 128), M(768, 256), M(768, 256), M(384, 256), M(384, 256), M(nz - 1, 96, 256),
                        pltpu.VMEM((6,) + gv.shape, f32), pltpu.VMEM((5,) + gv.shape, f32),
                        pltpu.SemaphoreType.DMA((ncopy,)), pltpu.SemaphoreType.DMA((ncopy,))],
        compiler_params=pltpu.CompilerParams(collective_id=2, has_side_effects=True, vmem_limit_bytes=60 << 20),
        name="reduce_all")(dx, gw, gq, gv)


def chip_pairs(nz, order_ref):
    me = lax.axis_index("ctx")
    z, y, c = me // 4, lax.rem(me // 2, 2), lax.rem(me, 2)

    def first(n):
        r, p = n // 4, n % 4
        a, b = p % 2, p // 2
        yy, cc = y + a - 2 * y * a, c + b - 2 * c * b
        return order_ref[y, 2 * (lax.rem(z - r + nz, nz) * 4 + yy * 2 + cc)]
    return Pairs(nz * 8, first)


def front_kernel(nz, order_ref, bqr, bvr, bor, g1r, s1r, bdr, g2r, s2r, bur, x_ref, wq_ref, wk_ref, wv_ref, wo_ref, wu_ref, wd_ref,
                 att, wo, wu, wd, sm, xall, wqkv, ot_o, lse_o, K_o, V_o, KT_o, qn_o, qt_o,
                 xs, ws, sms, K, V, KT, VT, qn, qt, qs, m_s, l_s, acc, d_s, sb, pb, wkvt, bkvt, ot, lse, o_s, send, recv, lsem):
    me, wi, z, y, c, low, to = places(nz)
    to["yc"] = (z * 4 + 3 - low, wi)
    half, R = 256, wq_ref.shape[0]
    local = []

    def copy(src, dst):
        cp = pltpu.make_async_copy(src, dst, lsem.at[len(local)])
        cp.start()
        local.append(cp)
        return cp

    own_x = copy(x_ref.at[y], xs.at[0, 0])
    own_w = [copy(w.at[:, rows_of(c * half, half, 128)], ws.at[rows_of(wi * R, R), pl.ds(i * half, half)]) for i, w in enumerate((wq_ref, wk_ref, wv_ref))]
    for i, v in enumerate((bqr, bvr, bor, g1r, s1r, bdr, g2r, s2r)):
        sms[wi, i:i + 1, :] = v[...].astype(f32).reshape(1, half)
    up_b = bur[...].astype(f32).reshape(1, 1024)
    for i in range(4):
        sms[wi, 8 + i:9 + i, :] = up_b[:, i * half:(i + 1) * half]
    sms[wi, 12:16, :] = jnp.zeros((4, half), f32)
    meet([to[k] for k in ("up", "down", "core", "y", "yc", "x")])
    w = Wires(send, recv)
    yx = w.go(x_ref.at[1 - y], xs.at[0, 1], to["y"])
    ring, core = {}, {}
    ring[1, 0] = w.go(x_ref.at[y], xs.at[1, 0], to["up"])
    core[0, 0] = w.go(x_ref.at[y], xs.at[0, 2], to["core"])
    wx = []
    for i, m in enumerate((wq_ref, wk_ref, wv_ref)):
        wx.append(w.go(m.at[:, rows_of(c * half, half, 128)], ws.at[rows_of(wi * R, R), pl.ds(i * half, half)], to["x"]))
    wx.append(w.go(sms.at[wi], sms.at[wi], to["x"]))
    big = []
    for m, full in ((wo_ref, wo), (wu_ref, wu), (wd_ref, wd)):
        n = m.shape[0]
        h = n // 2
        copy(m, full.at[rows_of(wi * n, n)])
        big.append((w.go(m.at[rows_of(c * h, h)], full.at[rows_of(wi * n + c * h, h)], to["x"]), full, rows_of((1 - wi) * n + c * h, h)))

    pairs = chip_pairs(nz, order_ref)
    diagonal(d_s)
    yx.wait_recv()
    ring[1, 1] = w.go(xs.at[0, 1], xs.at[1, 1], to["up"])
    core[0, 1] = w.go(xs.at[0, 1], xs.at[0, 3], to["core"])

    def pump(r, s):
        ring[r, s].wait_recv()
        if r < nz - 1:
            ring[r + 1, s] = w.go(xs.at[r, s], xs.at[r + 1, s], to["up"])
        core[r, s] = w.go(xs.at[r, s], xs.at[r, 2 + s], to["core"])

    shared = []

    def share(k):
        cp, full, where = big[k]
        cp.wait_recv()
        shared.append(w.go(full.at[where], full.at[where], to["core"]))

    pump(1, 0)
    for cp in own_w:
        cp.wait()
    for cp in wx:
        cp.wait_recv()
    copy(sms, sm)
    copy(ws, wqkv)
    wkvt[...] = turned(ws[:, 256:])
    bv = sms[c, 1:2, :]
    bkvt[...] = jnp.broadcast_to(bv, (8, half)).T[:, 0:1]
    own_x.wait()
    for s in range(2):
        core[0, s].wait_recv()
    project_queries(pairs, xs, ws.at[:, 0:256], sms.at[c, 0:1], qn, qt, qs)
    copy(qn, qn_o)
    copy(qt, qt_o)

    def chunk(r):
        project_chunk(pairs, r, xs, ws.at[:, 256:768], wkvt, sms.at[c, 1:2], bkvt, K, V, KT, VT)
        for a, b in ((xs, xall), (K, K_o), (V, V_o), (KT, KT_o)):
            copy(a.at[r], b.at[r])

    def attend(r, start, stop):
        def step(i, _):
            fwd_step(pairs, r, i, r == 0, K, VT, qs, m_s, l_s, acc, d_s, sb, pb)
            return 0
        lax.fori_loop(start, stop, step, 0)

    chunk(0)
    pump(1, 1)
    attend(0, 0, 2)
    attend(0, 2, 4)
    for r in range(1, nz):
        if r + 1 < nz:
            pump(r + 1, 0)
        for s in range(2):
            core[r, s].wait_recv()
        chunk(r)
        attend(r, 0, 2)
        if r + 1 < nz:
            pump(r + 1, 1)
            share(r - 1)
        attend(r, 2, 4)
    fwd_finish(pairs, m_s, l_s, acc, lse, ot, o_s)
    cols = pl.ds(pl.multiple_of(c * half, half), half)
    outs = [w.go(o_s.at[p], att.at[y, :, cols], to[k]) for p, k in ((1, "y"), (2, "core"), (3, "yc"))]
    copy(o_s.at[0], att.at[y, :, cols])
    copy(ot, ot_o)
    copy(lse, lse_o)
    share(2)
    for cp in outs + shared:
        cp.wait_recv()
    w.drain()
    for cp in local[4:]:
        cp.wait()


def front(nz, order, vectors, x, weights):
    A = pl.BlockSpec(memory_space=pltpu.HBM)
    V = pl.BlockSpec(memory_space=pltpu.VMEM)
    sds = jax.ShapeDtypeStruct
    M = pltpu.VMEM
    rows, dim = x.shape[1:]
    wq, wk, wv, wo, wu, wd = weights
    outs = [sds((2, rows, dim), bf16)] + [sds((2 * w.shape[0], w.shape[1]), bf16) for w in (wo, wu, wd)]
    outs += [sds((2, 16, 256), f32), sds((nz, 4, rows, dim), bf16), sds((dim, 768), bf16)] + list(fwd_outs(nz)[1:])
    scratch = [M((nz, 4, rows, dim), bf16), M((dim, 768), bf16), M((2, 16, 256), f32)]
    scratch += [M((nz, 2, 512, 256), bf16)] * 2 + [M((nz, 2, 256, 512), bf16)] * 2 + [M((4, 2, 128, 256), bf16), M((4, 2, 256, 128), bf16)]
    scratch += fwd_scratch(nz)[1:] + [M((256, 1), f32), M((4, 2, 256, 128), f32), M((4, 2, 1, 512), f32), M((4, 256, 256), bf16)]
    scratch += [pltpu.SemaphoreType.DMA((40,)), pltpu.SemaphoreType.DMA((40,)), pltpu.SemaphoreType.DMA((40,))]
    return pl.pallas_call(
        functools.partial(front_kernel, nz), out_shape=tuple(outs),
        in_specs=[pl.BlockSpec(memory_space=pltpu.SMEM)] + [V] * 9 + [A] * 7, out_specs=(A,) * len(outs), scratch_shapes=scratch,
        compiler_params=pltpu.CompilerParams(collective_id=1, has_side_effects=True, vmem_limit_bytes=58 << 20), name="front")(
            order, *vectors, x, *weights)


def body(block_in, block_order, w_query, b_query, w_key, w_value, b_value, w_out, b_out, gain_one, shift_one,
         w_up, b_up, w_down, b_down, gain_two, shift_two, cotangent, *, nc, nw):
    seqs, rows, dim = block_in.shape
    nz = nc // 4
    hb = rows // BLOCK
    half = dim // 2
    me = lax.axis_index("ctx")
    yy = (me // 2) % 2
    cc = me % 2
    zz = me // 4
    xor = lambda v: [(i, i ^ v) for i in range(nc)]
    ring = [(i, ((i // 4 + 1) % nz) * 4 + i % 4) for i in range(nc)]
    perm = lambda v, p: lax.ppermute(v, "ctx", p)
    gather = lambda v: lax.all_gather(v, "wt", axis=0, tiled=True)
    pick = lambda v, i: lax.dynamic_index_in_dim(v, i, 0, keepdims=False)

    ours = nw == 2 and nz == 4
    small = (b_query, b_value, b_out, gain_one, shift_one, b_down, gain_two, shift_two, b_up)
    by_seq = lambda a, b: jnp.where(yy == 0, jnp.concatenate([a, b], 0), jnp.concatenate([b, a], 0))
    r_ids = (zz - jnp.arange(nz, dtype=jnp.int32)) % nz
    quad = (me % 4) ^ jnp.array([0, 2, 1, 3], jnp.int32)
    order_row = pick(block_order, yy)
    slots = (r_ids[:, None, None] * 4 + quad[None, :, None]) * hb + jnp.arange(hb, dtype=jnp.int32)
    blk = order_row[slots.reshape(-1)]

    if ours:
        att, wo, wu, wd, sm, x_all, wqkv, ot, lse, k, v, kt, qn, qt = front(nz, block_order, small, block_in, (w_query, w_key, w_value, w_out, w_up, w_down))
        att = att.reshape(-1, dim)
    else:
        cols = lambda w: lax.dynamic_slice_in_dim(w, cc * half, half, 1)
        wqkv = gather(jnp.concatenate([cols(w_query), cols(w_key), cols(w_value)], axis=1))
        small = lax.all_gather(jnp.concatenate(small), "wt", axis=0)
        vec8 = jnp.transpose(small[:, :8 * dim // nw].reshape(nw, 8, dim // nw), (1, 0, 2)).reshape(8, 2, half)
        upb = small[:, 8 * dim // nw:].reshape(2, 4, half)
        sm = jnp.pad(jnp.concatenate([jnp.transpose(vec8, (1, 0, 2)), upb], axis=1).astype(f32), ((0, 0), (0, 4), (0, 0)))
        wo, wu, wd = gather(w_out), gather(w_up), gather(w_down)
        x_all = gather_all(nz, block_in)[0]
        o, ot, lse, k, v, kt, qn, qt = attn_fwd(nz, blk, x_all, wqkv, pick(sm, cc)[0:1], pick(sm, cc)[1:2])
        o_self, o_y, o_c, o_yc = o[0], perm(o[1], xor(2)), perm(o[2], xor(1)), perm(o[3], xor(3))
        mine, other = by_seq(o_self, o_y), by_seq(o_c, o_yc)
        att = jnp.where(cc == 0, jnp.concatenate([mine, other], 1), jnp.concatenate([other, mine], 1))

    out, dsm, d_o, gw, gv = dense(block_in.reshape(-1, dim), cotangent.reshape(-1, dim), att, wo, wu, wd, sm)

    d_o = d_o.reshape(seqs, rows, dim)
    d_own, d_oth = pick(d_o, yy), pick(d_o, 1 - yy)
    fh = lambda v, c: lax.dynamic_slice_in_dim(v, c * half, half, 1)
    do_all = jnp.concatenate([fh(d_own, cc), perm(fh(d_oth, cc), xor(2)), perm(fh(d_own, 1 - cc), xor(1)), perm(fh(d_oth, 1 - cc), xor(3))], axis=0)
    dx, gq, gb = attn_bwd(nz, blk, x_all, wqkv, k, v, kt, qn, qt, ot, lse, do_all.reshape(4, rows, half))
    gvec = jnp.zeros((24, dim), f32).at[:16].set(gv)
    gvec = lax.dynamic_update_slice(gvec, gb[0:1], (16, cc * half))
    gvec = lax.dynamic_update_slice(gvec, gb[1:2], (17, cc * half))
    wi = lax.axis_index("wt")
    ff, hr = w_up.shape[1], dim // 2
    nu = ff // dim
    if ours:
        dxo, go, gqo, gvec = reduce_all(nz, dx.reshape(nz, 4 * rows, dim), gw, gq, gvec)
        go = go.reshape(-1, dim)
        t_out = go[:hr].astype(f32)
        t_up = go[hr:hr + nu * hr].astype(f32).reshape(nu, hr, dim).transpose(1, 0, 2).reshape(hr, ff)
        t_down = go[hr + nu * hr:].astype(f32)
        gqo = gqo.reshape(2, 3, hr, half).transpose(1, 2, 0, 3).reshape(3, hr, dim)
        t_qkv = [gqo[i].astype(f32) for i in range(3)]
        dkv_sum = by_seq(dxo[0], dxo[1]).astype(f32)
    else:
        dx = dx.reshape(nz, 2, 2 * rows, dim)
        part = lambda r: dx[r, 0].astype(f32) + perm(dx[r, 1], xor(1)).astype(f32)
        acc = None
        for r in list(range(1, nz)) + [0]:
            acc = part(r) if acc is None else perm(acc.astype(bf16), ring).astype(f32) + part(r)
        from_y = perm(acc[rows:].astype(bf16), xor(2)).astype(f32)
        dkv_sum = by_seq(acc[:rows], from_y)
        gvec = lax.psum(gvec, ("ctx", "wt"))
        g_out = gw[:, :hr].reshape(dim, dim)
        g_up = gw[:, hr:hr + nu * hr].reshape(2, nu, hr, dim).transpose(0, 2, 1, 3).reshape(dim, ff)
        g_down = gw[:, hr + nu * hr:].reshape(ff, dim)
        gq3 = gq.reshape(2, 3, hr, half).transpose(1, 0, 2, 3).reshape(3, dim, half)
        g_qkv = lax.dynamic_update_slice(jnp.zeros((3, dim, dim), bf16), gq3, (0, 0, cc * half))
        total = lambda g: lax.psum(lax.psum_scatter(g, "wt", scatter_dimension=0, tiled=True), "ctx").astype(f32)
        t_out, t_up, t_down = total(g_out), total(g_up), total(g_down)
        t_qkv = [total(g_qkv[i]) for i in range(3)]
    grad_in = (dsm + dkv_sum).astype(bf16).reshape(seqs, rows, dim)

    def share(vv):
        n = vv.size // nw
        return lax.dynamic_slice_in_dim(vv.reshape(-1), wi * n, n, 0)
    return (out.reshape(seqs, rows, dim), grad_in, t_qkv[0], share(gvec[16]), t_qkv[1], t_qkv[2], share(gvec[17]), t_out, share(gvec[0]),
            share(gvec[1]), share(gvec[2]), t_up, share(gvec[8:8 + nu]), t_down, share(gvec[3]), share(gvec[4]), share(gvec[5]))


def solution(mesh):
    seq, mat, vec = P("wt", "ctx", None), P("wt", None), P("wt")
    ins = (seq, mat, mat, vec, mat, mat, vec, mat, vec, vec, vec, mat, vec, mat, vec, vec, vec, seq)
    outs = (seq, seq, mat, vec, mat, mat, vec, mat, vec, vec, vec, mat, vec, mat, vec, vec, vec)
    run = functools.partial(body, nc=mesh.shape["ctx"], nw=mesh.shape["wt"])
    return jax.shard_map(run, mesh=mesh, in_specs=ins, out_specs=outs, check_vma=False)
```

```python
import functools
import math

import jax
import jax.numpy as jnp
from jax import lax
from jax.experimental import pallas as pl
from jax.experimental.pallas import tpu as pltpu
from jax.sharding import PartitionSpec as P

norm_eps = 1e-05

BLOCK = 128
HEADS_HERE = 4
LOG2E = 1.4426950408889634
FAR = -1e30
bf16, f32 = jnp.bfloat16, jnp.float32
NT = (((1,), (1,)), ((), ()))
TN = (((0,), (0,)), ((), ()))


def dot(a, b, dims=(((1,), (0,)), ((), ()))):
    return lax.dot_general(a, b, dims, preferred_element_type=f32)


def turned(v):
    return v.astype(f32).T.astype(bf16)


def head_slices():
    return [(slice(64 * h, 64 * h + 64), slice(128 * h, 128 * h + 128)) for h in range(HEADS_HERE)]


class Pairs:
    def __init__(self, nb, first):
        self.nb, self.first = nb, first

    def first_lo(self, n):
        return self.first(n) < self.nb // 2

    def lo(self, n):
        b = self.first(n)
        return jnp.where(b < self.nb // 2, b, self.nb - 1 - b)

    def ordered(self, n, v):
        a, b = v[:BLOCK], v[BLOCK:]
        first = self.first_lo(n)
        return jnp.where(first, a, b), jnp.where(first, b, a)


def project_chunk(pairs, r, x_ref, wkv_ref, wkvt_ref, bkv_ref, bkvt_ref, K, V, KT, VT):
    def piece(p, _):
        x = jnp.concatenate(pairs.ordered(r * 4 + p, x_ref[r, p]), axis=0)
        kv = dot(x, wkv_ref[...])
        k, v = kv[:, :256].astype(bf16), (kv[:, 256:] + bkv_ref[...]).astype(bf16)
        kvt = dot(wkvt_ref[...], x, NT)
        kt, vt = kvt[:256].astype(bf16), (kvt[256:] + bkvt_ref[...]).astype(bf16)
        at = pl.ds(pl.multiple_of(p * BLOCK, BLOCK), BLOCK)
        for u in range(2):
            rows = slice(u * BLOCK, (u + 1) * BLOCK)
            K[r, u, at, :] = k[rows]
            V[r, u, at, :] = v[rows]
            KT[r, u, :, at] = kt[:, rows]
            VT[r, u, :, at] = vt[:, rows]
        return 0
    lax.fori_loop(0, 4, piece, 0)


def project_queries(pairs, x_ref, wq_ref, bq_ref, qn, qt, qs):
    qs[...] = jnp.zeros_like(qs)

    def piece(p, _):
        x = jnp.concatenate(pairs.ordered(p, x_ref[0, p]), axis=0)
        q = (dot(x, wq_ref[...]) + bq_ref[...]) * (LOG2E / 8.0)
        for u in range(2):
            mine = q[u * BLOCK:(u + 1) * BLOCK]
            qn[p, u] = mine.astype(bf16)
            t = mine.T.astype(bf16)
            qt[p, u] = t
            for hs, cs in head_slices():
                qs[p, u, hs, cs] = t[hs]
        return 0
    lax.fori_loop(0, 4, piece, 0)


def by_pair(vt, p16):
    return jnp.concatenate([dot(vt[0:128], p16[:, 0:256]), dot(vt[128:256], p16[:, 256:512])], axis=1)


def unpair(a):
    return jnp.concatenate([a[64 * (h % 2):64 * (h % 2) + 64, 128 * h:128 * h + 128] for h in range(HEADS_HERE)], axis=0)


def fwd_step(pairs, r, i, own, K, VT, qs, m_s, l_s, acc, d_s, sb, pb):
    col = lambda v: jnp.max(v, axis=0, keepdims=True)
    tot = lambda v: jnp.sum(v, axis=0, keepdims=True)
    lo_i = pairs.lo(i)
    pick = [lo_i > pairs.lo(r * 4 + j) for j in range(4)]
    sa = dot(K[r, 0], qs[i, 1])
    for j in range(4):
        u = jnp.where(pick[j], 0, 1)
        s = dot(K[r, u, j * BLOCK:(j + 1) * BLOCK, :], qs[i, u])
        if own:
            s = jnp.where(d_s[...] <= jnp.where(i == j, 0, 2 * BLOCK), s, FAR)
        sb[j] = s
    tops = [col(sb[j]) for j in range(4)]
    m_hi, m_lo = col(sa), None
    for j in range(4):
        m_hi = jnp.maximum(m_hi, jnp.where(pick[j], FAR, tops[j]))
        t = jnp.where(pick[j], tops[j], FAR)
        m_lo = t if m_lo is None else jnp.maximum(m_lo, t)
    if own:
        rows = pl.ds(pl.multiple_of(i * BLOCK, BLOCK), BLOCK)
        sd = jnp.where(d_s[...] <= 0, dot(K[r, 0, rows, :], qs[i, 0]), FAR)
        m_lo = jnp.maximum(m_lo, col(sd))
    else:
        old_hi, old_lo = m_s[i, 1], m_s[i, 0]
        m_hi, m_lo = jnp.maximum(m_hi, old_hi), jnp.maximum(m_lo, old_lo)
    pa = jnp.exp2(sa - m_hi)
    l_hi, l_lo = tot(pa), jnp.zeros((1, 512), f32)
    for j in range(4):
        p = jnp.exp2(sb[j] - jnp.where(pick[j], m_lo, m_hi))
        t = tot(p)
        l_hi = l_hi + jnp.where(pick[j], 0.0, t)
        l_lo = l_lo + jnp.where(pick[j], t, 0.0)
        low = p.astype(bf16)
        rows = slice(j * BLOCK, (j + 1) * BLOCK)
        zero = jnp.zeros_like(low)
        pb[0, rows, :] = jnp.where(pick[j], low, zero)
        pb[1, rows, :] = jnp.where(pick[j], zero, low)
    o_hi = by_pair(VT[r, 0], pa.astype(bf16)) + by_pair(VT[r, 1], pb[1])
    o_lo = by_pair(VT[r, 0], pb[0])
    if own:
        p = jnp.exp2(sd - m_lo)
        l_lo = l_lo + tot(p)
        at = pl.ds(pl.multiple_of(i * BLOCK, BLOCK), BLOCK)
        o_lo = o_lo + by_pair(VT[r, 0, :, at], p.astype(bf16))
        l_s[i, 1], l_s[i, 0] = l_hi, l_lo
        acc[i, 1], acc[i, 0] = o_hi, o_lo
    else:
        f_hi, f_lo = jnp.exp2(old_hi - m_hi), jnp.exp2(old_lo - m_lo)
        l_s[i, 1] = l_s[i, 1] * f_hi + l_hi
        l_s[i, 0] = l_s[i, 0] * f_lo + l_lo
        acc[i, 1] = acc[i, 1] * f_hi + o_hi
        acc[i, 0] = acc[i, 0] * f_lo + o_lo
    m_s[i, 1], m_s[i, 0] = m_hi, m_lo


def fwd_finish(pairs, m_s, l_s, acc, lse, ot, o_ref):
    def pair(i, _):
        first = pairs.first_lo(i)
        out = []
        for u in range(2):
            l = l_s[i, u]
            lse[i, u] = m_s[i, u] + jnp.log2(l)
            t = unpair(acc[i, u] * (1.0 / l))
            ot[i, u] = t
            out.append(t.T.astype(bf16))
        o_ref[i, 0:BLOCK, :] = jnp.where(first, out[0], out[1])
        o_ref[i, BLOCK:2 * BLOCK, :] = jnp.where(first, out[1], out[0])
        return 0
    lax.fori_loop(0, 4, pair, 0)


def diagonal(d_s):
    d_s[...] = lax.broadcasted_iota(jnp.int32, d_s.shape, 0) - (lax.broadcasted_iota(jnp.int32, d_s.shape, 1) & (BLOCK - 1))


def fwd_local(nz, blk_ref, x_ref, wqkv_ref, bq_ref, bkv_ref, bkvt_ref, o_ref, ot, lse, K, V, KT, qn, qt, VT, qs, m_s, l_s, acc, d_s, sb, pb, wkvt):
    pairs = Pairs(nz * 8, lambda n: blk_ref[2 * n])
    diagonal(d_s)
    wkvt[...] = turned(wqkv_ref[:, 256:])
    project_queries(pairs, x_ref, wqkv_ref.at[:, 0:256], bq_ref, qn, qt, qs)
    for r in range(nz):
        project_chunk(pairs, r, x_ref, wqkv_ref.at[:, 256:768], wkvt, bkv_ref, bkvt_ref, K, V, KT, VT)
        def step(i, _):
            fwd_step(pairs, r, i, r == 0, K, VT, qs, m_s, l_s, acc, d_s, sb, pb)
            return 0
        lax.fori_loop(0, 4, step, 0)
    fwd_finish(pairs, m_s, l_s, acc, lse, ot, o_ref)


def fwd_outs(nz):
    sds = jax.ShapeDtypeStruct
    kv = sds((nz, 2, 512, 256), bf16)
    return (sds((4, 256, 256), bf16), sds((4, 2, 256, 128), f32), sds((4, 2, 1, 512), f32), kv, kv, sds((nz, 2, 256, 512), bf16),
            sds((4, 2, 128, 256), bf16), sds((4, 2, 256, 128), bf16))


def fwd_scratch(nz):
    M = pltpu.VMEM
    return [M((nz, 2, 256, 512), bf16), M((4, 2, 256, 512), bf16), M((4, 2, 1, 512), f32), M((4, 2, 1, 512), f32), M((4, 2, 128, 512), f32),
            M((128, 512), jnp.int32), M((4, 128, 512), f32), M((2, 512, 512), bf16), M((512, 512), bf16)]


def attn_fwd(nz, blk, x, wqkv, bq, bkv):
    V = pl.BlockSpec(memory_space=pltpu.VMEM)
    return pl.pallas_call(
        functools.partial(fwd_local, nz), out_shape=fwd_outs(nz),
        in_specs=[pl.BlockSpec(memory_space=pltpu.SMEM)] + [V] * 5, out_specs=(V,) * 8, scratch_shapes=fwd_scratch(nz),
        compiler_params=pltpu.CompilerParams(vmem_limit_bytes=58 << 20), name="attn_fwd")(blk, x, wqkv, bq, bkv, bkv.reshape(256, 1))


def bwd_queries(pairs, do_ref, ot, qn, qt, qs, dos, qns, dons, dl):
    def piece(i, _):
        for u, do in enumerate(pairs.ordered(i, do_ref[i])):
            dot_t = do.astype(f32).T
            prod = dot_t * ot[i, u]
            low = dot_t.astype(bf16)
            q, t = qn[i, u], qt[i, u]
            for hs, cs in head_slices():
                qs[i, u, hs, cs] = t[hs]
                dos[i, u, hs, cs] = low[hs]
                qns[i, u, cs, hs] = q[:, hs]
                dons[i, u, cs, hs] = do[:, hs]
                dl[i, u, :, cs] = jnp.sum(prod[hs], axis=0, keepdims=True)
        return 0
    lax.fori_loop(0, 4, piece, 0)


def bwd_step(pairs, r, i, own, first, K, V, KT, qs, dos, qns, dons, lse, dl, dk, dv, dq, d_s, gb):
    lo_i = pairs.lo(i)
    pick = [lo_i > pairs.lo(r * 4 + j) for j in range(4)]

    def pieces(k, v, u, mask):
        s = dot(k, qs[i, u]) - lse[i, u]
        if mask is not None:
            s = jnp.where(d_s[...] <= mask, s, FAR)
        p = jnp.exp2(s)
        g = p * (dot(v, dos[i, u]) - dl[i, u])
        return p.astype(bf16), g.astype(bf16)

    p, g = pieces(K[r, 0], V[r, 0], 1, None)
    dv[0] += dot(p, dons[i, 1])
    dk[0] += dot(g, qns[i, 1])
    q_hi = by_pair(KT[r, 0], g)
    for j in range(4):
        u = jnp.where(pick[j], 0, 1)
        rows = slice(j * BLOCK, (j + 1) * BLOCK)
        p, g = pieces(K[r, u, rows, :], V[r, u, rows, :], u, jnp.where(i == j, 0, 2 * BLOCK) if own else None)
        gv, gk = dot(p, dons[i, u]), dot(g, qns[i, u])
        dv[0, rows, :] += jnp.where(pick[j], gv, 0.0)
        dv[1, rows, :] += jnp.where(pick[j], 0.0, gv)
        dk[0, rows, :] += jnp.where(pick[j], gk, 0.0)
        dk[1, rows, :] += jnp.where(pick[j], 0.0, gk)
        zero = jnp.zeros_like(g)
        gb[0, rows, :] = jnp.where(pick[j], g, zero)
        gb[1, rows, :] = jnp.where(pick[j], zero, g)
    q_hi = q_hi + by_pair(KT[r, 1], gb[1])
    q_lo = by_pair(KT[r, 0], gb[0])
    if own:
        rows = pl.ds(pl.multiple_of(i * BLOCK, BLOCK), BLOCK)
        p, g = pieces(K[r, 0, rows, :], V[r, 0, rows, :], 0, 0)
        dv[0, rows, :] += dot(p, dons[i, 0])
        dk[0, rows, :] += dot(g, qns[i, 0])
        q_lo = q_lo + by_pair(KT[r, 0, :, rows], g)
    if first:
        dq[i, 1], dq[i, 0] = q_hi, q_lo
    else:
        dq[i, 1] += q_hi
        dq[i, 0] += q_lo


def bwd_chunk_out(pairs, r, last, x_ref, wqkv_ref, dk, dv, dxq, dx, dw, db, gp):
    total = jnp.zeros((1, 256), f32)
    for p in range(4):
        at = slice(p * BLOCK, (p + 1) * BLOCK)
        g = [jnp.concatenate([(dk[u, at, :] * (1.0 / LOG2E)).astype(bf16), dv[u, at, :].astype(bf16)], axis=1) for u in range(2)]
        total = total + jnp.sum(g[0][:, 256:].astype(f32), axis=0, keepdims=True) + jnp.sum(g[1][:, 256:].astype(f32), axis=0, keepdims=True)
        first = pairs.first_lo(r * 4 + p)
        gp[p * 256:p * 256 + BLOCK, :] = jnp.where(first, g[0], g[1])
        gp[p * 256 + BLOCK:p * 256 + 256, :] = jnp.where(first, g[1], g[0])
    db[1:2, :] += total
    for p in (2, 3, 0, 1):
        rows = slice(p * 256, p * 256 + 256)
        d = dot(gp[rows, :], wqkv_ref[:, 256:768], NT)
        if last:
            d = d + dxq[p]
        dx[r, rows, :] = d.astype(bf16)
    dw[:, 256:768] += dot(x_ref[r].reshape(1024, 512), gp[...], TN)


def bwd_query_out(pairs, x_ref, wqkv_ref, dq, dxq, dw, db):
    def piece(i, _):
        t = [(unpair(dq[i, u]) * 0.125).T.astype(bf16) for u in range(2)]
        first = pairs.first_lo(i)
        g = jnp.concatenate([jnp.where(first, t[0], t[1]), jnp.where(first, t[1], t[0])], axis=0)
        dxq[i] = dot(g, wqkv_ref[:, 0:256], NT)
        dw[:, 0:256] += dot(x_ref[0, i], g, TN)
        db[0:1, :] += jnp.sum(g.astype(f32), axis=0, keepdims=True)
        return 0
    lax.fori_loop(0, 4, piece, 0)


def weight_rows(dw, gq):
    for k in range(2):
        for m in range(3):
            gq[k, m * 256:m * 256 + 256, :] = dw[k * 256:k * 256 + 256, m * 256:m * 256 + 256].astype(bf16)


def bwd_local(nz, blk_ref, x_ref, wqkv_ref, K, V, KT, qn, qt, ot, lse, do_ref, dx, gq, db, qs, dos, qns, dons, dl, dk, dv, dq, d_s, gb, dxq, dw, gp):
    pairs = Pairs(nz * 8, lambda n: blk_ref[2 * n])
    diagonal(d_s)
    dw[...] = jnp.zeros_like(dw)
    db[...] = jnp.zeros_like(db)
    for s in (qs, dos, qns, dons):
        s[...] = jnp.zeros_like(s)
    bwd_queries(pairs, do_ref, ot, qn, qt, qs, dos, qns, dons, dl)
    for r in list(range(1, nz)) + [0]:
        dk[...] = jnp.zeros_like(dk)
        dv[...] = jnp.zeros_like(dv)
        def step(i, _):
            bwd_step(pairs, r, i, r == 0, r == 1, K, V, KT, qs, dos, qns, dons, lse, dl, dk, dv, dq, d_s, gb)
            return 0
        lax.fori_loop(0, 4, step, 0)
        if r == 0:
            bwd_query_out(pairs, x_ref, wqkv_ref, dq, dxq, dw, db)
        bwd_chunk_out(pairs, r, r == 0, x_ref, wqkv_ref, dk, dv, dxq, dx, dw, db, gp)
    weight_rows(dw, gq)


def bwd_scratch():
    M = pltpu.VMEM
    return [M((4, 2, 256, 512), bf16), M((4, 2, 256, 512), bf16), M((4, 2, 512, 256), bf16), M((4, 2, 512, 256), bf16), M((4, 2, 1, 512), f32),
            M((2, 512, 256), f32), M((2, 512, 256), f32), M((4, 2, 128, 512), f32), M((128, 512), jnp.int32), M((2, 512, 512), bf16),
            M((4, 256, 512), f32), M((512, 768), f32)]


def attn_bwd(nz, blk, x, wqkv, K, V, KT, qn, qt, ot, lse, do):
    S = pl.BlockSpec(memory_space=pltpu.VMEM)
    sds = jax.ShapeDtypeStruct
    return pl.pallas_call(
        functools.partial(bwd_local, nz), out_shape=(sds((nz, 1024, 512), bf16), sds((2, 768, 256), bf16), sds((8, 256), f32)),
        in_specs=[pl.BlockSpec(memory_space=pltpu.SMEM)] + [S] * 10, out_specs=(S,) * 3, scratch_shapes=bwd_scratch() + [pltpu.VMEM((1024, 512), bf16)],
        compiler_params=pltpu.CompilerParams(vmem_limit_bytes=58 << 20), name="attn_bwd")(blk, x, wqkv, K, V, KT, qn, qt, ot, lse, do)


def dense_kernel(x_ref, cot_ref, att_ref, wo_ref, wu_ref, wd_ref, sm_ref,
                 out_ref, dsm_ref, do_ref, gw_ref, gv_ref, act_s, gp_s, norm_s, dpre_s):
    ff = wu_ref.shape[1]
    chunk = 512
    x = x_ref[...].astype(f32)
    vec = lambda i: jnp.concatenate([sm_ref[0, i:i + 1, :], sm_ref[1, i:i + 1, :]], axis=1)
    b_out, g1, s1, b_down, g2, s2 = (vec(i) for i in range(2, 8))
    mean = lambda v: jnp.mean(v, axis=-1, keepdims=True)
    col = lambda v: jnp.sum(v, axis=0, keepdims=True)
    mix = x + dot(att_ref[...], wo_ref[...]) + b_out
    cen = mix - mean(mix)
    r1 = lax.rsqrt(mean(cen * cen) + norm_eps)
    n1 = cen * r1
    normed = n1 * g1 + s1
    nlow = normed.astype(bf16)
    norm_s[...] = nlow
    ffn = None
    for f in range(0, ff, chunk):
        fs = slice(f, f + chunk)
        at = 8 + f % (ff // 2) // 256
        b_up = jnp.concatenate([sm_ref[2 * f // ff, at + k:at + k + 1, :] for k in range(chunk // 256)], axis=1)
        pre = dot(nlow, wu_ref[:, fs]) + b_up
        c0 = math.sqrt(2.0 / math.pi)
        sq = pre * pre
        th = jnp.tanh(c0 * pre * (1.0 + 0.044715 * sq))
        half = 0.5 * (1.0 + th)
        act = (pre * half).astype(bf16)
        act_s[:, fs] = act
        gp_s[:, fs] = half + 0.5 * pre * (1.0 - th * th) * (c0 * (1.0 + 3 * 0.044715 * sq))
        part = dot(act, wd_ref[fs, :])
        ffn = part if ffn is None else ffn + part
    summed = ffn + b_down + normed + x
    cen = summed - mean(summed)
    r2 = lax.rsqrt(mean(cen * cen) + norm_eps)
    n2 = cen * r2
    out_ref[...] = (n2 * g2 + s2).astype(bf16)
    up = cot_ref[...].astype(f32)
    gv_ref[4:5, :] = col(up * n2)
    gv_ref[5:6, :] = col(up)
    dn = up * g2
    dsum = r2 * (dn - mean(dn) - n2 * mean(dn * n2))
    dffn = dsum.astype(bf16)
    gv_ref[3:4, :] = col(dffn.astype(f32))
    dnorm = dsum
    half_rows = wo_ref.shape[0] // 2
    half_ff = ff // 2
    def put(g, at, rows):
        gw_ref[0, at:at + rows, :] = g[:rows].astype(bf16)
        gw_ref[1, at:at + rows, :] = g[rows:].astype(bf16)
    for f in range(0, ff, chunk):
        fs = slice(f, f + chunk)
        dact = dot(dffn, wd_ref[fs, :], NT)
        dpre = (dact * gp_s[:, fs]).astype(bf16)
        gv_ref[8 + f // chunk:9 + f // chunk, :] = col(dpre.astype(f32))
        dnorm = dnorm + dot(dpre, wu_ref[:, fs], NT)
        put(dot(norm_s[...], dpre, TN), half_rows + (f // chunk) * half_rows, half_rows)
        gd = dot(act_s[:, fs], dffn, TN).astype(bf16)
        base = half_rows * (1 + ff // chunk)
        which, off = f // half_ff, f % half_ff
        gw_ref[which, base + off:base + off + chunk, :] = gd
    gv_ref[1:2, :] = col(dnorm * n1)
    gv_ref[2:3, :] = col(dnorm)
    dn = dnorm * g1
    dmix = r1 * (dn - mean(dn) - n1 * mean(dn * n1))
    dsm_ref[...] = dsum + dmix
    dbr = dmix.astype(bf16)
    gv_ref[0:1, :] = col(dbr.astype(f32))
    do_ref[...] = dot(dbr, wo_ref[...], NT).astype(bf16)
    put(dot(att_ref[...], dbr, TN), 0, half_rows)


def dense(x, cot, att, wo, wu, wd, sm):
    V = pl.BlockSpec(memory_space=pltpu.VMEM)
    tok, dim = x.shape
    ff = wu.shape[1]
    rows = (2 * dim * ff + dim * dim) // 2 // dim
    return pl.pallas_call(
        dense_kernel,
        out_shape=(jax.ShapeDtypeStruct((tok, dim), bf16), jax.ShapeDtypeStruct((tok, dim), f32),
                   jax.ShapeDtypeStruct((tok, dim), bf16), jax.ShapeDtypeStruct((2, rows, dim), bf16),
                   jax.ShapeDtypeStruct((16, dim), f32)),
        in_specs=[V] * 7, out_specs=(V,) * 5,
        scratch_shapes=[pltpu.VMEM((tok, ff), bf16), pltpu.VMEM((tok, ff), f32), pltpu.VMEM((tok, dim), bf16),
                        pltpu.VMEM((8, 128), f32)],
        compiler_params=pltpu.CompilerParams(vmem_limit_bytes=56 << 20),
        name="dense")(x, cot, att, wo, wu, wd, sm)


MESH = pl.DeviceIdType.MESH


def places(nz):
    me, wi = lax.axis_index("ctx"), lax.axis_index("wt")
    z, y, c = me // 4, lax.rem(me // 2, 2), lax.rem(me, 2)
    low = lax.rem(me, 4)
    at = lambda zz, ll: (zz * 4 + ll, wi)
    to = dict(up=at(lax.rem(z + 1, nz), low), down=at(lax.rem(z + nz - 1, nz), low), core=at(z, low + 1 - 2 * c), y=at(z, low + 2 - 4 * y),
              x=(me, 1 - wi))
    return me, wi, z, y, c, low, to


def meet(targets):
    bar = pltpu.get_barrier_semaphore()
    for t in targets:
        pl.semaphore_signal(bar, inc=1, device_id=t, device_id_type=MESH)
    pl.semaphore_wait(bar, len(targets))


class Wires:
    def __init__(self, send, recv):
        self.send, self.recv, self.n, self.live = send, recv, 0, []

    def make(self, src, dst, to):
        cp = pltpu.make_async_remote_copy(src, dst, self.send.at[self.n], self.recv.at[self.n], device_id=to, device_id_type=MESH)
        self.n += 1
        return cp

    def go(self, src, dst, to):
        cp = self.make(src, dst, to)
        cp.start()
        self.live.append(cp)
        return cp

    def drain(self):
        for cp in self.live:
            cp.wait_send()


def rows_of(start, size, mult=16):
    return pl.ds(pl.multiple_of(start, mult), size)


def gather_kernel(nz, with_w, *refs):
    if with_w:
        (x_ref, wq_ref, wk_ref, wv_ref, wo_ref, wu_ref, wd_ref, sm_ref,
         xall, wqkv, wo, wu, wd, sm, send, recv, lsem) = refs
    else:
        x_ref, xall, send, recv, lsem = refs
    me, wi, z, y, c, low, to = places(nz)
    rows = x_ref.shape[1]
    local = []

    def copy(src, dst):
        cp = pltpu.make_async_copy(src, dst, lsem.at[len(local)])
        cp.start()
        local.append(cp)

    copy(x_ref.at[y], xall.at[0, 0])
    if with_w:
        R, half = wq_ref.shape[0], wq_ref.shape[1] // 2
        for i, w in enumerate((wq_ref, wk_ref, wv_ref)):
            copy(w.at[:, rows_of(c * half, half, 128)], wqkv.at[rows_of(wi * R, R), pl.ds(i * half, half)])
        for w, full in ((wo_ref, wo), (wu_ref, wu), (wd_ref, wd)):
            n = w.shape[0]
            copy(w, full.at[rows_of(wi * n, n)])
        copy(sm_ref, sm.at[wi])
    near = [to["up"], to["down"], to["core"], to["y"]] + ([to["x"]] if with_w else [])
    meet(near)
    wires = Wires(send, recv)
    yx = wires.go(x_ref.at[1 - y], xall.at[0, 1], to["y"])
    ring = {(1, 0): wires.go(x_ref.at[y], xall.at[1, 0], to["up"])}
    core = {(0, 0): wires.go(x_ref.at[y], xall.at[0, 2], to["core"])}
    if with_w:
        xs = []
        for i, w in enumerate((wq_ref, wk_ref, wv_ref)):
            xs.append(wires.go(w.at[:, rows_of(c * half, half, 128)], wqkv.at[rows_of(wi * R, R), pl.ds(i * half, half)], to["x"]))
        xs.append(wires.go(sm_ref, sm.at[wi], to["x"]))
        big = []
        for w, full in ((wo_ref, wo), (wu_ref, wu), (wd_ref, wd)):
            n = w.shape[0]
            h = n // 2
            cp = wires.go(w.at[rows_of(c * h, h)], full.at[rows_of(wi * n + c * h, h)], to["x"])
            big.append((cp, full, rows_of((1 - wi) * n + c * h, h)))
    yx.wait_recv()
    ring[1, 1] = wires.go(xall.at[0, 1], xall.at[1, 1], to["up"])
    core[0, 1] = wires.go(xall.at[0, 1], xall.at[0, 3], to["core"])
    shared = []
    for r in range(1, nz):
        for s in range(2):
            ring[r, s].wait_recv()
            if r < nz - 1:
                ring[r + 1, s] = wires.go(xall.at[r, s], xall.at[r + 1, s], to["up"])
            core[r, s] = wires.go(xall.at[r, s], xall.at[r, 2 + s], to["core"])
        if with_w and r - 1 < len(big):
            cp, full, where = big[r - 1]
            cp.wait_recv()
            shared.append(wires.go(full.at[where], full.at[where], to["core"]))
    if with_w:
        for cp, full, where in big[nz - 1:]:
            cp.wait_recv()
            shared.append(wires.go(full.at[where], full.at[where], to["core"]))
        for cp in xs + shared:
            cp.wait_recv()
    for cp in core.values():
        cp.wait_recv()
    wires.drain()
    for cp in local:
        cp.wait()


def gather_all(nz, x, weights=None, small=None):
    A = pl.BlockSpec(memory_space=pl.ANY)
    sds = jax.ShapeDtypeStruct
    rows, dim = x.shape[1:]
    outs = [sds((nz, 4, rows, dim), bf16)]
    ins = [x]
    ncopy = 1 + 2 * (nz - 1) + 2 * nz
    if weights is not None:
        wq, wk, wv, wo, wu, wd = weights
        ins += list(weights) + [small]
        outs += [sds((dim, 3 * dim // 2), bf16)] + [sds((2 * w.shape[0], w.shape[1]), bf16) for w in (wo, wu, wd)] + [sds((2,) + small.shape, bf16)]
        ncopy += 10
    return pl.pallas_call(
        functools.partial(gather_kernel, nz, weights is not None),
        out_shape=tuple(outs), in_specs=[A] * len(ins), out_specs=(A,) * len(outs),
        scratch_shapes=[pltpu.SemaphoreType.DMA((ncopy,)), pltpu.SemaphoreType.DMA((ncopy,)), pltpu.SemaphoreType.DMA((8,))],
        compiler_params=pltpu.CompilerParams(collective_id=1, has_side_effects=True, vmem_limit_bytes=16 << 20),
        name="gather_all")(*ins)


def add_into(dst, parts, rows, step=64):
    def body(i, _):
        r = rows_of(i * step, step)
        total = parts[0](r)[...].astype(f32)
        for p in parts[1:]:
            total = total + p(r)[...].astype(f32)
        d = dst(r)
        d[...] = total.astype(bf16)
        return 0
    lax.fori_loop(0, rows // step, body, 0)


def offset(ref, lead, start):
    def view(r):
        at = pl.ds(pl.multiple_of(start + r.start, 16), r.size)
        return ref.at[lead + (at,)]
    return view


def chip_pairs(nz, order_ref):
    me = lax.axis_index("ctx")
    z, y, c = me // 4, lax.rem(me // 2, 2), lax.rem(me, 2)

    def first(n):
        r, p = n // 4, n % 4
        a, b = p % 2, p // 2
        yy, cc = y + a - 2 * y * a, c + b - 2 * c * b
        return order_ref[y, 2 * (lax.rem(z - r + nz, nz) * 4 + yy * 2 + cc)]
    return Pairs(nz * 8, first)


def front_kernel(nz, order_ref, bqr, bvr, bor, g1r, s1r, bdr, g2r, s2r, bur, x_ref, wq_ref, wk_ref, wv_ref, wo_ref, wu_ref, wd_ref,
                 att, wo, wu, wd, sm, xall, wqkv, ot_o, lse_o, K_o, V_o, KT_o, qn_o, qt_o,
                 xs, ws, sms, K, V, KT, VT, qn, qt, qs, m_s, l_s, acc, d_s, sb, pb, wkvt, bkvt, ot, lse, o_s, send, recv, lsem):
    me, wi, z, y, c, low, to = places(nz)
    to["yc"] = (z * 4 + 3 - low, wi)
    half, R = 256, wq_ref.shape[0]
    local = []

    def copy(src, dst):
        cp = pltpu.make_async_copy(src, dst, lsem.at[len(local)])
        cp.start()
        local.append(cp)
        return cp

    own_x = copy(x_ref.at[y], xs.at[0, 0])
    own_w = [copy(w.at[:, rows_of(c * half, half, 128)], ws.at[rows_of(wi * R, R), pl.ds(i * half, half)]) for i, w in enumerate((wq_ref, wk_ref, wv_ref))]
    for i, v in enumerate((bqr, bvr, bor, g1r, s1r, bdr, g2r, s2r)):
        sms[wi, i:i + 1, :] = v[...].astype(f32).reshape(1, half)
    up_b = bur[...].astype(f32).reshape(1, 1024)
    for i in range(4):
        sms[wi, 8 + i:9 + i, :] = up_b[:, i * half:(i + 1) * half]
    sms[wi, 12:16, :] = jnp.zeros((4, half), f32)
    meet([to[k] for k in ("up", "down", "core", "y", "yc", "x")])
    w = Wires(send, recv)
    yx = w.go(x_ref.at[1 - y], xs.at[0, 1], to["y"])
    ring, core = {}, {}
    ring[1, 0] = w.go(x_ref.at[y], xs.at[1, 0], to["up"])
    core[0, 0] = w.go(x_ref.at[y], xs.at[0, 2], to["core"])
    wx = []
    for i, m in enumerate((wq_ref, wk_ref, wv_ref)):
        wx.append(w.go(m.at[:, rows_of(c * half, half, 128)], ws.at[rows_of(wi * R, R), pl.ds(i * half, half)], to["x"]))
    wx.append(w.go(sms.at[wi], sms.at[wi], to["x"]))
    big = []
    for m, full in ((wo_ref, wo), (wu_ref, wu), (wd_ref, wd)):
        n = m.shape[0]
        h = n // 2
        copy(m, full.at[rows_of(wi * n, n)])
        big.append((w.go(m.at[rows_of(c * h, h)], full.at[rows_of(wi * n + c * h, h)], to["x"]), full, rows_of((1 - wi) * n + c * h, h)))

    pairs = chip_pairs(nz, order_ref)
    diagonal(d_s)
    yx.wait_recv()
    ring[1, 1] = w.go(xs.at[0, 1], xs.at[1, 1], to["up"])
    core[0, 1] = w.go(xs.at[0, 1], xs.at[0, 3], to["core"])

    def pump(r, s):
        ring[r, s].wait_recv()
        if r < nz - 1:
            ring[r + 1, s] = w.go(xs.at[r, s], xs.at[r + 1, s], to["up"])
        core[r, s] = w.go(xs.at[r, s], xs.at[r, 2 + s], to["core"])

    shared = []

    def share(k):
        cp, full, where = big[k]
        cp.wait_recv()
        shared.append(w.go(full.at[where], full.at[where], to["core"]))

    pump(1, 0)
    for cp in own_w:
        cp.wait()
    for cp in wx:
        cp.wait_recv()
    copy(sms, sm)
    copy(ws, wqkv)
    wkvt[...] = turned(ws[:, 256:])
    bv = sms[c, 1:2, :]
    bkvt[...] = jnp.broadcast_to(bv, (8, half)).T[:, 0:1]
    own_x.wait()
    for s in range(2):
        core[0, s].wait_recv()
    project_queries(pairs, xs, ws.at[:, 0:256], sms.at[c, 0:1], qn, qt, qs)
    copy(qn, qn_o)
    copy(qt, qt_o)

    def chunk(r):
        project_chunk(pairs, r, xs, ws.at[:, 256:768], wkvt, sms.at[c, 1:2], bkvt, K, V, KT, VT)
        for a, b in ((xs, xall), (K, K_o), (V, V_o), (KT, KT_o)):
            copy(a.at[r], b.at[r])

    def attend(r, start, stop):
        def step(i, _):
            fwd_step(pairs, r, i, r == 0, K, VT, qs, m_s, l_s, acc, d_s, sb, pb)
            return 0
        lax.fori_loop(start, stop, step, 0)

    chunk(0)
    pump(1, 1)
    attend(0, 0, 2)
    attend(0, 2, 4)
    for r in range(1, nz):
        if r + 1 < nz:
            pump(r + 1, 0)
        for s in range(2):
            core[r, s].wait_recv()
        chunk(r)
        attend(r, 0, 2)
        if r + 1 < nz:
            pump(r + 1, 1)
            share(r - 1)
        attend(r, 2, 4)
    fwd_finish(pairs, m_s, l_s, acc, lse, ot, o_s)
    cols = pl.ds(pl.multiple_of(c * half, half), half)
    outs = [w.go(o_s.at[p], att.at[y, :, cols], to[k]) for p, k in ((1, "y"), (2, "core"), (3, "yc"))]
    copy(o_s.at[0], att.at[y, :, cols])
    copy(ot, ot_o)
    copy(lse, lse_o)
    share(2)
    for cp in outs + shared:
        cp.wait_recv()
    w.drain()
    for cp in local[4:]:
        cp.wait()


def front(nz, order, vectors, x, weights):
    A = pl.BlockSpec(memory_space=pltpu.HBM)
    V = pl.BlockSpec(memory_space=pltpu.VMEM)
    sds = jax.ShapeDtypeStruct
    M = pltpu.VMEM
    rows, dim = x.shape[1:]
    wq, wk, wv, wo, wu, wd = weights
    outs = [sds((2, rows, dim), bf16)] + [sds((2 * w.shape[0], w.shape[1]), bf16) for w in (wo, wu, wd)]
    outs += [sds((2, 16, 256), f32), sds((nz, 4, rows, dim), bf16), sds((dim, 768), bf16)] + list(fwd_outs(nz)[1:])
    scratch = [M((nz, 4, rows, dim), bf16), M((dim, 768), bf16), M((2, 16, 256), f32)]
    scratch += [M((nz, 2, 512, 256), bf16)] * 2 + [M((nz, 2, 256, 512), bf16)] * 2 + [M((4, 2, 128, 256), bf16), M((4, 2, 256, 128), bf16)]
    scratch += fwd_scratch(nz)[1:] + [M((256, 1), f32), M((4, 2, 256, 128), f32), M((4, 2, 1, 512), f32), M((4, 256, 256), bf16)]
    scratch += [pltpu.SemaphoreType.DMA((40,)), pltpu.SemaphoreType.DMA((40,)), pltpu.SemaphoreType.DMA((40,))]
    return pl.pallas_call(
        functools.partial(front_kernel, nz), out_shape=tuple(outs),
        in_specs=[pl.BlockSpec(memory_space=pltpu.SMEM)] + [V] * 9 + [A] * 7, out_specs=(A,) * len(outs), scratch_shapes=scratch,
        compiler_params=pltpu.CompilerParams(collective_id=1, has_side_effects=True, vmem_limit_bytes=58 << 20), name="front")(
            order, *vectors, x, *weights)


def back_kernel(nz, order_ref, gv_ref, do_ref, x_hbm, w_hbm, K_h, V_h, KT_h, qn_h, qt_h, ot_h, lse_h, gw_ref,
                dxo, go, gqo, gvo,
                xs, wqkv, K, V, KT, qn, qt, ot, lse, do, qs, dos, qns, dons, dl, dk, dv, dq, d_s, gb, dxq, dw, dx, gp, gq, db, outdx,
                dx_core, dx_in, cr, cs, xr, xs_, yr, ys_, zr, xrq, xsq, yrq, ysq, zrq, gsum, gqsum, gvs, gvr, send, recv, lsem):
    me, wi, z, y, c, low, to = places(nz)
    to["yc"] = (z * 4 + 3 - low, wi)
    zto = [(lax.rem(z + d, nz) * 4 + low, wi) for d in range(1, nz)]
    half, hrow = 256, 256
    w = Wires(send, recv)
    local = []

    def copy(src, dst):
        cp = pltpu.make_async_copy(src, dst, lsem.at[len(local)])
        cp.start()
        local.append(cp)
        return cp

    mine_gw = [copy(gw_ref.at[:, rows_of(s * 768 + c * 384, 384)], cs.at[s]) for s in range(3)]
    cols = pl.ds(pl.multiple_of(c * half, half), half)
    other = pl.ds(pl.multiple_of((1 - c) * half, half), half)
    first_in = [copy(do_ref.at[y, :, cols], do.at[0])] + [copy(a, b) for a, b in ((qn_h, qn), (qt_h, qt), (ot_h, ot), (lse_h, lse))]
    kv_in = {}
    for r in list(range(1, nz)) + [0]:
        kv_in[r] = [copy(a.at[r], b.at[r]) for a, b in ((K_h, K), (V_h, V), (KT_h, KT), (x_hbm, xs))]
    w_in = copy(w_hbm, wqkv)
    meet([to[k] for k in ("core", "y", "yc", "x")] + zto)
    dos_in = [w.go(do_ref.at[1 - y, :, cols], do.at[1], to["y"]), w.go(do_ref.at[y, :, other], do.at[2], to["core"]),
              w.go(do_ref.at[1 - y, :, other], do.at[3], to["yc"])]
    got = {}
    for s in range(3):
        got["c", s] = w.go(gw_ref.at[:, rows_of(s * 768 + (1 - c) * 384, 384)], cr.at[s], to["core"])

    width = [384, 384, 384, 768]
    n_y = [v // 2 for v in width]
    n_z = [v // (2 * nz) for v in width]
    X_in = [xr.at[s] for s in range(3)] + [xrq]
    X_sum = [xs_.at[s] for s in range(3)] + [xsq]
    Y_in = [yr.at[s] for s in range(3)] + [yrq]
    Y_sum = [ys_.at[s] for s in range(3)] + [ysq]
    Z_in = [zr.at[s] for s in range(3)] + [zrq]
    out = [gsum.at[s] for s in range(3)] + [gqsum]

    def x_send(s):
        if s < 3:
            mine_gw[s].wait()
            got["c", s].wait_recv()
            for k in (1 - wi, wi):
                add_into(offset(cs, (s, k), 0), [offset(cs, (s, k), 0), offset(cr, (s, k), 0)], 384, 128)
                if ("x", s) not in got:
                    got["x", s] = w.go(cs.at[s, k], X_in[s], to["x"])
        else:
            got["x", s] = w.go(gq.at[1 - wi], X_in[s], to["x"])

    def y_send(s):
        got["x", s].wait_recv()
        mine = offset(cs, (s, wi), 0) if s < 3 else offset(gq, (wi,), 0)
        add_into(offset(X_sum[s], (), 0), [mine, offset(X_in[s], (), 0)], width[s], 128)
        got["y", s] = w.go(X_sum[s].at[rows_of((1 - y) * n_y[s], n_y[s])], Y_in[s], to["y"])

    def z_send(s):
        got["y", s].wait_recv()
        add_into(offset(Y_sum[s], (), 0), [offset(X_sum[s], (), y * n_y[s]), offset(Y_in[s], (), 0)], n_y[s], 96)
        for d in range(1, nz):
            zd = lax.rem(z + d, nz)
            got["z", s, d] = w.go(Y_sum[s].at[rows_of(zd * n_z[s], n_z[s])], Z_in[s].at[d - 1], zto[d - 1])

    def z_share(s):
        for d in range(1, nz):
            got["z", s, d].wait_recv()
        base = c * width[s] + y * n_y[s] + z * n_z[s]
        add_into(offset(out[s], (), base), [offset(Y_sum[s], (), z * n_z[s])] + [offset(Z_in[s], (d,), 0) for d in range(nz - 1)], n_z[s], 48)
        at = rows_of(base, n_z[s])
        for d in range(1, nz):
            got["zs", s, d] = w.go(out[s].at[at], out[s].at[at], zto[d - 1])

    def y_share(s):
        for d in range(1, nz):
            got["zs", s, d].wait_recv()
        at = rows_of(c * width[s] + y * n_y[s], n_y[s])
        got["ys", s] = w.go(out[s].at[at], out[s].at[at], to["y"])

    def c_share(s):
        got["ys", s].wait_recv()
        at = rows_of(c * width[s], width[s])
        got["cs", s] = w.go(out[s].at[at], out[s].at[at], to["core"])

    def give(r):
        got["d", r] = w.go(dx.at[r, pl.ds(512, 512)], dx_core.at[r], to["core"])

    def fold(r):
        got["d", r].wait_recv()
        add_into(offset(dx, (r,), 0), [offset(dx, (r,), 0), offset(dx_core, (r,), 0)], 512, 128)

    def hop(r, h):
        if r != 1:
            got["r", r, h].wait_recv()
            dst = offset(dx, (r,), h * hrow) if r or h else offset(outdx, (0,), 0)
            add_into(dst, [offset(dx, (r,), h * hrow), offset(dx_in, (r,), h * hrow)], hrow, 128)
        at = pl.ds(h * hrow, hrow)
        if r:
            n = (r + 1) % nz
            got["r", n, h] = w.go(dx.at[r, at], dx_in.at[n, at], to["up"])
        elif h:
            got["dy"] = w.go(dx.at[0, at], outdx.at[1], to["y"])

    vec_to = [to["core"], to["y"], to["x"]] + [(zz * 4 + low, wi) for zz in (z + 1 - 2 * lax.rem(z, 2), z + 2 - 4 * (z // 2))]

    def vec_send(k):
        if k == 0:
            gvs[0] = jnp.zeros_like(gvs[0])
            gvs[0, 0:16, :] = gv_ref[...]
            zero = jnp.zeros((1, half), f32)
            for i in range(2):
                v = db[i:i + 1, :]
                gvs[0, 16 + i:17 + i, :] = jnp.concatenate([jnp.where(c == 0, v, zero), jnp.where(c == 0, zero, v)], axis=1)
        else:
            got["v", k - 1].wait_recv()
            gvs[k] = gvs[k - 1] + gvr[k - 1]
        if k < 5:
            got["v", k] = w.go(gvs.at[k], gvr.at[k], vec_to[k])
        else:
            gvo[...] = gvs[5]

    pairs = chip_pairs(nz, order_ref)
    diagonal(d_s)
    dw[...] = jnp.zeros_like(dw)
    db[...] = jnp.zeros_like(db)
    for s in (qs, dos, qns, dons):
        s[...] = jnp.zeros_like(s)
    x_send(0)
    for cp in first_in:
        cp.wait()
    for cp in dos_in:
        cp.wait_recv()
    bwd_queries(pairs, do, ot, qn, qt, qs, dos, qns, dons, dl)
    x_send(1)
    x_send(2)

    def attend(r, start, stop):
        def step(i, _):
            bwd_step(pairs, r, i, r == 0, r == 1, K, V, KT, qs, dos, qns, dons, lse, dl, dk, dv, dq, d_s, gb)
            return 0
        lax.fori_loop(start, stop, step, 0)

    middle = {1: lambda: y_send(0), 2: lambda: (fold(1), hop(1, 1), hop(1, 0), y_send(1)), 3: lambda: (fold(2), hop(2, 1), z_send(1)),
              0: lambda: (fold(3), hop(3, 1), z_send(2), z_share(1))}
    after = {1: lambda: z_send(0), 2: lambda: z_share(0), 3: lambda: (hop(2, 0), y_send(2), y_share(0)), 0: lambda: None}
    for r in kv_in:
        for cp in kv_in[r]:
            cp.wait()
    for r in list(range(1, nz)) + [0]:
        dk[...] = jnp.zeros_like(dk)
        dv[...] = jnp.zeros_like(dv)
        attend(r, 0, 2)
        middle[r]()
        attend(r, 2, 4)
        if r == 1:
            w_in.wait()
        if r == 0:
            hop(3, 0)
            bwd_query_out(pairs, xs, wqkv, dq, dxq, dw, db)
        bwd_chunk_out(pairs, r, r == 0, xs, wqkv, dk, dv, dxq, dx, dw, db, gp)
        give(r)
        after[r]()
    weight_rows(dw, gq)
    x_send(3)
    vec_send(0)
    z_share(2)
    fold(0)
    hop(0, 1)
    y_share(1)
    vec_send(1)
    c_share(0)
    y_send(3)
    hop(0, 0)
    vec_send(2)
    y_share(2)
    z_send(3)
    vec_send(3)
    c_share(1)
    z_share(3)
    vec_send(4)
    c_share(2)
    y_share(3)
    vec_send(5)
    for s in range(3):
        got["cs", s].wait_recv()
        copy(gsum.at[s], go.at[s])
    c_share(3)
    got["dy"].wait_recv()
    copy(outdx, dxo)
    got["cs", 3].wait_recv()
    copy(gqsum, gqo)
    w.drain()
    for cp in local[-5:]:
        cp.wait()


def back(nz, order, gv, do, x_all, wqkv, k, v, kt, qn, qt, ot, lse, gw):
    A = pl.BlockSpec(memory_space=pltpu.HBM)
    V = pl.BlockSpec(memory_space=pltpu.VMEM)
    sds = jax.ShapeDtypeStruct
    B = lambda *s: pltpu.VMEM(s, bf16)
    F = lambda *s: pltpu.VMEM(s, f32)
    ins = (x_all, wqkv, k, v, kt, qn, qt, ot, lse)
    scratch = [pltpu.VMEM(a.shape, a.dtype) for a in ins] + [B(4, 256, 256)] + bwd_scratch()
    scratch += [B(nz, 1024, 512), B(1024, 512), B(2, 768, 256), F(8, 256), B(2, 256, 512)]
    scratch += [B(nz, 512, 512), B(nz, 512, 512), B(3, 2, 384, 512), B(3, 2, 384, 512), B(3, 384, 512), B(3, 384, 512), B(3, 192, 512), B(3, 192, 512),
                B(3, nz - 1, 48, 512), B(768, 256), B(768, 256), B(384, 256), B(384, 256), B(nz - 1, 96, 256), B(3, 768, 512), B(1536, 256),
                F(6, 24, 512), F(5, 24, 512)]
    scratch += [pltpu.SemaphoreType.DMA((80,)), pltpu.SemaphoreType.DMA((80,)), pltpu.SemaphoreType.DMA((40,))]
    return pl.pallas_call(
        functools.partial(back_kernel, nz),
        out_shape=(sds((2, 256, 512), bf16), sds((3, 768, 512), bf16), sds((1536, 256), bf16), sds((24, 512), f32)),
        in_specs=[pl.BlockSpec(memory_space=pltpu.SMEM), V] + [A] * 11, out_specs=(A, A, A, V), scratch_shapes=scratch,
        compiler_params=pltpu.CompilerParams(collective_id=2, has_side_effects=True, vmem_limit_bytes=62 << 20), name="back")(order, gv, do, *ins, gw)


def last_kernel(nu, go_ref, gq_ref, gv_ref, dx_ref, dsm_ref, gin, dwq, dbq, dwk, dwv, dbv, dwo, dbo, dg1, ds1, dwu, dbu, dwd, dbd, dg2, ds2):
    wi, y = lax.axis_index("wt"), lax.rem(lax.axis_index("ctx") // 2, 2)
    for s in range(2):
        seq = jnp.where(y == 0, s, 1 - s)
        gin[s] = (dsm_ref[s] + dx_ref[seq].astype(f32)).astype(bf16)
    hr = dwq.shape[0]
    for i, o in enumerate((dwq, dwk, dwv)):
        for k in range(2):
            o[:, k * 256:k * 256 + 256] = gq_ref[k * 3 * hr + i * hr:k * 3 * hr + (i + 1) * hr, :].astype(f32)
    dwo[...] = go_ref[0:hr, :].astype(f32)
    for k in range(nu):
        dwu[:, k * 512:k * 512 + 512] = go_ref[hr + k * hr:2 * hr + k * hr, :].astype(f32)
    dwd[...] = go_ref[hr + nu * hr:, :].astype(f32)

    def row(i):
        v = gv_ref[i:i + 1, :]
        return jnp.where(wi == 0, v[:, :256], v[:, 256:])

    for o, i in ((dbo, 0), (dg1, 1), (ds1, 2), (dbd, 3), (dg2, 4), (ds2, 5), (dbq, 16), (dbv, 17)):
        o[...] = row(i).reshape(256)
    h = nu // 2
    a, b = [jnp.concatenate([gv_ref[8 + k * h + i:9 + k * h + i, :] for i in range(h)], axis=1) for k in range(2)]
    dbu[...] = jnp.where(wi == 0, a, b).reshape(a.shape[1])


def last(nu, go, gqo, gv, dxo, dsm):
    V = pl.BlockSpec(memory_space=pltpu.VMEM)
    f = lambda *s: jax.ShapeDtypeStruct(s, f32)
    ff = nu * 512
    outs = (jax.ShapeDtypeStruct((2, 256, 512), bf16), f(256, 512), f(256), f(256, 512), f(256, 512), f(256), f(256, 512), f(256), f(256), f(256),
            f(256, ff), f(ff // 2), f(ff // 2, 512), f(256), f(256), f(256))
    return pl.pallas_call(functools.partial(last_kernel, nu), out_shape=outs, in_specs=[V] * 5, out_specs=(V,) * 16,
                          compiler_params=pltpu.CompilerParams(vmem_limit_bytes=56 << 20), name="last")(go, gqo, gv, dxo, dsm)


def body(block_in, block_order, w_query, b_query, w_key, w_value, b_value, w_out, b_out, gain_one, shift_one,
         w_up, b_up, w_down, b_down, gain_two, shift_two, cotangent, *, nc, nw):
    seqs, rows, dim = block_in.shape
    nz = nc // 4
    hb = rows // BLOCK
    half = dim // 2
    me = lax.axis_index("ctx")
    yy = (me // 2) % 2
    cc = me % 2
    zz = me // 4
    xor = lambda v: [(i, i ^ v) for i in range(nc)]
    ring = [(i, ((i // 4 + 1) % nz) * 4 + i % 4) for i in range(nc)]
    perm = lambda v, p: lax.ppermute(v, "ctx", p)
    gather = lambda v: lax.all_gather(v, "wt", axis=0, tiled=True)
    pick = lambda v, i: lax.dynamic_index_in_dim(v, i, 0, keepdims=False)

    ours = nw == 2 and nz == 4
    small = (b_query, b_value, b_out, gain_one, shift_one, b_down, gain_two, shift_two, b_up)
    by_seq = lambda a, b: jnp.where(yy == 0, jnp.concatenate([a, b], 0), jnp.concatenate([b, a], 0))
    r_ids = (zz - jnp.arange(nz, dtype=jnp.int32)) % nz
    quad = (me % 4) ^ jnp.array([0, 2, 1, 3], jnp.int32)
    order_row = pick(block_order, yy)
    slots = (r_ids[:, None, None] * 4 + quad[None, :, None]) * hb + jnp.arange(hb, dtype=jnp.int32)
    blk = order_row[slots.reshape(-1)]

    if ours:
        att, wo, wu, wd, sm, x_all, wqkv, ot, lse, k, v, kt, qn, qt = front(nz, block_order, small, block_in, (w_query, w_key, w_value, w_out, w_up, w_down))
        att = att.reshape(-1, dim)
    else:
        cols = lambda w: lax.dynamic_slice_in_dim(w, cc * half, half, 1)
        wqkv = gather(jnp.concatenate([cols(w_query), cols(w_key), cols(w_value)], axis=1))
        small = lax.all_gather(jnp.concatenate(small), "wt", axis=0)
        vec8 = jnp.transpose(small[:, :8 * dim // nw].reshape(nw, 8, dim // nw), (1, 0, 2)).reshape(8, 2, half)
        upb = small[:, 8 * dim // nw:].reshape(2, 4, half)
        sm = jnp.pad(jnp.concatenate([jnp.transpose(vec8, (1, 0, 2)), upb], axis=1).astype(f32), ((0, 0), (0, 4), (0, 0)))
        wo, wu, wd = gather(w_out), gather(w_up), gather(w_down)
        x_all = gather_all(nz, block_in)[0]
        o, ot, lse, k, v, kt, qn, qt = attn_fwd(nz, blk, x_all, wqkv, pick(sm, cc)[0:1], pick(sm, cc)[1:2])
        o_self, o_y, o_c, o_yc = o[0], perm(o[1], xor(2)), perm(o[2], xor(1)), perm(o[3], xor(3))
        mine, other = by_seq(o_self, o_y), by_seq(o_c, o_yc)
        att = jnp.where(cc == 0, jnp.concatenate([mine, other], 1), jnp.concatenate([other, mine], 1))

    out, dsm, d_o, gw, gv = dense(block_in.reshape(-1, dim), cotangent.reshape(-1, dim), att, wo, wu, wd, sm)

    if ours:
        dxo, go, gqo, gvec = back(nz, block_order, gv, d_o.reshape(seqs, rows, dim), x_all, wqkv, k, v, kt, qn, qt, ot, lse, gw)
        return (out.reshape(seqs, rows, dim),) + tuple(last(w_up.shape[1] // dim, go.reshape(-1, dim), gqo, gvec, dxo, dsm.reshape(seqs, rows, dim)))
    d_o = d_o.reshape(seqs, rows, dim)
    d_own, d_oth = pick(d_o, yy), pick(d_o, 1 - yy)
    fh = lambda v, c: lax.dynamic_slice_in_dim(v, c * half, half, 1)
    do_all = jnp.concatenate([fh(d_own, cc), perm(fh(d_oth, cc), xor(2)), perm(fh(d_own, 1 - cc), xor(1)), perm(fh(d_oth, 1 - cc), xor(3))], axis=0)
    dx, gq, gb = attn_bwd(nz, blk, x_all, wqkv, k, v, kt, qn, qt, ot, lse, do_all.reshape(4, rows, half))
    gvec = jnp.zeros((24, dim), f32).at[:16].set(gv)
    gvec = lax.dynamic_update_slice(gvec, gb[0:1], (16, cc * half))
    gvec = lax.dynamic_update_slice(gvec, gb[1:2], (17, cc * half))
    wi = lax.axis_index("wt")
    ff, hr = w_up.shape[1], dim // 2
    nu = ff // dim
    dx = dx.reshape(nz, 2, 2 * rows, dim)
    part = lambda r: dx[r, 0].astype(f32) + perm(dx[r, 1], xor(1)).astype(f32)
    acc = None
    for r in list(range(1, nz)) + [0]:
        acc = part(r) if acc is None else perm(acc.astype(bf16), ring).astype(f32) + part(r)
    from_y = perm(acc[rows:].astype(bf16), xor(2)).astype(f32)
    dkv_sum = by_seq(acc[:rows], from_y)
    gvec = lax.psum(gvec, ("ctx", "wt"))
    g_out = gw[:, :hr].reshape(dim, dim)
    g_up = gw[:, hr:hr + nu * hr].reshape(2, nu, hr, dim).transpose(0, 2, 1, 3).reshape(dim, ff)
    g_down = gw[:, hr + nu * hr:].reshape(ff, dim)
    gq3 = gq.reshape(2, 3, hr, half).transpose(1, 0, 2, 3).reshape(3, dim, half)
    g_qkv = lax.dynamic_update_slice(jnp.zeros((3, dim, dim), bf16), gq3, (0, 0, cc * half))
    total = lambda g: lax.psum(lax.psum_scatter(g, "wt", scatter_dimension=0, tiled=True), "ctx").astype(f32)
    t_out, t_up, t_down = total(g_out), total(g_up), total(g_down)
    t_qkv = [total(g_qkv[i]) for i in range(3)]
    grad_in = (dsm + dkv_sum).astype(bf16).reshape(seqs, rows, dim)

    def share(vv):
        n = vv.size // nw
        return lax.dynamic_slice_in_dim(vv.reshape(-1), wi * n, n, 0)
    return (out.reshape(seqs, rows, dim), grad_in, t_qkv[0], share(gvec[16]), t_qkv[1], t_qkv[2], share(gvec[17]), t_out, share(gvec[0]),
            share(gvec[1]), share(gvec[2]), t_up, share(gvec[8:8 + nu]), t_down, share(gvec[3]), share(gvec[4]), share(gvec[5]))


def solution(mesh):
    seq, mat, vec = P("wt", "ctx", None), P("wt", None), P("wt")
    ins = (seq, mat, mat, vec, mat, mat, vec, mat, vec, vec, vec, mat, vec, mat, vec, vec, vec, seq)
    outs = (seq, seq, mat, vec, mat, mat, vec, mat, vec, vec, vec, mat, vec, mat, vec, vec, vec)
    run = functools.partial(body, nc=mesh.shape["ctx"], nw=mesh.shape["wt"])
    return jax.shard_map(run, mesh=mesh, in_specs=ins, out_specs=outs, check_vma=False)
```

```python
import functools
import math

import jax
import jax.numpy as jnp
from jax import lax
from jax.experimental import pallas as pl
from jax.experimental.pallas import tpu as pltpu
from jax.sharding import PartitionSpec as P

norm_eps = 1e-05

BLOCK = 128
HEADS_HERE = 4
LOG2E = 1.4426950408889634
FAR = -1e30
bf16, f32 = jnp.bfloat16, jnp.float32
NT = (((1,), (1,)), ((), ()))
TN = (((0,), (0,)), ((), ()))


def dot(a, b, dims=(((1,), (0,)), ((), ()))):
    return lax.dot_general(a, b, dims, preferred_element_type=f32)


def turned(v):
    return v.astype(f32).T.astype(bf16)


def head_slices():
    return [(slice(64 * h, 64 * h + 64), slice(128 * h, 128 * h + 128)) for h in range(HEADS_HERE)]


class Pairs:
    def __init__(self, nb, first):
        self.nb, self.first = nb, first

    def first_lo(self, n):
        return self.first(n) < self.nb // 2

    def lo(self, n):
        b = self.first(n)
        return jnp.where(b < self.nb // 2, b, self.nb - 1 - b)

    def ordered(self, n, v):
        a, b = v[:BLOCK], v[BLOCK:]
        first = self.first_lo(n)
        return jnp.where(first, a, b), jnp.where(first, b, a)


def project_chunk(pairs, r, x_ref, wkv_ref, wkvt_ref, bkv_ref, bkvt_ref, K, V, KT, VT):
    def piece(p, _):
        x = jnp.concatenate(pairs.ordered(r * 4 + p, x_ref[r, p]), axis=0)
        kv = dot(x, wkv_ref[...])
        k, v = kv[:, :256].astype(bf16), (kv[:, 256:] + bkv_ref[...]).astype(bf16)
        kvt = dot(wkvt_ref[...], x, NT)
        kt, vt = kvt[:256].astype(bf16), (kvt[256:] + bkvt_ref[...]).astype(bf16)
        at = pl.ds(pl.multiple_of(p * BLOCK, BLOCK), BLOCK)
        for u in range(2):
            rows = slice(u * BLOCK, (u + 1) * BLOCK)
            K[r, u, at, :] = k[rows]
            V[r, u, at, :] = v[rows]
            KT[r, u, :, at] = kt[:, rows]
            VT[r, u, :, at] = vt[:, rows]
        return 0
    lax.fori_loop(0, 4, piece, 0)


def project_queries(pairs, x_ref, wq_ref, bq_ref, qn, qt, qs):
    qs[...] = jnp.zeros_like(qs)

    def piece(p, _):
        x = jnp.concatenate(pairs.ordered(p, x_ref[0, p]), axis=0)
        q = (dot(x, wq_ref[...]) + bq_ref[...]) * (LOG2E / 8.0)
        for u in range(2):
            mine = q[u * BLOCK:(u + 1) * BLOCK]
            qn[p, u] = mine.astype(bf16)
            t = mine.T.astype(bf16)
            qt[p, u] = t
            for hs, cs in head_slices():
                qs[p, u, hs, cs] = t[hs]
        return 0
    lax.fori_loop(0, 4, piece, 0)


def by_pair(vt, p16):
    return jnp.concatenate([dot(vt[0:128], p16[:, 0:256]), dot(vt[128:256], p16[:, 256:512])], axis=1)


def unpair(a):
    return jnp.concatenate([a[64 * (h % 2):64 * (h % 2) + 64, 128 * h:128 * h + 128] for h in range(HEADS_HERE)], axis=0)


def fwd_step(pairs, r, i, own, K, VT, qs, m_s, l_s, acc, d_s, sb, pb):
    col = lambda v: jnp.max(v, axis=0, keepdims=True)
    tot = lambda v: jnp.sum(v, axis=0, keepdims=True)
    lo_i = pairs.lo(i)
    pick = [lo_i > pairs.lo(r * 4 + j) for j in range(4)]
    sa = dot(K[r, 0], qs[i, 1])
    for j in range(4):
        u = jnp.where(pick[j], 0, 1)
        s = dot(K[r, u, j * BLOCK:(j + 1) * BLOCK, :], qs[i, u])
        if own:
            s = jnp.where(d_s[...] <= jnp.where(i == j, 0, 2 * BLOCK), s, FAR)
        sb[j] = s
    tops = [col(sb[j]) for j in range(4)]
    m_hi, m_lo = col(sa), None
    for j in range(4):
        m_hi = jnp.maximum(m_hi, jnp.where(pick[j], FAR, tops[j]))
        t = jnp.where(pick[j], tops[j], FAR)
        m_lo = t if m_lo is None else jnp.maximum(m_lo, t)
    if own:
        rows = pl.ds(pl.multiple_of(i * BLOCK, BLOCK), BLOCK)
        sd = jnp.where(d_s[...] <= 0, dot(K[r, 0, rows, :], qs[i, 0]), FAR)
        m_lo = jnp.maximum(m_lo, col(sd))
    else:
        old_hi, old_lo = m_s[i, 1], m_s[i, 0]
        m_hi, m_lo = jnp.maximum(m_hi, old_hi), jnp.maximum(m_lo, old_lo)
    pa = jnp.exp2(sa - m_hi)
    l_hi, l_lo = tot(pa), jnp.zeros((1, 512), f32)
    for j in range(4):
        p = jnp.exp2(sb[j] - jnp.where(pick[j], m_lo, m_hi))
        t = tot(p)
        l_hi = l_hi + jnp.where(pick[j], 0.0, t)
        l_lo = l_lo + jnp.where(pick[j], t, 0.0)
        low = p.astype(bf16)
        rows = slice(j * BLOCK, (j + 1) * BLOCK)
        zero = jnp.zeros_like(low)
        pb[0, rows, :] = jnp.where(pick[j], low, zero)
        pb[1, rows, :] = jnp.where(pick[j], zero, low)
    o_hi = by_pair(VT[r, 0], pa.astype(bf16)) + by_pair(VT[r, 1], pb[1])
    o_lo = by_pair(VT[r, 0], pb[0])
    if own:
        p = jnp.exp2(sd - m_lo)
        l_lo = l_lo + tot(p)
        at = pl.ds(pl.multiple_of(i * BLOCK, BLOCK), BLOCK)
        o_lo = o_lo + by_pair(VT[r, 0, :, at], p.astype(bf16))
        l_s[i, 1], l_s[i, 0] = l_hi, l_lo
        acc[i, 1], acc[i, 0] = o_hi, o_lo
    else:
        f_hi, f_lo = jnp.exp2(old_hi - m_hi), jnp.exp2(old_lo - m_lo)
        l_s[i, 1] = l_s[i, 1] * f_hi + l_hi
        l_s[i, 0] = l_s[i, 0] * f_lo + l_lo
        acc[i, 1] = acc[i, 1] * f_hi + o_hi
        acc[i, 0] = acc[i, 0] * f_lo + o_lo
    m_s[i, 1], m_s[i, 0] = m_hi, m_lo


def fwd_finish(pairs, m_s, l_s, acc, lse, ot, o_ref):
    def pair(i, _):
        first = pairs.first_lo(i)
        out = []
        for u in range(2):
            l = l_s[i, u]
            lse[i, u] = m_s[i, u] + jnp.log2(l)
            t = unpair(acc[i, u] * (1.0 / l))
            ot[i, u] = t
            out.append(t.T.astype(bf16))
        o_ref[i, 0:BLOCK, :] = jnp.where(first, out[0], out[1])
        o_ref[i, BLOCK:2 * BLOCK, :] = jnp.where(first, out[1], out[0])
        return 0
    lax.fori_loop(0, 4, pair, 0)


def diagonal(d_s):
    d_s[...] = lax.broadcasted_iota(jnp.int32, d_s.shape, 0) - (lax.broadcasted_iota(jnp.int32, d_s.shape, 1) & (BLOCK - 1))


def fwd_local(nz, blk_ref, x_ref, wqkv_ref, bq_ref, bkv_ref, bkvt_ref, o_ref, ot, lse, K, V, KT, qn, qt, VT, qs, m_s, l_s, acc, d_s, sb, pb, wkvt):
    pairs = Pairs(nz * 8, lambda n: blk_ref[2 * n])
    diagonal(d_s)
    wkvt[...] = turned(wqkv_ref[:, 256:])
    project_queries(pairs, x_ref, wqkv_ref.at[:, 0:256], bq_ref, qn, qt, qs)
    for r in range(nz):
        project_chunk(pairs, r, x_ref, wqkv_ref.at[:, 256:768], wkvt, bkv_ref, bkvt_ref, K, V, KT, VT)
        def step(i, _):
            fwd_step(pairs, r, i, r == 0, K, VT, qs, m_s, l_s, acc, d_s, sb, pb)
            return 0
        lax.fori_loop(0, 4, step, 0)
    fwd_finish(pairs, m_s, l_s, acc, lse, ot, o_ref)


def fwd_outs(nz):
    sds = jax.ShapeDtypeStruct
    kv = sds((nz, 2, 512, 256), bf16)
    return (sds((4, 256, 256), bf16), sds((4, 2, 256, 128), f32), sds((4, 2, 1, 512), f32), kv, kv, sds((nz, 2, 256, 512), bf16),
            sds((4, 2, 128, 256), bf16), sds((4, 2, 256, 128), bf16))


def fwd_scratch(nz):
    M = pltpu.VMEM
    return [M((nz, 2, 256, 512), bf16), M((4, 2, 256, 512), bf16), M((4, 2, 1, 512), f32), M((4, 2, 1, 512), f32), M((4, 2, 128, 512), f32),
            M((128, 512), jnp.int32), M((4, 128, 512), f32), M((2, 512, 512), bf16), M((512, 512), bf16)]


def attn_fwd(nz, blk, x, wqkv, bq, bkv):
    V = pl.BlockSpec(memory_space=pltpu.VMEM)
    return pl.pallas_call(
        functools.partial(fwd_local, nz), out_shape=fwd_outs(nz),
        in_specs=[pl.BlockSpec(memory_space=pltpu.SMEM)] + [V] * 5, out_specs=(V,) * 8, scratch_shapes=fwd_scratch(nz),
        compiler_params=pltpu.CompilerParams(vmem_limit_bytes=58 << 20), name="attn_fwd")(blk, x, wqkv, bq, bkv, bkv.reshape(256, 1))


def bwd_queries(pairs, do_ref, ot, qn, qt, qs, dos, qns, dons, dl):
    def piece(i, _):
        for u, do in enumerate(pairs.ordered(i, do_ref[i])):
            dot_t = do.astype(f32).T
            prod = dot_t * ot[i, u]
            low = dot_t.astype(bf16)
            q, t = qn[i, u], qt[i, u]
            for hs, cs in head_slices():
                qs[i, u, hs, cs] = t[hs]
                dos[i, u, hs, cs] = low[hs]
                qns[i, u, cs, hs] = q[:, hs]
                dons[i, u, cs, hs] = do[:, hs]
                dl[i, u, :, cs] = jnp.sum(prod[hs], axis=0, keepdims=True)
        return 0
    lax.fori_loop(0, 4, piece, 0)


def bwd_step(pairs, r, i, own, first, K, V, KT, qs, dos, qns, dons, lse, dl, dk, dv, dq, d_s, gb, js=(0, 1, 2, 3)):
    lo_i = pairs.lo(i)
    pick = {j: lo_i > pairs.lo(r * 4 + j) for j in js}
    part = slice(js[0] * BLOCK, js[-1] * BLOCK + BLOCK)

    def pieces(k, v, u, mask):
        s = dot(k, qs[i, u]) - lse[i, u]
        if mask is not None:
            s = jnp.where(d_s[...] <= mask, s, FAR)
        p = jnp.exp2(s)
        g = p * (dot(v, dos[i, u]) - dl[i, u])
        return p.astype(bf16), g.astype(bf16)

    p, g = pieces(K[r, 0, part, :], V[r, 0, part, :], 1, None)
    dv[0, part, :] += dot(p, dons[i, 1])
    dk[0, part, :] += dot(g, qns[i, 1])
    q_hi = by_pair(KT[r, 0, :, part], g)
    for j in js:
        u = jnp.where(pick[j], 0, 1)
        rows = slice(j * BLOCK, (j + 1) * BLOCK)
        p, g = pieces(K[r, u, rows, :], V[r, u, rows, :], u, jnp.where(i == j, 0, 2 * BLOCK) if own else None)
        gv, gk = dot(p, dons[i, u]), dot(g, qns[i, u])
        dv[0, rows, :] += jnp.where(pick[j], gv, 0.0)
        dv[1, rows, :] += jnp.where(pick[j], 0.0, gv)
        dk[0, rows, :] += jnp.where(pick[j], gk, 0.0)
        dk[1, rows, :] += jnp.where(pick[j], 0.0, gk)
        zero = jnp.zeros_like(g)
        gb[0, rows, :] = jnp.where(pick[j], g, zero)
        gb[1, rows, :] = jnp.where(pick[j], zero, g)
    q_hi = q_hi + by_pair(KT[r, 1, :, part], gb[1, part, :])
    q_lo = by_pair(KT[r, 0, :, part], gb[0, part, :])
    if own:
        rows = pl.ds(pl.multiple_of(i * BLOCK, BLOCK), BLOCK)
        p, g = pieces(K[r, 0, rows, :], V[r, 0, rows, :], 0, 0)
        dv[0, rows, :] += dot(p, dons[i, 0])
        dk[0, rows, :] += dot(g, qns[i, 0])
        q_lo = q_lo + by_pair(KT[r, 0, :, rows], g)
    if first:
        dq[i, 1], dq[i, 0] = q_hi, q_lo
    else:
        dq[i, 1] += q_hi
        dq[i, 0] += q_lo


def bwd_chunk_weights(pairs, r, x_ref, dk, dv, dw, db, gp, js=(0, 1, 2, 3)):
    total = jnp.zeros((1, 256), f32)
    for p in js:
        at = slice(p * BLOCK, (p + 1) * BLOCK)
        g = [jnp.concatenate([(dk[u, at, :] * (1.0 / LOG2E)).astype(bf16), dv[u, at, :].astype(bf16)], axis=1) for u in range(2)]
        total = total + jnp.sum(g[0][:, 256:].astype(f32), axis=0, keepdims=True) + jnp.sum(g[1][:, 256:].astype(f32), axis=0, keepdims=True)
        first = pairs.first_lo(r * 4 + p)
        gp[p * 256:p * 256 + BLOCK, :] = jnp.where(first, g[0], g[1])
        gp[p * 256 + BLOCK:p * 256 + 256, :] = jnp.where(first, g[1], g[0])
    db[1:2, :] += total
    n = len(js)
    dw[:, 256:768] += dot(x_ref[r, js[0]:js[0] + n].reshape(n * 256, 512), gp[js[0] * 256:(js[0] + n) * 256, :], TN)


def bwd_chunk_rows(r, last, wqkv_ref, dxq, dx, gp, js=(1, 3, 0, 2)):
    for p in js:
        rows = slice(p * 256, p * 256 + 256)
        d = dot(gp[rows, :], wqkv_ref[:, 256:768], NT)
        if last:
            d = d + dxq[p]
        dx[r, rows, :] = d.astype(bf16)


def bwd_query_out(pairs, x_ref, wqkv_ref, dq, dxq, dw, db):
    def piece(i, _):
        t = [(unpair(dq[i, u]) * 0.125).T.astype(bf16) for u in range(2)]
        first = pairs.first_lo(i)
        g = jnp.concatenate([jnp.where(first, t[0], t[1]), jnp.where(first, t[1], t[0])], axis=0)
        dxq[i] = dot(g, wqkv_ref[:, 0:256], NT)
        dw[:, 0:256] += dot(x_ref[0, i], g, TN)
        db[0:1, :] += jnp.sum(g.astype(f32), axis=0, keepdims=True)
        return 0
    lax.fori_loop(0, 4, piece, 0)


def weight_rows(dw, gq):
    for k in range(2):
        for m in range(3):
            gq[k, m * 256:m * 256 + 256, :] = dw[k * 256:k * 256 + 256, m * 256:m * 256 + 256].astype(bf16)


def bwd_local(nz, blk_ref, x_ref, wqkv_ref, K, V, KT, qn, qt, ot, lse, do_ref, dx, gq, db, qs, dos, qns, dons, dl, dk, dv, dq, d_s, gb, dxq, dw, gp):
    pairs = Pairs(nz * 8, lambda n: blk_ref[2 * n])
    diagonal(d_s)
    dw[...] = jnp.zeros_like(dw)
    db[...] = jnp.zeros_like(db)
    for s in (qs, dos, qns, dons):
        s[...] = jnp.zeros_like(s)
    bwd_queries(pairs, do_ref, ot, qn, qt, qs, dos, qns, dons, dl)
    for r in list(range(1, nz)) + [0]:
        dk[...] = jnp.zeros_like(dk)
        dv[...] = jnp.zeros_like(dv)
        def step(i, _):
            bwd_step(pairs, r, i, r == 0, r == 1, K, V, KT, qs, dos, qns, dons, lse, dl, dk, dv, dq, d_s, gb)
            return 0
        lax.fori_loop(0, 4, step, 0)
        if r == 0:
            bwd_query_out(pairs, x_ref, wqkv_ref, dq, dxq, dw, db)
        bwd_chunk_weights(pairs, r, x_ref, dk, dv, dw, db, gp)
        bwd_chunk_rows(r, r == 0, wqkv_ref, dxq, dx, gp)
    weight_rows(dw, gq)


def bwd_scratch():
    M = pltpu.VMEM
    return [M((4, 2, 256, 512), bf16), M((4, 2, 256, 512), bf16), M((4, 2, 512, 256), bf16), M((4, 2, 512, 256), bf16), M((4, 2, 1, 512), f32),
            M((2, 512, 256), f32), M((2, 512, 256), f32), M((4, 2, 128, 512), f32), M((128, 512), jnp.int32), M((2, 512, 512), bf16),
            M((4, 256, 512), f32), M((512, 768), f32)]


def attn_bwd(nz, blk, x, wqkv, K, V, KT, qn, qt, ot, lse, do):
    S = pl.BlockSpec(memory_space=pltpu.VMEM)
    sds = jax.ShapeDtypeStruct
    return pl.pallas_call(
        functools.partial(bwd_local, nz), out_shape=(sds((nz, 1024, 512), bf16), sds((2, 768, 256), bf16), sds((8, 256), f32)),
        in_specs=[pl.BlockSpec(memory_space=pltpu.SMEM)] + [S] * 10, out_specs=(S,) * 3, scratch_shapes=bwd_scratch() + [pltpu.VMEM((1024, 512), bf16)],
        compiler_params=pltpu.CompilerParams(vmem_limit_bytes=58 << 20), name="attn_bwd")(blk, x, wqkv, K, V, KT, qn, qt, ot, lse, do)


def dense_kernel(x_ref, cot_ref, att_ref, wo_ref, wu_ref, wd_ref, sm_ref,
                 out_ref, dsm_ref, do_ref, gw_ref, gv_ref, act_s, gp_s, norm_s, dpre_s):
    ff = wu_ref.shape[1]
    chunk = 512
    x = x_ref[...].astype(f32)
    vec = lambda i: jnp.concatenate([sm_ref[0, i:i + 1, :], sm_ref[1, i:i + 1, :]], axis=1)
    b_out, g1, s1, b_down, g2, s2 = (vec(i) for i in range(2, 8))
    mean = lambda v: jnp.mean(v, axis=-1, keepdims=True)
    col = lambda v: jnp.sum(v, axis=0, keepdims=True)
    mix = x + dot(att_ref[...], wo_ref[...]) + b_out
    cen = mix - mean(mix)
    r1 = lax.rsqrt(mean(cen * cen) + norm_eps)
    n1 = cen * r1
    normed = n1 * g1 + s1
    nlow = normed.astype(bf16)
    norm_s[...] = nlow
    ffn = None
    for f in range(0, ff, chunk):
        fs = slice(f, f + chunk)
        at = 8 + f % (ff // 2) // 256
        b_up = jnp.concatenate([sm_ref[2 * f // ff, at + k:at + k + 1, :] for k in range(chunk // 256)], axis=1)
        pre = dot(nlow, wu_ref[:, fs]) + b_up
        c0 = math.sqrt(2.0 / math.pi)
        sq = pre * pre
        th = jnp.tanh(c0 * pre * (1.0 + 0.044715 * sq))
        half = 0.5 * (1.0 + th)
        act = (pre * half).astype(bf16)
        act_s[:, fs] = act
        gp_s[:, fs] = half + 0.5 * pre * (1.0 - th * th) * (c0 * (1.0 + 3 * 0.044715 * sq))
        part = dot(act, wd_ref[fs, :])
        ffn = part if ffn is None else ffn + part
    summed = ffn + b_down + normed + x
    cen = summed - mean(summed)
    r2 = lax.rsqrt(mean(cen * cen) + norm_eps)
    n2 = cen * r2
    out_ref[...] = (n2 * g2 + s2).astype(bf16)
    up = cot_ref[...].astype(f32)
    gv_ref[4:5, :] = col(up * n2)
    gv_ref[5:6, :] = col(up)
    dn = up * g2
    dsum = r2 * (dn - mean(dn) - n2 * mean(dn * n2))
    dffn = dsum.astype(bf16)
    gv_ref[3:4, :] = col(dffn.astype(f32))
    dnorm = dsum
    half_rows = wo_ref.shape[0] // 2
    half_ff = ff // 2
    def put(g, at, rows):
        gw_ref[0, at:at + rows, :] = g[:rows].astype(bf16)
        gw_ref[1, at:at + rows, :] = g[rows:].astype(bf16)
    for f in range(0, ff, chunk):
        fs = slice(f, f + chunk)
        dact = dot(dffn, wd_ref[fs, :], NT)
        dpre = (dact * gp_s[:, fs]).astype(bf16)
        gv_ref[8 + f // chunk:9 + f // chunk, :] = col(dpre.astype(f32))
        dnorm = dnorm + dot(dpre, wu_ref[:, fs], NT)
        put(dot(norm_s[...], dpre, TN), half_rows + (f // chunk) * half_rows, half_rows)
        gd = dot(act_s[:, fs], dffn, TN).astype(bf16)
        base = half_rows * (1 + ff // chunk)
        which, off = f // half_ff, f % half_ff
        gw_ref[which, base + off:base + off + chunk, :] = gd
    gv_ref[1:2, :] = col(dnorm * n1)
    gv_ref[2:3, :] = col(dnorm)
    dn = dnorm * g1
    dmix = r1 * (dn - mean(dn) - n1 * mean(dn * n1))
    dsm_ref[...] = dsum + dmix
    dbr = dmix.astype(bf16)
    gv_ref[0:1, :] = col(dbr.astype(f32))
    do_ref[...] = dot(dbr, wo_ref[...], NT).astype(bf16)
    put(dot(att_ref[...], dbr, TN), 0, half_rows)


def dense(x, cot, att, wo, wu, wd, sm):
    V = pl.BlockSpec(memory_space=pltpu.VMEM)
    tok, dim = x.shape
    ff = wu.shape[1]
    rows = (2 * dim * ff + dim * dim) // 2 // dim
    return pl.pallas_call(
        dense_kernel,
        out_shape=(jax.ShapeDtypeStruct((tok, dim), bf16), jax.ShapeDtypeStruct((tok, dim), f32),
                   jax.ShapeDtypeStruct((tok, dim), bf16), jax.ShapeDtypeStruct((2, rows, dim), bf16),
                   jax.ShapeDtypeStruct((16, dim), f32)),
        in_specs=[V] * 7, out_specs=(V,) * 5,
        scratch_shapes=[pltpu.VMEM((tok, ff), bf16), pltpu.VMEM((tok, ff), f32), pltpu.VMEM((tok, dim), bf16),
                        pltpu.VMEM((8, 128), f32)],
        compiler_params=pltpu.CompilerParams(vmem_limit_bytes=56 << 20),
        name="dense")(x, cot, att, wo, wu, wd, sm)


MESH = pl.DeviceIdType.MESH


def places(nz):
    me, wi = lax.axis_index("ctx"), lax.axis_index("wt")
    z, y, c = me // 4, lax.rem(me // 2, 2), lax.rem(me, 2)
    low = lax.rem(me, 4)
    at = lambda zz, ll: (zz * 4 + ll, wi)
    to = dict(up=at(lax.rem(z + 1, nz), low), down=at(lax.rem(z + nz - 1, nz), low), core=at(z, low + 1 - 2 * c), y=at(z, low + 2 - 4 * y),
              x=(me, 1 - wi))
    return me, wi, z, y, c, low, to


def meet(targets):
    bar = pltpu.get_barrier_semaphore()
    for t in targets:
        pl.semaphore_signal(bar, inc=1, device_id=t, device_id_type=MESH)
    pl.semaphore_wait(bar, len(targets))


class Wires:
    def __init__(self, send, recv):
        self.send, self.recv, self.n, self.live = send, recv, 0, []

    def make(self, src, dst, to):
        cp = pltpu.make_async_remote_copy(src, dst, self.send.at[self.n], self.recv.at[self.n], device_id=to, device_id_type=MESH)
        self.n += 1
        self.live.append(cp)
        return cp

    def go(self, src, dst, to):
        cp = self.make(src, dst, to)
        cp.start()
        return cp

    def drain(self):
        for cp in self.live:
            cp.wait_send()


def rows_of(start, size, mult=16):
    return pl.ds(pl.multiple_of(start, mult), size)


def gather_kernel(nz, with_w, *refs):
    if with_w:
        (x_ref, wq_ref, wk_ref, wv_ref, wo_ref, wu_ref, wd_ref, sm_ref,
         xall, wqkv, wo, wu, wd, sm, send, recv, lsem) = refs
    else:
        x_ref, xall, send, recv, lsem = refs
    me, wi, z, y, c, low, to = places(nz)
    rows = x_ref.shape[1]
    local = []

    def copy(src, dst):
        cp = pltpu.make_async_copy(src, dst, lsem.at[len(local)])
        cp.start()
        local.append(cp)

    copy(x_ref.at[y], xall.at[0, 0])
    if with_w:
        R, half = wq_ref.shape[0], wq_ref.shape[1] // 2
        for i, w in enumerate((wq_ref, wk_ref, wv_ref)):
            copy(w.at[:, rows_of(c * half, half, 128)], wqkv.at[rows_of(wi * R, R), pl.ds(i * half, half)])
        for w, full in ((wo_ref, wo), (wu_ref, wu), (wd_ref, wd)):
            n = w.shape[0]
            copy(w, full.at[rows_of(wi * n, n)])
        copy(sm_ref, sm.at[wi])
    near = [to["up"], to["down"], to["core"], to["y"]] + ([to["x"]] if with_w else [])
    meet(near)
    wires = Wires(send, recv)
    yx = wires.go(x_ref.at[1 - y], xall.at[0, 2], to["y"])
    ring = {(1, 0): wires.go(x_ref.at[y], xall.at[1, 0], to["up"])}
    core = {(0, 0): wires.go(x_ref.at[y], xall.at[0, 1], to["core"])}
    if with_w:
        xs = []
        for i, w in enumerate((wq_ref, wk_ref, wv_ref)):
            xs.append(wires.go(w.at[:, rows_of(c * half, half, 128)], wqkv.at[rows_of(wi * R, R), pl.ds(i * half, half)], to["x"]))
        xs.append(wires.go(sm_ref, sm.at[wi], to["x"]))
        big = []
        for w, full in ((wo_ref, wo), (wu_ref, wu), (wd_ref, wd)):
            n = w.shape[0]
            h = n // 2
            cp = wires.go(w.at[rows_of(c * h, h)], full.at[rows_of(wi * n + c * h, h)], to["x"])
            big.append((cp, full, rows_of((1 - wi) * n + c * h, h)))
    yx.wait_recv()
    ring[1, 1] = wires.go(xall.at[0, 2], xall.at[1, 2], to["up"])
    core[0, 1] = wires.go(xall.at[0, 2], xall.at[0, 3], to["core"])
    shared = []
    for r in range(1, nz):
        for s in range(2):
            ring[r, s].wait_recv()
            if r < nz - 1:
                ring[r + 1, s] = wires.go(xall.at[r, 2 * s], xall.at[r + 1, 2 * s], to["up"])
            core[r, s] = wires.go(xall.at[r, 2 * s], xall.at[r, 2 * s + 1], to["core"])
        if with_w and r - 1 < len(big):
            cp, full, where = big[r - 1]
            cp.wait_recv()
            shared.append(wires.go(full.at[where], full.at[where], to["core"]))
    if with_w:
        for cp, full, where in big[nz - 1:]:
            cp.wait_recv()
            shared.append(wires.go(full.at[where], full.at[where], to["core"]))
        for cp in xs + shared:
            cp.wait_recv()
    for cp in core.values():
        cp.wait_recv()
    wires.drain()
    for cp in local:
        cp.wait()


def gather_all(nz, x, weights=None, small=None):
    A = pl.BlockSpec(memory_space=pl.ANY)
    sds = jax.ShapeDtypeStruct
    rows, dim = x.shape[1:]
    outs = [sds((nz, 4, rows, dim), bf16)]
    ins = [x]
    ncopy = 1 + 2 * (nz - 1) + 2 * nz
    if weights is not None:
        wq, wk, wv, wo, wu, wd = weights
        ins += list(weights) + [small]
        outs += [sds((dim, 3 * dim // 2), bf16)] + [sds((2 * w.shape[0], w.shape[1]), bf16) for w in (wo, wu, wd)] + [sds((2,) + small.shape, bf16)]
        ncopy += 10
    return pl.pallas_call(
        functools.partial(gather_kernel, nz, weights is not None),
        out_shape=tuple(outs), in_specs=[A] * len(ins), out_specs=(A,) * len(outs),
        scratch_shapes=[pltpu.SemaphoreType.DMA((ncopy,)), pltpu.SemaphoreType.DMA((ncopy,)), pltpu.SemaphoreType.DMA((8,))],
        compiler_params=pltpu.CompilerParams(collective_id=1, has_side_effects=True, vmem_limit_bytes=16 << 20),
        name="gather_all")(*ins)


def add_into(dst, parts, rows, step=64):
    def body(i, _):
        r = rows_of(i * step, step)
        total = parts[0](r)[...].astype(f32)
        for p in parts[1:]:
            total = total + p(r)[...].astype(f32)
        d = dst(r)
        d[...] = total.astype(bf16)
        return 0
    lax.fori_loop(0, rows // step, body, 0)


def offset(ref, lead, start):
    def view(r):
        at = pl.ds(pl.multiple_of(start + r.start, 16), r.size)
        return ref.at[lead + (at,)]
    return view


def chip_pairs(nz, order_ref):
    me = lax.axis_index("ctx")
    z, y, c = me // 4, lax.rem(me // 2, 2), lax.rem(me, 2)

    def first(n):
        r, p = n // 4, n % 4
        a, b = p // 2, p % 2
        yy, cc = y + a - 2 * y * a, c + b - 2 * c * b
        return order_ref[y, 2 * (lax.rem(z - r + nz, nz) * 4 + yy * 2 + cc)]
    return Pairs(nz * 8, first)


def front_kernel(nz, order_ref, bqr, bvr, bor, g1r, s1r, bdr, g2r, s2r, bur, x_ref, wq_ref, wk_ref, wv_ref, wo_ref, wu_ref, wd_ref,
                 att, wo, wu, wd, sm, xall, wqkv, ot_o, lse_o, K_o, V_o, KT_o, qn_o, qt_o,
                 xs, ws, sms, wos, wus, wds, K, V, KT, VT, qn, qt, qs, m_s, l_s, acc, d_s, sb, pb, wkvt, bkvt, ot, lse, o_s, send, recv, lsem):
    me, wi, z, y, c, low, to = places(nz)
    to["yc"] = (z * 4 + 3 - low, wi)
    half, R = 256, wq_ref.shape[0]
    local = []

    def copy(src, dst):
        cp = pltpu.make_async_copy(src, dst, lsem.at[len(local)])
        cp.start()
        local.append(cp)
        return cp

    own_x = copy(x_ref.at[y], xs.at[0, 0])
    own_w = [copy(w.at[:, rows_of(c * half, half, 128)], ws.at[rows_of(wi * R, R), pl.ds(i * half, half)]) for i, w in enumerate((wq_ref, wk_ref, wv_ref))]
    for i, v in enumerate((bqr, bvr, bor, g1r, s1r, bdr, g2r, s2r)):
        sms[wi, i:i + 1, :] = v[...].astype(f32).reshape(1, half)
    up_b = bur[...].astype(f32).reshape(1, 1024)
    for i in range(4):
        sms[wi, 8 + i:9 + i, :] = up_b[:, i * half:(i + 1) * half]
    sms[wi, 12:16, :] = jnp.zeros((4, half), f32)
    meet([to[k] for k in ("up", "down", "core", "y", "yc", "x")])
    w = Wires(send, recv)
    yx = w.go(x_ref.at[1 - y], xs.at[0, 2], to["y"])
    ring, core = {}, {}
    ring[1, 0] = w.go(x_ref.at[y], xs.at[1, 0], to["up"])
    core[0, 0] = w.go(x_ref.at[y], xs.at[0, 1], to["core"])
    wx = []
    for i, m in enumerate((wq_ref, wk_ref, wv_ref)):
        wx.append(w.go(m.at[:, rows_of(c * half, half, 128)], ws.at[rows_of(wi * R, R), pl.ds(i * half, half)], to["x"]))
    wx.append(w.go(sms.at[wi], sms.at[wi], to["x"]))
    big = []
    for m, full in ((wo_ref, wos), (wu_ref, wus), (wd_ref, wds)):
        n = m.shape[0]
        h = n // 2
        copy(m, full.at[rows_of(wi * n, n)])
        big.append((m.at[rows_of(c * h, h)], full.at[rows_of(wi * n + c * h, h)], full, rows_of((1 - wi) * n + c * h, h)))

    pairs = chip_pairs(nz, order_ref)
    diagonal(d_s)
    yx.wait_recv()
    ring[1, 1] = w.go(xs.at[0, 2], xs.at[1, 2], to["up"])
    core[0, 1] = w.go(xs.at[0, 2], xs.at[0, 3], to["core"])

    def pump(r, s):
        ring[r, s].wait_recv()
        if r < nz - 1:
            ring[r + 1, s] = w.go(xs.at[r, 2 * s], xs.at[r + 1, 2 * s], to["up"])
        core[r, s] = w.go(xs.at[r, 2 * s], xs.at[r, 2 * s + 1], to["core"])

    shared = []

    def share(k):
        cp, full, where = sent[k]
        cp.wait_recv()
        shared.append(w.go(full.at[where], full.at[where], to["core"]))

    pump(1, 0)
    for cp in own_w:
        cp.wait()
    for cp in wx:
        cp.wait_recv()
    sent = [(w.go(src, dst, to["x"]), full, where) for src, dst, full, where in big]
    copy(sms, sm)
    copy(ws, wqkv)
    wkvt[...] = turned(ws[:, 256:])
    bv = sms[c, 1:2, :]
    bkvt[...] = jnp.broadcast_to(bv, (8, half)).T[:, 0:1]
    own_x.wait()
    for s in range(2):
        core[0, s].wait_recv()
    project_queries(pairs, xs, ws.at[:, 0:256], sms.at[c, 0:1], qn, qt, qs)
    copy(qn, qn_o)
    copy(qt, qt_o)

    def chunk(r):
        project_chunk(pairs, r, xs, ws.at[:, 256:768], wkvt, sms.at[c, 1:2], bkvt, K, V, KT, VT)
        for a, b in ((xs, xall), (K, K_o), (V, V_o), (KT, KT_o)):
            copy(a.at[r], b.at[r])

    def attend(r, start, stop):
        def step(i, _):
            fwd_step(pairs, r, i, r == 0, K, VT, qs, m_s, l_s, acc, d_s, sb, pb)
            return 0
        lax.fori_loop(start, stop, step, 0)

    chunk(0)
    pump(1, 1)
    attend(0, 0, 2)
    attend(0, 2, 4)
    for r in range(1, nz):
        if r + 1 < nz:
            pump(r + 1, 0)
        for s in range(2):
            core[r, s].wait_recv()
        chunk(r)
        attend(r, 0, 2)
        if r + 1 < nz:
            pump(r + 1, 1)
            share(r - 1)
        attend(r, 2, 4)
    fwd_finish(pairs, m_s, l_s, acc, lse, ot, o_s)
    cols = pl.ds(pl.multiple_of(c * half, half), half)
    outs = [w.go(o_s.at[p], att.at[y, :, cols], to[k]) for p, k in ((1, "core"), (2, "y"), (3, "yc"))]
    copy(o_s.at[0], att.at[y, :, cols])
    copy(ot, ot_o)
    copy(lse, lse_o)
    share(2)
    for k, (a, b) in enumerate(((wos, wo), (wus, wu), (wds, wd))):
        shared[k].wait_recv()
        local[4 + k].wait()
        copy(a, b)
    for cp in outs:
        cp.wait_recv()
    w.drain()
    for cp in local[7:]:
        cp.wait()


def front(nz, order, vectors, x, weights):
    A = pl.BlockSpec(memory_space=pltpu.HBM)
    V = pl.BlockSpec(memory_space=pltpu.VMEM)
    sds = jax.ShapeDtypeStruct
    M = pltpu.VMEM
    rows, dim = x.shape[1:]
    wq, wk, wv, wo, wu, wd = weights
    outs = [sds((2, rows, dim), bf16)] + [sds((2 * w.shape[0], w.shape[1]), bf16) for w in (wo, wu, wd)]
    outs += [sds((2, 16, 256), f32), sds((nz, 4, rows, dim), bf16), sds((dim, 768), bf16)] + list(fwd_outs(nz)[1:])
    scratch = [M((nz, 4, rows, dim), bf16), M((dim, 768), bf16), M((2, 16, 256), f32)] + [M(o.shape, bf16) for o in outs[1:4]]
    scratch += [M((nz, 2, 512, 256), bf16)] * 2 + [M((nz, 2, 256, 512), bf16)] * 2 + [M((4, 2, 128, 256), bf16), M((4, 2, 256, 128), bf16)]
    scratch += fwd_scratch(nz)[1:] + [M((256, 1), f32), M((4, 2, 256, 128), f32), M((4, 2, 1, 512), f32), M((4, 256, 256), bf16)]
    scratch += [pltpu.SemaphoreType.DMA((40,)), pltpu.SemaphoreType.DMA((40,)), pltpu.SemaphoreType.DMA((40,))]
    return pl.pallas_call(
        functools.partial(front_kernel, nz), out_shape=tuple(outs),
        in_specs=[pl.BlockSpec(memory_space=pltpu.SMEM)] + [V] * 9 + [A] * 7, out_specs=(A,) * len(outs), scratch_shapes=scratch,
        compiler_params=pltpu.CompilerParams(collective_id=1, has_side_effects=True, vmem_limit_bytes=58 << 20), name="front")(
            order, *vectors, x, *weights)


def back_kernel(nz, order_ref, gv_ref, do_ref, x_hbm, w_hbm, K_h, V_h, KT_h, qn_h, qt_h, ot_h, lse_h, gw_ref,
                dxo, go, gqo, gvo,
                xs, wqkv, K, V, KT, qn, qt, ot, lse, do, qs, dos, qns, dons, dl, dk, dv, dq, d_s, gb, dxq, dw, dx, gp, gq, db, outdx,
                dx_core, dx_in, cr, cs, xr, xs_, yr, ys_, za, zs, zb, xrq, xsq, yrq, ysq, zrq, gsum, gqsum, gvs, gvr, send, recv, lsem):
    me, wi, z, y, c, low, to = places(nz)
    to["yc"] = (z * 4 + 3 - low, wi)
    zto = [(lax.rem(z + d, nz) * 4 + low, wi) for d in range(1, nz)]
    half, hrow = 256, 256
    w = Wires(send, recv)
    local = []

    def copy(src, dst):
        cp = pltpu.make_async_copy(src, dst, lsem.at[len(local)])
        cp.start()
        local.append(cp)
        return cp

    cols = pl.ds(pl.multiple_of(c * half, half), half)
    other = pl.ds(pl.multiple_of((1 - c) * half, half), half)
    meet([to[k] for k in ("core", "y", "yc", "x")] + zto)
    dos_in = [w.go(do_ref.at[1 - y, :, cols], do.at[2], to["y"]), w.go(do_ref.at[1 - y, :, other], do.at[3], to["yc"]),
              w.go(do_ref.at[y, :, other], do.at[1], to["core"])]
    got = {}
    for s in range(3):
        got["c", s] = w.go(gw_ref.at[:, rows_of(s * 768 + (1 - c) * 384, 384)], cr.at[s], to["core"])
    mine_gw = [copy(gw_ref.at[:, rows_of(s * 768 + c * 384, 384)], cs.at[s]) for s in range(3)]
    first_in = [copy(do_ref.at[y, :, cols], do.at[0])] + [copy(a, b) for a, b in ((qn_h, qn), (qt_h, qt), (ot_h, ot), (lse_h, lse))]
    kv_in = {}
    for r in list(range(1, nz)) + [0]:
        kv_in[r] = [copy(a.at[r], b.at[r]) for a, b in ((K_h, K), (V_h, V), (KT_h, KT), (x_hbm, xs))]
    w_in = copy(w_hbm, wqkv)

    n = range(5)
    wide = [384, 192, 48]
    zp = (z + 1 - 2 * lax.rem(z, 2)) * 4 + low, wi
    zq = (z + 2 - 4 * (z // 2)) * 4 + low, wi
    odd, far = lax.rem(z, 2), z // 2
    X_in = [xr.at[s] for s in range(3)] + [xrq.at[s] for s in range(2)]
    X_sum = [xs_.at[s] for s in range(3)] + [xsq.at[s] for s in range(2)]
    Y_in = [yr.at[s] for s in range(3)] + [yrq.at[s] for s in range(2)]
    Y_sum = [ys_.at[s] for s in range(3)] + [ysq.at[s] for s in range(2)]
    Z_in = [zrq.at[s] for s in range(2)]
    out = [gsum.at[s] for s in range(3)] + [gqsum.at[s] for s in range(2)]
    start_c, start_y = c * 384, c * 384 + y * 192
    at_c, at_y = rows_of(start_c, 384), rows_of(start_y, 192)
    pos = odd * 2 + far
    start_p, start_h = start_y + pos * 48, start_y + odd * 96
    at_p, at_h = rows_of(start_p, 48), rows_of(start_h, 96)
    start_z = start_y + z * 48
    at_z = rows_of(start_z, 48)
    theirs = rows_of((1 - y) * 192, 192)
    for s in n:
        got["x", s] = w.make(cs.at[s, 1 - wi] if s < 3 else gq.at[1 - wi, pl.ds((s - 3) * 384, 384)], X_in[s], to["x"])
        got["y", s] = w.make(X_sum[s].at[theirs], Y_in[s], to["y"])
        got["ys", s] = w.make(out[s].at[at_y], out[s].at[at_y], to["y"])
        got["cs", s] = w.make(out[s].at[at_c], out[s].at[at_c], to["core"])
        if s < 3:
            got["za", s] = w.make(ys_.at[s, rows_of((1 - odd) * 96, 96)], za.at[s], zp)
            got["zb", s] = w.make(zs.at[s, rows_of((1 - far) * 48, 48)], zb.at[s], zq)
            got["zc", s] = w.make(out[s].at[at_p], out[s].at[at_p], zq)
            got["zd", s] = w.make(out[s].at[at_h], out[s].at[at_h], zp)
        else:
            for d in range(1, nz):
                got["z", s, d] = w.make(Y_sum[s].at[rows_of(lax.rem(z + d, nz) * 48, 48)], Z_in[s - 3].at[d - 1], zto[d - 1])
                got["zs", s, d] = w.make(out[s].at[at_z], out[s].at[at_z], zto[d - 1])

    def x_send(s):
        if s < 3:
            mine_gw[s].wait()
            got["c", s].wait_recv()
            add_into(offset(cs, (s, 1 - wi), 0), [offset(cs, (s, 1 - wi), 0), offset(cr, (s, 1 - wi), 0)], 384, 128)
            got["x", s].start()
            add_into(offset(cs, (s, wi), 0), [offset(cs, (s, wi), 0), offset(cr, (s, wi), 0)], 384, 128)
        else:
            got["x", s].start()

    def y_send(s):
        got["x", s].wait_recv()
        mine = lambda lo: offset(cs, (s, wi), lo) if s < 3 else offset(gq, (wi,), (s - 3) * 384 + lo)
        for half_y in (1 - y, y):
            lo = half_y * 192
            add_into(offset(X_sum[s], (), lo), [mine(lo), offset(X_in[s], (), lo)], 192, 96)
            if half_y is not y:
                got["y", s].start()

    def z_a(s):
        got["y", s].wait_recv()
        add_into(offset(ys_, (s,), 0), [offset(xs_, (s,), y * 192), offset(yr, (s,), 0)], 192, 96)
        got["za", s].start()

    def z_b(s):
        got["za", s].wait_recv()
        add_into(offset(zs, (s,), 0), [offset(ys_, (s,), odd * 96), offset(za, (s,), 0)], 96, 96)
        got["zb", s].start()

    def z_c(s):
        got["zb", s].wait_recv()
        add_into(offset(out[s], (), start_p), [offset(zs, (s,), far * 48), offset(zb, (s,), 0)], 48, 48)
        got["zc", s].start()

    def z_d(s):
        got["zc", s].wait_recv()
        got["zd", s].start()

    def z_send(s):
        got["y", s].wait_recv()
        add_into(offset(Y_sum[s], (), 0), [offset(X_sum[s], (), y * 192), offset(Y_in[s], (), 0)], 192, 192)
        for d in range(1, nz):
            got["z", s, d].start()

    def z_share(s):
        for d in range(1, nz):
            got["z", s, d].wait_recv()
        add_into(offset(out[s], (), start_z), [offset(Y_sum[s], (), z * 48)] + [offset(Z_in[s - 3], (d,), 0) for d in range(nz - 1)], 48, 48)
        for d in range(1, nz):
            got["zs", s, d].start()

    def y_share(s):
        for k in (["zd"] if s < 3 else [("zs", d) for d in range(1, nz)]):
            got[(k, s) if s < 3 else (k[0], s, k[1])].wait_recv()
        got["ys", s].start()

    def c_share(s):
        got["ys", s].wait_recv()
        got["cs", s].start()

    for r in range(nz):
        for h in range(2):
            at = pl.ds(h * 512, hrow)
            got["d", r, h] = w.make(dx.at[r, pl.ds(h * 512 + hrow, hrow)], dx_core.at[r, h], to["core"])
            if r:
                got["r", (r + 1) % nz, h] = w.make(dx.at[r, at], dx_in.at[(r + 1) % nz, h], to["up"])
    got["dy"] = w.make(dx.at[0, pl.ds(512, hrow)], outdx.at[1], to["y"])

    def give(r, h):
        got["d", r, h].start()

    def fold(r, h):
        got["d", r, h].wait_recv()
        add_into(offset(dx, (r,), h * 512), [offset(dx, (r,), h * 512), offset(dx_core, (r, h), 0)], hrow, 128)
        if r == 1:
            got["r", 2, h].start()

    def hop(r, h):
        got["r", r, h].wait_recv()
        dst = offset(dx, (r,), h * 512) if r or h else offset(outdx, (0,), 0)
        add_into(dst, [offset(dx, (r,), h * 512), offset(dx_in, (r, h), 0)], hrow, 128)
        if r:
            got["r", (r + 1) % nz, h].start()
        elif h:
            got["dy"].start()

    vec_to = [to["core"], to["y"], to["x"]] + [(zz * 4 + low, wi) for zz in (z + 1 - 2 * lax.rem(z, 2), z + 2 - 4 * (z // 2))]

    def vec_send(k):
        if k == 0:
            gvs[0] = jnp.zeros_like(gvs[0])
            gvs[0, 0:16, :] = gv_ref[...]
            zero = jnp.zeros((1, half), f32)
            for i in range(2):
                v = db[i:i + 1, :]
                gvs[0, 16 + i:17 + i, :] = jnp.concatenate([jnp.where(c == 0, v, zero), jnp.where(c == 0, zero, v)], axis=1)
        else:
            got["v", k - 1].wait_recv()
            gvs[k] = gvs[k - 1] + gvr[k - 1]
        if k < 5:
            got["v", k].start()
        else:
            gvo[...] = gvs[5]

    pairs = chip_pairs(nz, order_ref)
    for k in range(5):
        got["v", k] = w.make(gvs.at[k], gvr.at[k], vec_to[k])
    diagonal(d_s)
    dw[...] = jnp.zeros_like(dw)
    db[...] = jnp.zeros_like(db)
    for s in (qs, dos, qns, dons):
        s[...] = jnp.zeros_like(s)
    x_send(0)
    for cp in first_in:
        cp.wait()
    for cp in dos_in:
        cp.wait_recv()
    bwd_queries(pairs, do, ot, qn, qt, qs, dos, qns, dons, dl)
    for r in kv_in:
        for cp in kv_in[r]:
            cp.wait()
    w_in.wait()
    hooks = plan(dict(x=x_send, y=y_send, za=z_a, zb=z_b, zc=z_c, zd=z_d, ys=y_share, cs=c_share, fold=fold, hop=hop, z=z_send, zs=z_share, vec=vec_send))
    hook = lambda *k: hooks[k]() if k in hooks else None
    hook("pre")
    for r in list(range(1, nz)) + [0]:
        dk[...] = jnp.zeros_like(dk)
        dv[...] = jnp.zeros_like(dv)
        for n, js in enumerate(((2, 3), (0, 1)) if r == 1 else ((0, 1, 2, 3),)):
            def step(i, _):
                bwd_step(pairs, r, i, r == 0, r == 1 and n == 0, K, V, KT, qs, dos, qns, dons, lse, dl, dk, dv, dq, d_s, gb, js)
                for k in range(4):
                    if (r, n, k) in hooks:
                        pl.when(i == k)(hooks[r, n, k])
                return 0
            lax.fori_loop(0, 4, step, 0)
            if r == 0:
                bwd_query_out(pairs, xs, wqkv, dq, dxq, dw, db)
                hook(0, 0, "q")
            bwd_chunk_weights(pairs, r, xs, dk, dv, dw, db, gp, js)
            if r == 0:
                weight_rows(dw, gq)
                x_send(3)
            hook(r, n, "w")
            bwd_chunk_rows(r, r == 0, wqkv, dxq, dx, gp, [p for p in (3, 1, 2, 0) if p in js])
            for h in (1, 0):
                if 2 * h in js:
                    give(r, h)
            hook(r, n, "r")
    hook("tail")
    for s in range(5):
        got["cs", s].wait_recv()
        copy(gsum.at[s], go.at[s]) if s < 3 else copy(gqsum.at[s - 3], gqo.at[s - 3])
    got["dy"].wait_recv()
    copy(outdx, dxo)
    w.drain()
    for cp in local[-6:]:
        cp.wait()


PLAN = {
    (1, 0, "r"): (("x", 2),),
    (1, 1, 2): (("y", 0),),
    (1, 1, "r"): (("fold", 1, 1),),
    (2, 0, 2): (("x", 1), ("fold", 1, 0), ("za", 0),),
    (2, 0, "r"): (("y", 2),),
    (3, 0, 2): (("zb", 0),),
    (3, 0, 3): (("za", 2), ("fold", 2, 0), ("y", 1),),
    (3, 0, "r"): (("zc", 0), ("hop", 2, 0),),
    (0, 0, 2): (("za", 1),),
    (0, 0, "q"): (("zb", 2), ("zd", 0), ("fold", 2, 1),),
    (0, 0, "w"): (("hop", 2, 1), ("zc", 2), ("vec", 0), ("zb", 1), ("fold", 3, 1), ("fold", 3, 0), ("y", 3), ("x", 4), ("zd", 2), ("zc", 1), ("ys",
        0), ("z", 3), ("y", 4),),
    (0, 0, "r"): (("zd", 1), ("fold", 0, 1), ("hop", 3, 1), ("zs", 3), ("ys", 2), ("z", 4),),
    "tail": (("fold", 0, 0), ("vec", 1), ("ys", 1), ("ys", 3), ("vec", 2), ("cs", 0), ("zs", 4), ("vec", 3), ("hop", 3, 0), ("cs", 2), ("hop", 0, 1),
        ("cs", 1), ("ys", 4), ("cs", 3), ("vec", 4), ("cs", 4), ("vec", 5), ("hop", 0, 0),),
}


def plan(ops):
    def run(items):
        def go():
            for name, *a in items:
                ops[name](*a)
        return go
    return {k if isinstance(k, tuple) else (k,): run(v) for k, v in PLAN.items()}


def back(nz, order, gv, do, x_all, wqkv, k, v, kt, qn, qt, ot, lse, gw):
    A = pl.BlockSpec(memory_space=pltpu.HBM)
    V = pl.BlockSpec(memory_space=pltpu.VMEM)
    sds = jax.ShapeDtypeStruct
    B = lambda *s: pltpu.VMEM(s, bf16)
    F = lambda *s: pltpu.VMEM(s, f32)
    ins = (x_all, wqkv, k, v, kt, qn, qt, ot, lse)
    scratch = [pltpu.VMEM(a.shape, a.dtype) for a in ins] + [B(4, 256, 256)] + bwd_scratch()
    scratch += [B(nz, 1024, 512), B(1024, 512), B(2, 768, 256), F(8, 256), B(2, 256, 512)]
    scratch += [B(nz, 2, 256, 512), B(nz, 2, 256, 512), B(3, 2, 384, 512), B(3, 2, 384, 512), B(3, 384, 512), B(3, 384, 512), B(3, 192, 512), B(3, 192, 512),
                B(3, 96, 512), B(3, 96, 512), B(3, 48, 512), B(2, 384, 256), B(2, 384, 256), B(2, 192, 256), B(2, 192, 256), B(2, nz - 1, 48, 256),
                B(3, 768, 512), B(2, 768, 256),
                F(6, 24, 512), F(5, 24, 512)]
    scratch += [pltpu.SemaphoreType.DMA((80,)), pltpu.SemaphoreType.DMA((80,)), pltpu.SemaphoreType.DMA((40,))]
    return pl.pallas_call(
        functools.partial(back_kernel, nz),
        out_shape=(sds((2, 256, 512), bf16), sds((3, 768, 512), bf16), sds((2, 768, 256), bf16), sds((24, 512), f32)),
        in_specs=[pl.BlockSpec(memory_space=pltpu.SMEM), V] + [A] * 11, out_specs=(A, A, A, V), scratch_shapes=scratch,
        compiler_params=pltpu.CompilerParams(collective_id=2, has_side_effects=True, vmem_limit_bytes=62 << 20), name="back")(order, gv, do, *ins, gw)


def last_kernel(nu, go_ref, gq_ref, gv_ref, dx_ref, dsm_ref, gin, dwq, dbq, dwk, dwv, dbv, dwo, dbo, dg1, ds1, dwu, dbu, dwd, dbd, dg2, ds2):
    wi, y = lax.axis_index("wt"), lax.rem(lax.axis_index("ctx") // 2, 2)
    for s in range(2):
        seq = jnp.where(y == 0, s, 1 - s)
        gin[s] = (dsm_ref[s] + dx_ref[seq].astype(f32)).astype(bf16)
    hr = dwq.shape[0]
    for k in range(2):
        at, low = slice(k * 256, k * 256 + 256), k * 384
        dwq[:, at] = gq_ref[0, low:low + 256, :].astype(f32)
        dwk[0:128, at] = gq_ref[0, low + 256:low + 384, :].astype(f32)
        dwk[128:256, at] = gq_ref[1, low:low + 128, :].astype(f32)
        dwv[:, at] = gq_ref[1, low + 128:low + 384, :].astype(f32)
    dwo[...] = go_ref[0:hr, :].astype(f32)
    for k in range(nu):
        dwu[:, k * 512:k * 512 + 512] = go_ref[hr + k * hr:2 * hr + k * hr, :].astype(f32)
    dwd[...] = go_ref[hr + nu * hr:, :].astype(f32)

    def row(i):
        v = gv_ref[i:i + 1, :]
        return jnp.where(wi == 0, v[:, :256], v[:, 256:])

    for o, i in ((dbo, 0), (dg1, 1), (ds1, 2), (dbd, 3), (dg2, 4), (ds2, 5), (dbq, 16), (dbv, 17)):
        o[...] = row(i).reshape(256)
    h = nu // 2
    a, b = [jnp.concatenate([gv_ref[8 + k * h + i:9 + k * h + i, :] for i in range(h)], axis=1) for k in range(2)]
    dbu[...] = jnp.where(wi == 0, a, b).reshape(a.shape[1])


def last(nu, go, gqo, gv, dxo, dsm):
    V = pl.BlockSpec(memory_space=pltpu.VMEM)
    f = lambda *s: jax.ShapeDtypeStruct(s, f32)
    ff = nu * 512
    outs = (jax.ShapeDtypeStruct((2, 256, 512), bf16), f(256, 512), f(256), f(256, 512), f(256, 512), f(256), f(256, 512), f(256), f(256), f(256),
            f(256, ff), f(ff // 2), f(ff // 2, 512), f(256), f(256), f(256))
    return pl.pallas_call(functools.partial(last_kernel, nu), out_shape=outs, in_specs=[V] * 5, out_specs=(V,) * 16,
                          compiler_params=pltpu.CompilerParams(vmem_limit_bytes=56 << 20), name="last")(go, gqo, gv, dxo, dsm)


def body(block_in, block_order, w_query, b_query, w_key, w_value, b_value, w_out, b_out, gain_one, shift_one,
         w_up, b_up, w_down, b_down, gain_two, shift_two, cotangent, *, nc, nw):
    seqs, rows, dim = block_in.shape
    nz = nc // 4
    hb = rows // BLOCK
    half = dim // 2
    me = lax.axis_index("ctx")
    yy = (me // 2) % 2
    cc = me % 2
    zz = me // 4
    xor = lambda v: [(i, i ^ v) for i in range(nc)]
    ring = [(i, ((i // 4 + 1) % nz) * 4 + i % 4) for i in range(nc)]
    perm = lambda v, p: lax.ppermute(v, "ctx", p)
    gather = lambda v: lax.all_gather(v, "wt", axis=0, tiled=True)
    pick = lambda v, i: lax.dynamic_index_in_dim(v, i, 0, keepdims=False)

    ours = nw == 2 and nz == 4
    small = (b_query, b_value, b_out, gain_one, shift_one, b_down, gain_two, shift_two, b_up)
    by_seq = lambda a, b: jnp.where(yy == 0, jnp.concatenate([a, b], 0), jnp.concatenate([b, a], 0))
    r_ids = (zz - jnp.arange(nz, dtype=jnp.int32)) % nz
    quad = (me % 4) ^ jnp.array([0, 1, 2, 3], jnp.int32)
    order_row = pick(block_order, yy)
    slots = (r_ids[:, None, None] * 4 + quad[None, :, None]) * hb + jnp.arange(hb, dtype=jnp.int32)
    blk = order_row[slots.reshape(-1)]

    if ours:
        att, wo, wu, wd, sm, x_all, wqkv, ot, lse, k, v, kt, qn, qt = front(nz, block_order, small, block_in, (w_query, w_key, w_value, w_out, w_up, w_down))
        att = att.reshape(-1, dim)
    else:
        cols = lambda w: lax.dynamic_slice_in_dim(w, cc * half, half, 1)
        wqkv = gather(jnp.concatenate([cols(w_query), cols(w_key), cols(w_value)], axis=1))
        small = lax.all_gather(jnp.concatenate(small), "wt", axis=0)
        vec8 = jnp.transpose(small[:, :8 * dim // nw].reshape(nw, 8, dim // nw), (1, 0, 2)).reshape(8, 2, half)
        upb = small[:, 8 * dim // nw:].reshape(2, 4, half)
        sm = jnp.pad(jnp.concatenate([jnp.transpose(vec8, (1, 0, 2)), upb], axis=1).astype(f32), ((0, 0), (0, 4), (0, 0)))
        wo, wu, wd = gather(w_out), gather(w_up), gather(w_down)
        x_all = gather_all(nz, block_in)[0]
        o, ot, lse, k, v, kt, qn, qt = attn_fwd(nz, blk, x_all, wqkv, pick(sm, cc)[0:1], pick(sm, cc)[1:2])
        o_self, o_c, o_y, o_yc = o[0], perm(o[1], xor(1)), perm(o[2], xor(2)), perm(o[3], xor(3))
        mine, other = by_seq(o_self, o_y), by_seq(o_c, o_yc)
        att = jnp.where(cc == 0, jnp.concatenate([mine, other], 1), jnp.concatenate([other, mine], 1))

    out, dsm, d_o, gw, gv = dense(block_in.reshape(-1, dim), cotangent.reshape(-1, dim), att, wo, wu, wd, sm)

    if ours:
        dxo, go, gqo, gvec = back(nz, block_order, gv, d_o.reshape(seqs, rows, dim), x_all, wqkv, k, v, kt, qn, qt, ot, lse, gw)
        return (out.reshape(seqs, rows, dim),) + tuple(last(w_up.shape[1] // dim, go.reshape(-1, dim), gqo, gvec, dxo, dsm.reshape(seqs, rows, dim)))
    d_o = d_o.reshape(seqs, rows, dim)
    d_own, d_oth = pick(d_o, yy), pick(d_o, 1 - yy)
    fh = lambda v, c: lax.dynamic_slice_in_dim(v, c * half, half, 1)
    do_all = jnp.concatenate([fh(d_own, cc), perm(fh(d_own, 1 - cc), xor(1)), perm(fh(d_oth, cc), xor(2)), perm(fh(d_oth, 1 - cc), xor(3))], axis=0)
    dx, gq, gb = attn_bwd(nz, blk, x_all, wqkv, k, v, kt, qn, qt, ot, lse, do_all.reshape(4, rows, half))
    gvec = jnp.zeros((24, dim), f32).at[:16].set(gv)
    gvec = lax.dynamic_update_slice(gvec, gb[0:1], (16, cc * half))
    gvec = lax.dynamic_update_slice(gvec, gb[1:2], (17, cc * half))
    wi = lax.axis_index("wt")
    ff, hr = w_up.shape[1], dim // 2
    nu = ff // dim
    dx = jnp.transpose(dx.reshape(nz, 2, 2, rows, dim), (0, 2, 1, 3, 4)).reshape(nz, 2, 2 * rows, dim)
    part = lambda r: dx[r, 0].astype(f32) + perm(dx[r, 1], xor(1)).astype(f32)
    acc = None
    for r in list(range(1, nz)) + [0]:
        acc = part(r) if acc is None else perm(acc.astype(bf16), ring).astype(f32) + part(r)
    from_y = perm(acc[rows:].astype(bf16), xor(2)).astype(f32)
    dkv_sum = by_seq(acc[:rows], from_y)
    gvec = lax.psum(gvec, ("ctx", "wt"))
    g_out = gw[:, :hr].reshape(dim, dim)
    g_up = gw[:, hr:hr + nu * hr].reshape(2, nu, hr, dim).transpose(0, 2, 1, 3).reshape(dim, ff)
    g_down = gw[:, hr + nu * hr:].reshape(ff, dim)
    gq3 = gq.reshape(2, 3, hr, half).transpose(1, 0, 2, 3).reshape(3, dim, half)
    g_qkv = lax.dynamic_update_slice(jnp.zeros((3, dim, dim), bf16), gq3, (0, 0, cc * half))
    total = lambda g: lax.psum(lax.psum_scatter(g, "wt", scatter_dimension=0, tiled=True), "ctx").astype(f32)
    t_out, t_up, t_down = total(g_out), total(g_up), total(g_down)
    t_qkv = [total(g_qkv[i]) for i in range(3)]
    grad_in = (dsm + dkv_sum).astype(bf16).reshape(seqs, rows, dim)

    def share(vv):
        n = vv.size // nw
        return lax.dynamic_slice_in_dim(vv.reshape(-1), wi * n, n, 0)
    return (out.reshape(seqs, rows, dim), grad_in, t_qkv[0], share(gvec[16]), t_qkv[1], t_qkv[2], share(gvec[17]), t_out, share(gvec[0]),
            share(gvec[1]), share(gvec[2]), t_up, share(gvec[8:8 + nu]), t_down, share(gvec[3]), share(gvec[4]), share(gvec[5]))


def solution(mesh):
    seq, mat, vec = P("wt", "ctx", None), P("wt", None), P("wt")
    ins = (seq, mat, mat, vec, mat, mat, vec, mat, vec, vec, vec, mat, vec, mat, vec, vec, vec, seq)
    outs = (seq, seq, mat, vec, mat, mat, vec, mat, vec, vec, vec, mat, vec, mat, vec, vec, vec)
    run = functools.partial(body, nc=mesh.shape["ctx"], nw=mesh.shape["wt"])
    return jax.shard_map(run, mesh=mesh, in_specs=ins, out_specs=outs, check_vma=False)
```

```python
import functools
import math

import jax
import jax.numpy as jnp
from jax import lax
from jax.experimental import pallas as pl
from jax.experimental.pallas import tpu as pltpu
from jax.sharding import PartitionSpec as P

norm_eps = 1e-05

BLOCK = 128
HEADS_HERE = 4
LOG2E = 1.4426950408889634
FAR = -1e30
bf16, f32 = jnp.bfloat16, jnp.float32
NT = (((1,), (1,)), ((), ()))
TN = (((0,), (0,)), ((), ()))


def dot(a, b, dims=(((1,), (0,)), ((), ()))):
    return lax.dot_general(a, b, dims, preferred_element_type=f32)


def turned(v):
    return v.astype(f32).T.astype(bf16)


def head_slices():
    return [(slice(64 * h, 64 * h + 64), slice(128 * h, 128 * h + 128)) for h in range(HEADS_HERE)]


class Pairs:
    def __init__(self, nb, first):
        self.nb, self.first = nb, first

    def first_lo(self, n):
        return self.first(n) < self.nb // 2

    def lo(self, n):
        b = self.first(n)
        return jnp.where(b < self.nb // 2, b, self.nb - 1 - b)

    def ordered(self, n, v):
        a, b = v[:BLOCK], v[BLOCK:]
        first = self.first_lo(n)
        return jnp.where(first, a, b), jnp.where(first, b, a)


def project_chunk(pairs, r, x_ref, wkv_ref, wkvt_ref, bkv_ref, bkvt_ref, K, V, KT, VT, start=0, stop=4):
    def piece(p, _):
        x = jnp.concatenate(pairs.ordered(r * 4 + p, x_ref[r, p]), axis=0)
        kv = dot(x, wkv_ref[...])
        k, v = kv[:, :256].astype(bf16), (kv[:, 256:] + bkv_ref[...]).astype(bf16)
        kvt = dot(wkvt_ref[...], x, NT)
        kt, vt = kvt[:256].astype(bf16), (kvt[256:] + bkvt_ref[...]).astype(bf16)
        at = pl.ds(pl.multiple_of(p * BLOCK, BLOCK), BLOCK)
        for u in range(2):
            rows = slice(u * BLOCK, (u + 1) * BLOCK)
            K[r, u, at, :] = k[rows]
            V[r, u, at, :] = v[rows]
            KT[r, u, :, at] = kt[:, rows]
            VT[r, u, :, at] = vt[:, rows]
        return 0
    lax.fori_loop(start, stop, piece, 0)


def project_queries(pairs, x_ref, wq_ref, bq_ref, qn, qt, qs):
    qs[...] = jnp.zeros_like(qs)

    def piece(p, _):
        x = jnp.concatenate(pairs.ordered(p, x_ref[0, p]), axis=0)
        q = (dot(x, wq_ref[...]) + bq_ref[...]) * (LOG2E / 8.0)
        for u in range(2):
            mine = q[u * BLOCK:(u + 1) * BLOCK]
            qn[p, u] = mine.astype(bf16)
            t = mine.T.astype(bf16)
            qt[p, u] = t
            for hs, cs in head_slices():
                qs[p, u, hs, cs] = t[hs]
        return 0
    lax.fori_loop(0, 4, piece, 0)


def by_pair(vt, p16):
    return jnp.concatenate([dot(vt[0:128], p16[:, 0:256]), dot(vt[128:256], p16[:, 256:512])], axis=1)


def unpair(a):
    return jnp.concatenate([a[64 * (h % 2):64 * (h % 2) + 64, 128 * h:128 * h + 128] for h in range(HEADS_HERE)], axis=0)


def fwd_step(pairs, r, i, own, K, VT, qs, m_s, l_s, acc, d_s, sb, pb, js=(0, 1, 2, 3)):
    part = slice(js[0] * BLOCK, js[-1] * BLOCK + BLOCK)
    col = lambda v: jnp.max(v, axis=0, keepdims=True)
    tot = lambda v: jnp.sum(v, axis=0, keepdims=True)
    lo_i = pairs.lo(i)
    pick = {j: lo_i > pairs.lo(r * 4 + j) for j in js}
    sa = dot(K[r, 0, part, :], qs[i, 1])
    for j in js:
        u = jnp.where(pick[j], 0, 1)
        s = dot(K[r, u, j * BLOCK:(j + 1) * BLOCK, :], qs[i, u])
        if own:
            s = jnp.where(d_s[...] <= jnp.where(i == j, 0, 2 * BLOCK), s, FAR)
        sb[j] = s
    tops = {j: col(sb[j]) for j in js}
    m_hi, m_lo = col(sa), None
    for j in js:
        m_hi = jnp.maximum(m_hi, jnp.where(pick[j], FAR, tops[j]))
        t = jnp.where(pick[j], tops[j], FAR)
        m_lo = t if m_lo is None else jnp.maximum(m_lo, t)
    if own:
        rows = pl.ds(pl.multiple_of(i * BLOCK, BLOCK), BLOCK)
        sd = jnp.where(d_s[...] <= 0, dot(K[r, 0, rows, :], qs[i, 0]), FAR)
        m_lo = jnp.maximum(m_lo, col(sd))
    else:
        old_hi, old_lo = m_s[i, 1], m_s[i, 0]
        m_hi, m_lo = jnp.maximum(m_hi, old_hi), jnp.maximum(m_lo, old_lo)
    pa = jnp.exp2(sa - m_hi)
    l_hi, l_lo = tot(pa), jnp.zeros((1, 512), f32)
    for j in js:
        p = jnp.exp2(sb[j] - jnp.where(pick[j], m_lo, m_hi))
        t = tot(p)
        l_hi = l_hi + jnp.where(pick[j], 0.0, t)
        l_lo = l_lo + jnp.where(pick[j], t, 0.0)
        low = p.astype(bf16)
        rows = slice(j * BLOCK, (j + 1) * BLOCK)
        zero = jnp.zeros_like(low)
        pb[0, rows, :] = jnp.where(pick[j], low, zero)
        pb[1, rows, :] = jnp.where(pick[j], zero, low)
    o_hi = by_pair(VT[r, 0, :, part], pa.astype(bf16)) + by_pair(VT[r, 1, :, part], pb[1, part, :])
    o_lo = by_pair(VT[r, 0, :, part], pb[0, part, :])
    if own:
        p = jnp.exp2(sd - m_lo)
        l_lo = l_lo + tot(p)
        at = pl.ds(pl.multiple_of(i * BLOCK, BLOCK), BLOCK)
        o_lo = o_lo + by_pair(VT[r, 0, :, at], p.astype(bf16))
        l_s[i, 1], l_s[i, 0] = l_hi, l_lo
        acc[i, 1], acc[i, 0] = o_hi, o_lo
    else:
        f_hi, f_lo = jnp.exp2(old_hi - m_hi), jnp.exp2(old_lo - m_lo)
        l_s[i, 1] = l_s[i, 1] * f_hi + l_hi
        l_s[i, 0] = l_s[i, 0] * f_lo + l_lo
        acc[i, 1] = acc[i, 1] * f_hi + o_hi
        acc[i, 0] = acc[i, 0] * f_lo + o_lo
    m_s[i, 1], m_s[i, 0] = m_hi, m_lo


def fwd_finish(pairs, i, m_s, l_s, acc, lse, ot, o_ref):
    first = pairs.first_lo(i)
    out = []
    for u in range(2):
        l = l_s[i, u]
        lse[i, u] = m_s[i, u] + jnp.log2(l)
        t = unpair(acc[i, u] * (1.0 / l))
        ot[i, u] = t
        out.append(t.T.astype(bf16))
    o_ref[i, 0:BLOCK, :] = jnp.where(first, out[0], out[1])
    o_ref[i, BLOCK:2 * BLOCK, :] = jnp.where(first, out[1], out[0])


def diagonal(d_s):
    d_s[...] = lax.broadcasted_iota(jnp.int32, d_s.shape, 0) - (lax.broadcasted_iota(jnp.int32, d_s.shape, 1) & (BLOCK - 1))


def fwd_local(nz, blk_ref, x_ref, wqkv_ref, bq_ref, bkv_ref, bkvt_ref, o_ref, ot, lse, K, V, KT, qn, qt, VT, qs, m_s, l_s, acc, d_s, sb, pb, wkvt):
    pairs = Pairs(nz * 8, lambda n: blk_ref[2 * n])
    diagonal(d_s)
    wkvt[...] = turned(wqkv_ref[:, 256:])
    project_queries(pairs, x_ref, wqkv_ref.at[:, 0:256], bq_ref, qn, qt, qs)
    for r in range(nz):
        project_chunk(pairs, r, x_ref, wqkv_ref.at[:, 256:768], wkvt, bkv_ref, bkvt_ref, K, V, KT, VT)
        def step(i, _):
            fwd_step(pairs, r, i, r == 0, K, VT, qs, m_s, l_s, acc, d_s, sb, pb)
            return 0
        lax.fori_loop(0, 4, step, 0)
    for i in range(4):
        fwd_finish(pairs, i, m_s, l_s, acc, lse, ot, o_ref)


def fwd_outs(nz):
    sds = jax.ShapeDtypeStruct
    kv = sds((nz, 2, 512, 256), bf16)
    return (sds((4, 256, 256), bf16), sds((4, 2, 256, 128), f32), sds((4, 2, 1, 512), f32), kv, kv, sds((nz, 2, 256, 512), bf16),
            sds((4, 2, 128, 256), bf16), sds((4, 2, 256, 128), bf16))


def fwd_scratch(nz):
    M = pltpu.VMEM
    return [M((nz, 2, 256, 512), bf16), M((4, 2, 256, 512), bf16), M((4, 2, 1, 512), f32), M((4, 2, 1, 512), f32), M((4, 2, 128, 512), f32),
            M((128, 512), jnp.int32), M((4, 128, 512), f32), M((2, 512, 512), bf16), M((512, 512), bf16)]


def attn_fwd(nz, blk, x, wqkv, bq, bkv):
    V = pl.BlockSpec(memory_space=pltpu.VMEM)
    return pl.pallas_call(
        functools.partial(fwd_local, nz), out_shape=fwd_outs(nz),
        in_specs=[pl.BlockSpec(memory_space=pltpu.SMEM)] + [V] * 5, out_specs=(V,) * 8, scratch_shapes=fwd_scratch(nz),
        compiler_params=pltpu.CompilerParams(vmem_limit_bytes=58 << 20), name="attn_fwd")(blk, x, wqkv, bq, bkv, bkv.reshape(256, 1))


def bwd_query(pairs, i, do_ref, ot, qn, qt, qs, dos, qns, dons, dl):
    for u, do in enumerate(pairs.ordered(i, do_ref[i])):
        dot_t = do.astype(f32).T
        prod = dot_t * ot[i, u]
        low = dot_t.astype(bf16)
        q, t = qn[i, u], qt[i, u]
        for hs, cs in head_slices():
            qs[i, u, hs, cs] = t[hs]
            dos[i, u, hs, cs] = low[hs]
            qns[i, u, cs, hs] = q[:, hs]
            dons[i, u, cs, hs] = do[:, hs]
            dl[i, u, :, cs] = jnp.sum(prod[hs], axis=0, keepdims=True)


def bwd_step(pairs, r, i, own, first, K, V, KT, qs, dos, qns, dons, lse, dl, dk, dv, dq, d_s, gb, js=(0, 1, 2, 3)):
    lo_i = pairs.lo(i)
    pick = {j: lo_i > pairs.lo(r * 4 + j) for j in js}
    part = slice(js[0] * BLOCK, js[-1] * BLOCK + BLOCK)

    def pieces(k, v, u, mask):
        s = dot(k, qs[i, u]) - lse[i, u]
        if mask is not None:
            s = jnp.where(d_s[...] <= mask, s, FAR)
        p = jnp.exp2(s)
        g = p * (dot(v, dos[i, u]) - dl[i, u])
        return p.astype(bf16), g.astype(bf16)

    p, g = pieces(K[r, 0, part, :], V[r, 0, part, :], 1, None)
    dv[0, part, :] += dot(p, dons[i, 1])
    dk[0, part, :] += dot(g, qns[i, 1])
    q_hi = by_pair(KT[r, 0, :, part], g)
    for j in js:
        u = jnp.where(pick[j], 0, 1)
        rows = slice(j * BLOCK, (j + 1) * BLOCK)
        p, g = pieces(K[r, u, rows, :], V[r, u, rows, :], u, jnp.where(i == j, 0, 2 * BLOCK) if own else None)
        gv, gk = dot(p, dons[i, u]), dot(g, qns[i, u])
        dv[0, rows, :] += jnp.where(pick[j], gv, 0.0)
        dv[1, rows, :] += jnp.where(pick[j], 0.0, gv)
        dk[0, rows, :] += jnp.where(pick[j], gk, 0.0)
        dk[1, rows, :] += jnp.where(pick[j], 0.0, gk)
        zero = jnp.zeros_like(g)
        gb[0, rows, :] = jnp.where(pick[j], g, zero)
        gb[1, rows, :] = jnp.where(pick[j], zero, g)
    q_hi = q_hi + by_pair(KT[r, 1, :, part], gb[1, part, :])
    q_lo = by_pair(KT[r, 0, :, part], gb[0, part, :])
    if own:
        rows = pl.ds(pl.multiple_of(i * BLOCK, BLOCK), BLOCK)
        p, g = pieces(K[r, 0, rows, :], V[r, 0, rows, :], 0, 0)
        dv[0, rows, :] += dot(p, dons[i, 0])
        dk[0, rows, :] += dot(g, qns[i, 0])
        q_lo = q_lo + by_pair(KT[r, 0, :, rows], g)
    if first:
        dq[i, 1], dq[i, 0] = q_hi, q_lo
    else:
        dq[i, 1] += q_hi
        dq[i, 0] += q_lo


def bwd_chunk_weights(pairs, r, x_ref, dk, dv, dw, db, gp, js=(0, 1, 2, 3)):
    total = jnp.zeros((1, 256), f32)
    for p in js:
        at = slice(p * BLOCK, (p + 1) * BLOCK)
        g = [jnp.concatenate([(dk[u, at, :] * (1.0 / LOG2E)).astype(bf16), dv[u, at, :].astype(bf16)], axis=1) for u in range(2)]
        total = total + jnp.sum(g[0][:, 256:].astype(f32), axis=0, keepdims=True) + jnp.sum(g[1][:, 256:].astype(f32), axis=0, keepdims=True)
        first = pairs.first_lo(r * 4 + p)
        gp[p * 256:p * 256 + BLOCK, :] = jnp.where(first, g[0], g[1])
        gp[p * 256 + BLOCK:p * 256 + 256, :] = jnp.where(first, g[1], g[0])
    db[1:2, :] += total
    n = len(js)
    dw[:, 256:768] += dot(x_ref[r, js[0]:js[0] + n].reshape(n * 256, 512), gp[js[0] * 256:(js[0] + n) * 256, :], TN)


def bwd_chunk_rows(r, last, wqkv_ref, dxq, dx, gp, js=(1, 3, 0, 2)):
    for p in js:
        rows = slice(p * 256, p * 256 + 256)
        d = dot(gp[rows, :], wqkv_ref[:, 256:768], NT)
        if last:
            d = d + dxq[p]
        dx[r, rows, :] = d.astype(bf16)


def bwd_query_out(pairs, x_ref, wqkv_ref, dq, dxq, dw, db):
    def piece(i, _):
        t = [(unpair(dq[i, u]) * 0.125).T.astype(bf16) for u in range(2)]
        first = pairs.first_lo(i)
        g = jnp.concatenate([jnp.where(first, t[0], t[1]), jnp.where(first, t[1], t[0])], axis=0)
        dxq[i] = dot(g, wqkv_ref[:, 0:256], NT)
        dw[:, 0:256] += dot(x_ref[0, i], g, TN)
        db[0:1, :] += jnp.sum(g.astype(f32), axis=0, keepdims=True)
        return 0
    lax.fori_loop(0, 4, piece, 0)


def weight_rows(dw, gq):
    for k in range(2):
        for m in range(3):
            gq[k, m * 256:m * 256 + 256, :] = dw[k * 256:k * 256 + 256, m * 256:m * 256 + 256].astype(bf16)


def bwd_local(nz, blk_ref, x_ref, wqkv_ref, K, V, KT, qn, qt, ot, lse, do_ref, dx, gq, db, qs, dos, qns, dons, dl, dk, dv, dq, d_s, gb, dxq, dw, gp):
    pairs = Pairs(nz * 8, lambda n: blk_ref[2 * n])
    diagonal(d_s)
    dw[...] = jnp.zeros_like(dw)
    db[...] = jnp.zeros_like(db)
    for s in (qs, dos, qns, dons):
        s[...] = jnp.zeros_like(s)
    for i in range(4):
        bwd_query(pairs, i, do_ref, ot, qn, qt, qs, dos, qns, dons, dl)
    for r in list(range(1, nz)) + [0]:
        dk[...] = jnp.zeros_like(dk)
        dv[...] = jnp.zeros_like(dv)
        def step(i, _):
            bwd_step(pairs, r, i, r == 0, r == 1, K, V, KT, qs, dos, qns, dons, lse, dl, dk, dv, dq, d_s, gb)
            return 0
        lax.fori_loop(0, 4, step, 0)
        if r == 0:
            bwd_query_out(pairs, x_ref, wqkv_ref, dq, dxq, dw, db)
        bwd_chunk_weights(pairs, r, x_ref, dk, dv, dw, db, gp)
        bwd_chunk_rows(r, r == 0, wqkv_ref, dxq, dx, gp)
    weight_rows(dw, gq)


def bwd_scratch():
    M = pltpu.VMEM
    return [M((4, 2, 256, 512), bf16), M((4, 2, 256, 512), bf16), M((4, 2, 512, 256), bf16), M((4, 2, 512, 256), bf16), M((4, 2, 1, 512), f32),
            M((2, 512, 256), f32), M((2, 512, 256), f32), M((4, 2, 128, 512), f32), M((128, 512), jnp.int32), M((2, 512, 512), bf16),
            M((4, 256, 512), f32), M((512, 768), f32)]


def attn_bwd(nz, blk, x, wqkv, K, V, KT, qn, qt, ot, lse, do):
    S = pl.BlockSpec(memory_space=pltpu.VMEM)
    sds = jax.ShapeDtypeStruct
    return pl.pallas_call(
        functools.partial(bwd_local, nz), out_shape=(sds((nz, 1024, 512), bf16), sds((2, 768, 256), bf16), sds((8, 256), f32)),
        in_specs=[pl.BlockSpec(memory_space=pltpu.SMEM)] + [S] * 10, out_specs=(S,) * 3, scratch_shapes=bwd_scratch() + [pltpu.VMEM((1024, 512), bf16)],
        compiler_params=pltpu.CompilerParams(vmem_limit_bytes=58 << 20), name="attn_bwd")(blk, x, wqkv, K, V, KT, qn, qt, ot, lse, do)


def dense_kernel(x_ref, cot_ref, att_ref, wo_ref, wu_ref, wd_ref, sm_ref,
                 out_ref, dsm_ref, do_ref, gw_ref, gv_ref, act_s, gp_s, norm_s, dpre_s):
    ff = wu_ref.shape[1]
    chunk = 512
    x = x_ref[...].astype(f32)
    vec = lambda i: jnp.concatenate([sm_ref[0, i:i + 1, :], sm_ref[1, i:i + 1, :]], axis=1)
    b_out, g1, s1, b_down, g2, s2 = (vec(i) for i in range(2, 8))
    mean = lambda v: jnp.mean(v, axis=-1, keepdims=True)
    col = lambda v: jnp.sum(v, axis=0, keepdims=True)
    mix = x + dot(att_ref[...], wo_ref[...]) + b_out
    cen = mix - mean(mix)
    r1 = lax.rsqrt(mean(cen * cen) + norm_eps)
    n1 = cen * r1
    normed = n1 * g1 + s1
    nlow = normed.astype(bf16)
    norm_s[...] = nlow
    ffn = None
    for f in range(0, ff, chunk):
        fs = slice(f, f + chunk)
        at = 8 + f % (ff // 2) // 256
        b_up = jnp.concatenate([sm_ref[2 * f // ff, at + k:at + k + 1, :] for k in range(chunk // 256)], axis=1)
        pre = dot(nlow, wu_ref[:, fs]) + b_up
        c0 = math.sqrt(2.0 / math.pi)
        sq = pre * pre
        th = jnp.tanh(c0 * pre * (1.0 + 0.044715 * sq))
        half = 0.5 * (1.0 + th)
        act = (pre * half).astype(bf16)
        act_s[:, fs] = act
        gp_s[:, fs] = half + 0.5 * pre * (1.0 - th * th) * (c0 * (1.0 + 3 * 0.044715 * sq))
        part = dot(act, wd_ref[fs, :])
        ffn = part if ffn is None else ffn + part
    summed = ffn + b_down + normed + x
    cen = summed - mean(summed)
    r2 = lax.rsqrt(mean(cen * cen) + norm_eps)
    n2 = cen * r2
    out_ref[...] = (n2 * g2 + s2).astype(bf16)
    up = cot_ref[...].astype(f32)
    gv_ref[4:5, :] = col(up * n2)
    gv_ref[5:6, :] = col(up)
    dn = up * g2
    dsum = r2 * (dn - mean(dn) - n2 * mean(dn * n2))
    dffn = dsum.astype(bf16)
    gv_ref[3:4, :] = col(dffn.astype(f32))
    dnorm = dsum
    half_rows = wo_ref.shape[0] // 2
    half_ff = ff // 2
    def put(g, at, rows):
        gw_ref[0, at:at + rows, :] = g[:rows].astype(bf16)
        gw_ref[1, at:at + rows, :] = g[rows:].astype(bf16)
    for f in range(0, ff, chunk):
        fs = slice(f, f + chunk)
        dact = dot(dffn, wd_ref[fs, :], NT)
        dpre = (dact * gp_s[:, fs]).astype(bf16)
        gv_ref[8 + f // chunk:9 + f // chunk, :] = col(dpre.astype(f32))
        dnorm = dnorm + dot(dpre, wu_ref[:, fs], NT)
        put(dot(norm_s[...], dpre, TN), half_rows + (f // chunk) * half_rows, half_rows)
        gd = dot(act_s[:, fs], dffn, TN).astype(bf16)
        base = half_rows * (1 + ff // chunk)
        which, off = f // half_ff, f % half_ff
        gw_ref[which, base + off:base + off + chunk, :] = gd
    gv_ref[1:2, :] = col(dnorm * n1)
    gv_ref[2:3, :] = col(dnorm)
    dn = dnorm * g1
    dmix = r1 * (dn - mean(dn) - n1 * mean(dn * n1))
    dsm_ref[...] = dsum + dmix
    dbr = dmix.astype(bf16)
    gv_ref[0:1, :] = col(dbr.astype(f32))
    do_ref[...] = dot(dbr, wo_ref[...], NT).astype(bf16)
    put(dot(att_ref[...], dbr, TN), 0, half_rows)


def dense(x, cot, att, wo, wu, wd, sm):
    V = pl.BlockSpec(memory_space=pltpu.VMEM)
    tok, dim = x.shape
    ff = wu.shape[1]
    rows = (2 * dim * ff + dim * dim) // 2 // dim
    return pl.pallas_call(
        dense_kernel,
        out_shape=(jax.ShapeDtypeStruct((tok, dim), bf16), jax.ShapeDtypeStruct((tok, dim), f32),
                   jax.ShapeDtypeStruct((tok, dim), bf16), jax.ShapeDtypeStruct((2, rows, dim), bf16),
                   jax.ShapeDtypeStruct((16, dim), f32)),
        in_specs=[V] * 7, out_specs=(V,) * 5,
        scratch_shapes=[pltpu.VMEM((tok, ff), bf16), pltpu.VMEM((tok, ff), f32), pltpu.VMEM((tok, dim), bf16),
                        pltpu.VMEM((8, 128), f32)],
        compiler_params=pltpu.CompilerParams(vmem_limit_bytes=56 << 20),
        name="dense")(x, cot, att, wo, wu, wd, sm)


MESH = pl.DeviceIdType.MESH


def places(nz):
    me, wi = lax.axis_index("ctx"), lax.axis_index("wt")
    z, y, c = me // 4, lax.rem(me // 2, 2), lax.rem(me, 2)
    low = lax.rem(me, 4)
    at = lambda zz, ll: (zz * 4 + ll, wi)
    to = dict(up=at(lax.rem(z + 1, nz), low), down=at(lax.rem(z + nz - 1, nz), low), core=at(z, low + 1 - 2 * c), y=at(z, low + 2 - 4 * y),
              x=(me, 1 - wi))
    return me, wi, z, y, c, low, to


def meet(targets):
    bar = pltpu.get_barrier_semaphore()
    for t in targets:
        pl.semaphore_signal(bar, inc=1, device_id=t, device_id_type=MESH)
    pl.semaphore_wait(bar, len(targets))


class Wires:
    def __init__(self, send, recv):
        self.send, self.recv, self.n, self.live = send, recv, 0, []

    def make(self, src, dst, to):
        cp = pltpu.make_async_remote_copy(src, dst, self.send.at[self.n], self.recv.at[self.n], device_id=to, device_id_type=MESH)
        self.n += 1
        self.live.append(cp)
        return cp

    def go(self, src, dst, to):
        cp = self.make(src, dst, to)
        cp.start()
        return cp

    def drain(self):
        for cp in self.live:
            cp.wait_send()


def rows_of(start, size, mult=16):
    return pl.ds(pl.multiple_of(start, mult), size)


def gather_kernel(nz, with_w, *refs):
    if with_w:
        (x_ref, wq_ref, wk_ref, wv_ref, wo_ref, wu_ref, wd_ref, sm_ref,
         xall, wqkv, wo, wu, wd, sm, send, recv, lsem) = refs
    else:
        x_ref, xall, send, recv, lsem = refs
    me, wi, z, y, c, low, to = places(nz)
    rows = x_ref.shape[1]
    local = []

    def copy(src, dst):
        cp = pltpu.make_async_copy(src, dst, lsem.at[len(local)])
        cp.start()
        local.append(cp)

    copy(x_ref.at[y], xall.at[0, 0])
    if with_w:
        R, half = wq_ref.shape[0], wq_ref.shape[1] // 2
        for i, w in enumerate((wq_ref, wk_ref, wv_ref)):
            copy(w.at[:, rows_of(c * half, half, 128)], wqkv.at[rows_of(wi * R, R), pl.ds(i * half, half)])
        for w, full in ((wo_ref, wo), (wu_ref, wu), (wd_ref, wd)):
            n = w.shape[0]
            copy(w, full.at[rows_of(wi * n, n)])
        copy(sm_ref, sm.at[wi])
    near = [to["up"], to["down"], to["core"], to["y"]] + ([to["x"]] if with_w else [])
    meet(near)
    wires = Wires(send, recv)
    yx = wires.go(x_ref.at[1 - y], xall.at[0, 2], to["y"])
    ring = {(1, 0): wires.go(x_ref.at[y], xall.at[1, 0], to["up"])}
    core = {(0, 0): wires.go(x_ref.at[y], xall.at[0, 1], to["core"])}
    if with_w:
        xs = []
        for i, w in enumerate((wq_ref, wk_ref, wv_ref)):
            xs.append(wires.go(w.at[:, rows_of(c * half, half, 128)], wqkv.at[rows_of(wi * R, R), pl.ds(i * half, half)], to["x"]))
        xs.append(wires.go(sm_ref, sm.at[wi], to["x"]))
        big = []
        for w, full in ((wo_ref, wo), (wu_ref, wu), (wd_ref, wd)):
            n = w.shape[0]
            h = n // 2
            cp = wires.go(w.at[rows_of(c * h, h)], full.at[rows_of(wi * n + c * h, h)], to["x"])
            big.append((cp, full, rows_of((1 - wi) * n + c * h, h)))
    yx.wait_recv()
    ring[1, 1] = wires.go(xall.at[0, 2], xall.at[1, 2], to["up"])
    core[0, 1] = wires.go(xall.at[0, 2], xall.at[0, 3], to["core"])
    shared = []
    for r in range(1, nz):
        for s in range(2):
            ring[r, s].wait_recv()
            if r < nz - 1:
                ring[r + 1, s] = wires.go(xall.at[r, 2 * s], xall.at[r + 1, 2 * s], to["up"])
            core[r, s] = wires.go(xall.at[r, 2 * s], xall.at[r, 2 * s + 1], to["core"])
        if with_w and r - 1 < len(big):
            cp, full, where = big[r - 1]
            cp.wait_recv()
            shared.append(wires.go(full.at[where], full.at[where], to["core"]))
    if with_w:
        for cp, full, where in big[nz - 1:]:
            cp.wait_recv()
            shared.append(wires.go(full.at[where], full.at[where], to["core"]))
        for cp in xs + shared:
            cp.wait_recv()
    for cp in core.values():
        cp.wait_recv()
    wires.drain()
    for cp in local:
        cp.wait()


def gather_all(nz, x, weights=None, small=None):
    A = pl.BlockSpec(memory_space=pl.ANY)
    sds = jax.ShapeDtypeStruct
    rows, dim = x.shape[1:]
    outs = [sds((nz, 4, rows, dim), bf16)]
    ins = [x]
    ncopy = 1 + 2 * (nz - 1) + 2 * nz
    if weights is not None:
        wq, wk, wv, wo, wu, wd = weights
        ins += list(weights) + [small]
        outs += [sds((dim, 3 * dim // 2), bf16)] + [sds((2 * w.shape[0], w.shape[1]), bf16) for w in (wo, wu, wd)] + [sds((2,) + small.shape, bf16)]
        ncopy += 10
    return pl.pallas_call(
        functools.partial(gather_kernel, nz, weights is not None),
        out_shape=tuple(outs), in_specs=[A] * len(ins), out_specs=(A,) * len(outs),
        scratch_shapes=[pltpu.SemaphoreType.DMA((ncopy,)), pltpu.SemaphoreType.DMA((ncopy,)), pltpu.SemaphoreType.DMA((8,))],
        compiler_params=pltpu.CompilerParams(collective_id=1, has_side_effects=True, vmem_limit_bytes=16 << 20),
        name="gather_all")(*ins)


def add_into(dst, parts, rows, step=64):
    def body(i, _):
        r = rows_of(i * step, step)
        total = parts[0](r)[...].astype(f32)
        for p in parts[1:]:
            total = total + p(r)[...].astype(f32)
        d = dst(r)
        d[...] = total.astype(bf16)
        return 0
    lax.fori_loop(0, rows // step, body, 0)


def offset(ref, lead, start):
    def view(r):
        at = pl.ds(pl.multiple_of(start + r.start, 16), r.size)
        return ref.at[lead + (at,)]
    return view


def chip_pairs(nz, order_ref):
    me = lax.axis_index("ctx")
    z, y, c = me // 4, lax.rem(me // 2, 2), lax.rem(me, 2)

    def first(n):
        r, p = n // 4, n % 4
        a, b = p // 2, p % 2
        yy, cc = y + a - 2 * y * a, c + b - 2 * c * b
        return order_ref[y, 2 * (lax.rem(z - r + nz, nz) * 4 + yy * 2 + cc)]
    return Pairs(nz * 8, first)


def front_kernel(nz, order_ref, bqr, bvr, bor, g1r, s1r, bdr, g2r, s2r, bur, x_ref, wq_ref, wk_ref, wv_ref, wo_ref, wu_ref, wd_ref,
                 att, wo, wu, wd, sm, xall, wqkv, ot_o, lse_o, K_o, V_o, KT_o, qn_o, qt_o,
                 xs, ws, sms, wos, wus, wds, K, V, KT, VT, qn, qt, qs, m_s, l_s, acc, d_s, sb, pb, wkvt, bkvt, ot, lse, o_s, send, recv, lsem):
    me, wi, z, y, c, low, to = places(nz)
    to["yc"] = (z * 4 + 3 - low, wi)
    half, R = 256, wq_ref.shape[0]
    local = []

    def copy(src, dst):
        cp = pltpu.make_async_copy(src, dst, lsem.at[len(local)])
        cp.start()
        local.append(cp)
        return cp

    own_x = copy(x_ref.at[y], xs.at[0, 0])
    own_w = [copy(w.at[:, rows_of(c * half, half, 128)], ws.at[rows_of(wi * R, R), pl.ds(i * half, half)]) for i, w in enumerate((wq_ref, wk_ref, wv_ref))]
    for i, v in enumerate((bqr, bvr, bor, g1r, s1r, bdr, g2r, s2r)):
        sms[wi, i:i + 1, :] = v[...].astype(f32).reshape(1, half)
    up_b = bur[...].astype(f32).reshape(1, 1024)
    for i in range(4):
        sms[wi, 8 + i:9 + i, :] = up_b[:, i * half:(i + 1) * half]
    sms[wi, 12:16, :] = jnp.zeros((4, half), f32)
    meet([to[k] for k in ("up", "down", "core", "y", "yc", "x")])
    w = Wires(send, recv)
    yx = w.go(x_ref.at[1 - y], xs.at[0, 2], to["y"])
    ring, core = {}, {}
    ring[1, 0] = w.go(x_ref.at[y], xs.at[1, 0], to["up"])
    core[0, 0] = w.go(x_ref.at[y], xs.at[0, 1], to["core"])
    wx = []
    for i, m in enumerate((wq_ref, wk_ref, wv_ref)):
        wx.append(w.go(m.at[:, rows_of(c * half, half, 128)], ws.at[rows_of(wi * R, R), pl.ds(i * half, half)], to["x"]))
    wx.append(w.go(sms.at[wi], sms.at[wi], to["x"]))
    big = []
    for m, full in ((wo_ref, wos), (wu_ref, wus), (wd_ref, wds)):
        n = m.shape[0]
        h = n // 2
        copy(m, full.at[rows_of(wi * n, n)])
        big.append((m.at[rows_of(c * h, h)], full.at[rows_of(wi * n + c * h, h)], full, rows_of((1 - wi) * n + c * h, h)))

    pairs = chip_pairs(nz, order_ref)
    diagonal(d_s)
    yx.wait_recv()
    ring[1, 1] = w.go(xs.at[0, 2], xs.at[1, 2], to["up"])
    core[0, 1] = w.go(xs.at[0, 2], xs.at[0, 3], to["core"])

    def pump(r, s):
        ring[r, s].wait_recv()
        if r < nz - 1:
            ring[r + 1, s] = w.go(xs.at[r, 2 * s], xs.at[r + 1, 2 * s], to["up"])
        core[r, s] = w.go(xs.at[r, 2 * s], xs.at[r, 2 * s + 1], to["core"])

    shared = []

    def share(k):
        cp, full, where = sent[k]
        cp.wait_recv()
        shared.append(w.go(full.at[where], full.at[where], to["core"]))

    pump(1, 0)
    for cp in own_w:
        cp.wait()
    for cp in wx:
        cp.wait_recv()
    sent = [(w.go(src, dst, to["x"]), full, where) for src, dst, full, where in big]
    copy(sms, sm)
    copy(ws, wqkv)
    wkvt[...] = turned(ws[:, 256:])
    bv = sms[c, 1:2, :]
    bkvt[...] = jnp.broadcast_to(bv, (8, half)).T[:, 0:1]
    own_x.wait()
    core[0, 0].wait_recv()
    core[0, 1].wait_recv()
    project_queries(pairs, xs, ws.at[:, 0:256], sms.at[c, 0:1], qn, qt, qs)
    copy(qn, qn_o)
    copy(qt, qt_o)

    def bring(r, s):
        if r:
            core[r, s].wait_recv()
        project_chunk(pairs, r, xs, ws.at[:, 256:768], wkvt, sms.at[c, 1:2], bkvt, K, V, KT, VT, 2 * s, 2 * s + 2)
        for a, b in ((xs, xall), (K, K_o), (V, V_o), (KT, KT_o)):
            if s:
                copy(a.at[r], b.at[r])

    def attend(r, js, last=False):
        def step(n, _):
            i = lax.rem(n + 2, 4) if last else n
            fwd_step(pairs, r, i, r == 0, K, VT, qs, m_s, l_s, acc, d_s, sb, pb, js)
            if last:
                fwd_finish(pairs, i, m_s, l_s, acc, lse, ot, o_s)
                for p in outs:
                    pl.when(i == p)(outs[p].start)
            return 0
        lax.fori_loop(0, 4, step, 0)

    def half_chunk(r, s, last=False):
        bring(r, s)
        attend(r, (2 * s, 2 * s + 1), last)

    cols = pl.ds(pl.multiple_of(c * half, half), half)
    outs = {p: w.make(o_s.at[p], att.at[y, :, cols], to[k]) for p, k in ((2, "y"), (3, "yc"), (1, "core"))}
    bring(0, 0)
    bring(0, 1)
    pump(1, 1)
    attend(0, (0, 1, 2, 3))
    for k, (a, b) in enumerate(((wos, wo), (wus, wu), (wds, wd))):
        local[4 + k].wait()
        n = a.shape[0] // 2
        copy(a.at[rows_of(wi * n, n)], b.at[rows_of(wi * n, n)])
    pump(2, 0)
    for r in range(1, nz - 1):
        half_chunk(r, 0)
        if r > 1:
            pump(r + 1, 0)
        half_chunk(r, 1)
        if r < nz - 2:
            pump(r + 1, 1)
    half_chunk(nz - 1, 0)
    pump(nz - 1, 1)
    half_chunk(nz - 1, 1, True)
    copy(o_s.at[0], att.at[y, :, cols])
    copy(ot, ot_o)
    copy(lse, lse_o)
    for k, (a, b) in enumerate(((wos, wo), (wus, wu), (wds, wd))):
        share(k)
        copy(a.at[sent[k][2]], b.at[sent[k][2]])
    for k, (a, b) in enumerate(((wos, wo), (wus, wu), (wds, wd))):
        shared[k].wait_recv()
        n = a.shape[0] // 2
        where = rows_of((1 - wi) * n + (1 - c) * (n // 2), n // 2)
        copy(a.at[where], b.at[where])
    for cp in outs.values():
        cp.wait_recv()
    w.drain()
    for cp in local[7:]:
        cp.wait()


def front(nz, order, vectors, x, weights):
    A = pl.BlockSpec(memory_space=pltpu.HBM)
    V = pl.BlockSpec(memory_space=pltpu.VMEM)
    sds = jax.ShapeDtypeStruct
    M = pltpu.VMEM
    rows, dim = x.shape[1:]
    wq, wk, wv, wo, wu, wd = weights
    outs = [sds((2, rows, dim), bf16)] + [sds((2 * w.shape[0], w.shape[1]), bf16) for w in (wo, wu, wd)]
    outs += [sds((2, 16, 256), f32), sds((nz, 4, rows, dim), bf16), sds((dim, 768), bf16)] + list(fwd_outs(nz)[1:])
    scratch = [M((nz, 4, rows, dim), bf16), M((dim, 768), bf16), M((2, 16, 256), f32)] + [M(o.shape, bf16) for o in outs[1:4]]
    scratch += [M((nz, 2, 512, 256), bf16)] * 2 + [M((nz, 2, 256, 512), bf16)] * 2 + [M((4, 2, 128, 256), bf16), M((4, 2, 256, 128), bf16)]
    scratch += fwd_scratch(nz)[1:] + [M((256, 1), f32), M((4, 2, 256, 128), f32), M((4, 2, 1, 512), f32), M((4, 256, 256), bf16)]
    scratch += [pltpu.SemaphoreType.DMA((40,)), pltpu.SemaphoreType.DMA((40,)), pltpu.SemaphoreType.DMA((40,))]
    return pl.pallas_call(
        functools.partial(front_kernel, nz), out_shape=tuple(outs),
        in_specs=[pl.BlockSpec(memory_space=pltpu.SMEM)] + [V] * 9 + [A] * 7, out_specs=(A,) * len(outs), scratch_shapes=scratch,
        compiler_params=pltpu.CompilerParams(collective_id=1, has_side_effects=True, vmem_limit_bytes=58 << 20), name="front")(
            order, *vectors, x, *weights)


def back_kernel(nz, order_ref, gv_ref, do_ref, x_hbm, w_hbm, K_h, V_h, KT_h, qn_h, qt_h, ot_h, lse_h, gw_ref,
                dxo, go, gqo, gvo,
                xs, wqkv, K, V, KT, qn, qt, ot, lse, do, qs, dos, qns, dons, dl, dk, dv, dq, d_s, gb, dxq, dw, dx, gp, gq, db, outdx,
                dx_core, dx_in, cr, cs, xr, xs_, yr, ys_, za, zs, zb, xrq, xsq, yrq, ysq, zrq, gsum, gqsum, gvs, gvr, send, recv, lsem):
    me, wi, z, y, c, low, to = places(nz)
    to["yc"] = (z * 4 + 3 - low, wi)
    zto = [(lax.rem(z + d, nz) * 4 + low, wi) for d in range(1, nz)]
    half, hrow = 256, 256
    w = Wires(send, recv)
    local = []

    def copy(src, dst):
        cp = pltpu.make_async_copy(src, dst, lsem.at[len(local)])
        cp.start()
        local.append(cp)
        return cp

    cols = pl.ds(pl.multiple_of(c * half, half), half)
    other = pl.ds(pl.multiple_of((1 - c) * half, half), half)
    meet([to[k] for k in ("core", "y", "yc", "x")] + zto)
    dos_in = [w.go(do_ref.at[1 - y, :, cols], do.at[2], to["y"]), w.go(do_ref.at[1 - y, :, other], do.at[3], to["yc"]),
              w.go(do_ref.at[y, :, other], do.at[1], to["core"])]
    got = {}
    for s in range(3):
        got["c", s] = w.go(gw_ref.at[:, rows_of(s * 768 + (1 - c) * 384, 384)], cr.at[s], to["core"])
    mine_gw = [copy(gw_ref.at[:, rows_of(s * 768 + c * 384, 384)], cs.at[s]) for s in range(3)]
    first_in = [copy(do_ref.at[y, :, cols], do.at[0])] + [copy(a, b) for a, b in ((qn_h, qn), (qt_h, qt), (ot_h, ot), (lse_h, lse))]
    kv_in = {}
    for r in list(range(1, nz)) + [0]:
        kv_in[r] = [copy(a.at[r], b.at[r]) for a, b in ((K_h, K), (V_h, V), (KT_h, KT))]
    for r in kv_in:
        kv_in[r].append(copy(x_hbm.at[r], xs.at[r]))
    w_in = copy(w_hbm, wqkv)

    n = range(5)
    wide = [384, 192, 48]
    zp = (z + 1 - 2 * lax.rem(z, 2)) * 4 + low, wi
    zq = (z + 2 - 4 * (z // 2)) * 4 + low, wi
    odd, far = lax.rem(z, 2), z // 2
    X_in = [xr.at[s] for s in range(3)] + [xrq.at[s] for s in range(2)]
    X_sum = [xs_.at[s] for s in range(3)] + [xsq.at[s] for s in range(2)]
    Y_in = [yr.at[s] for s in range(3)] + [yrq.at[s] for s in range(2)]
    Y_sum = [ys_.at[s] for s in range(3)] + [ysq.at[s] for s in range(2)]
    Z_in = [zrq.at[s] for s in range(2)]
    out = [gsum.at[s] for s in range(3)] + [gqsum.at[s] for s in range(2)]
    start_c, start_y = c * 384, c * 384 + y * 192
    at_c, at_y = rows_of(start_c, 384), rows_of(start_y, 192)
    pos = odd * 2 + far
    start_p, start_h = start_y + pos * 48, start_y + odd * 96
    at_p, at_h = rows_of(start_p, 48), rows_of(start_h, 96)
    start_z = start_y + z * 48
    at_z = rows_of(start_z, 48)
    theirs = rows_of((1 - y) * 192, 192)
    for s in n:
        got["x", s] = w.make(cs.at[s, 1 - wi] if s < 3 else gq.at[1 - wi, pl.ds((s - 3) * 384, 384)], X_in[s], to["x"])
        got["y", s] = w.make(X_sum[s].at[theirs], Y_in[s], to["y"])
        got["ys", s] = w.make(out[s].at[at_y], out[s].at[at_y], to["y"])
        got["cs", s] = w.make(out[s].at[at_c], out[s].at[at_c], to["core"])
        if s < 3:
            got["za", s] = w.make(ys_.at[s, rows_of((1 - odd) * 96, 96)], za.at[s], zp)
            got["zb", s] = w.make(zs.at[s, rows_of((1 - far) * 48, 48)], zb.at[s], zq)
            got["zc", s] = w.make(out[s].at[at_p], out[s].at[at_p], zq)
            got["zd", s] = w.make(out[s].at[at_h], out[s].at[at_h], zp)
        else:
            for d in range(1, nz):
                got["z", s, d] = w.make(Y_sum[s].at[rows_of(lax.rem(z + d, nz) * 48, 48)], Z_in[s - 3].at[d - 1], zto[d - 1])
                got["zs", s, d] = w.make(out[s].at[at_z], out[s].at[at_z], zto[d - 1])

    def x_send(s):
        if s < 3:
            mine_gw[s].wait()
            got["c", s].wait_recv()
            add_into(offset(cs, (s, 1 - wi), 0), [offset(cs, (s, 1 - wi), 0), offset(cr, (s, 1 - wi), 0)], 384, 128)
            got["x", s].start()
            add_into(offset(cs, (s, wi), 0), [offset(cs, (s, wi), 0), offset(cr, (s, wi), 0)], 384, 128)
        else:
            got["x", s].start()

    def y_send(s):
        got["x", s].wait_recv()
        mine = lambda lo: offset(cs, (s, wi), lo) if s < 3 else offset(gq, (wi,), (s - 3) * 384 + lo)
        for half_y in (1 - y, y):
            lo = half_y * 192
            add_into(offset(X_sum[s], (), lo), [mine(lo), offset(X_in[s], (), lo)], 192, 96)
            if half_y is not y:
                got["y", s].start()

    def z_a(s):
        got["y", s].wait_recv()
        add_into(offset(ys_, (s,), 0), [offset(xs_, (s,), y * 192), offset(yr, (s,), 0)], 192, 96)
        got["za", s].start()

    def z_b(s):
        got["za", s].wait_recv()
        add_into(offset(zs, (s,), 0), [offset(ys_, (s,), odd * 96), offset(za, (s,), 0)], 96, 96)
        got["zb", s].start()

    def z_c(s):
        got["zb", s].wait_recv()
        add_into(offset(out[s], (), start_p), [offset(zs, (s,), far * 48), offset(zb, (s,), 0)], 48, 48)
        got["zc", s].start()

    def z_d(s):
        got["zc", s].wait_recv()
        got["zd", s].start()

    def z_send(s):
        got["y", s].wait_recv()
        add_into(offset(Y_sum[s], (), 0), [offset(X_sum[s], (), y * 192), offset(Y_in[s], (), 0)], 192, 192)
        for d in range(1, nz):
            got["z", s, d].start()

    def z_share(s):
        for d in range(1, nz):
            got["z", s, d].wait_recv()
        add_into(offset(out[s], (), start_z), [offset(Y_sum[s], (), z * 48)] + [offset(Z_in[s - 3], (d,), 0) for d in range(nz - 1)], 48, 48)
        for d in range(1, nz):
            got["zs", s, d].start()

    def y_share(s):
        for k in (["zd"] if s < 3 else [("zs", d) for d in range(1, nz)]):
            got[(k, s) if s < 3 else (k[0], s, k[1])].wait_recv()
        got["ys", s].start()

    def c_share(s):
        got["ys", s].wait_recv()
        got["cs", s].start()

    for r in range(nz):
        for h in range(2):
            at = pl.ds(h * 512, hrow)
            got["d", r, h] = w.make(dx.at[r, pl.ds(h * 512 + hrow, hrow)], dx_core.at[r, h], to["core"])
            if r:
                got["r", (r + 1) % nz, h] = w.make(dx.at[r, at], dx_in.at[(r + 1) % nz, h], to["up"])
    got["dy"] = w.make(dx.at[0, pl.ds(512, hrow)], outdx.at[1], to["y"])

    def give(r, h):
        got["d", r, h].start()

    def fold(r, h):
        got["d", r, h].wait_recv()
        add_into(offset(dx, (r,), h * 512), [offset(dx, (r,), h * 512), offset(dx_core, (r, h), 0)], hrow, 128)
        if r == 1:
            got["r", 2, h].start()

    def hop(r, h):
        got["r", r, h].wait_recv()
        dst = offset(dx, (r,), h * 512) if r or h else offset(outdx, (0,), 0)
        add_into(dst, [offset(dx, (r,), h * 512), offset(dx_in, (r, h), 0)], hrow, 128)
        if r:
            got["r", (r + 1) % nz, h].start()
        elif h:
            got["dy"].start()

    vec_to = [to["core"], to["y"], to["x"]] + [(zz * 4 + low, wi) for zz in (z + 1 - 2 * lax.rem(z, 2), z + 2 - 4 * (z // 2))]

    def vec_send(k):
        if k == 0:
            gvs[0] = jnp.zeros_like(gvs[0])
            gvs[0, 0:16, :] = gv_ref[...]
            zero = jnp.zeros((1, half), f32)
            for i in range(2):
                v = db[i:i + 1, :]
                gvs[0, 16 + i:17 + i, :] = jnp.concatenate([jnp.where(c == 0, v, zero), jnp.where(c == 0, zero, v)], axis=1)
        else:
            got["v", k - 1].wait_recv()
            gvs[k] = gvs[k - 1] + gvr[k - 1]
        if k < 5:
            got["v", k].start()
        else:
            gvo[...] = gvs[5]

    pairs = chip_pairs(nz, order_ref)
    for k in range(5):
        got["v", k] = w.make(gvs.at[k], gvr.at[k], vec_to[k])
    diagonal(d_s)
    dw[...] = jnp.zeros_like(dw)
    db[...] = jnp.zeros_like(db)
    for s in (qs, dos, qns, dons):
        s[...] = jnp.zeros_like(s)
    x_send(0)
    for cp in first_in:
        cp.wait()
    for r in kv_in:
        for cp in kv_in[r][:3]:
            cp.wait()
    dos_in[2].wait_recv()
    hooks = plan(dict(x=x_send, y=y_send, za=z_a, zb=z_b, zc=z_c, zd=z_d, ys=y_share, cs=c_share, fold=fold, hop=hop, z=z_send, zs=z_share, vec=vec_send))
    hook = lambda *k: hooks[k]() if k in hooks else None
    hook("pre")
    for r in list(range(1, nz)) + [0]:
        dk[...] = jnp.zeros_like(dk)
        dv[...] = jnp.zeros_like(dv)
        for n, js in enumerate(((2, 3), (0, 1)) if r == 1 else ((0, 1, 2, 3),)):
            def step(i, _):
                if r == 1 and n == 0:
                    for k in range(2):
                        pl.when(i == 2)(dos_in[k].wait_recv)
                    bwd_query(pairs, i, do, ot, qn, qt, qs, dos, qns, dons, dl)
                bwd_step(pairs, r, i, r == 0, r == 1 and n == 0, K, V, KT, qs, dos, qns, dons, lse, dl, dk, dv, dq, d_s, gb, js)
                for k in range(4):
                    if (r, n, k) in hooks:
                        pl.when(i == k)(hooks[r, n, k])
                return 0
            lax.fori_loop(0, 4, step, 0)
            if r == 1 and n == 0:
                for q in kv_in:
                    kv_in[q][3].wait()
                w_in.wait()
            if r == 0:
                bwd_query_out(pairs, xs, wqkv, dq, dxq, dw, db)
                hook(0, 0, "q")
            bwd_chunk_weights(pairs, r, xs, dk, dv, dw, db, gp, js)
            if r == 0:
                weight_rows(dw, gq)
                x_send(3)
            hook(r, n, "w")
            bwd_chunk_rows(r, r == 0, wqkv, dxq, dx, gp, [p for p in (3, 1, 2, 0) if p in js])
            for h in (1, 0):
                if 2 * h in js:
                    give(r, h)
            hook(r, n, "r")
    hook("tail")
    for s in range(5):
        got["cs", s].wait_recv()
        copy(gsum.at[s], go.at[s]) if s < 3 else copy(gqsum.at[s - 3], gqo.at[s - 3])
    got["dy"].wait_recv()
    copy(outdx, dxo)
    w.drain()
    for cp in local[-6:]:
        cp.wait()


PLAN = {
    (1, 0, "r"): (("x", 2),),
    (1, 1, 2): (("y", 0),),
    (1, 1, "r"): (("fold", 1, 1),),
    (2, 0, 2): (("x", 1), ("fold", 1, 0), ("za", 0),),
    (2, 0, "r"): (("y", 2),),
    (3, 0, 2): (("zb", 0),),
    (3, 0, 3): (("za", 2), ("fold", 2, 0), ("y", 1),),
    (3, 0, "r"): (("zc", 0), ("hop", 2, 0),),
    (0, 0, 2): (("za", 1),),
    (0, 0, "q"): (("zb", 2), ("zd", 0), ("fold", 2, 1),),
    (0, 0, "w"): (("hop", 2, 1), ("zc", 2), ("vec", 0), ("zb", 1), ("fold", 3, 1), ("fold", 3, 0), ("y", 3), ("x", 4), ("zd", 2), ("zc", 1), ("ys",
        0), ("z", 3), ("y", 4),),
    (0, 0, "r"): (("zd", 1), ("fold", 0, 1), ("hop", 3, 1), ("zs", 3), ("ys", 2), ("z", 4),),
    "tail": (("fold", 0, 0), ("vec", 1), ("ys", 1), ("ys", 3), ("vec", 2), ("cs", 0), ("zs", 4), ("vec", 3), ("hop", 3, 0), ("cs", 2), ("hop", 0, 1),
        ("cs", 1), ("ys", 4), ("cs", 3), ("vec", 4), ("cs", 4), ("vec", 5), ("hop", 0, 0),),
}


def plan(ops):
    def run(items):
        def go():
            for name, *a in items:
                ops[name](*a)
        return go
    return {k if isinstance(k, tuple) else (k,): run(v) for k, v in PLAN.items()}


def back(nz, order, gv, do, x_all, wqkv, k, v, kt, qn, qt, ot, lse, gw):
    A = pl.BlockSpec(memory_space=pltpu.HBM)
    V = pl.BlockSpec(memory_space=pltpu.VMEM)
    sds = jax.ShapeDtypeStruct
    B = lambda *s: pltpu.VMEM(s, bf16)
    F = lambda *s: pltpu.VMEM(s, f32)
    ins = (x_all, wqkv, k, v, kt, qn, qt, ot, lse)
    scratch = [pltpu.VMEM(a.shape, a.dtype) for a in ins] + [B(4, 256, 256)] + bwd_scratch()
    scratch += [B(nz, 1024, 512), B(1024, 512), B(2, 768, 256), F(8, 256), B(2, 256, 512)]
    scratch += [B(nz, 2, 256, 512), B(nz, 2, 256, 512), B(3, 2, 384, 512), B(3, 2, 384, 512), B(3, 384, 512), B(3, 384, 512), B(3, 192, 512), B(3, 192, 512),
                B(3, 96, 512), B(3, 96, 512), B(3, 48, 512), B(2, 384, 256), B(2, 384, 256), B(2, 192, 256), B(2, 192, 256), B(2, nz - 1, 48, 256),
                B(3, 768, 512), B(2, 768, 256),
                F(6, 24, 512), F(5, 24, 512)]
    scratch += [pltpu.SemaphoreType.DMA((80,)), pltpu.SemaphoreType.DMA((80,)), pltpu.SemaphoreType.DMA((40,))]
    return pl.pallas_call(
        functools.partial(back_kernel, nz),
        out_shape=(sds((2, 256, 512), bf16), sds((3, 768, 512), bf16), sds((2, 768, 256), bf16), sds((24, 512), f32)),
        in_specs=[pl.BlockSpec(memory_space=pltpu.SMEM), V] + [A] * 11, out_specs=(A, A, A, V), scratch_shapes=scratch,
        compiler_params=pltpu.CompilerParams(collective_id=2, has_side_effects=True, vmem_limit_bytes=62 << 20), name="back")(order, gv, do, *ins, gw)


def last_kernel(nu, go_ref, gq_ref, gv_ref, dx_ref, dsm_ref, gin, dwq, dbq, dwk, dwv, dbv, dwo, dbo, dg1, ds1, dwu, dbu, dwd, dbd, dg2, ds2):
    wi, y = lax.axis_index("wt"), lax.rem(lax.axis_index("ctx") // 2, 2)
    for s in range(2):
        seq = jnp.where(y == 0, s, 1 - s)
        gin[s] = (dsm_ref[s] + dx_ref[seq].astype(f32)).astype(bf16)
    hr = dwq.shape[0]
    for k in range(2):
        at, low = slice(k * 256, k * 256 + 256), k * 384
        dwq[:, at] = gq_ref[0, low:low + 256, :].astype(f32)
        dwk[0:128, at] = gq_ref[0, low + 256:low + 384, :].astype(f32)
        dwk[128:256, at] = gq_ref[1, low:low + 128, :].astype(f32)
        dwv[:, at] = gq_ref[1, low + 128:low + 384, :].astype(f32)
    dwo[...] = go_ref[0:hr, :].astype(f32)
    for k in range(nu):
        dwu[:, k * 512:k * 512 + 512] = go_ref[hr + k * hr:2 * hr + k * hr, :].astype(f32)
    dwd[...] = go_ref[hr + nu * hr:, :].astype(f32)

    def row(i):
        v = gv_ref[i:i + 1, :]
        return jnp.where(wi == 0, v[:, :256], v[:, 256:])

    for o, i in ((dbo, 0), (dg1, 1), (ds1, 2), (dbd, 3), (dg2, 4), (ds2, 5), (dbq, 16), (dbv, 17)):
        o[...] = row(i).reshape(256)
    h = nu // 2
    a, b = [jnp.concatenate([gv_ref[8 + k * h + i:9 + k * h + i, :] for i in range(h)], axis=1) for k in range(2)]
    dbu[...] = jnp.where(wi == 0, a, b).reshape(a.shape[1])


def last(nu, go, gqo, gv, dxo, dsm):
    V = pl.BlockSpec(memory_space=pltpu.VMEM)
    f = lambda *s: jax.ShapeDtypeStruct(s, f32)
    ff = nu * 512
    outs = (jax.ShapeDtypeStruct((2, 256, 512), bf16), f(256, 512), f(256), f(256, 512), f(256, 512), f(256), f(256, 512), f(256), f(256), f(256),
            f(256, ff), f(ff // 2), f(ff // 2, 512), f(256), f(256), f(256))
    return pl.pallas_call(functools.partial(last_kernel, nu), out_shape=outs, in_specs=[V] * 5, out_specs=(V,) * 16,
                          compiler_params=pltpu.CompilerParams(vmem_limit_bytes=56 << 20), name="last")(go, gqo, gv, dxo, dsm)


def body(block_in, block_order, w_query, b_query, w_key, w_value, b_value, w_out, b_out, gain_one, shift_one,
         w_up, b_up, w_down, b_down, gain_two, shift_two, cotangent, *, nc, nw):
    seqs, rows, dim = block_in.shape
    nz = nc // 4
    hb = rows // BLOCK
    half = dim // 2
    me = lax.axis_index("ctx")
    yy = (me // 2) % 2
    cc = me % 2
    zz = me // 4
    xor = lambda v: [(i, i ^ v) for i in range(nc)]
    ring = [(i, ((i // 4 + 1) % nz) * 4 + i % 4) for i in range(nc)]
    perm = lambda v, p: lax.ppermute(v, "ctx", p)
    gather = lambda v: lax.all_gather(v, "wt", axis=0, tiled=True)
    pick = lambda v, i: lax.dynamic_index_in_dim(v, i, 0, keepdims=False)

    ours = nw == 2 and nz == 4
    small = (b_query, b_value, b_out, gain_one, shift_one, b_down, gain_two, shift_two, b_up)
    by_seq = lambda a, b: jnp.where(yy == 0, jnp.concatenate([a, b], 0), jnp.concatenate([b, a], 0))
    r_ids = (zz - jnp.arange(nz, dtype=jnp.int32)) % nz
    quad = (me % 4) ^ jnp.array([0, 1, 2, 3], jnp.int32)
    order_row = pick(block_order, yy)
    slots = (r_ids[:, None, None] * 4 + quad[None, :, None]) * hb + jnp.arange(hb, dtype=jnp.int32)
    blk = order_row[slots.reshape(-1)]

    if ours:
        att, wo, wu, wd, sm, x_all, wqkv, ot, lse, k, v, kt, qn, qt = front(nz, block_order, small, block_in, (w_query, w_key, w_value, w_out, w_up, w_down))
        att = att.reshape(-1, dim)
    else:
        cols = lambda w: lax.dynamic_slice_in_dim(w, cc * half, half, 1)
        wqkv = gather(jnp.concatenate([cols(w_query), cols(w_key), cols(w_value)], axis=1))
        small = lax.all_gather(jnp.concatenate(small), "wt", axis=0)
        vec8 = jnp.transpose(small[:, :8 * dim // nw].reshape(nw, 8, dim // nw), (1, 0, 2)).reshape(8, 2, half)
        upb = small[:, 8 * dim // nw:].reshape(2, 4, half)
        sm = jnp.pad(jnp.concatenate([jnp.transpose(vec8, (1, 0, 2)), upb], axis=1).astype(f32), ((0, 0), (0, 4), (0, 0)))
        wo, wu, wd = gather(w_out), gather(w_up), gather(w_down)
        x_all = gather_all(nz, block_in)[0]
        o, ot, lse, k, v, kt, qn, qt = attn_fwd(nz, blk, x_all, wqkv, pick(sm, cc)[0:1], pick(sm, cc)[1:2])
        o_self, o_c, o_y, o_yc = o[0], perm(o[1], xor(1)), perm(o[2], xor(2)), perm(o[3], xor(3))
        mine, other = by_seq(o_self, o_y), by_seq(o_c, o_yc)
        att = jnp.where(cc == 0, jnp.concatenate([mine, other], 1), jnp.concatenate([other, mine], 1))

    out, dsm, d_o, gw, gv = dense(block_in.reshape(-1, dim), cotangent.reshape(-1, dim), att, wo, wu, wd, sm)

    if ours:
        dxo, go, gqo, gvec = back(nz, block_order, gv, d_o.reshape(seqs, rows, dim), x_all, wqkv, k, v, kt, qn, qt, ot, lse, gw)
        return (out.reshape(seqs, rows, dim),) + tuple(last(w_up.shape[1] // dim, go.reshape(-1, dim), gqo, gvec, dxo, dsm.reshape(seqs, rows, dim)))
    d_o = d_o.reshape(seqs, rows, dim)
    d_own, d_oth = pick(d_o, yy), pick(d_o, 1 - yy)
    fh = lambda v, c: lax.dynamic_slice_in_dim(v, c * half, half, 1)
    do_all = jnp.concatenate([fh(d_own, cc), perm(fh(d_own, 1 - cc), xor(1)), perm(fh(d_oth, cc), xor(2)), perm(fh(d_oth, 1 - cc), xor(3))], axis=0)
    dx, gq, gb = attn_bwd(nz, blk, x_all, wqkv, k, v, kt, qn, qt, ot, lse, do_all.reshape(4, rows, half))
    gvec = jnp.zeros((24, dim), f32).at[:16].set(gv)
    gvec = lax.dynamic_update_slice(gvec, gb[0:1], (16, cc * half))
    gvec = lax.dynamic_update_slice(gvec, gb[1:2], (17, cc * half))
    wi = lax.axis_index("wt")
    ff, hr = w_up.shape[1], dim // 2
    nu = ff // dim
    dx = jnp.transpose(dx.reshape(nz, 2, 2, rows, dim), (0, 2, 1, 3, 4)).reshape(nz, 2, 2 * rows, dim)
    part = lambda r: dx[r, 0].astype(f32) + perm(dx[r, 1], xor(1)).astype(f32)
    acc = None
    for r in list(range(1, nz)) + [0]:
        acc = part(r) if acc is None else perm(acc.astype(bf16), ring).astype(f32) + part(r)
    from_y = perm(acc[rows:].astype(bf16), xor(2)).astype(f32)
    dkv_sum = by_seq(acc[:rows], from_y)
    gvec = lax.psum(gvec, ("ctx", "wt"))
    g_out = gw[:, :hr].reshape(dim, dim)
    g_up = gw[:, hr:hr + nu * hr].reshape(2, nu, hr, dim).transpose(0, 2, 1, 3).reshape(dim, ff)
    g_down = gw[:, hr + nu * hr:].reshape(ff, dim)
    gq3 = gq.reshape(2, 3, hr, half).transpose(1, 0, 2, 3).reshape(3, dim, half)
    g_qkv = lax.dynamic_update_slice(jnp.zeros((3, dim, dim), bf16), gq3, (0, 0, cc * half))
    total = lambda g: lax.psum(lax.psum_scatter(g, "wt", scatter_dimension=0, tiled=True), "ctx").astype(f32)
    t_out, t_up, t_down = total(g_out), total(g_up), total(g_down)
    t_qkv = [total(g_qkv[i]) for i in range(3)]
    grad_in = (dsm + dkv_sum).astype(bf16).reshape(seqs, rows, dim)

    def share(vv):
        n = vv.size // nw
        return lax.dynamic_slice_in_dim(vv.reshape(-1), wi * n, n, 0)
    return (out.reshape(seqs, rows, dim), grad_in, t_qkv[0], share(gvec[16]), t_qkv[1], t_qkv[2], share(gvec[17]), t_out, share(gvec[0]),
            share(gvec[1]), share(gvec[2]), t_up, share(gvec[8:8 + nu]), t_down, share(gvec[3]), share(gvec[4]), share(gvec[5]))


def solution(mesh):
    seq, mat, vec = P("wt", "ctx", None), P("wt", None), P("wt")
    ins = (seq, mat, mat, vec, mat, mat, vec, mat, vec, vec, vec, mat, vec, mat, vec, vec, vec, seq)
    outs = (seq, seq, mat, vec, mat, mat, vec, mat, vec, vec, vec, mat, vec, mat, vec, vec, vec)
    run = functools.partial(body, nc=mesh.shape["ctx"], nw=mesh.shape["wt"])
    return jax.shard_map(run, mesh=mesh, in_specs=ins, out_specs=outs, check_vma=False)
```

```python
import functools
import math

import jax
import jax.numpy as jnp
from jax import lax
from jax.experimental import pallas as pl
from jax.experimental.pallas import tpu as pltpu
from jax.sharding import PartitionSpec as P

norm_eps = 1e-05

BLOCK = 128
HEADS_HERE = 4
LOG2E = 1.4426950408889634
FAR = -1e30
bf16, f32 = jnp.bfloat16, jnp.float32
NT = (((1,), (1,)), ((), ()))
TN = (((0,), (0,)), ((), ()))


def dot(a, b, dims=(((1,), (0,)), ((), ()))):
    return lax.dot_general(a, b, dims, preferred_element_type=f32)


def turned(v):
    return v.astype(f32).T.astype(bf16)


def head_slices():
    return [(slice(64 * h, 64 * h + 64), slice(128 * h, 128 * h + 128)) for h in range(HEADS_HERE)]


class Pairs:
    def __init__(self, nb, first):
        self.nb, self.first = nb, first

    def first_lo(self, n):
        return self.first(n) < self.nb // 2

    def lo(self, n):
        b = self.first(n)
        return jnp.where(b < self.nb // 2, b, self.nb - 1 - b)

    def ordered(self, n, v):
        a, b = v[:BLOCK], v[BLOCK:]
        first = self.first_lo(n)
        return jnp.where(first, a, b), jnp.where(first, b, a)


def project_chunk(pairs, r, x_ref, wkv_ref, wkvt_ref, bkv_ref, bkvt_ref, K, V, KT, VT, start=0, stop=4):
    def piece(p, _):
        x = jnp.concatenate(pairs.ordered(r * 4 + p, x_ref[r, p]), axis=0)
        kv = dot(x, wkv_ref[...])
        k, v = kv[:, :256].astype(bf16), (kv[:, 256:] + bkv_ref[...]).astype(bf16)
        kvt = dot(wkvt_ref[...], x, NT)
        kt, vt = kvt[:256].astype(bf16), (kvt[256:] + bkvt_ref[...]).astype(bf16)
        at = pl.ds(pl.multiple_of(p * BLOCK, BLOCK), BLOCK)
        for u in range(2):
            rows = slice(u * BLOCK, (u + 1) * BLOCK)
            K[r, u, at, :] = k[rows]
            V[r, u, at, :] = v[rows]
            KT[r, u, :, at] = kt[:, rows]
            VT[r, u, :, at] = vt[:, rows]
        return 0
    lax.fori_loop(start, stop, piece, 0)


def project_queries(pairs, x_ref, wq_ref, bq_ref, qn, qt, qs):
    qs[...] = jnp.zeros_like(qs)

    def piece(p, _):
        x = jnp.concatenate(pairs.ordered(p, x_ref[0, p]), axis=0)
        q = (dot(x, wq_ref[...]) + bq_ref[...]) * (LOG2E / 8.0)
        for u in range(2):
            mine = q[u * BLOCK:(u + 1) * BLOCK]
            qn[p, u] = mine.astype(bf16)
            t = mine.T.astype(bf16)
            qt[p, u] = t
            for hs, cs in head_slices():
                qs[p, u, hs, cs] = t[hs]
        return 0
    lax.fori_loop(0, 4, piece, 0)


def by_pair(vt, p16):
    return jnp.concatenate([dot(vt[0:128], p16[:, 0:256]), dot(vt[128:256], p16[:, 256:512])], axis=1)


def unpair(a):
    return jnp.concatenate([a[64 * (h % 2):64 * (h % 2) + 64, 128 * h:128 * h + 128] for h in range(HEADS_HERE)], axis=0)


def fwd_step(pairs, r, i, own, K, VT, qs, m_s, l_s, acc, d_s, sb, pb, js=(0, 1, 2, 3)):
    part = slice(js[0] * BLOCK, js[-1] * BLOCK + BLOCK)
    col = lambda v: jnp.max(v, axis=0, keepdims=True)
    tot = lambda v: jnp.sum(v, axis=0, keepdims=True)
    lo_i = pairs.lo(i)
    pick = {j: lo_i > pairs.lo(r * 4 + j) for j in js}
    sa = dot(K[r, 0, part, :], qs[i, 1])
    for j in js:
        u = jnp.where(pick[j], 0, 1)
        s = dot(K[r, u, j * BLOCK:(j + 1) * BLOCK, :], qs[i, u])
        if own:
            s = jnp.where(d_s[...] <= jnp.where(i == j, 0, 2 * BLOCK), s, FAR)
        sb[j] = s
    tops = {j: col(sb[j]) for j in js}
    m_hi, m_lo = col(sa), None
    for j in js:
        m_hi = jnp.maximum(m_hi, jnp.where(pick[j], FAR, tops[j]))
        t = jnp.where(pick[j], tops[j], FAR)
        m_lo = t if m_lo is None else jnp.maximum(m_lo, t)
    if own:
        rows = pl.ds(pl.multiple_of(i * BLOCK, BLOCK), BLOCK)
        sd = jnp.where(d_s[...] <= 0, dot(K[r, 0, rows, :], qs[i, 0]), FAR)
        m_lo = jnp.maximum(m_lo, col(sd))
    else:
        old_hi, old_lo = m_s[i, 1], m_s[i, 0]
        m_hi, m_lo = jnp.maximum(m_hi, old_hi), jnp.maximum(m_lo, old_lo)
    pa = jnp.exp2(sa - m_hi)
    l_hi, l_lo = tot(pa), jnp.zeros((1, 512), f32)
    for j in js:
        p = jnp.exp2(sb[j] - jnp.where(pick[j], m_lo, m_hi))
        t = tot(p)
        l_hi = l_hi + jnp.where(pick[j], 0.0, t)
        l_lo = l_lo + jnp.where(pick[j], t, 0.0)
        low = p.astype(bf16)
        rows = slice(j * BLOCK, (j + 1) * BLOCK)
        zero = jnp.zeros_like(low)
        pb[0, rows, :] = jnp.where(pick[j], low, zero)
        pb[1, rows, :] = jnp.where(pick[j], zero, low)
    o_hi = by_pair(VT[r, 0, :, part], pa.astype(bf16)) + by_pair(VT[r, 1, :, part], pb[1, part, :])
    o_lo = by_pair(VT[r, 0, :, part], pb[0, part, :])
    if own:
        p = jnp.exp2(sd - m_lo)
        l_lo = l_lo + tot(p)
        at = pl.ds(pl.multiple_of(i * BLOCK, BLOCK), BLOCK)
        o_lo = o_lo + by_pair(VT[r, 0, :, at], p.astype(bf16))
        l_s[i, 1], l_s[i, 0] = l_hi, l_lo
        acc[i, 1], acc[i, 0] = o_hi, o_lo
    else:
        f_hi, f_lo = jnp.exp2(old_hi - m_hi), jnp.exp2(old_lo - m_lo)
        l_s[i, 1] = l_s[i, 1] * f_hi + l_hi
        l_s[i, 0] = l_s[i, 0] * f_lo + l_lo
        acc[i, 1] = acc[i, 1] * f_hi + o_hi
        acc[i, 0] = acc[i, 0] * f_lo + o_lo
    m_s[i, 1], m_s[i, 0] = m_hi, m_lo


def fwd_finish(pairs, i, m_s, l_s, acc, lse, ot, o_ref):
    first = pairs.first_lo(i)
    out = []
    for u in range(2):
        l = l_s[i, u]
        lse[i, u] = m_s[i, u] + jnp.log2(l)
        t = unpair(acc[i, u] * (1.0 / l))
        ot[i, u] = t
        out.append(t.T.astype(bf16))
    o_ref[i, 0:BLOCK, :] = jnp.where(first, out[0], out[1])
    o_ref[i, BLOCK:2 * BLOCK, :] = jnp.where(first, out[1], out[0])


def diagonal(d_s):
    d_s[...] = lax.broadcasted_iota(jnp.int32, d_s.shape, 0) - (lax.broadcasted_iota(jnp.int32, d_s.shape, 1) & (BLOCK - 1))


def fwd_local(nz, blk_ref, x_ref, wqkv_ref, bq_ref, bkv_ref, bkvt_ref, o_ref, ot, lse, K, V, KT, qn, qt, VT, qs, m_s, l_s, acc, d_s, sb, pb, wkvt):
    pairs = Pairs(nz * 8, lambda n: blk_ref[2 * n])
    diagonal(d_s)
    wkvt[...] = turned(wqkv_ref[:, 256:])
    project_queries(pairs, x_ref, wqkv_ref.at[:, 0:256], bq_ref, qn, qt, qs)
    for r in range(nz):
        project_chunk(pairs, r, x_ref, wqkv_ref.at[:, 256:768], wkvt, bkv_ref, bkvt_ref, K, V, KT, VT)
        def step(i, _):
            fwd_step(pairs, r, i, r == 0, K, VT, qs, m_s, l_s, acc, d_s, sb, pb)
            return 0
        lax.fori_loop(0, 4, step, 0)
    for i in range(4):
        fwd_finish(pairs, i, m_s, l_s, acc, lse, ot, o_ref)


def fwd_outs(nz):
    sds = jax.ShapeDtypeStruct
    kv = sds((nz, 2, 512, 256), bf16)
    return (sds((4, 256, 256), bf16), sds((4, 2, 256, 128), f32), sds((4, 2, 1, 512), f32), kv, kv, sds((nz, 2, 256, 512), bf16),
            sds((4, 2, 128, 256), bf16), sds((4, 2, 256, 128), bf16))


def fwd_scratch(nz):
    M = pltpu.VMEM
    return [M((nz, 2, 256, 512), bf16), M((4, 2, 256, 512), bf16), M((4, 2, 1, 512), f32), M((4, 2, 1, 512), f32), M((4, 2, 128, 512), f32),
            M((128, 512), jnp.int32), M((4, 128, 512), f32), M((2, 512, 512), bf16), M((512, 512), bf16)]


def attn_fwd(nz, blk, x, wqkv, bq, bkv):
    V = pl.BlockSpec(memory_space=pltpu.VMEM)
    return pl.pallas_call(
        functools.partial(fwd_local, nz), out_shape=fwd_outs(nz),
        in_specs=[pl.BlockSpec(memory_space=pltpu.SMEM)] + [V] * 5, out_specs=(V,) * 8, scratch_shapes=fwd_scratch(nz),
        compiler_params=pltpu.CompilerParams(vmem_limit_bytes=58 << 20), name="attn_fwd")(blk, x, wqkv, bq, bkv, bkv.reshape(256, 1))


def bwd_query(pairs, i, do_ref, ot, qn, qt, qs, dos, qns, dons, dl):
    for u, do in enumerate(pairs.ordered(i, do_ref[i])):
        dot_t = do.astype(f32).T
        prod = dot_t * ot[i, u]
        low = dot_t.astype(bf16)
        q, t = qn[i, u], qt[i, u]
        for hs, cs in head_slices():
            qs[i, u, hs, cs] = t[hs]
            dos[i, u, hs, cs] = low[hs]
            qns[i, u, cs, hs] = q[:, hs]
            dons[i, u, cs, hs] = do[:, hs]
            dl[i, u, :, cs] = jnp.sum(prod[hs], axis=0, keepdims=True)


def bwd_step(pairs, r, i, own, first, K, V, KT, qs, dos, qns, dons, lse, dl, dk, dv, dq, d_s, gb, js=(0, 1, 2, 3)):
    lo_i = pairs.lo(i)
    pick = {j: lo_i > pairs.lo(r * 4 + j) for j in js}
    part = slice(js[0] * BLOCK, js[-1] * BLOCK + BLOCK)

    def pieces(k, v, u, mask):
        s = dot(k, qs[i, u]) - lse[i, u]
        if mask is not None:
            s = jnp.where(d_s[...] <= mask, s, FAR)
        p = jnp.exp2(s)
        g = p * (dot(v, dos[i, u]) - dl[i, u])
        return p.astype(bf16), g.astype(bf16)

    p, g = pieces(K[r][0, part, :], V[r][0, part, :], 1, None)
    dv[0, part, :] += dot(p, dons[i, 1])
    dk[0, part, :] += dot(g, qns[i, 1])
    q_hi = by_pair(KT[r][0, :, part], g)
    for j in js:
        u = jnp.where(pick[j], 0, 1)
        rows = slice(j * BLOCK, (j + 1) * BLOCK)
        p, g = pieces(K[r][u, rows, :], V[r][u, rows, :], u, jnp.where(i == j, 0, 2 * BLOCK) if own else None)
        gv, gk = dot(p, dons[i, u]), dot(g, qns[i, u])
        dv[0, rows, :] += jnp.where(pick[j], gv, 0.0)
        dv[1, rows, :] += jnp.where(pick[j], 0.0, gv)
        dk[0, rows, :] += jnp.where(pick[j], gk, 0.0)
        dk[1, rows, :] += jnp.where(pick[j], 0.0, gk)
        zero = jnp.zeros_like(g)
        gb[0, rows, :] = jnp.where(pick[j], g, zero)
        gb[1, rows, :] = jnp.where(pick[j], zero, g)
    q_hi = q_hi + by_pair(KT[r][1, :, part], gb[1, part, :])
    q_lo = by_pair(KT[r][0, :, part], gb[0, part, :])
    if own:
        rows = pl.ds(pl.multiple_of(i * BLOCK, BLOCK), BLOCK)
        p, g = pieces(K[r][0, rows, :], V[r][0, rows, :], 0, 0)
        dv[0, rows, :] += dot(p, dons[i, 0])
        dk[0, rows, :] += dot(g, qns[i, 0])
        q_lo = q_lo + by_pair(KT[r][0, :, rows], g)
    if first:
        dq[i, 1], dq[i, 0] = q_hi, q_lo
    else:
        dq[i, 1] += q_hi
        dq[i, 0] += q_lo


def bwd_chunk_weights(pairs, r, x_ref, dk, dv, dw, db, gp, js=(0, 1, 2, 3)):
    total = jnp.zeros((1, 256), f32)
    for p in js:
        at = slice(p * BLOCK, (p + 1) * BLOCK)
        g = [jnp.concatenate([(dk[u, at, :] * (1.0 / LOG2E)).astype(bf16), dv[u, at, :].astype(bf16)], axis=1) for u in range(2)]
        total = total + jnp.sum(g[0][:, 256:].astype(f32), axis=0, keepdims=True) + jnp.sum(g[1][:, 256:].astype(f32), axis=0, keepdims=True)
        first = pairs.first_lo(r * 4 + p)
        gp[p * 256:p * 256 + BLOCK, :] = jnp.where(first, g[0], g[1])
        gp[p * 256 + BLOCK:p * 256 + 256, :] = jnp.where(first, g[1], g[0])
    db[1:2, :] += total
    n = len(js)
    dw[:, 256:768] += dot(x_ref[r, js[0]:js[0] + n].reshape(n * 256, 512), gp[js[0] * 256:(js[0] + n) * 256, :], TN)


def bwd_chunk_rows(r, last, wqkv_ref, dxq, dx, gp, js=(1, 3, 0, 2)):
    for p in js:
        rows = slice(p * 256, p * 256 + 256)
        d = dot(gp[rows, :], wqkv_ref[:, 256:768], NT)
        if last:
            d = d + dxq[p]
        dx[r, rows, :] = d.astype(bf16)


def bwd_query_out(pairs, x_ref, wqkv_ref, dq, dxq, dw, db):
    def piece(i, _):
        t = [(unpair(dq[i, u]) * 0.125).T.astype(bf16) for u in range(2)]
        first = pairs.first_lo(i)
        g = jnp.concatenate([jnp.where(first, t[0], t[1]), jnp.where(first, t[1], t[0])], axis=0)
        dxq[i] = dot(g, wqkv_ref[:, 0:256], NT)
        dw[:, 0:256] += dot(x_ref[0, i], g, TN)
        db[0:1, :] += jnp.sum(g.astype(f32), axis=0, keepdims=True)
        return 0
    lax.fori_loop(0, 4, piece, 0)


def weight_rows(dw, gq):
    for k in range(2):
        for m in range(3):
            gq[k, m * 256:m * 256 + 256, :] = dw[k * 256:k * 256 + 256, m * 256:m * 256 + 256].astype(bf16)


def bwd_local(nz, blk_ref, x_ref, wqkv_ref, K, V, KT, qn, qt, ot, lse, do_ref, dx, gq, db, qs, dos, qns, dons, dl, dk, dv, dq, d_s, gb, dxq, dw, gp):
    pairs = Pairs(nz * 8, lambda n: blk_ref[2 * n])
    kv = [[a.at[r] for r in range(nz)] for a in (K, V, KT)]
    diagonal(d_s)
    dw[...] = jnp.zeros_like(dw)
    db[...] = jnp.zeros_like(db)
    for s in (qs, dos, qns, dons):
        s[...] = jnp.zeros_like(s)
    for i in range(4):
        bwd_query(pairs, i, do_ref, ot, qn, qt, qs, dos, qns, dons, dl)
    for r in list(range(1, nz)) + [0]:
        dk[...] = jnp.zeros_like(dk)
        dv[...] = jnp.zeros_like(dv)
        def step(i, _):
            bwd_step(pairs, r, i, r == 0, r == 1, *kv, qs, dos, qns, dons, lse, dl, dk, dv, dq, d_s, gb)
            return 0
        lax.fori_loop(0, 4, step, 0)
        if r == 0:
            bwd_query_out(pairs, x_ref, wqkv_ref, dq, dxq, dw, db)
        bwd_chunk_weights(pairs, r, x_ref, dk, dv, dw, db, gp)
        bwd_chunk_rows(r, r == 0, wqkv_ref, dxq, dx, gp)
    weight_rows(dw, gq)


def bwd_scratch():
    M = pltpu.VMEM
    return [M((4, 2, 256, 512), bf16), M((4, 2, 256, 512), bf16), M((4, 2, 512, 256), bf16), M((4, 2, 512, 256), bf16), M((4, 2, 1, 512), f32),
            M((2, 512, 256), f32), M((2, 512, 256), f32), M((4, 2, 128, 512), f32), M((128, 512), jnp.int32), M((2, 512, 512), bf16),
            M((4, 256, 512), f32), M((512, 768), f32)]


def attn_bwd(nz, blk, x, wqkv, K, V, KT, qn, qt, ot, lse, do):
    S = pl.BlockSpec(memory_space=pltpu.VMEM)
    sds = jax.ShapeDtypeStruct
    return pl.pallas_call(
        functools.partial(bwd_local, nz), out_shape=(sds((nz, 1024, 512), bf16), sds((2, 768, 256), bf16), sds((8, 256), f32)),
        in_specs=[pl.BlockSpec(memory_space=pltpu.SMEM)] + [S] * 10, out_specs=(S,) * 3, scratch_shapes=bwd_scratch() + [pltpu.VMEM((1024, 512), bf16)],
        compiler_params=pltpu.CompilerParams(vmem_limit_bytes=58 << 20), name="attn_bwd")(blk, x, wqkv, K, V, KT, qn, qt, ot, lse, do)


def dense_kernel(x_ref, cot_ref, att_ref, wo_ref, wu_ref, wd_ref, sm_ref,
                 out_ref, dsm_ref, do_ref, gw_ref, gv_ref, act_s, gp_s, norm_s, dpre_s):
    ff = wu_ref.shape[1]
    chunk = 512
    x = x_ref[...].astype(f32)
    vec = lambda i: jnp.concatenate([sm_ref[0, i:i + 1, :], sm_ref[1, i:i + 1, :]], axis=1)
    b_out, g1, s1, b_down, g2, s2 = (vec(i) for i in range(2, 8))
    mean = lambda v: jnp.mean(v, axis=-1, keepdims=True)
    col = lambda v: jnp.sum(v, axis=0, keepdims=True)
    mix = x + dot(att_ref[...], wo_ref[...]) + b_out
    cen = mix - mean(mix)
    r1 = lax.rsqrt(mean(cen * cen) + norm_eps)
    n1 = cen * r1
    normed = n1 * g1 + s1
    nlow = normed.astype(bf16)
    norm_s[...] = nlow
    ffn = None
    for f in range(0, ff, chunk):
        fs = slice(f, f + chunk)
        at = 8 + f % (ff // 2) // 256
        b_up = jnp.concatenate([sm_ref[2 * f // ff, at + k:at + k + 1, :] for k in range(chunk // 256)], axis=1)
        pre = dot(nlow, wu_ref[:, fs]) + b_up
        c0 = math.sqrt(2.0 / math.pi)
        sq = pre * pre
        th = jnp.tanh(c0 * pre * (1.0 + 0.044715 * sq))
        half = 0.5 * (1.0 + th)
        act = (pre * half).astype(bf16)
        act_s[:, fs] = act
        gp_s[:, fs] = half + 0.5 * pre * (1.0 - th * th) * (c0 * (1.0 + 3 * 0.044715 * sq))
        part = dot(act, wd_ref[fs, :])
        ffn = part if ffn is None else ffn + part
    summed = ffn + b_down + normed + x
    cen = summed - mean(summed)
    r2 = lax.rsqrt(mean(cen * cen) + norm_eps)
    n2 = cen * r2
    out_ref[...] = (n2 * g2 + s2).astype(bf16)
    up = cot_ref[...].astype(f32)
    gv_ref[4:5, :] = col(up * n2)
    gv_ref[5:6, :] = col(up)
    dn = up * g2
    dsum = r2 * (dn - mean(dn) - n2 * mean(dn * n2))
    dffn = dsum.astype(bf16)
    gv_ref[3:4, :] = col(dffn.astype(f32))
    dnorm = dsum
    half_rows = wo_ref.shape[0] // 2
    half_ff = ff // 2
    def put(g, at, rows):
        gw_ref[0, at:at + rows, :] = g[:rows].astype(bf16)
        gw_ref[1, at:at + rows, :] = g[rows:].astype(bf16)
    for f in range(0, ff, chunk):
        fs = slice(f, f + chunk)
        dact = dot(dffn, wd_ref[fs, :], NT)
        dpre = (dact * gp_s[:, fs]).astype(bf16)
        gv_ref[8 + f // chunk:9 + f // chunk, :] = col(dpre.astype(f32))
        dnorm = dnorm + dot(dpre, wu_ref[:, fs], NT)
        put(dot(norm_s[...], dpre, TN), half_rows + (f // chunk) * half_rows, half_rows)
        gd = dot(act_s[:, fs], dffn, TN).astype(bf16)
        base = half_rows * (1 + ff // chunk)
        which, off = f // half_ff, f % half_ff
        gw_ref[which, base + off:base + off + chunk, :] = gd
    gv_ref[1:2, :] = col(dnorm * n1)
    gv_ref[2:3, :] = col(dnorm)
    dn = dnorm * g1
    dmix = r1 * (dn - mean(dn) - n1 * mean(dn * n1))
    dsm_ref[...] = dsum + dmix
    dbr = dmix.astype(bf16)
    gv_ref[0:1, :] = col(dbr.astype(f32))
    do_ref[...] = dot(dbr, wo_ref[...], NT).astype(bf16)
    put(dot(att_ref[...], dbr, TN), 0, half_rows)


def dense(x, cot, att, wo, wu, wd, sm):
    V = pl.BlockSpec(memory_space=pltpu.VMEM)
    tok, dim = x.shape
    ff = wu.shape[1]
    rows = (2 * dim * ff + dim * dim) // 2 // dim
    return pl.pallas_call(
        dense_kernel,
        out_shape=(jax.ShapeDtypeStruct((tok, dim), bf16), jax.ShapeDtypeStruct((tok, dim), f32),
                   jax.ShapeDtypeStruct((tok, dim), bf16), jax.ShapeDtypeStruct((2, rows, dim), bf16),
                   jax.ShapeDtypeStruct((16, dim), f32)),
        in_specs=[V] * 7, out_specs=(V,) * 5,
        scratch_shapes=[pltpu.VMEM((tok, ff), bf16), pltpu.VMEM((tok, ff), f32), pltpu.VMEM((tok, dim), bf16),
                        pltpu.VMEM((8, 128), f32)],
        compiler_params=pltpu.CompilerParams(vmem_limit_bytes=56 << 20),
        name="dense")(x, cot, att, wo, wu, wd, sm)


MESH = pl.DeviceIdType.MESH


def places(nz):
    me, wi = lax.axis_index("ctx"), lax.axis_index("wt")
    z, y, c = me // 4, lax.rem(me // 2, 2), lax.rem(me, 2)
    low = lax.rem(me, 4)
    at = lambda zz, ll: (zz * 4 + ll, wi)
    to = dict(up=at(lax.rem(z + 1, nz), low), down=at(lax.rem(z + nz - 1, nz), low), core=at(z, low + 1 - 2 * c), y=at(z, low + 2 - 4 * y),
              x=(me, 1 - wi))
    return me, wi, z, y, c, low, to


def meet(targets):
    bar = pltpu.get_barrier_semaphore()
    for t in targets:
        pl.semaphore_signal(bar, inc=1, device_id=t, device_id_type=MESH)
    pl.semaphore_wait(bar, len(targets))


class Wires:
    def __init__(self, send, recv):
        self.send, self.recv, self.n, self.live = send, recv, 0, []

    def make(self, src, dst, to):
        cp = pltpu.make_async_remote_copy(src, dst, self.send.at[self.n], self.recv.at[self.n], device_id=to, device_id_type=MESH)
        self.n += 1
        self.live.append(cp)
        return cp

    def go(self, src, dst, to):
        cp = self.make(src, dst, to)
        cp.start()
        return cp

    def drain(self):
        for cp in self.live:
            cp.wait_send()


def rows_of(start, size, mult=16):
    return pl.ds(pl.multiple_of(start, mult), size)


def gather_kernel(nz, with_w, *refs):
    if with_w:
        (x_ref, wq_ref, wk_ref, wv_ref, wo_ref, wu_ref, wd_ref, sm_ref,
         xall, wqkv, wo, wu, wd, sm, send, recv, lsem) = refs
    else:
        x_ref, xall, send, recv, lsem = refs
    me, wi, z, y, c, low, to = places(nz)
    rows = x_ref.shape[1]
    local = []

    def copy(src, dst):
        cp = pltpu.make_async_copy(src, dst, lsem.at[len(local)])
        cp.start()
        local.append(cp)

    copy(x_ref.at[y], xall.at[0, 0])
    if with_w:
        R, half = wq_ref.shape[0], wq_ref.shape[1] // 2
        for i, w in enumerate((wq_ref, wk_ref, wv_ref)):
            copy(w.at[:, rows_of(c * half, half, 128)], wqkv.at[rows_of(wi * R, R), pl.ds(i * half, half)])
        for w, full in ((wo_ref, wo), (wu_ref, wu), (wd_ref, wd)):
            n = w.shape[0]
            copy(w, full.at[rows_of(wi * n, n)])
        copy(sm_ref, sm.at[wi])
    near = [to["up"], to["down"], to["core"], to["y"]] + ([to["x"]] if with_w else [])
    meet(near)
    wires = Wires(send, recv)
    yx = wires.go(x_ref.at[1 - y], xall.at[0, 2], to["y"])
    ring = {(1, 0): wires.go(x_ref.at[y], xall.at[1, 0], to["up"])}
    core = {(0, 0): wires.go(x_ref.at[y], xall.at[0, 1], to["core"])}
    if with_w:
        xs = []
        for i, w in enumerate((wq_ref, wk_ref, wv_ref)):
            xs.append(wires.go(w.at[:, rows_of(c * half, half, 128)], wqkv.at[rows_of(wi * R, R), pl.ds(i * half, half)], to["x"]))
        xs.append(wires.go(sm_ref, sm.at[wi], to["x"]))
        big = []
        for w, full in ((wo_ref, wo), (wu_ref, wu), (wd_ref, wd)):
            n = w.shape[0]
            h = n // 2
            cp = wires.go(w.at[rows_of(c * h, h)], full.at[rows_of(wi * n + c * h, h)], to["x"])
            big.append((cp, full, rows_of((1 - wi) * n + c * h, h)))
    yx.wait_recv()
    ring[1, 1] = wires.go(xall.at[0, 2], xall.at[1, 2], to["up"])
    core[0, 1] = wires.go(xall.at[0, 2], xall.at[0, 3], to["core"])
    shared = []
    for r in range(1, nz):
        for s in range(2):
            ring[r, s].wait_recv()
            if r < nz - 1:
                ring[r + 1, s] = wires.go(xall.at[r, 2 * s], xall.at[r + 1, 2 * s], to["up"])
            core[r, s] = wires.go(xall.at[r, 2 * s], xall.at[r, 2 * s + 1], to["core"])
        if with_w and r - 1 < len(big):
            cp, full, where = big[r - 1]
            cp.wait_recv()
            shared.append(wires.go(full.at[where], full.at[where], to["core"]))
    if with_w:
        for cp, full, where in big[nz - 1:]:
            cp.wait_recv()
            shared.append(wires.go(full.at[where], full.at[where], to["core"]))
        for cp in xs + shared:
            cp.wait_recv()
    for cp in core.values():
        cp.wait_recv()
    wires.drain()
    for cp in local:
        cp.wait()


def gather_all(nz, x, weights=None, small=None):
    A = pl.BlockSpec(memory_space=pl.ANY)
    sds = jax.ShapeDtypeStruct
    rows, dim = x.shape[1:]
    outs = [sds((nz, 4, rows, dim), bf16)]
    ins = [x]
    ncopy = 1 + 2 * (nz - 1) + 2 * nz
    if weights is not None:
        wq, wk, wv, wo, wu, wd = weights
        ins += list(weights) + [small]
        outs += [sds((dim, 3 * dim // 2), bf16)] + [sds((2 * w.shape[0], w.shape[1]), bf16) for w in (wo, wu, wd)] + [sds((2,) + small.shape, bf16)]
        ncopy += 10
    return pl.pallas_call(
        functools.partial(gather_kernel, nz, weights is not None),
        out_shape=tuple(outs), in_specs=[A] * len(ins), out_specs=(A,) * len(outs),
        scratch_shapes=[pltpu.SemaphoreType.DMA((ncopy,)), pltpu.SemaphoreType.DMA((ncopy,)), pltpu.SemaphoreType.DMA((8,))],
        compiler_params=pltpu.CompilerParams(collective_id=1, has_side_effects=True, vmem_limit_bytes=16 << 20),
        name="gather_all")(*ins)


def add_into(dst, parts, rows, step=64):
    def body(i, _):
        r = rows_of(i * step, step)
        total = parts[0](r)[...].astype(f32)
        for p in parts[1:]:
            total = total + p(r)[...].astype(f32)
        d = dst(r)
        d[...] = total.astype(bf16)
        return 0
    lax.fori_loop(0, rows // step, body, 0)


def offset(ref, lead, start):
    def view(r):
        at = pl.ds(pl.multiple_of(start + r.start, 16), r.size)
        return ref.at[lead + (at,)]
    return view


def chip_pairs(nz, order_ref):
    me = lax.axis_index("ctx")
    z, y, c = me // 4, lax.rem(me // 2, 2), lax.rem(me, 2)

    def first(n):
        r, p = n // 4, n % 4
        a, b = p // 2, p % 2
        yy, cc = y + a - 2 * y * a, c + b - 2 * c * b
        return order_ref[y, 2 * (lax.rem(z - r + nz, nz) * 4 + yy * 2 + cc)]
    return Pairs(nz * 8, first)


def front_kernel(nz, order_ref, bqr, bvr, bor, g1r, s1r, bdr, g2r, s2r, bur, x_ref, wq_ref, wk_ref, wv_ref, wo_ref, wu_ref, wd_ref,
                 att, wo, wu, wd, sm, xall, wqkv, ot_o, lse_o, K_o, V_o, KT_o, qn_o, qt_o,
                 xs, ws, sms, wos, wus, wds, K, V, KT, VT, qn, qt, qs, m_s, l_s, acc, d_s, sb, pb, wkvt, bkvt, ot, lse, o_s, send, recv, lsem):
    me, wi, z, y, c, low, to = places(nz)
    to["yc"] = (z * 4 + 3 - low, wi)
    half, R = 256, wq_ref.shape[0]
    local = []

    def copy(src, dst):
        cp = pltpu.make_async_copy(src, dst, lsem.at[len(local)])
        cp.start()
        local.append(cp)
        return cp

    own_x = copy(x_ref.at[y], xs.at[0, 0])
    own_w = [copy(w.at[:, rows_of(c * half, half, 128)], ws.at[rows_of(wi * R, R), pl.ds(i * half, half)]) for i, w in enumerate((wq_ref, wk_ref, wv_ref))]
    for i, v in enumerate((bqr, bvr, bor, g1r, s1r, bdr, g2r, s2r)):
        sms[wi, i:i + 1, :] = v[...].astype(f32).reshape(1, half)
    up_b = bur[...].astype(f32).reshape(1, 1024)
    for i in range(4):
        sms[wi, 8 + i:9 + i, :] = up_b[:, i * half:(i + 1) * half]
    sms[wi, 12:16, :] = jnp.zeros((4, half), f32)
    meet([to[k] for k in ("up", "down", "core", "y", "yc", "x")])
    w = Wires(send, recv)
    yx = w.go(x_ref.at[1 - y], xs.at[0, 2], to["y"])
    ring, core = {}, {}
    ring[1, 0] = w.go(x_ref.at[y], xs.at[1, 0], to["up"])
    core[0, 0] = w.go(x_ref.at[y], xs.at[0, 1], to["core"])
    wx = []
    for i, m in enumerate((wq_ref, wk_ref, wv_ref)):
        wx.append(w.go(m.at[:, rows_of(c * half, half, 128)], ws.at[rows_of(wi * R, R), pl.ds(i * half, half)], to["x"]))
    wx.append(w.go(sms.at[wi], sms.at[wi], to["x"]))
    big = []
    for m, full in ((wo_ref, wos), (wu_ref, wus), (wd_ref, wds)):
        n = m.shape[0]
        h = n // 2
        copy(m, full.at[rows_of(wi * n, n)])
        big.append((m.at[rows_of(c * h, h)], full.at[rows_of(wi * n + c * h, h)], full, rows_of((1 - wi) * n + c * h, h)))

    pairs = chip_pairs(nz, order_ref)
    diagonal(d_s)
    yx.wait_recv()
    ring[1, 1] = w.go(xs.at[0, 2], xs.at[1, 2], to["up"])
    core[0, 1] = w.go(xs.at[0, 2], xs.at[0, 3], to["core"])

    def pump(r, s):
        ring[r, s].wait_recv()
        if r < nz - 1:
            ring[r + 1, s] = w.go(xs.at[r, 2 * s], xs.at[r + 1, 2 * s], to["up"])
        core[r, s] = w.go(xs.at[r, 2 * s], xs.at[r, 2 * s + 1], to["core"])

    shared = []

    def share(k):
        cp, full, where = sent[k]
        cp.wait_recv()
        shared.append(w.go(full.at[where], (wo, wu, wd)[k].at[where], to["core"]))

    pump(1, 0)
    for cp in own_w:
        cp.wait()
    for cp in wx:
        cp.wait_recv()
    sent = [(w.go(src, dst, to["x"]), full, where) for src, dst, full, where in big]
    copy(sms, sm)
    copy(ws, wqkv)
    wkvt[...] = turned(ws[:, 256:])
    bv = sms[c, 1:2, :]
    bkvt[...] = jnp.broadcast_to(bv, (8, half)).T[:, 0:1]
    own_x.wait()
    core[0, 0].wait_recv()
    core[0, 1].wait_recv()
    project_queries(pairs, xs, ws.at[:, 0:256], sms.at[c, 0:1], qn, qt, qs)
    copy(qn, qn_o)
    copy(qt, qt_o)

    def bring(r, s):
        if r:
            core[r, s].wait_recv()
        project_chunk(pairs, r, xs, ws.at[:, 256:768], wkvt, sms.at[c, 1:2], bkvt, K, V, KT, VT, 2 * s, 2 * s + 2)
        for a, b in ((xs, xall), (K, K_o), (V, V_o), (KT, KT_o)):
            if s:
                copy(a.at[r], b.at[r])

    def attend(r, js, last=False):
        def step(n, _):
            i = lax.rem(n + 2, 4) if last else n
            fwd_step(pairs, r, i, r == 0, K, VT, qs, m_s, l_s, acc, d_s, sb, pb, js)
            if last:
                fwd_finish(pairs, i, m_s, l_s, acc, lse, ot, o_s)
                for p in outs:
                    pl.when(i == p)(outs[p].start)
            return 0
        lax.fori_loop(0, 4, step, 0)

    def half_chunk(r, s, last=False):
        bring(r, s)
        attend(r, (2 * s, 2 * s + 1), last)

    cols = pl.ds(pl.multiple_of(c * half, half), half)
    outs = {p: w.make(o_s.at[p], att.at[y, :, cols], to[k]) for p, k in ((2, "y"), (3, "yc"), (1, "core"))}
    bring(0, 0)
    bring(0, 1)
    pump(1, 1)
    attend(0, (0, 1, 2, 3))
    for k, (a, b) in enumerate(((wos, wo), (wus, wu), (wds, wd))):
        local[4 + k].wait()
        n = a.shape[0] // 2
        copy(a.at[rows_of(wi * n, n)], b.at[rows_of(wi * n, n)])
    pump(2, 0)
    for r in range(1, nz - 1):
        half_chunk(r, 0)
        if r > 1:
            pump(r + 1, 0)
        half_chunk(r, 1)
        if r < nz - 2:
            pump(r + 1, 1)
    half_chunk(nz - 1, 0)
    pump(nz - 1, 1)
    half_chunk(nz - 1, 1, True)
    copy(o_s.at[0], att.at[y, :, cols])
    copy(ot, ot_o)
    copy(lse, lse_o)
    for k, (a, b) in enumerate(((wos, wo), (wus, wu), (wds, wd))):
        share(k)
        copy(a.at[sent[k][2]], b.at[sent[k][2]])
    for cp in shared:
        cp.wait_recv()
    for cp in outs.values():
        cp.wait_recv()
    w.drain()
    for cp in local[7:]:
        cp.wait()


def front(nz, order, vectors, x, weights):
    A = pl.BlockSpec(memory_space=pltpu.HBM)
    V = pl.BlockSpec(memory_space=pltpu.VMEM)
    sds = jax.ShapeDtypeStruct
    M = pltpu.VMEM
    rows, dim = x.shape[1:]
    wq, wk, wv, wo, wu, wd = weights
    outs = [sds((2, rows, dim), bf16)] + [sds((2 * w.shape[0], w.shape[1]), bf16) for w in (wo, wu, wd)]
    outs += [sds((2, 16, 256), f32), sds((nz, 4, rows, dim), bf16), sds((dim, 768), bf16)] + list(fwd_outs(nz)[1:])
    scratch = [M((nz, 4, rows, dim), bf16), M((dim, 768), bf16), M((2, 16, 256), f32)] + [M(o.shape, bf16) for o in outs[1:4]]
    scratch += [M((nz, 2, 512, 256), bf16)] * 2 + [M((nz, 2, 256, 512), bf16)] * 2 + [M((4, 2, 128, 256), bf16), M((4, 2, 256, 128), bf16)]
    scratch += fwd_scratch(nz)[1:] + [M((256, 1), f32), M((4, 2, 256, 128), f32), M((4, 2, 1, 512), f32), M((4, 256, 256), bf16)]
    scratch += [pltpu.SemaphoreType.DMA((40,)), pltpu.SemaphoreType.DMA((40,)), pltpu.SemaphoreType.DMA((40,))]
    return pl.pallas_call(
        functools.partial(front_kernel, nz), out_shape=tuple(outs),
        in_specs=[pl.BlockSpec(memory_space=pltpu.SMEM)] + [V] * 9 + [A] * 7, out_specs=(A,) * len(outs), scratch_shapes=scratch,
        compiler_params=pltpu.CompilerParams(collective_id=1, has_side_effects=True, vmem_limit_bytes=58 << 20), name="front")(
            order, *vectors, x, *weights)


def back_kernel(nz, order_ref, gv_ref, do_ref, x_hbm, w_hbm, K_h, V_h, KT_h, qn_h, qt_h, ot_h, lse_h, gw_ref,
                dxo, go, gqo, gvo,
                xs, wqkv, K, V, KT, qn, qt, ot, lse, do, qs, dos, qns, dons, dl, dk, dv, dq, d_s, gb, dxq, dw, dx, gp, gq, db, outdx,
                dx_core, dx_in, cr, cs, xr, xs_, yr, ys_, za, zs, zb, xrq, xsq, yrq, ysq, zrq, gsum, gqsum, gvs, gvr, send, recv, lsem):
    me, wi, z, y, c, low, to = places(nz)
    to["yc"] = (z * 4 + 3 - low, wi)
    zto = [(lax.rem(z + d, nz) * 4 + low, wi) for d in range(1, nz)]
    half, hrow = 256, 256
    w = Wires(send, recv)
    local = []

    def copy(src, dst):
        cp = pltpu.make_async_copy(src, dst, lsem.at[len(local)])
        cp.start()
        local.append(cp)
        return cp

    cols = pl.ds(pl.multiple_of(c * half, half), half)
    other = pl.ds(pl.multiple_of((1 - c) * half, half), half)
    meet([to[k] for k in ("core", "y", "yc", "x")] + zto)
    dos_in = [w.go(do_ref.at[1 - y, :, cols], do.at[2], to["y"]), w.go(do_ref.at[1 - y, :, other], do.at[3], to["yc"]),
              w.go(do_ref.at[y, :, other], do.at[1], to["core"])]
    got = {}
    for s in range(3):
        got["c", s] = w.go(gw_ref.at[:, rows_of(s * 768 + (1 - c) * 384, 384)], cr.at[s], to["core"])
    mine_gw = [copy(gw_ref.at[:, rows_of(s * 768 + c * 384, 384)], cs.at[s]) for s in range(3)]
    first_in = [copy(do_ref.at[y, :, cols], do.at[0])] + [copy(a, b) for a, b in ((qn_h, qn), (qt_h, qt), (ot_h, ot), (lse_h, lse))]
    kv_in = {}
    for r in list(range(1, nz)) + [0]:
        kv_in[r] = [copy(a.at[r], b[r]) for a, b in ((K_h, K), (V_h, V), (KT_h, KT))]
    for r in kv_in:
        kv_in[r].append(copy(x_hbm.at[r], xs.at[r]))
    w_in = copy(w_hbm, wqkv)

    n = range(5)
    wide = [384, 192, 48]
    zp = (z + 1 - 2 * lax.rem(z, 2)) * 4 + low, wi
    zq = (z + 2 - 4 * (z // 2)) * 4 + low, wi
    odd, far = lax.rem(z, 2), z // 2
    X_in = [xr.at[s] for s in range(3)] + [xrq.at[s] for s in range(2)]
    X_sum = [xs_.at[s] for s in range(3)] + [xsq.at[s] for s in range(2)]
    Y_in = [yr.at[s] for s in range(3)] + [yrq.at[s] for s in range(2)]
    Y_sum = [ys_.at[s] for s in range(3)] + [ysq.at[s] for s in range(2)]
    Z_in = [zrq.at[s] for s in range(2)]
    out = [gsum.at[s] for s in range(3)] + [gqsum.at[s] for s in range(2)]
    done = [go.at[s] for s in range(3)] + [gqo.at[s] for s in range(2)]
    start_c, start_y = c * 384, c * 384 + y * 192
    at_c, at_y = rows_of(start_c, 384), rows_of(start_y, 192)
    pos = odd * 2 + far
    start_p, start_h = start_y + pos * 48, start_y + odd * 96
    at_p, at_h = rows_of(start_p, 48), rows_of(start_h, 96)
    start_z = start_y + z * 48
    at_z = rows_of(start_z, 48)
    theirs = rows_of((1 - y) * 192, 192)
    for s in n:
        got["x", s] = w.make(cs.at[s, 1 - wi] if s < 3 else gq.at[1 - wi, pl.ds((s - 3) * 384, 384)], X_in[s], to["x"])
        got["y", s] = w.make(X_sum[s].at[theirs], Y_in[s], to["y"])
        got["ys", s] = w.make(out[s].at[at_y], out[s].at[at_y], to["y"])
        got["cs", s] = w.make(out[s].at[at_c], done[s].at[at_c], to["core"])
        if s < 3:
            got["za", s] = w.make(ys_.at[s, rows_of((1 - odd) * 96, 96)], za.at[s], zp)
            got["zb", s] = w.make(zs.at[s, rows_of((1 - far) * 48, 48)], zb.at[s], zq)
            got["zc", s] = w.make(out[s].at[at_p], out[s].at[at_p], zq)
            got["zd", s] = w.make(out[s].at[at_h], out[s].at[at_h], zp)
        else:
            for d in range(1, nz):
                got["z", s, d] = w.make(Y_sum[s].at[rows_of(lax.rem(z + d, nz) * 48, 48)], Z_in[s - 3].at[d - 1], zto[d - 1])
                got["zs", s, d] = w.make(out[s].at[at_z], out[s].at[at_z], zto[d - 1])

    def x_send(s):
        if s < 3:
            mine_gw[s].wait()
            got["c", s].wait_recv()
            add_into(offset(cs, (s, 1 - wi), 0), [offset(cs, (s, 1 - wi), 0), offset(cr, (s, 1 - wi), 0)], 384, 128)
            got["x", s].start()
            add_into(offset(cs, (s, wi), 0), [offset(cs, (s, wi), 0), offset(cr, (s, wi), 0)], 384, 128)
        else:
            got["x", s].start()

    def y_send(s):
        got["x", s].wait_recv()
        mine = lambda lo: offset(cs, (s, wi), lo) if s < 3 else offset(gq, (wi,), (s - 3) * 384 + lo)
        for half_y in (1 - y, y):
            lo = half_y * 192
            add_into(offset(X_sum[s], (), lo), [mine(lo), offset(X_in[s], (), lo)], 192, 96)
            if half_y is not y:
                got["y", s].start()

    def z_a(s):
        got["y", s].wait_recv()
        add_into(offset(ys_, (s,), 0), [offset(xs_, (s,), y * 192), offset(yr, (s,), 0)], 192, 96)
        got["za", s].start()

    def z_b(s):
        got["za", s].wait_recv()
        add_into(offset(zs, (s,), 0), [offset(ys_, (s,), odd * 96), offset(za, (s,), 0)], 96, 96)
        got["zb", s].start()

    def z_c(s):
        got["zb", s].wait_recv()
        add_into(offset(out[s], (), start_p), [offset(zs, (s,), far * 48), offset(zb, (s,), 0)], 48, 48)
        got["zc", s].start()

    def z_d(s):
        got["zc", s].wait_recv()
        got["zd", s].start()

    def z_send(s):
        got["y", s].wait_recv()
        add_into(offset(Y_sum[s], (), 0), [offset(X_sum[s], (), y * 192), offset(Y_in[s], (), 0)], 192, 192)
        for d in range(1, nz):
            got["z", s, d].start()

    def z_share(s):
        for d in range(1, nz):
            got["z", s, d].wait_recv()
        add_into(offset(out[s], (), start_z), [offset(Y_sum[s], (), z * 48)] + [offset(Z_in[s - 3], (d,), 0) for d in range(nz - 1)], 48, 48)
        for d in range(1, nz):
            got["zs", s, d].start()

    def y_share(s):
        for k in (["zd"] if s < 3 else [("zs", d) for d in range(1, nz)]):
            got[(k, s) if s < 3 else (k[0], s, k[1])].wait_recv()
        got["ys", s].start()

    def c_share(s):
        got["ys", s].wait_recv()
        got["cs", s].start()
        copy(out[s].at[at_c], done[s].at[at_c])

    for r in range(nz):
        for h in range(2):
            at = pl.ds(h * 512, hrow)
            got["d", r, h] = w.make(dx.at[r, pl.ds(h * 512 + hrow, hrow)], dx_core.at[r, h], to["core"])
            if r:
                got["r", (r + 1) % nz, h] = w.make(dx.at[r, at], dx_in.at[(r + 1) % nz, h], to["up"])
    got["dy"] = w.make(dx.at[0, pl.ds(512, hrow)], dxo.at[1], to["y"])

    def give(r, h):
        got["d", r, h].start()

    def fold(r, h):
        got["d", r, h].wait_recv()
        add_into(offset(dx, (r,), h * 512), [offset(dx, (r,), h * 512), offset(dx_core, (r, h), 0)], hrow, 128)
        if r == 1:
            got["r", 2, h].start()

    def hop(r, h):
        got["r", r, h].wait_recv()
        dst = offset(dx, (r,), h * 512) if r or h else offset(outdx, (0,), 0)
        add_into(dst, [offset(dx, (r,), h * 512), offset(dx_in, (r, h), 0)], hrow, 128)
        if r:
            got["r", (r + 1) % nz, h].start()
        elif h:
            got["dy"].start()
        else:
            copy(outdx.at[0], dxo.at[0])

    vec_to = [to["core"], to["y"], to["x"]] + [(zz * 4 + low, wi) for zz in (z + 1 - 2 * lax.rem(z, 2), z + 2 - 4 * (z // 2))]

    def vec_send(k):
        if k == 0:
            gvs[0] = jnp.zeros_like(gvs[0])
            gvs[0, 0:16, :] = gv_ref[...]
            zero = jnp.zeros((1, half), f32)
            for i in range(2):
                v = db[i:i + 1, :]
                gvs[0, 16 + i:17 + i, :] = jnp.concatenate([jnp.where(c == 0, v, zero), jnp.where(c == 0, zero, v)], axis=1)
        else:
            got["v", k - 1].wait_recv()
            gvs[k] = gvs[k - 1] + gvr[k - 1]
        if k < 5:
            got["v", k].start()
        else:
            gvo[...] = gvs[5]

    pairs = chip_pairs(nz, order_ref)
    for k in range(5):
        got["v", k] = w.make(gvs.at[k], gvr.at[k], vec_to[k])
    diagonal(d_s)
    dw[...] = jnp.zeros_like(dw)
    db[...] = jnp.zeros_like(db)
    for s in (qs, dos, qns, dons):
        s[...] = jnp.zeros_like(s)
    x_send(0)
    for cp in first_in:
        cp.wait()
    dos_in[2].wait_recv()
    hooks = plan(dict(x=x_send, y=y_send, za=z_a, zb=z_b, zc=z_c, zd=z_d, ys=y_share, cs=c_share, fold=fold, hop=hop, z=z_send, zs=z_share, vec=vec_send))
    hook = lambda *k: hooks[k]() if k in hooks else None
    hook("pre")
    for r in list(range(1, nz)) + [0]:
        dk[...] = jnp.zeros_like(dk)
        dv[...] = jnp.zeros_like(dv)
        for cp in kv_in[r][:3]:
            cp.wait()
        for n, js in enumerate(((2, 3), (0, 1)) if r == 1 else ((0, 1, 2, 3),)):
            def step(i, _):
                if r == 1 and n == 0:
                    for k in range(2):
                        pl.when(i == 2)(dos_in[k].wait_recv)
                    bwd_query(pairs, i, do, ot, qn, qt, qs, dos, qns, dons, dl)
                bwd_step(pairs, r, i, r == 0, r == 1 and n == 0, K, V, KT, qs, dos, qns, dons, lse, dl, dk, dv, dq, d_s, gb, js)
                for k in range(4):
                    if (r, n, k) in hooks:
                        pl.when(i == k)(hooks[r, n, k])
                return 0
            lax.fori_loop(0, 4, step, 0)
            if r == 1 and n == 0:
                for q in kv_in:
                    kv_in[q][3].wait()
                w_in.wait()
            if r == 0:
                bwd_query_out(pairs, xs, wqkv, dq, dxq, dw, db)
                hook(0, 0, "q")
            bwd_chunk_weights(pairs, r, xs, dk, dv, dw, db, gp, js)
            if r == 0:
                weight_rows(dw, gq)
                x_send(3)
            hook(r, n, "w")
            bwd_chunk_rows(r, r == 0, wqkv, dxq, dx, gp, [p for p in (3, 1, 2, 0) if p in js])
            for h in (1, 0):
                if 2 * h in js:
                    give(r, h)
            hook(r, n, "r")
    hook("tail")
    for s in range(5):
        got["cs", s].wait_recv()
    got["dy"].wait_recv()
    w.drain()
    for cp in local[-6:]:
        cp.wait()


PLAN = {
    (1, 0, "r"): (("x", 2),),
    (1, 1, 1): (("fold", 1, 1),),
    (1, 1, 2): (("y", 0),),
    (2, 0, 2): (("x", 1), ("fold", 1, 0), ("za", 0),),
    (2, 0, "r"): (("y", 2),),
    (3, 0, 2): (("zb", 0),),
    (3, 0, 3): (("za", 2), ("fold", 2, 0), ("y", 1),),
    (3, 0, "r"): (("zc", 0), ("hop", 2, 0),),
    (0, 0, 2): (("za", 1),),
    (0, 0, "q"): (("zb", 2), ("zd", 0), ("fold", 2, 1),),
    (0, 0, "w"): (("hop", 2, 1), ("zc", 2), ("vec", 0), ("zb", 1), ("fold", 3, 1), ("fold", 3, 0), ("y", 3), ("x", 4), ("zd", 2), ("zc", 1), ("ys",
        0), ("z", 3), ("y", 4),),
    (0, 0, "r"): (("zd", 1), ("fold", 0, 1), ("hop", 3, 1), ("zs", 3), ("ys", 2), ("z", 4),),
    "tail": (("fold", 0, 0), ("vec", 1), ("ys", 1), ("ys", 3), ("vec", 2), ("cs", 0), ("zs", 4), ("vec", 3), ("hop", 3, 0), ("cs", 2), ("hop", 0, 1),
        ("cs", 1), ("ys", 4), ("cs", 3), ("vec", 4), ("cs", 4), ("vec", 5), ("hop", 0, 0),),
}


def plan(ops):
    def run(items):
        def go():
            for name, *a in items:
                ops[name](*a)
        return go
    return {k if isinstance(k, tuple) else (k,): run(v) for k, v in PLAN.items()}


def back(nz, order, gv, do, x_all, wqkv, k, v, kt, qn, qt, ot, lse, gw):
    A = pl.BlockSpec(memory_space=pltpu.HBM)
    V = pl.BlockSpec(memory_space=pltpu.VMEM)
    sds = jax.ShapeDtypeStruct
    B = lambda *s: pltpu.VMEM(s, bf16)
    F = lambda *s: pltpu.VMEM(s, f32)
    ins = (x_all, wqkv, k, v, kt, qn, qt, ot, lse)
    scratch = [[pltpu.VMEM(a.shape[1:], a.dtype)] * nz if any(a is b for b in (k, v, kt)) else pltpu.VMEM(a.shape, a.dtype) for a in ins] + [B(4, 256, 256)] + bwd_scratch()
    scratch += [B(nz, 1024, 512), B(1024, 512), B(2, 768, 256), F(8, 256), B(1, 256, 512)]
    scratch += [B(nz, 2, 256, 512), B(nz, 2, 256, 512), B(3, 2, 384, 512), B(3, 2, 384, 512), B(3, 384, 512), B(3, 384, 512), B(3, 192, 512), B(3, 192, 512),
                B(3, 96, 512), B(3, 96, 512), B(3, 48, 512), B(2, 384, 256), B(2, 384, 256), B(2, 192, 256), B(2, 192, 256), B(2, nz - 1, 48, 256),
                B(3, 768, 512), B(2, 768, 256),
                F(6, 24, 512), F(5, 24, 512)]
    scratch += [pltpu.SemaphoreType.DMA((80,)), pltpu.SemaphoreType.DMA((80,)), pltpu.SemaphoreType.DMA((40,))]
    return pl.pallas_call(
        functools.partial(back_kernel, nz),
        out_shape=(sds((2, 256, 512), bf16), sds((3, 768, 512), bf16), sds((2, 768, 256), bf16), sds((24, 512), f32)),
        in_specs=[pl.BlockSpec(memory_space=pltpu.SMEM), V] + [A] * 11, out_specs=(A, A, A, V), scratch_shapes=scratch,
        compiler_params=pltpu.CompilerParams(collective_id=2, has_side_effects=True, vmem_limit_bytes=62 << 20), name="back")(order, gv, do, *ins, gw)


def last_kernel(nu, go_ref, gq_ref, gv_ref, dx_ref, dsm_ref, gin, dwq, dbq, dwk, dwv, dbv, dwo, dbo, dg1, ds1, dwu, dbu, dwd, dbd, dg2, ds2):
    wi, y = lax.axis_index("wt"), lax.rem(lax.axis_index("ctx") // 2, 2)
    for s in range(2):
        seq = jnp.where(y == 0, s, 1 - s)
        gin[s] = (dsm_ref[s] + dx_ref[seq].astype(f32)).astype(bf16)
    hr = dwq.shape[0]
    for k in range(2):
        at, low = slice(k * 256, k * 256 + 256), k * 384
        dwq[:, at] = gq_ref[0, low:low + 256, :].astype(f32)
        dwk[0:128, at] = gq_ref[0, low + 256:low + 384, :].astype(f32)
        dwk[128:256, at] = gq_ref[1, low:low + 128, :].astype(f32)
        dwv[:, at] = gq_ref[1, low + 128:low + 384, :].astype(f32)
    dwo[...] = go_ref[0:hr, :].astype(f32)
    for k in range(nu):
        dwu[:, k * 512:k * 512 + 512] = go_ref[hr + k * hr:2 * hr + k * hr, :].astype(f32)
    dwd[...] = go_ref[hr + nu * hr:, :].astype(f32)

    def row(i):
        v = gv_ref[i:i + 1, :]
        return jnp.where(wi == 0, v[:, :256], v[:, 256:])

    for o, i in ((dbo, 0), (dg1, 1), (ds1, 2), (dbd, 3), (dg2, 4), (ds2, 5), (dbq, 16), (dbv, 17)):
        o[...] = row(i).reshape(256)
    h = nu // 2
    a, b = [jnp.concatenate([gv_ref[8 + k * h + i:9 + k * h + i, :] for i in range(h)], axis=1) for k in range(2)]
    dbu[...] = jnp.where(wi == 0, a, b).reshape(a.shape[1])


def last(nu, go, gqo, gv, dxo, dsm):
    V = pl.BlockSpec(memory_space=pltpu.VMEM)
    f = lambda *s: jax.ShapeDtypeStruct(s, f32)
    ff = nu * 512
    outs = (jax.ShapeDtypeStruct((2, 256, 512), bf16), f(256, 512), f(256), f(256, 512), f(256, 512), f(256), f(256, 512), f(256), f(256), f(256),
            f(256, ff), f(ff // 2), f(ff // 2, 512), f(256), f(256), f(256))
    return pl.pallas_call(functools.partial(last_kernel, nu), out_shape=outs, in_specs=[V] * 5, out_specs=(V,) * 16,
                          compiler_params=pltpu.CompilerParams(vmem_limit_bytes=56 << 20), name="last")(go, gqo, gv, dxo, dsm)


def body(block_in, block_order, w_query, b_query, w_key, w_value, b_value, w_out, b_out, gain_one, shift_one,
         w_up, b_up, w_down, b_down, gain_two, shift_two, cotangent, *, nc, nw):
    seqs, rows, dim = block_in.shape
    nz = nc // 4
    hb = rows // BLOCK
    half = dim // 2
    me = lax.axis_index("ctx")
    yy = (me // 2) % 2
    cc = me % 2
    zz = me // 4
    xor = lambda v: [(i, i ^ v) for i in range(nc)]
    ring = [(i, ((i // 4 + 1) % nz) * 4 + i % 4) for i in range(nc)]
    perm = lambda v, p: lax.ppermute(v, "ctx", p)
    gather = lambda v: lax.all_gather(v, "wt", axis=0, tiled=True)
    pick = lambda v, i: lax.dynamic_index_in_dim(v, i, 0, keepdims=False)

    ours = nw == 2 and nz == 4
    small = (b_query, b_value, b_out, gain_one, shift_one, b_down, gain_two, shift_two, b_up)
    by_seq = lambda a, b: jnp.where(yy == 0, jnp.concatenate([a, b], 0), jnp.concatenate([b, a], 0))
    r_ids = (zz - jnp.arange(nz, dtype=jnp.int32)) % nz
    quad = (me % 4) ^ jnp.array([0, 1, 2, 3], jnp.int32)
    order_row = pick(block_order, yy)
    slots = (r_ids[:, None, None] * 4 + quad[None, :, None]) * hb + jnp.arange(hb, dtype=jnp.int32)
    blk = order_row[slots.reshape(-1)]

    if ours:
        att, wo, wu, wd, sm, x_all, wqkv, ot, lse, k, v, kt, qn, qt = front(nz, block_order, small, block_in, (w_query, w_key, w_value, w_out, w_up, w_down))
        att = att.reshape(-1, dim)
    else:
        cols = lambda w: lax.dynamic_slice_in_dim(w, cc * half, half, 1)
        wqkv = gather(jnp.concatenate([cols(w_query), cols(w_key), cols(w_value)], axis=1))
        small = lax.all_gather(jnp.concatenate(small), "wt", axis=0)
        vec8 = jnp.transpose(small[:, :8 * dim // nw].reshape(nw, 8, dim // nw), (1, 0, 2)).reshape(8, 2, half)
        upb = small[:, 8 * dim // nw:].reshape(2, 4, half)
        sm = jnp.pad(jnp.concatenate([jnp.transpose(vec8, (1, 0, 2)), upb], axis=1).astype(f32), ((0, 0), (0, 4), (0, 0)))
        wo, wu, wd = gather(w_out), gather(w_up), gather(w_down)
        x_all = gather_all(nz, block_in)[0]
        o, ot, lse, k, v, kt, qn, qt = attn_fwd(nz, blk, x_all, wqkv, pick(sm, cc)[0:1], pick(sm, cc)[1:2])
        o_self, o_c, o_y, o_yc = o[0], perm(o[1], xor(1)), perm(o[2], xor(2)), perm(o[3], xor(3))
        mine, other = by_seq(o_self, o_y), by_seq(o_c, o_yc)
        att = jnp.where(cc == 0, jnp.concatenate([mine, other], 1), jnp.concatenate([other, mine], 1))

    out, dsm, d_o, gw, gv = dense(block_in.reshape(-1, dim), cotangent.reshape(-1, dim), att, wo, wu, wd, sm)

    if ours:
        dxo, go, gqo, gvec = back(nz, block_order, gv, d_o.reshape(seqs, rows, dim), x_all, wqkv, k, v, kt, qn, qt, ot, lse, gw)
        return (out.reshape(seqs, rows, dim),) + tuple(last(w_up.shape[1] // dim, go.reshape(-1, dim), gqo, gvec, dxo, dsm.reshape(seqs, rows, dim)))
    d_o = d_o.reshape(seqs, rows, dim)
    d_own, d_oth = pick(d_o, yy), pick(d_o, 1 - yy)
    fh = lambda v, c: lax.dynamic_slice_in_dim(v, c * half, half, 1)
    do_all = jnp.concatenate([fh(d_own, cc), perm(fh(d_own, 1 - cc), xor(1)), perm(fh(d_oth, cc), xor(2)), perm(fh(d_oth, 1 - cc), xor(3))], axis=0)
    dx, gq, gb = attn_bwd(nz, blk, x_all, wqkv, k, v, kt, qn, qt, ot, lse, do_all.reshape(4, rows, half))
    gvec = jnp.zeros((24, dim), f32).at[:16].set(gv)
    gvec = lax.dynamic_update_slice(gvec, gb[0:1], (16, cc * half))
    gvec = lax.dynamic_update_slice(gvec, gb[1:2], (17, cc * half))
    wi = lax.axis_index("wt")
    ff, hr = w_up.shape[1], dim // 2
    nu = ff // dim
    dx = jnp.transpose(dx.reshape(nz, 2, 2, rows, dim), (0, 2, 1, 3, 4)).reshape(nz, 2, 2 * rows, dim)
    part = lambda r: dx[r, 0].astype(f32) + perm(dx[r, 1], xor(1)).astype(f32)
    acc = None
    for r in list(range(1, nz)) + [0]:
        acc = part(r) if acc is None else perm(acc.astype(bf16), ring).astype(f32) + part(r)
    from_y = perm(acc[rows:].astype(bf16), xor(2)).astype(f32)
    dkv_sum = by_seq(acc[:rows], from_y)
    gvec = lax.psum(gvec, ("ctx", "wt"))
    g_out = gw[:, :hr].reshape(dim, dim)
    g_up = gw[:, hr:hr + nu * hr].reshape(2, nu, hr, dim).transpose(0, 2, 1, 3).reshape(dim, ff)
    g_down = gw[:, hr + nu * hr:].reshape(ff, dim)
    gq3 = gq.reshape(2, 3, hr, half).transpose(1, 0, 2, 3).reshape(3, dim, half)
    g_qkv = lax.dynamic_update_slice(jnp.zeros((3, dim, dim), bf16), gq3, (0, 0, cc * half))
    total = lambda g: lax.psum(lax.psum_scatter(g, "wt", scatter_dimension=0, tiled=True), "ctx").astype(f32)
    t_out, t_up, t_down = total(g_out), total(g_up), total(g_down)
    t_qkv = [total(g_qkv[i]) for i in range(3)]
    grad_in = (dsm + dkv_sum).astype(bf16).reshape(seqs, rows, dim)

    def share(vv):
        n = vv.size // nw
        return lax.dynamic_slice_in_dim(vv.reshape(-1), wi * n, n, 0)
    return (out.reshape(seqs, rows, dim), grad_in, t_qkv[0], share(gvec[16]), t_qkv[1], t_qkv[2], share(gvec[17]), t_out, share(gvec[0]),
            share(gvec[1]), share(gvec[2]), t_up, share(gvec[8:8 + nu]), t_down, share(gvec[3]), share(gvec[4]), share(gvec[5]))


def solution(mesh):
    seq, mat, vec = P("wt", "ctx", None), P("wt", None), P("wt")
    ins = (seq, mat, mat, vec, mat, mat, vec, mat, vec, vec, vec, mat, vec, mat, vec, vec, vec, seq)
    outs = (seq, seq, mat, vec, mat, mat, vec, mat, vec, vec, vec, mat, vec, mat, vec, vec, vec)
    run = functools.partial(body, nc=mesh.shape["ctx"], nw=mesh.shape["wt"])
    return jax.shard_map(run, mesh=mesh, in_specs=ins, out_specs=outs, check_vma=False)
```

```python
import functools
import math

import jax
import jax.numpy as jnp
from jax import lax
from jax.experimental import pallas as pl
from jax.experimental.pallas import tpu as pltpu
from jax.sharding import PartitionSpec as P

norm_eps = 1e-05

BLOCK = 128
HEADS_HERE = 4
LOG2E = 1.4426950408889634
FAR = -1e30
bf16, f32 = jnp.bfloat16, jnp.float32
NT = (((1,), (1,)), ((), ()))
TN = (((0,), (0,)), ((), ()))


def dot(a, b, dims=(((1,), (0,)), ((), ()))):
    return lax.dot_general(a, b, dims, preferred_element_type=f32)


def turned(v):
    return v.astype(f32).T.astype(bf16)


def head_slices():
    return [(slice(64 * h, 64 * h + 64), slice(128 * h, 128 * h + 128)) for h in range(HEADS_HERE)]


class Pairs:
    def __init__(self, nb, first):
        self.nb, self.first = nb, first

    def first_lo(self, n):
        return self.first(n) < self.nb // 2

    def lo(self, n):
        b = self.first(n)
        return jnp.where(b < self.nb // 2, b, self.nb - 1 - b)

    def ordered(self, n, v):
        a, b = v[:BLOCK], v[BLOCK:]
        first = self.first_lo(n)
        return jnp.where(first, a, b), jnp.where(first, b, a)


def project_chunk(pairs, r, x_ref, wkv_ref, wkvt_ref, bkv_ref, bkvt_ref, K, V, KT, VT, start=0, stop=4):
    def piece(p, _):
        x = jnp.concatenate(pairs.ordered(r * 4 + p, x_ref[r, p]), axis=0)
        kv = dot(x, wkv_ref[...])
        k, v = kv[:, :256].astype(bf16), (kv[:, 256:] + bkv_ref[...]).astype(bf16)
        kvt = dot(wkvt_ref[...], x, NT)
        kt, vt = kvt[:256].astype(bf16), (kvt[256:] + bkvt_ref[...]).astype(bf16)
        at = pl.ds(pl.multiple_of(p * BLOCK, BLOCK), BLOCK)
        for u in range(2):
            rows = slice(u * BLOCK, (u + 1) * BLOCK)
            K[r, u, at, :] = k[rows]
            V[r, u, at, :] = v[rows]
            KT[r, u, :, at] = kt[:, rows]
            VT[r, u, :, at] = vt[:, rows]
        return 0
    lax.fori_loop(start, stop, piece, 0)


def project_queries(pairs, x_ref, wq_ref, bq_ref, qn, qt, qs):
    qs[...] = jnp.zeros_like(qs)

    def piece(p, _):
        x = jnp.concatenate(pairs.ordered(p, x_ref[0, p]), axis=0)
        q = (dot(x, wq_ref[...]) + bq_ref[...]) * (LOG2E / 8.0)
        for u in range(2):
            mine = q[u * BLOCK:(u + 1) * BLOCK]
            qn[p, u] = mine.astype(bf16)
            t = mine.T.astype(bf16)
            qt[p, u] = t
            for hs, cs in head_slices():
                qs[p, u, hs, cs] = t[hs]
        return 0
    lax.fori_loop(0, 4, piece, 0)


def by_pair(vt, p16):
    return jnp.concatenate([dot(vt[0:128], p16[:, 0:256]), dot(vt[128:256], p16[:, 256:512])], axis=1)


def unpair(a):
    return jnp.concatenate([a[64 * (h % 2):64 * (h % 2) + 64, 128 * h:128 * h + 128] for h in range(HEADS_HERE)], axis=0)


def fwd_step(pairs, r, i, own, K, VT, qs, m_s, l_s, acc, d_s, sb, pb, js=(0, 1, 2, 3)):
    part = slice(js[0] * BLOCK, js[-1] * BLOCK + BLOCK)
    col = lambda v: jnp.max(v, axis=0, keepdims=True)
    tot = lambda v: jnp.sum(v, axis=0, keepdims=True)
    lo_i = pairs.lo(i)
    pick = {j: lo_i > pairs.lo(r * 4 + j) for j in js}
    sa = dot(K[r, 0, part, :], qs[i, 1])
    for j in js:
        u = jnp.where(pick[j], 0, 1)
        s = dot(K[r, u, j * BLOCK:(j + 1) * BLOCK, :], qs[i, u])
        if own:
            s = jnp.where(d_s[...] <= jnp.where(i == j, 0, 2 * BLOCK), s, FAR)
        sb[j] = s
    tops = {j: col(sb[j]) for j in js}
    m_hi, m_lo = col(sa), None
    for j in js:
        m_hi = jnp.maximum(m_hi, jnp.where(pick[j], FAR, tops[j]))
        t = jnp.where(pick[j], tops[j], FAR)
        m_lo = t if m_lo is None else jnp.maximum(m_lo, t)
    if own:
        rows = pl.ds(pl.multiple_of(i * BLOCK, BLOCK), BLOCK)
        sd = jnp.where(d_s[...] <= 0, dot(K[r, 0, rows, :], qs[i, 0]), FAR)
        m_lo = jnp.maximum(m_lo, col(sd))
    else:
        old_hi, old_lo = m_s[i, 1], m_s[i, 0]
        m_hi, m_lo = jnp.maximum(m_hi, old_hi), jnp.maximum(m_lo, old_lo)
    pa = jnp.exp2(sa - m_hi)
    l_hi, l_lo = tot(pa), jnp.zeros((1, 512), f32)
    for j in js:
        p = jnp.exp2(sb[j] - jnp.where(pick[j], m_lo, m_hi))
        t = tot(p)
        l_hi = l_hi + jnp.where(pick[j], 0.0, t)
        l_lo = l_lo + jnp.where(pick[j], t, 0.0)
        low = p.astype(bf16)
        rows = slice(j * BLOCK, (j + 1) * BLOCK)
        zero = jnp.zeros_like(low)
        pb[0, rows, :] = jnp.where(pick[j], low, zero)
        pb[1, rows, :] = jnp.where(pick[j], zero, low)
    o_hi = by_pair(VT[r, 0, :, part], pa.astype(bf16)) + by_pair(VT[r, 1, :, part], pb[1, part, :])
    o_lo = by_pair(VT[r, 0, :, part], pb[0, part, :])
    if own:
        p = jnp.exp2(sd - m_lo)
        l_lo = l_lo + tot(p)
        at = pl.ds(pl.multiple_of(i * BLOCK, BLOCK), BLOCK)
        o_lo = o_lo + by_pair(VT[r, 0, :, at], p.astype(bf16))
        l_s[i, 1], l_s[i, 0] = l_hi, l_lo
        acc[i, 1], acc[i, 0] = o_hi, o_lo
    else:
        f_hi, f_lo = jnp.exp2(old_hi - m_hi), jnp.exp2(old_lo - m_lo)
        l_s[i, 1] = l_s[i, 1] * f_hi + l_hi
        l_s[i, 0] = l_s[i, 0] * f_lo + l_lo
        acc[i, 1] = acc[i, 1] * f_hi + o_hi
        acc[i, 0] = acc[i, 0] * f_lo + o_lo
    m_s[i, 1], m_s[i, 0] = m_hi, m_lo


def fwd_finish(pairs, i, m_s, l_s, acc, lse, ot, o_ref):
    first = pairs.first_lo(i)
    out = []
    for u in range(2):
        l = l_s[i, u]
        lse[i, u] = m_s[i, u] + jnp.log2(l)
        t = unpair(acc[i, u] * (1.0 / l))
        ot[i, u] = t
        out.append(t.T.astype(bf16))
    o_ref[i, 0:BLOCK, :] = jnp.where(first, out[0], out[1])
    o_ref[i, BLOCK:2 * BLOCK, :] = jnp.where(first, out[1], out[0])


def diagonal(d_s):
    d_s[...] = lax.broadcasted_iota(jnp.int32, d_s.shape, 0) - (lax.broadcasted_iota(jnp.int32, d_s.shape, 1) & (BLOCK - 1))


def fwd_local(nz, blk_ref, x_ref, wqkv_ref, bq_ref, bkv_ref, bkvt_ref, o_ref, ot, lse, K, V, KT, qn, qt, VT, qs, m_s, l_s, acc, d_s, sb, pb, wkvt):
    pairs = Pairs(nz * 8, lambda n: blk_ref[2 * n])
    diagonal(d_s)
    wkvt[...] = turned(wqkv_ref[:, 256:])
    project_queries(pairs, x_ref, wqkv_ref.at[:, 0:256], bq_ref, qn, qt, qs)
    for r in range(nz):
        project_chunk(pairs, r, x_ref, wqkv_ref.at[:, 256:768], wkvt, bkv_ref, bkvt_ref, K, V, KT, VT)
        def step(i, _):
            fwd_step(pairs, r, i, r == 0, K, VT, qs, m_s, l_s, acc, d_s, sb, pb)
            return 0
        lax.fori_loop(0, 4, step, 0)
    for i in range(4):
        fwd_finish(pairs, i, m_s, l_s, acc, lse, ot, o_ref)


def fwd_outs(nz):
    sds = jax.ShapeDtypeStruct
    kv = sds((nz, 2, 512, 256), bf16)
    return (sds((4, 256, 256), bf16), sds((4, 2, 256, 128), f32), sds((4, 2, 1, 512), f32), kv, kv, sds((nz, 2, 256, 512), bf16),
            sds((4, 2, 128, 256), bf16), sds((4, 2, 256, 128), bf16))


def fwd_scratch(nz):
    M = pltpu.VMEM
    return [M((nz, 2, 256, 512), bf16), M((4, 2, 256, 512), bf16), M((4, 2, 1, 512), f32), M((4, 2, 1, 512), f32), M((4, 2, 128, 512), f32),
            M((128, 512), jnp.int32), M((4, 128, 512), f32), M((2, 512, 512), bf16), M((512, 512), bf16)]


def attn_fwd(nz, blk, x, wqkv, bq, bkv):
    V = pl.BlockSpec(memory_space=pltpu.VMEM)
    return pl.pallas_call(
        functools.partial(fwd_local, nz), out_shape=fwd_outs(nz),
        in_specs=[pl.BlockSpec(memory_space=pltpu.SMEM)] + [V] * 5, out_specs=(V,) * 8, scratch_shapes=fwd_scratch(nz),
        compiler_params=pltpu.CompilerParams(vmem_limit_bytes=58 << 20), name="attn_fwd")(blk, x, wqkv, bq, bkv, bkv.reshape(256, 1))


def bwd_query(pairs, i, do_ref, ot, qn, qt, qs, dos, qns, dons, dl):
    for u, do in enumerate(pairs.ordered(i, do_ref[i])):
        dot_t = do.astype(f32).T
        prod = dot_t * ot[i, u]
        low = dot_t.astype(bf16)
        q, t = qn[i, u], qt[i, u]
        for hs, cs in head_slices():
            qs[i, u, hs, cs] = t[hs]
            dos[i, u, hs, cs] = low[hs]
            qns[i, u, cs, hs] = q[:, hs]
            dons[i, u, cs, hs] = do[:, hs]
            dl[i, u, :, cs] = jnp.sum(prod[hs], axis=0, keepdims=True)


def bwd_step(pairs, r, i, own, first, K, V, KT, qs, dos, qns, dons, lse, dl, dk, dv, dq, d_s, gb, js=(0, 1, 2, 3)):
    lo_i = pairs.lo(i)
    pick = {j: lo_i > pairs.lo(r * 4 + j) for j in js}
    part = slice(js[0] * BLOCK, js[-1] * BLOCK + BLOCK)

    def pieces(k, v, u, mask):
        s = dot(k, qs[i, u]) - lse[i, u]
        if mask is not None:
            s = jnp.where(d_s[...] <= mask, s, FAR)
        p = jnp.exp2(s)
        g = p * (dot(v, dos[i, u]) - dl[i, u])
        return p.astype(bf16), g.astype(bf16)

    p, g = pieces(K[r][0, part, :], V[r][0, part, :], 1, None)
    dv[0, part, :] += dot(p, dons[i, 1])
    dk[0, part, :] += dot(g, qns[i, 1])
    q_hi = by_pair(KT[r][0, :, part], g)
    for j in js:
        u = jnp.where(pick[j], 0, 1)
        rows = slice(j * BLOCK, (j + 1) * BLOCK)
        p, g = pieces(K[r][u, rows, :], V[r][u, rows, :], u, jnp.where(i == j, 0, 2 * BLOCK) if own else None)
        gv, gk = dot(p, dons[i, u]), dot(g, qns[i, u])
        dv[0, rows, :] += jnp.where(pick[j], gv, 0.0)
        dv[1, rows, :] += jnp.where(pick[j], 0.0, gv)
        dk[0, rows, :] += jnp.where(pick[j], gk, 0.0)
        dk[1, rows, :] += jnp.where(pick[j], 0.0, gk)
        zero = jnp.zeros_like(g)
        gb[0, rows, :] = jnp.where(pick[j], g, zero)
        gb[1, rows, :] = jnp.where(pick[j], zero, g)
    q_hi = q_hi + by_pair(KT[r][1, :, part], gb[1, part, :])
    q_lo = by_pair(KT[r][0, :, part], gb[0, part, :])
    if own:
        rows = pl.ds(pl.multiple_of(i * BLOCK, BLOCK), BLOCK)
        p, g = pieces(K[r][0, rows, :], V[r][0, rows, :], 0, 0)
        dv[0, rows, :] += dot(p, dons[i, 0])
        dk[0, rows, :] += dot(g, qns[i, 0])
        q_lo = q_lo + by_pair(KT[r][0, :, rows], g)
    if first:
        dq[i, 1], dq[i, 0] = q_hi, q_lo
    else:
        dq[i, 1] += q_hi
        dq[i, 0] += q_lo


def bwd_chunk_weights(pairs, r, x_ref, dk, dv, dw, db, gp, js=(0, 1, 2, 3)):
    total = jnp.zeros((1, 256), f32)
    for p in js:
        at = slice(p * BLOCK, (p + 1) * BLOCK)
        g = [jnp.concatenate([(dk[u, at, :] * (1.0 / LOG2E)).astype(bf16), dv[u, at, :].astype(bf16)], axis=1) for u in range(2)]
        total = total + jnp.sum(g[0][:, 256:].astype(f32), axis=0, keepdims=True) + jnp.sum(g[1][:, 256:].astype(f32), axis=0, keepdims=True)
        first = pairs.first_lo(r * 4 + p)
        gp[p * 256:p * 256 + BLOCK, :] = jnp.where(first, g[0], g[1])
        gp[p * 256 + BLOCK:p * 256 + 256, :] = jnp.where(first, g[1], g[0])
    db[1:2, :] += total
    n = len(js)
    dw[:, 256:768] += dot(x_ref[r, js[0]:js[0] + n].reshape(n * 256, 512), gp[js[0] * 256:(js[0] + n) * 256, :], TN)


def bwd_chunk_rows(r, last, wqkv_ref, dxq, dx, gp, js=(1, 3, 0, 2)):
    for p in js:
        rows = slice(p * 256, p * 256 + 256)
        d = dot(gp[rows, :], wqkv_ref[:, 256:768], NT)
        if last:
            d = d + dxq[p]
        dx[r, rows, :] = d.astype(bf16)


def bwd_query_out(pairs, x_ref, wqkv_ref, dq, dxq, dw, db):
    def piece(i, _):
        t = [(unpair(dq[i, u]) * 0.125).T.astype(bf16) for u in range(2)]
        first = pairs.first_lo(i)
        g = jnp.concatenate([jnp.where(first, t[0], t[1]), jnp.where(first, t[1], t[0])], axis=0)
        dxq[i] = dot(g, wqkv_ref[:, 0:256], NT)
        dw[:, 0:256] += dot(x_ref[0, i], g, TN)
        db[0:1, :] += jnp.sum(g.astype(f32), axis=0, keepdims=True)
        return 0
    lax.fori_loop(0, 4, piece, 0)


def weight_rows(dw, gq):
    for k in range(2):
        for m in range(3):
            gq[k, m * 256:m * 256 + 256, :] = dw[k * 256:k * 256 + 256, m * 256:m * 256 + 256].astype(bf16)


def bwd_local(nz, blk_ref, x_ref, wqkv_ref, K, V, KT, qn, qt, ot, lse, do_ref, dx, gq, db, qs, dos, qns, dons, dl, dk, dv, dq, d_s, gb, dxq, dw, gp):
    pairs = Pairs(nz * 8, lambda n: blk_ref[2 * n])
    kv = [[a.at[r] for r in range(nz)] for a in (K, V, KT)]
    diagonal(d_s)
    dw[...] = jnp.zeros_like(dw)
    db[...] = jnp.zeros_like(db)
    for s in (qs, dos, qns, dons):
        s[...] = jnp.zeros_like(s)
    for i in range(4):
        bwd_query(pairs, i, do_ref, ot, qn, qt, qs, dos, qns, dons, dl)
    for r in list(range(1, nz)) + [0]:
        dk[...] = jnp.zeros_like(dk)
        dv[...] = jnp.zeros_like(dv)
        def step(i, _):
            bwd_step(pairs, r, i, r == 0, r == 1, *kv, qs, dos, qns, dons, lse, dl, dk, dv, dq, d_s, gb)
            return 0
        lax.fori_loop(0, 4, step, 0)
        if r == 0:
            bwd_query_out(pairs, x_ref, wqkv_ref, dq, dxq, dw, db)
        bwd_chunk_weights(pairs, r, x_ref, dk, dv, dw, db, gp)
        bwd_chunk_rows(r, r == 0, wqkv_ref, dxq, dx, gp)
    weight_rows(dw, gq)


def bwd_scratch():
    M = pltpu.VMEM
    return [M((4, 2, 256, 512), bf16), M((4, 2, 256, 512), bf16), M((4, 2, 512, 256), bf16), M((4, 2, 512, 256), bf16), M((4, 2, 1, 512), f32),
            M((2, 512, 256), f32), M((2, 512, 256), f32), M((4, 2, 128, 512), f32), M((128, 512), jnp.int32), M((2, 512, 512), bf16),
            M((4, 256, 512), f32), M((512, 768), f32)]


def attn_bwd(nz, blk, x, wqkv, K, V, KT, qn, qt, ot, lse, do):
    S = pl.BlockSpec(memory_space=pltpu.VMEM)
    sds = jax.ShapeDtypeStruct
    return pl.pallas_call(
        functools.partial(bwd_local, nz), out_shape=(sds((nz, 1024, 512), bf16), sds((2, 768, 256), bf16), sds((8, 256), f32)),
        in_specs=[pl.BlockSpec(memory_space=pltpu.SMEM)] + [S] * 10, out_specs=(S,) * 3, scratch_shapes=bwd_scratch() + [pltpu.VMEM((1024, 512), bf16)],
        compiler_params=pltpu.CompilerParams(vmem_limit_bytes=58 << 20), name="attn_bwd")(blk, x, wqkv, K, V, KT, qn, qt, ot, lse, do)


def dense_kernel(x_ref, cot_ref, att_ref, wo_ref, wu_ref, wd_ref, sm_ref,
                 out_ref, dsm_ref, do_ref, gw_ref, gv_ref, act_s, gp_s, norm_s, dpre_s):
    ff = wu_ref.shape[1]
    chunk = 512
    x = x_ref[...].astype(f32)
    vec = lambda i: jnp.concatenate([sm_ref[0, i:i + 1, :], sm_ref[1, i:i + 1, :]], axis=1)
    b_out, g1, s1, b_down, g2, s2 = (vec(i) for i in range(2, 8))
    mean = lambda v: jnp.mean(v, axis=-1, keepdims=True)
    col = lambda v: jnp.sum(v, axis=0, keepdims=True)
    mix = x + dot(att_ref[...], wo_ref[...]) + b_out
    cen = mix - mean(mix)
    r1 = lax.rsqrt(mean(cen * cen) + norm_eps)
    n1 = cen * r1
    normed = n1 * g1 + s1
    nlow = normed.astype(bf16)
    norm_s[...] = nlow
    ffn = None
    for f in range(0, ff, chunk):
        fs = slice(f, f + chunk)
        at = 8 + f % (ff // 2) // 256
        b_up = jnp.concatenate([sm_ref[2 * f // ff, at + k:at + k + 1, :] for k in range(chunk // 256)], axis=1)
        pre = dot(nlow, wu_ref[:, fs]) + b_up
        c0 = math.sqrt(2.0 / math.pi)
        sq = pre * pre
        th = jnp.tanh(c0 * pre * (1.0 + 0.044715 * sq))
        half = 0.5 * (1.0 + th)
        act = (pre * half).astype(bf16)
        act_s[:, fs] = act
        gp_s[:, fs] = half + 0.5 * pre * (1.0 - th * th) * (c0 * (1.0 + 3 * 0.044715 * sq))
        part = dot(act, wd_ref[fs, :])
        ffn = part if ffn is None else ffn + part
    summed = ffn + b_down + normed + x
    cen = summed - mean(summed)
    r2 = lax.rsqrt(mean(cen * cen) + norm_eps)
    n2 = cen * r2
    out_ref[...] = (n2 * g2 + s2).astype(bf16)
    up = cot_ref[...].astype(f32)
    gv_ref[4:5, :] = col(up * n2)
    gv_ref[5:6, :] = col(up)
    dn = up * g2
    dsum = r2 * (dn - mean(dn) - n2 * mean(dn * n2))
    dffn = dsum.astype(bf16)
    gv_ref[3:4, :] = col(dffn.astype(f32))
    dnorm = dsum
    half_rows = wo_ref.shape[0] // 2
    half_ff = ff // 2
    def put(g, at, rows):
        gw_ref[0, at:at + rows, :] = g[:rows].astype(bf16)
        gw_ref[1, at:at + rows, :] = g[rows:].astype(bf16)
    for f in range(0, ff, chunk):
        fs = slice(f, f + chunk)
        dact = dot(dffn, wd_ref[fs, :], NT)
        dpre = (dact * gp_s[:, fs]).astype(bf16)
        gv_ref[8 + f // chunk:9 + f // chunk, :] = col(dpre.astype(f32))
        dnorm = dnorm + dot(dpre, wu_ref[:, fs], NT)
        put(dot(norm_s[...], dpre, TN), half_rows + (f // chunk) * half_rows, half_rows)
        gd = dot(act_s[:, fs], dffn, TN).astype(bf16)
        base = half_rows * (1 + ff // chunk)
        which, off = f // half_ff, f % half_ff
        gw_ref[which, base + off:base + off + chunk, :] = gd
    gv_ref[1:2, :] = col(dnorm * n1)
    gv_ref[2:3, :] = col(dnorm)
    dn = dnorm * g1
    dmix = r1 * (dn - mean(dn) - n1 * mean(dn * n1))
    dsm_ref[...] = dsum + dmix
    dbr = dmix.astype(bf16)
    gv_ref[0:1, :] = col(dbr.astype(f32))
    do_ref[...] = dot(dbr, wo_ref[...], NT).astype(bf16)
    put(dot(att_ref[...], dbr, TN), 0, half_rows)


def dense(x, cot, att, wo, wu, wd, sm):
    V = pl.BlockSpec(memory_space=pltpu.VMEM)
    tok, dim = x.shape
    ff = wu.shape[1]
    rows = (2 * dim * ff + dim * dim) // 2 // dim
    return pl.pallas_call(
        dense_kernel,
        out_shape=(jax.ShapeDtypeStruct((tok, dim), bf16), jax.ShapeDtypeStruct((tok, dim), f32),
                   jax.ShapeDtypeStruct((tok, dim), bf16), jax.ShapeDtypeStruct((2, rows, dim), bf16),
                   jax.ShapeDtypeStruct((16, dim), f32)),
        in_specs=[V] * 7, out_specs=(V,) * 5,
        scratch_shapes=[pltpu.VMEM((tok, ff), bf16), pltpu.VMEM((tok, ff), f32), pltpu.VMEM((tok, dim), bf16),
                        pltpu.VMEM((8, 128), f32)],
        compiler_params=pltpu.CompilerParams(vmem_limit_bytes=56 << 20),
        name="dense")(x, cot, att, wo, wu, wd, sm)


MESH = pl.DeviceIdType.MESH


def places(nz):
    me, wi = lax.axis_index("ctx"), lax.axis_index("wt")
    z, y, c = me // 4, lax.rem(me // 2, 2), lax.rem(me, 2)
    low = lax.rem(me, 4)
    at = lambda zz, ll: (zz * 4 + ll, wi)
    to = dict(up=at(lax.rem(z + 1, nz), low), down=at(lax.rem(z + nz - 1, nz), low), core=at(z, low + 1 - 2 * c), y=at(z, low + 2 - 4 * y),
              x=(me, 1 - wi))
    return me, wi, z, y, c, low, to


def meet(targets):
    bar = pltpu.get_barrier_semaphore()
    for t in targets:
        pl.semaphore_signal(bar, inc=1, device_id=t, device_id_type=MESH)
    pl.semaphore_wait(bar, len(targets))


class Wires:
    def __init__(self, send, recv):
        self.send, self.recv, self.n, self.live = send, recv, 0, []

    def make(self, src, dst, to):
        cp = pltpu.make_async_remote_copy(src, dst, self.send.at[self.n], self.recv.at[self.n], device_id=to, device_id_type=MESH)
        self.n += 1
        self.live.append(cp)
        return cp

    def go(self, src, dst, to):
        cp = self.make(src, dst, to)
        cp.start()
        return cp

    def drain(self):
        for cp in self.live:
            cp.wait_send()


def rows_of(start, size, mult=16):
    return pl.ds(pl.multiple_of(start, mult), size)


def gather_kernel(nz, with_w, *refs):
    if with_w:
        (x_ref, wq_ref, wk_ref, wv_ref, wo_ref, wu_ref, wd_ref, sm_ref,
         xall, wqkv, wo, wu, wd, sm, send, recv, lsem) = refs
    else:
        x_ref, xall, send, recv, lsem = refs
    me, wi, z, y, c, low, to = places(nz)
    rows = x_ref.shape[1]
    local = []

    def copy(src, dst):
        cp = pltpu.make_async_copy(src, dst, lsem.at[len(local)])
        cp.start()
        local.append(cp)

    copy(x_ref.at[y], xall.at[0, 0])
    if with_w:
        R, half = wq_ref.shape[0], wq_ref.shape[1] // 2
        for i, w in enumerate((wq_ref, wk_ref, wv_ref)):
            copy(w.at[:, rows_of(c * half, half, 128)], wqkv.at[rows_of(wi * R, R), pl.ds(i * half, half)])
        for w, full in ((wo_ref, wo), (wu_ref, wu), (wd_ref, wd)):
            n = w.shape[0]
            copy(w, full.at[rows_of(wi * n, n)])
        copy(sm_ref, sm.at[wi])
    near = [to["up"], to["down"], to["core"], to["y"]] + ([to["x"]] if with_w else [])
    meet(near)
    wires = Wires(send, recv)
    yx = wires.go(x_ref.at[1 - y], xall.at[0, 2], to["y"])
    ring = {(1, 0): wires.go(x_ref.at[y], xall.at[1, 0], to["up"])}
    core = {(0, 0): wires.go(x_ref.at[y], xall.at[0, 1], to["core"])}
    if with_w:
        xs = []
        for i, w in enumerate((wq_ref, wk_ref, wv_ref)):
            xs.append(wires.go(w.at[:, rows_of(c * half, half, 128)], wqkv.at[rows_of(wi * R, R), pl.ds(i * half, half)], to["x"]))
        xs.append(wires.go(sm_ref, sm.at[wi], to["x"]))
        big = []
        for w, full in ((wo_ref, wo), (wu_ref, wu), (wd_ref, wd)):
            n = w.shape[0]
            h = n // 2
            cp = wires.go(w.at[rows_of(c * h, h)], full.at[rows_of(wi * n + c * h, h)], to["x"])
            big.append((cp, full, rows_of((1 - wi) * n + c * h, h)))
    yx.wait_recv()
    ring[1, 1] = wires.go(xall.at[0, 2], xall.at[1, 2], to["up"])
    core[0, 1] = wires.go(xall.at[0, 2], xall.at[0, 3], to["core"])
    shared = []
    for r in range(1, nz):
        for s in range(2):
            ring[r, s].wait_recv()
            if r < nz - 1:
                ring[r + 1, s] = wires.go(xall.at[r, 2 * s], xall.at[r + 1, 2 * s], to["up"])
            core[r, s] = wires.go(xall.at[r, 2 * s], xall.at[r, 2 * s + 1], to["core"])
        if with_w and r - 1 < len(big):
            cp, full, where = big[r - 1]
            cp.wait_recv()
            shared.append(wires.go(full.at[where], full.at[where], to["core"]))
    if with_w:
        for cp, full, where in big[nz - 1:]:
            cp.wait_recv()
            shared.append(wires.go(full.at[where], full.at[where], to["core"]))
        for cp in xs + shared:
            cp.wait_recv()
    for cp in core.values():
        cp.wait_recv()
    wires.drain()
    for cp in local:
        cp.wait()


def gather_all(nz, x, weights=None, small=None):
    A = pl.BlockSpec(memory_space=pl.ANY)
    sds = jax.ShapeDtypeStruct
    rows, dim = x.shape[1:]
    outs = [sds((nz, 4, rows, dim), bf16)]
    ins = [x]
    ncopy = 1 + 2 * (nz - 1) + 2 * nz
    if weights is not None:
        wq, wk, wv, wo, wu, wd = weights
        ins += list(weights) + [small]
        outs += [sds((dim, 3 * dim // 2), bf16)] + [sds((2 * w.shape[0], w.shape[1]), bf16) for w in (wo, wu, wd)] + [sds((2,) + small.shape, bf16)]
        ncopy += 10
    return pl.pallas_call(
        functools.partial(gather_kernel, nz, weights is not None),
        out_shape=tuple(outs), in_specs=[A] * len(ins), out_specs=(A,) * len(outs),
        scratch_shapes=[pltpu.SemaphoreType.DMA((ncopy,)), pltpu.SemaphoreType.DMA((ncopy,)), pltpu.SemaphoreType.DMA((8,))],
        compiler_params=pltpu.CompilerParams(collective_id=1, has_side_effects=True, vmem_limit_bytes=16 << 20),
        name="gather_all")(*ins)


def add_into(dst, parts, rows, step=64):
    def body(i, _):
        r = rows_of(i * step, step)
        total = parts[0](r)[...].astype(f32)
        for p in parts[1:]:
            total = total + p(r)[...].astype(f32)
        d = dst(r)
        d[...] = total.astype(bf16)
        return 0
    lax.fori_loop(0, rows // step, body, 0)


def offset(ref, lead, start):
    def view(r):
        at = pl.ds(pl.multiple_of(start + r.start, 16), r.size)
        return ref.at[lead + (at,)]
    return view


def chip_pairs(nz, order_ref):
    me = lax.axis_index("ctx")
    z, y, c = me // 4, lax.rem(me // 2, 2), lax.rem(me, 2)

    def first(n):
        r, p = n // 4, n % 4
        a, b = p // 2, p % 2
        yy, cc = y + a - 2 * y * a, c + b - 2 * c * b
        return order_ref[y, 2 * (lax.rem(z - r + nz, nz) * 4 + yy * 2 + cc)]
    return Pairs(nz * 8, first)


def front_kernel(nz, order_ref, bqr, bvr, bor, g1r, s1r, bdr, g2r, s2r, bur, x_ref, wq_ref, wk_ref, wv_ref, wo_ref, wu_ref, wd_ref,
                 att, wo, wu, wd, sm, xall, wqkv, ot_o, lse_o, K_o, V_o, KT_o, qn_o, qt_o,
                 xs, ws, sms, wos, wus, wds, K, V, KT, VT, qn, qt, qs, m_s, l_s, acc, d_s, sb, pb, wkvt, bkvt, ot, lse, o_s, send, recv, lsem):
    me, wi, z, y, c, low, to = places(nz)
    to["yc"] = (z * 4 + 3 - low, wi)
    half, R = 256, wq_ref.shape[0]
    local = []

    def copy(src, dst):
        cp = pltpu.make_async_copy(src, dst, lsem.at[len(local)])
        cp.start()
        local.append(cp)
        return cp

    own_x = copy(x_ref.at[y], xs.at[0, 0])
    own_w = [copy(w.at[:, rows_of(c * half, half, 128)], ws.at[rows_of(wi * R, R), pl.ds(i * half, half)]) for i, w in enumerate((wq_ref, wk_ref, wv_ref))]
    for i, v in enumerate((bqr, bvr, bor, g1r, s1r, bdr, g2r, s2r)):
        sms[wi, i:i + 1, :] = v[...].astype(f32).reshape(1, half)
    up_b = bur[...].astype(f32).reshape(1, 1024)
    for i in range(4):
        sms[wi, 8 + i:9 + i, :] = up_b[:, i * half:(i + 1) * half]
    sms[wi, 12:16, :] = jnp.zeros((4, half), f32)
    meet([to[k] for k in ("up", "down", "core", "y", "yc", "x")])
    w = Wires(send, recv)
    yx = w.go(x_ref.at[1 - y], xs.at[0, 2], to["y"])
    ring, core = {}, {}
    ring[1, 0] = w.go(x_ref.at[y], xs.at[1, 0], to["up"])
    core[0, 0] = w.go(x_ref.at[y], xs.at[0, 1], to["core"])
    wx = []
    for i, m in enumerate((wq_ref, wk_ref, wv_ref)):
        wx.append(w.go(m.at[:, rows_of(c * half, half, 128)], ws.at[rows_of(wi * R, R), pl.ds(i * half, half)], to["x"]))
    wx.append(w.go(sms.at[wi], sms.at[wi], to["x"]))
    big = []
    for m, full in ((wo_ref, wos), (wu_ref, wus), (wd_ref, wds)):
        n = m.shape[0]
        h = n // 2
        copy(m, full.at[rows_of(wi * n, n)])
        big.append((m.at[rows_of(c * h, h)], full.at[rows_of(wi * n + c * h, h)], full, rows_of((1 - wi) * n + c * h, h)))

    pairs = chip_pairs(nz, order_ref)
    diagonal(d_s)
    yx.wait_recv()
    ring[1, 1] = w.go(xs.at[0, 2], xs.at[1, 2], to["up"])
    core[0, 1] = w.go(xs.at[0, 2], xs.at[0, 3], to["core"])

    def pump(r, s):
        ring[r, s].wait_recv()
        if r < nz - 1:
            ring[r + 1, s] = w.go(xs.at[r, 2 * s], xs.at[r + 1, 2 * s], to["up"])
        core[r, s] = w.go(xs.at[r, 2 * s], xs.at[r, 2 * s + 1], to["core"])

    shared = []

    def share(k):
        cp, full, where = sent[k]
        cp.wait_recv()
        shared.append(w.go(full.at[where], (wo, wu, wd)[k].at[where], to["core"]))

    pump(1, 0)
    for cp in own_w:
        cp.wait()
    for cp in wx:
        cp.wait_recv()
    sent = [(w.go(src, dst, to["x"]), full, where) for src, dst, full, where in big]
    copy(sms, sm)
    copy(ws, wqkv)
    wkvt[...] = turned(ws[:, 256:])
    bv = sms[c, 1:2, :]
    bkvt[...] = jnp.broadcast_to(bv, (8, half)).T[:, 0:1]
    own_x.wait()
    core[0, 0].wait_recv()
    core[0, 1].wait_recv()
    project_queries(pairs, xs, ws.at[:, 0:256], sms.at[c, 0:1], qn, qt, qs)
    copy(qn, qn_o)
    copy(qt, qt_o)

    def bring(r, s):
        if r:
            core[r, s].wait_recv()
        project_chunk(pairs, r, xs, ws.at[:, 256:768], wkvt, sms.at[c, 1:2], bkvt, K, V, KT, VT, 2 * s, 2 * s + 2)
        for a, b in ((xs, xall), (K, K_o), (V, V_o), (KT, KT_o)):
            if s:
                copy(a.at[r], b.at[r])

    def attend(r, js, last=False):
        def step(n, _):
            i = lax.rem(n + 2, 4) if last else n
            fwd_step(pairs, r, i, r == 0, K, VT, qs, m_s, l_s, acc, d_s, sb, pb, js)
            if last:
                fwd_finish(pairs, i, m_s, l_s, acc, lse, ot, o_s)
                for p in outs:
                    pl.when(i == p)(outs[p].start)
            return 0
        lax.fori_loop(0, 4, step, 0)

    def half_chunk(r, s, last=False):
        bring(r, s)
        attend(r, (2 * s, 2 * s + 1), last)

    cols = pl.ds(pl.multiple_of(c * half, half), half)
    outs = {p: w.make(o_s.at[p], att.at[y, :, cols], to[k]) for p, k in ((2, "y"), (3, "yc"), (1, "core"))}
    bring(0, 0)
    bring(0, 1)
    pump(1, 1)
    attend(0, (0, 1, 2, 3))
    for k, (a, b) in enumerate(((wos, wo), (wus, wu), (wds, wd))):
        local[4 + k].wait()
        n = a.shape[0] // 2
        copy(a.at[rows_of(wi * n, n)], b.at[rows_of(wi * n, n)])
    pump(2, 0)
    for r in range(1, nz - 1):
        half_chunk(r, 0)
        if r > 1:
            pump(r + 1, 0)
        half_chunk(r, 1)
        if r < nz - 2:
            pump(r + 1, 1)
    half_chunk(nz - 1, 0)
    pump(nz - 1, 1)
    half_chunk(nz - 1, 1, True)
    copy(o_s.at[0], att.at[y, :, cols])
    copy(ot, ot_o)
    copy(lse, lse_o)
    for k, (a, b) in enumerate(((wos, wo), (wus, wu), (wds, wd))):
        share(k)
        copy(a.at[sent[k][2]], b.at[sent[k][2]])
    for cp in shared:
        cp.wait_recv()
    for cp in outs.values():
        cp.wait_recv()
    w.drain()
    for cp in local[7:]:
        cp.wait()


def front(nz, order, vectors, x, weights):
    A = pl.BlockSpec(memory_space=pltpu.HBM)
    V = pl.BlockSpec(memory_space=pltpu.VMEM)
    sds = jax.ShapeDtypeStruct
    M = pltpu.VMEM
    rows, dim = x.shape[1:]
    wq, wk, wv, wo, wu, wd = weights
    outs = [sds((2, rows, dim), bf16)] + [sds((2 * w.shape[0], w.shape[1]), bf16) for w in (wo, wu, wd)]
    outs += [sds((2, 16, 256), f32), sds((nz, 4, rows, dim), bf16), sds((dim, 768), bf16)] + list(fwd_outs(nz)[1:])
    scratch = [M((nz, 4, rows, dim), bf16), M((dim, 768), bf16), M((2, 16, 256), f32)] + [M(o.shape, bf16) for o in outs[1:4]]
    scratch += [M((nz, 2, 512, 256), bf16)] * 2 + [M((nz, 2, 256, 512), bf16)] * 2 + [M((4, 2, 128, 256), bf16), M((4, 2, 256, 128), bf16)]
    scratch += fwd_scratch(nz)[1:] + [M((256, 1), f32), M((4, 2, 256, 128), f32), M((4, 2, 1, 512), f32), M((4, 256, 256), bf16)]
    scratch += [pltpu.SemaphoreType.DMA((40,)), pltpu.SemaphoreType.DMA((40,)), pltpu.SemaphoreType.DMA((40,))]
    return pl.pallas_call(
        functools.partial(front_kernel, nz), out_shape=tuple(outs),
        in_specs=[pl.BlockSpec(memory_space=pltpu.SMEM)] + [V] * 9 + [A] * 7, out_specs=(A,) * len(outs), scratch_shapes=scratch,
        compiler_params=pltpu.CompilerParams(collective_id=1, has_side_effects=True, vmem_limit_bytes=58 << 20), name="front")(
            order, *vectors, x, *weights)


def back_kernel(nz, order_ref, gv_ref, do_ref, x_hbm, w_hbm, K_h, V_h, KT_h, qn_h, qt_h, ot_h, lse_h, gw_ref,
                dxo, go, gqo, gvo,
                xs, wqkv, K, V, KT, qn, qt, ot, lse, do, qs, dos, qns, dons, dl, dk, dv, dq, d_s, gb, dxq, dw, dx, gp, gq, db, outdx,
                dx_core, dx_in, cr, cs, xr, xs_, yr, ys_, za, zs, zb, xrq, xsq, yrq, ysq, zrq, gsum, gqsum, gvs, gvr, send, recv, lsem):
    me, wi, z, y, c, low, to = places(nz)
    to["yc"] = (z * 4 + 3 - low, wi)
    zto = [(lax.rem(z + d, nz) * 4 + low, wi) for d in range(1, nz)]
    half, hrow = 256, 256
    w = Wires(send, recv)
    local = []

    def copy(src, dst):
        cp = pltpu.make_async_copy(src, dst, lsem.at[len(local)])
        cp.start()
        local.append(cp)
        return cp

    cols = pl.ds(pl.multiple_of(c * half, half), half)
    other = pl.ds(pl.multiple_of((1 - c) * half, half), half)
    meet([to[k] for k in ("core", "y", "yc", "x")] + zto)
    dos_in = [w.go(do_ref.at[1 - y, :, cols], do.at[2], to["y"]), w.go(do_ref.at[1 - y, :, other], do.at[3], to["yc"]),
              w.go(do_ref.at[y, :, other], do.at[1], to["core"])]
    got = {}
    for s in range(3):
        got["c", s] = w.go(gw_ref.at[:, rows_of(s * 768 + (1 - c) * 384, 384)], cr.at[s], to["core"])
    mine_gw = [copy(gw_ref.at[:, rows_of(s * 768 + c * 384, 384)], cs.at[s]) for s in range(3)]
    first_in = [copy(do_ref.at[y, :, cols], do.at[0])] + [copy(a, b) for a, b in ((qn_h, qn), (qt_h, qt), (ot_h, ot), (lse_h, lse))]
    kv_in = {}
    for r in list(range(1, nz)) + [0]:
        kv_in[r] = [copy(a.at[r], b[r]) for a, b in ((K_h, K), (V_h, V), (KT_h, KT))]
    for r in kv_in:
        kv_in[r].append(copy(x_hbm.at[r], xs.at[r]))
    w_in = copy(w_hbm, wqkv)

    n = range(5)
    wide = [384, 192, 48]
    zp = (z + 1 - 2 * lax.rem(z, 2)) * 4 + low, wi
    zq = (z + 2 - 4 * (z // 2)) * 4 + low, wi
    odd, far = lax.rem(z, 2), z // 2
    X_in = [xr.at[s] for s in range(3)] + [xrq.at[s] for s in range(2)]
    X_sum = [xs_.at[s] for s in range(3)] + [xsq.at[s] for s in range(2)]
    Y_in = [yr.at[s] for s in range(3)] + [yrq.at[s] for s in range(2)]
    Y_sum = [ys_.at[s] for s in range(3)] + [ysq.at[s] for s in range(2)]
    Z_in = [zrq.at[s] for s in range(2)]
    out = [gsum.at[s] for s in range(3)] + [gqsum.at[s] for s in range(2)]
    done = [go.at[s] for s in range(3)] + [gqo.at[s] for s in range(2)]
    start_c, start_y = c * 384, c * 384 + y * 192
    at_c, at_y = rows_of(start_c, 384), rows_of(start_y, 192)
    pos = odd * 2 + far
    start_p, start_h = start_y + pos * 48, start_y + odd * 96
    at_p, at_h = rows_of(start_p, 48), rows_of(start_h, 96)
    start_z = start_y + z * 48
    at_z = rows_of(start_z, 48)
    theirs = rows_of((1 - y) * 192, 192)
    for s in n:
        got["x", s] = w.make(cs.at[s, 1 - wi] if s < 3 else gq.at[1 - wi, pl.ds((s - 3) * 384, 384)], X_in[s], to["x"])
        got["y", s] = w.make(X_sum[s].at[theirs], Y_in[s], to["y"])
        got["ys", s] = w.make(out[s].at[at_y], out[s].at[at_y], to["y"])
        got["cs", s] = w.make(out[s].at[at_c], done[s].at[at_c], to["core"])
        if s < 3:
            got["za", s] = w.make(ys_.at[s, rows_of((1 - odd) * 96, 96)], za.at[s], zp)
            got["zb", s] = w.make(zs.at[s, rows_of((1 - far) * 48, 48)], zb.at[s], zq)
            got["zc", s] = w.make(out[s].at[at_p], out[s].at[at_p], zq)
            got["zd", s] = w.make(out[s].at[at_h], out[s].at[at_h], zp)
        else:
            for d in range(1, nz):
                got["z", s, d] = w.make(Y_sum[s].at[rows_of(lax.rem(z + d, nz) * 48, 48)], Z_in[s - 3].at[d - 1], zto[d - 1])
                got["zs", s, d] = w.make(out[s].at[at_z], out[s].at[at_z], zto[d - 1])

    def x_send(s):
        if s < 3:
            mine_gw[s].wait()
            got["c", s].wait_recv()
            add_into(offset(cs, (s, 1 - wi), 0), [offset(cs, (s, 1 - wi), 0), offset(cr, (s, 1 - wi), 0)], 384, 128)
            got["x", s].start()
            add_into(offset(cs, (s, wi), 0), [offset(cs, (s, wi), 0), offset(cr, (s, wi), 0)], 384, 128)
        else:
            got["x", s].start()

    def y_send(s):
        got["x", s].wait_recv()
        mine = lambda lo: offset(cs, (s, wi), lo) if s < 3 else offset(gq, (wi,), (s - 3) * 384 + lo)
        for half_y in (1 - y, y):
            lo = half_y * 192
            add_into(offset(X_sum[s], (), lo), [mine(lo), offset(X_in[s], (), lo)], 192, 96)
            if half_y is not y:
                got["y", s].start()

    def z_a(s):
        got["y", s].wait_recv()
        add_into(offset(ys_, (s,), 0), [offset(xs_, (s,), y * 192), offset(yr, (s,), 0)], 192, 96)
        got["za", s].start()

    def z_b(s):
        got["za", s].wait_recv()
        add_into(offset(zs, (s,), 0), [offset(ys_, (s,), odd * 96), offset(za, (s,), 0)], 96, 96)
        got["zb", s].start()

    def z_c(s):
        got["zb", s].wait_recv()
        add_into(offset(out[s], (), start_p), [offset(zs, (s,), far * 48), offset(zb, (s,), 0)], 48, 48)
        got["zc", s].start()

    def z_d(s):
        got["zc", s].wait_recv()
        got["zd", s].start()

    def z_send(s):
        got["y", s].wait_recv()
        add_into(offset(Y_sum[s], (), 0), [offset(X_sum[s], (), y * 192), offset(Y_in[s], (), 0)], 192, 192)
        for d in range(1, nz):
            got["z", s, d].start()

    def z_share(s):
        for d in range(1, nz):
            got["z", s, d].wait_recv()
        add_into(offset(out[s], (), start_z), [offset(Y_sum[s], (), z * 48)] + [offset(Z_in[s - 3], (d,), 0) for d in range(nz - 1)], 48, 48)
        for d in range(1, nz):
            got["zs", s, d].start()

    def y_share(s):
        for k in (["zd"] if s < 3 else [("zs", d) for d in range(1, nz)]):
            got[(k, s) if s < 3 else (k[0], s, k[1])].wait_recv()
        got["ys", s].start()

    def c_share(s):
        got["ys", s].wait_recv()
        got["cs", s].start()
        copy(out[s].at[at_c], done[s].at[at_c])

    for r in range(nz):
        for h in range(2):
            at = pl.ds(h * 512, hrow)
            got["d", r, h] = w.make(dx.at[r, pl.ds(h * 512 + hrow, hrow)], dx_core.at[r, h], to["core"])
            if r:
                got["r", (r + 1) % nz, h] = w.make(dx.at[r, at], dx_in.at[(r + 1) % nz, h], to["up"])
    got["dy"] = w.make(dx.at[0, pl.ds(512, hrow)], dxo.at[1], to["y"])

    def give(r, h):
        got["d", r, h].start()

    def fold(r, h):
        got["d", r, h].wait_recv()
        add_into(offset(dx, (r,), h * 512), [offset(dx, (r,), h * 512), offset(dx_core, (r, h), 0)], hrow, 128)
        if r == 1:
            got["r", 2, h].start()

    def hop(r, h):
        got["r", r, h].wait_recv()
        dst = offset(dx, (r,), h * 512) if r or h else offset(outdx, (0,), 0)
        add_into(dst, [offset(dx, (r,), h * 512), offset(dx_in, (r, h), 0)], hrow, 128)
        if r:
            got["r", (r + 1) % nz, h].start()
        elif h:
            got["dy"].start()
        else:
            copy(outdx.at[0], dxo.at[0])

    vec_to = [to["core"], to["y"], to["x"]] + [(zz * 4 + low, wi) for zz in (z + 1 - 2 * lax.rem(z, 2), z + 2 - 4 * (z // 2))]

    def vec_send(k):
        if k == 0:
            gvs[0] = jnp.zeros_like(gvs[0])
            gvs[0, 0:16, :] = gv_ref[...]
            zero = jnp.zeros((1, half), f32)
            for i in range(2):
                v = db[i:i + 1, :]
                gvs[0, 16 + i:17 + i, :] = jnp.concatenate([jnp.where(c == 0, v, zero), jnp.where(c == 0, zero, v)], axis=1)
        else:
            got["v", k - 1].wait_recv()
            gvs[k] = gvs[k - 1] + gvr[k - 1]
        if k < 5:
            got["v", k].start()
        else:
            gvo[...] = gvs[5]

    pairs = chip_pairs(nz, order_ref)
    for k in range(5):
        got["v", k] = w.make(gvs.at[k], gvr.at[k], vec_to[k])
    diagonal(d_s)
    dw[...] = jnp.zeros_like(dw)
    db[...] = jnp.zeros_like(db)
    for s in (qs, dos, qns, dons):
        s[...] = jnp.zeros_like(s)
    x_send(0)
    for cp in first_in:
        cp.wait()
    dos_in[2].wait_recv()
    hooks = plan(dict(x=x_send, y=y_send, za=z_a, zb=z_b, zc=z_c, zd=z_d, ys=y_share, cs=c_share, fold=fold, hop=hop, z=z_send, zs=z_share, vec=vec_send))
    hook = lambda *k: hooks[k]() if k in hooks else None
    hook("pre")
    for r in list(range(1, nz)) + [0]:
        dk[...] = jnp.zeros_like(dk)
        dv[...] = jnp.zeros_like(dv)
        for cp in kv_in[r][:3]:
            cp.wait()
        for n, js in enumerate(((2, 3), (0, 1)) if r == 1 else ((0, 1, 2, 3),)):
            def step(i, _):
                if r == 1 and n == 0:
                    for k in range(2):
                        pl.when(i == 2)(dos_in[k].wait_recv)
                    bwd_query(pairs, i, do, ot, qn, qt, qs, dos, qns, dons, dl)
                bwd_step(pairs, r, i, r == 0, r == 1 and n == 0, K, V, KT, qs, dos, qns, dons, lse, dl, dk, dv, dq, d_s, gb, js)
                for k in range(4):
                    if (r, n, k) in hooks:
                        pl.when(i == k)(hooks[r, n, k])
                return 0
            lax.fori_loop(0, 4, step, 0)
            if r == 1 and n == 0:
                for q in kv_in:
                    kv_in[q][3].wait()
                w_in.wait()
            if r == 0:
                bwd_query_out(pairs, xs, wqkv, dq, dxq, dw, db)
                hook(0, 0, "q")
            bwd_chunk_weights(pairs, r, xs, dk, dv, dw, db, gp, js)
            if r == 0:
                weight_rows(dw, gq)
                x_send(3)
            hook(r, n, "w")
            bwd_chunk_rows(r, r == 0, wqkv, dxq, dx, gp, [p for p in (3, 1, 2, 0) if p in js])
            for h in (1, 0):
                if 2 * h in js:
                    give(r, h)
            hook(r, n, "r")
    hook("tail")
    for s in range(5):
        got["cs", s].wait_recv()
    got["dy"].wait_recv()
    w.drain()
    for cp in local[-6:]:
        cp.wait()


PLAN = {
    (1, 0, "r"): (("x", 2),),
    (1, 1, 1): (("fold", 1, 1),),
    (1, 1, 2): (("y", 0),),
    (2, 0, 2): (("x", 1), ("fold", 1, 0), ("za", 0),),
    (2, 0, "r"): (("y", 2),),
    (3, 0, 2): (("zb", 0),),
    (3, 0, 3): (("za", 2), ("fold", 2, 0), ("y", 1),),
    (3, 0, "r"): (("zc", 0), ("hop", 2, 0),),
    (0, 0, 0): (("fold", 2, 1), ("hop", 2, 1),),
    (0, 0, 2): (("za", 1),),
    (0, 0, "q"): (("zb", 2), ("zd", 0), ),
    (0, 0, "w"): (("zc", 2), ("vec", 0), ("zb", 1), ("fold", 3, 1), ("fold", 3, 0), ("y", 3), ("x", 4), ("zd", 2), ("zc", 1), ("ys",
        0), ("z", 3), ("y", 4),),
    (0, 0, "r"): (("zd", 1), ("fold", 0, 1), ("hop", 3, 1), ("zs", 3), ("ys", 2), ("z", 4),),
    "tail": (("fold", 0, 0), ("vec", 1), ("ys", 1), ("ys", 3), ("vec", 2), ("cs", 0), ("zs", 4), ("vec", 3), ("hop", 3, 0), ("cs", 2), ("hop", 0, 1),
        ("cs", 1), ("ys", 4), ("cs", 3), ("vec", 4), ("cs", 4), ("vec", 5), ("hop", 0, 0),),
}


def plan(ops):
    def run(items):
        def go():
            for name, *a in items:
                ops[name](*a)
        return go
    return {k if isinstance(k, tuple) else (k,): run(v) for k, v in PLAN.items()}


def back(nz, order, gv, do, x_all, wqkv, k, v, kt, qn, qt, ot, lse, gw):
    A = pl.BlockSpec(memory_space=pltpu.HBM)
    V = pl.BlockSpec(memory_space=pltpu.VMEM)
    sds = jax.ShapeDtypeStruct
    B = lambda *s: pltpu.VMEM(s, bf16)
    F = lambda *s: pltpu.VMEM(s, f32)
    ins = (x_all, wqkv, k, v, kt, qn, qt, ot, lse)
    scratch = [[pltpu.VMEM(a.shape[1:], a.dtype)] * nz if any(a is b for b in (k, v, kt)) else pltpu.VMEM(a.shape, a.dtype) for a in ins] + [B(4, 256, 256)] + bwd_scratch()
    scratch += [B(nz, 1024, 512), B(1024, 512), B(2, 768, 256), F(8, 256), B(1, 256, 512)]
    scratch += [B(nz, 2, 256, 512), B(nz, 2, 256, 512), B(3, 2, 384, 512), B(3, 2, 384, 512), B(3, 384, 512), B(3, 384, 512), B(3, 192, 512), B(3, 192, 512),
                B(3, 96, 512), B(3, 96, 512), B(3, 48, 512), B(2, 384, 256), B(2, 384, 256), B(2, 192, 256), B(2, 192, 256), B(2, nz - 1, 48, 256),
                B(3, 768, 512), B(2, 768, 256),
                F(6, 24, 512), F(5, 24, 512)]
    scratch += [pltpu.SemaphoreType.DMA((80,)), pltpu.SemaphoreType.DMA((80,)), pltpu.SemaphoreType.DMA((40,))]
    return pl.pallas_call(
        functools.partial(back_kernel, nz),
        out_shape=(sds((2, 256, 512), bf16), sds((3, 768, 512), bf16), sds((2, 768, 256), bf16), sds((24, 512), f32)),
        in_specs=[pl.BlockSpec(memory_space=pltpu.SMEM), V] + [A] * 11, out_specs=(A, A, A, V), scratch_shapes=scratch,
        compiler_params=pltpu.CompilerParams(collective_id=2, has_side_effects=True, vmem_limit_bytes=62 << 20), name="back")(order, gv, do, *ins, gw)


def last_kernel(nu, go_ref, gq_ref, gv_ref, dx_ref, dsm_ref, gin, dwq, dbq, dwk, dwv, dbv, dwo, dbo, dg1, ds1, dwu, dbu, dwd, dbd, dg2, ds2):
    wi, y = lax.axis_index("wt"), lax.rem(lax.axis_index("ctx") // 2, 2)
    for s in range(2):
        seq = jnp.where(y == 0, s, 1 - s)
        gin[s] = (dsm_ref[s] + dx_ref[seq].astype(f32)).astype(bf16)
    hr = dwq.shape[0]
    for k in range(2):
        at, low = slice(k * 256, k * 256 + 256), k * 384
        dwq[:, at] = gq_ref[0, low:low + 256, :].astype(f32)
        dwk[0:128, at] = gq_ref[0, low + 256:low + 384, :].astype(f32)
        dwk[128:256, at] = gq_ref[1, low:low + 128, :].astype(f32)
        dwv[:, at] = gq_ref[1, low + 128:low + 384, :].astype(f32)
    dwo[...] = go_ref[0:hr, :].astype(f32)
    for k in range(nu):
        dwu[:, k * 512:k * 512 + 512] = go_ref[hr + k * hr:2 * hr + k * hr, :].astype(f32)
    dwd[...] = go_ref[hr + nu * hr:, :].astype(f32)

    def row(i):
        v = gv_ref[i:i + 1, :]
        return jnp.where(wi == 0, v[:, :256], v[:, 256:])

    for o, i in ((dbo, 0), (dg1, 1), (ds1, 2), (dbd, 3), (dg2, 4), (ds2, 5), (dbq, 16), (dbv, 17)):
        o[...] = row(i).reshape(256)
    h = nu // 2
    a, b = [jnp.concatenate([gv_ref[8 + k * h + i:9 + k * h + i, :] for i in range(h)], axis=1) for k in range(2)]
    dbu[...] = jnp.where(wi == 0, a, b).reshape(a.shape[1])


def last(nu, go, gqo, gv, dxo, dsm):
    V = pl.BlockSpec(memory_space=pltpu.VMEM)
    f = lambda *s: jax.ShapeDtypeStruct(s, f32)
    ff = nu * 512
    outs = (jax.ShapeDtypeStruct((2, 256, 512), bf16), f(256, 512), f(256), f(256, 512), f(256, 512), f(256), f(256, 512), f(256), f(256), f(256),
            f(256, ff), f(ff // 2), f(ff // 2, 512), f(256), f(256), f(256))
    return pl.pallas_call(functools.partial(last_kernel, nu), out_shape=outs, in_specs=[V] * 5, out_specs=(V,) * 16,
                          compiler_params=pltpu.CompilerParams(vmem_limit_bytes=56 << 20), name="last")(go, gqo, gv, dxo, dsm)


def body(block_in, block_order, w_query, b_query, w_key, w_value, b_value, w_out, b_out, gain_one, shift_one,
         w_up, b_up, w_down, b_down, gain_two, shift_two, cotangent, *, nc, nw):
    seqs, rows, dim = block_in.shape
    nz = nc // 4
    hb = rows // BLOCK
    half = dim // 2
    me = lax.axis_index("ctx")
    yy = (me // 2) % 2
    cc = me % 2
    zz = me // 4
    xor = lambda v: [(i, i ^ v) for i in range(nc)]
    ring = [(i, ((i // 4 + 1) % nz) * 4 + i % 4) for i in range(nc)]
    perm = lambda v, p: lax.ppermute(v, "ctx", p)
    gather = lambda v: lax.all_gather(v, "wt", axis=0, tiled=True)
    pick = lambda v, i: lax.dynamic_index_in_dim(v, i, 0, keepdims=False)

    ours = nw == 2 and nz == 4
    small = (b_query, b_value, b_out, gain_one, shift_one, b_down, gain_two, shift_two, b_up)
    by_seq = lambda a, b: jnp.where(yy == 0, jnp.concatenate([a, b], 0), jnp.concatenate([b, a], 0))
    r_ids = (zz - jnp.arange(nz, dtype=jnp.int32)) % nz
    quad = (me % 4) ^ jnp.array([0, 1, 2, 3], jnp.int32)
    order_row = pick(block_order, yy)
    slots = (r_ids[:, None, None] * 4 + quad[None, :, None]) * hb + jnp.arange(hb, dtype=jnp.int32)
    blk = order_row[slots.reshape(-1)]

    if ours:
        att, wo, wu, wd, sm, x_all, wqkv, ot, lse, k, v, kt, qn, qt = front(nz, block_order, small, block_in, (w_query, w_key, w_value, w_out, w_up, w_down))
        att = att.reshape(-1, dim)
    else:
        cols = lambda w: lax.dynamic_slice_in_dim(w, cc * half, half, 1)
        wqkv = gather(jnp.concatenate([cols(w_query), cols(w_key), cols(w_value)], axis=1))
        small = lax.all_gather(jnp.concatenate(small), "wt", axis=0)
        vec8 = jnp.transpose(small[:, :8 * dim // nw].reshape(nw, 8, dim // nw), (1, 0, 2)).reshape(8, 2, half)
        upb = small[:, 8 * dim // nw:].reshape(2, 4, half)
        sm = jnp.pad(jnp.concatenate([jnp.transpose(vec8, (1, 0, 2)), upb], axis=1).astype(f32), ((0, 0), (0, 4), (0, 0)))
        wo, wu, wd = gather(w_out), gather(w_up), gather(w_down)
        x_all = gather_all(nz, block_in)[0]
        o, ot, lse, k, v, kt, qn, qt = attn_fwd(nz, blk, x_all, wqkv, pick(sm, cc)[0:1], pick(sm, cc)[1:2])
        o_self, o_c, o_y, o_yc = o[0], perm(o[1], xor(1)), perm(o[2], xor(2)), perm(o[3], xor(3))
        mine, other = by_seq(o_self, o_y), by_seq(o_c, o_yc)
        att = jnp.where(cc == 0, jnp.concatenate([mine, other], 1), jnp.concatenate([other, mine], 1))

    out, dsm, d_o, gw, gv = dense(block_in.reshape(-1, dim), cotangent.reshape(-1, dim), att, wo, wu, wd, sm)

    if ours:
        dxo, go, gqo, gvec = back(nz, block_order, gv, d_o.reshape(seqs, rows, dim), x_all, wqkv, k, v, kt, qn, qt, ot, lse, gw)
        return (out.reshape(seqs, rows, dim),) + tuple(last(w_up.shape[1] // dim, go.reshape(-1, dim), gqo, gvec, dxo, dsm.reshape(seqs, rows, dim)))
    d_o = d_o.reshape(seqs, rows, dim)
    d_own, d_oth = pick(d_o, yy), pick(d_o, 1 - yy)
    fh = lambda v, c: lax.dynamic_slice_in_dim(v, c * half, half, 1)
    do_all = jnp.concatenate([fh(d_own, cc), perm(fh(d_own, 1 - cc), xor(1)), perm(fh(d_oth, cc), xor(2)), perm(fh(d_oth, 1 - cc), xor(3))], axis=0)
    dx, gq, gb = attn_bwd(nz, blk, x_all, wqkv, k, v, kt, qn, qt, ot, lse, do_all.reshape(4, rows, half))
    gvec = jnp.zeros((24, dim), f32).at[:16].set(gv)
    gvec = lax.dynamic_update_slice(gvec, gb[0:1], (16, cc * half))
    gvec = lax.dynamic_update_slice(gvec, gb[1:2], (17, cc * half))
    wi = lax.axis_index("wt")
    ff, hr = w_up.shape[1], dim // 2
    nu = ff // dim
    dx = jnp.transpose(dx.reshape(nz, 2, 2, rows, dim), (0, 2, 1, 3, 4)).reshape(nz, 2, 2 * rows, dim)
    part = lambda r: dx[r, 0].astype(f32) + perm(dx[r, 1], xor(1)).astype(f32)
    acc = None
    for r in list(range(1, nz)) + [0]:
        acc = part(r) if acc is None else perm(acc.astype(bf16), ring).astype(f32) + part(r)
    from_y = perm(acc[rows:].astype(bf16), xor(2)).astype(f32)
    dkv_sum = by_seq(acc[:rows], from_y)
    gvec = lax.psum(gvec, ("ctx", "wt"))
    g_out = gw[:, :hr].reshape(dim, dim)
    g_up = gw[:, hr:hr + nu * hr].reshape(2, nu, hr, dim).transpose(0, 2, 1, 3).reshape(dim, ff)
    g_down = gw[:, hr + nu * hr:].reshape(ff, dim)
    gq3 = gq.reshape(2, 3, hr, half).transpose(1, 0, 2, 3).reshape(3, dim, half)
    g_qkv = lax.dynamic_update_slice(jnp.zeros((3, dim, dim), bf16), gq3, (0, 0, cc * half))
    total = lambda g: lax.psum(lax.psum_scatter(g, "wt", scatter_dimension=0, tiled=True), "ctx").astype(f32)
    t_out, t_up, t_down = total(g_out), total(g_up), total(g_down)
    t_qkv = [total(g_qkv[i]) for i in range(3)]
    grad_in = (dsm + dkv_sum).astype(bf16).reshape(seqs, rows, dim)

    def share(vv):
        n = vv.size // nw
        return lax.dynamic_slice_in_dim(vv.reshape(-1), wi * n, n, 0)
    return (out.reshape(seqs, rows, dim), grad_in, t_qkv[0], share(gvec[16]), t_qkv[1], t_qkv[2], share(gvec[17]), t_out, share(gvec[0]),
            share(gvec[1]), share(gvec[2]), t_up, share(gvec[8:8 + nu]), t_down, share(gvec[3]), share(gvec[4]), share(gvec[5]))


def solution(mesh):
    seq, mat, vec = P("wt", "ctx", None), P("wt", None), P("wt")
    ins = (seq, mat, mat, vec, mat, mat, vec, mat, vec, vec, vec, mat, vec, mat, vec, vec, vec, seq)
    outs = (seq, seq, mat, vec, mat, mat, vec, mat, vec, vec, vec, mat, vec, mat, vec, vec, vec)
    run = functools.partial(body, nc=mesh.shape["ctx"], nw=mesh.shape["wt"])
    return jax.shard_map(run, mesh=mesh, in_specs=ins, out_specs=outs, check_vma=False)
```

```python
import functools
import math

import jax
import jax.numpy as jnp
from jax import lax
from jax.experimental import pallas as pl
from jax.experimental.pallas import tpu as pltpu
from jax.sharding import PartitionSpec as P

norm_eps = 1e-05

BLOCK = 128
HEADS_HERE = 4
LOG2E = 1.4426950408889634
FAR = -1e30
bf16, f32 = jnp.bfloat16, jnp.float32
NT = (((1,), (1,)), ((), ()))
TN = (((0,), (0,)), ((), ()))


def dot(a, b, dims=(((1,), (0,)), ((), ()))):
    return lax.dot_general(a, b, dims, preferred_element_type=f32)


def turned(v):
    return v.astype(f32).T.astype(bf16)


def head_slices():
    return [(slice(64 * h, 64 * h + 64), slice(128 * h, 128 * h + 128)) for h in range(HEADS_HERE)]


class Pairs:
    def __init__(self, nb, first):
        self.nb, self.first = nb, first

    def first_lo(self, n):
        return self.first(n) < self.nb // 2

    def lo(self, n):
        b = self.first(n)
        return jnp.where(b < self.nb // 2, b, self.nb - 1 - b)

    def ordered(self, n, v):
        a, b = v[:BLOCK], v[BLOCK:]
        first = self.first_lo(n)
        return jnp.where(first, a, b), jnp.where(first, b, a)


def project_chunk(pairs, r, x_ref, wkv_ref, wkvt_ref, bkv_ref, bkvt_ref, K, V, KT, VT, start=0, stop=4):
    def piece(p, _):
        x = jnp.concatenate(pairs.ordered(r * 4 + p, x_ref[r, p]), axis=0)
        kv = dot(x, wkv_ref[...])
        k, v = kv[:, :256].astype(bf16), (kv[:, 256:] + bkv_ref[...]).astype(bf16)
        kvt = dot(wkvt_ref[...], x, NT)
        kt, vt = kvt[:256].astype(bf16), (kvt[256:] + bkvt_ref[...]).astype(bf16)
        at = pl.ds(pl.multiple_of(p * BLOCK, BLOCK), BLOCK)
        for u in range(2):
            rows = slice(u * BLOCK, (u + 1) * BLOCK)
            K[r, u, at, :] = k[rows]
            V[r, u, at, :] = v[rows]
            KT[r, u, :, at] = kt[:, rows]
            VT[r, u, :, at] = vt[:, rows]
        return 0
    lax.fori_loop(start, stop, piece, 0)


def project_queries(pairs, x_ref, wq_ref, bq_ref, qn, qt, qs):
    qs[...] = jnp.zeros_like(qs)

    def piece(p, _):
        x = jnp.concatenate(pairs.ordered(p, x_ref[0, p]), axis=0)
        q = (dot(x, wq_ref[...]) + bq_ref[...]) * (LOG2E / 8.0)
        for u in range(2):
            mine = q[u * BLOCK:(u + 1) * BLOCK]
            qn[p, u] = mine.astype(bf16)
            t = mine.T.astype(bf16)
            qt[p, u] = t
            for hs, cs in head_slices():
                qs[p, u, hs, cs] = t[hs]
        return 0
    lax.fori_loop(0, 4, piece, 0)


def by_pair(vt, p16):
    return jnp.concatenate([dot(vt[0:128], p16[:, 0:256]), dot(vt[128:256], p16[:, 256:512])], axis=1)


def unpair(a):
    return jnp.concatenate([a[64 * (h % 2):64 * (h % 2) + 64, 128 * h:128 * h + 128] for h in range(HEADS_HERE)], axis=0)


def fwd_step(pairs, r, i, own, K, VT, qs, m_s, l_s, acc, d_s, sb, pb, js=(0, 1, 2, 3)):
    part = slice(js[0] * BLOCK, js[-1] * BLOCK + BLOCK)
    col = lambda v: jnp.max(v, axis=0, keepdims=True)
    tot = lambda v: jnp.sum(v, axis=0, keepdims=True)
    lo_i = pairs.lo(i)
    pick = {j: lo_i > pairs.lo(r * 4 + j) for j in js}
    sa = dot(K[r, 0, part, :], qs[i, 1])
    for j in js:
        u = jnp.where(pick[j], 0, 1)
        s = dot(K[r, u, j * BLOCK:(j + 1) * BLOCK, :], qs[i, u])
        if own:
            s = jnp.where(d_s[...] <= jnp.where(i == j, 0, 2 * BLOCK), s, FAR)
        sb[j] = s
    tops = {j: col(sb[j]) for j in js}
    m_hi, m_lo = col(sa), None
    for j in js:
        m_hi = jnp.maximum(m_hi, jnp.where(pick[j], FAR, tops[j]))
        t = jnp.where(pick[j], tops[j], FAR)
        m_lo = t if m_lo is None else jnp.maximum(m_lo, t)
    if own:
        rows = pl.ds(pl.multiple_of(i * BLOCK, BLOCK), BLOCK)
        sd = jnp.where(d_s[...] <= 0, dot(K[r, 0, rows, :], qs[i, 0]), FAR)
        m_lo = jnp.maximum(m_lo, col(sd))
    else:
        old_hi, old_lo = m_s[i, 1], m_s[i, 0]
        m_hi, m_lo = jnp.maximum(m_hi, old_hi), jnp.maximum(m_lo, old_lo)
    pa = jnp.exp2(sa - m_hi)
    l_hi, l_lo = tot(pa), jnp.zeros((1, 512), f32)
    for j in js:
        p = jnp.exp2(sb[j] - jnp.where(pick[j], m_lo, m_hi))
        t = tot(p)
        l_hi = l_hi + jnp.where(pick[j], 0.0, t)
        l_lo = l_lo + jnp.where(pick[j], t, 0.0)
        low = p.astype(bf16)
        rows = slice(j * BLOCK, (j + 1) * BLOCK)
        zero = jnp.zeros_like(low)
        pb[0, rows, :] = jnp.where(pick[j], low, zero)
        pb[1, rows, :] = jnp.where(pick[j], zero, low)
    o_hi = by_pair(VT[r, 0, :, part], pa.astype(bf16)) + by_pair(VT[r, 1, :, part], pb[1, part, :])
    o_lo = by_pair(VT[r, 0, :, part], pb[0, part, :])
    if own:
        p = jnp.exp2(sd - m_lo)
        l_lo = l_lo + tot(p)
        at = pl.ds(pl.multiple_of(i * BLOCK, BLOCK), BLOCK)
        o_lo = o_lo + by_pair(VT[r, 0, :, at], p.astype(bf16))
        l_s[i, 1], l_s[i, 0] = l_hi, l_lo
        acc[i, 1], acc[i, 0] = o_hi, o_lo
    else:
        f_hi, f_lo = jnp.exp2(old_hi - m_hi), jnp.exp2(old_lo - m_lo)
        l_s[i, 1] = l_s[i, 1] * f_hi + l_hi
        l_s[i, 0] = l_s[i, 0] * f_lo + l_lo
        acc[i, 1] = acc[i, 1] * f_hi + o_hi
        acc[i, 0] = acc[i, 0] * f_lo + o_lo
    m_s[i, 1], m_s[i, 0] = m_hi, m_lo


def fwd_finish(pairs, i, m_s, l_s, acc, lse, ot, o_ref):
    first = pairs.first_lo(i)
    out = []
    for u in range(2):
        l = l_s[i, u]
        lse[i, u] = m_s[i, u] + jnp.log2(l)
        t = unpair(acc[i, u] * (1.0 / l))
        ot[i, u] = t
        out.append(t.T.astype(bf16))
    o_ref[i, 0:BLOCK, :] = jnp.where(first, out[0], out[1])
    o_ref[i, BLOCK:2 * BLOCK, :] = jnp.where(first, out[1], out[0])


def diagonal(d_s):
    d_s[...] = lax.broadcasted_iota(jnp.int32, d_s.shape, 0) - (lax.broadcasted_iota(jnp.int32, d_s.shape, 1) & (BLOCK - 1))


def fwd_local(nz, blk_ref, x_ref, wqkv_ref, bq_ref, bkv_ref, bkvt_ref, o_ref, ot, lse, K, V, KT, qn, qt, VT, qs, m_s, l_s, acc, d_s, sb, pb, wkvt):
    pairs = Pairs(nz * 8, lambda n: blk_ref[2 * n])
    diagonal(d_s)
    wkvt[...] = turned(wqkv_ref[:, 256:])
    project_queries(pairs, x_ref, wqkv_ref.at[:, 0:256], bq_ref, qn, qt, qs)
    for r in range(nz):
        project_chunk(pairs, r, x_ref, wqkv_ref.at[:, 256:768], wkvt, bkv_ref, bkvt_ref, K, V, KT, VT)
        def step(i, _):
            fwd_step(pairs, r, i, r == 0, K, VT, qs, m_s, l_s, acc, d_s, sb, pb)
            return 0
        lax.fori_loop(0, 4, step, 0)
    for i in range(4):
        fwd_finish(pairs, i, m_s, l_s, acc, lse, ot, o_ref)


def fwd_outs(nz):
    sds = jax.ShapeDtypeStruct
    kv = sds((nz, 2, 512, 256), bf16)
    return (sds((4, 256, 256), bf16), sds((4, 2, 256, 128), f32), sds((4, 2, 1, 512), f32), kv, kv, sds((nz, 2, 256, 512), bf16),
            sds((4, 2, 128, 256), bf16), sds((4, 2, 256, 128), bf16))


def fwd_scratch(nz):
    M = pltpu.VMEM
    return [M((nz, 2, 256, 512), bf16), M((4, 2, 256, 512), bf16), M((4, 2, 1, 512), f32), M((4, 2, 1, 512), f32), M((4, 2, 128, 512), f32),
            M((128, 512), jnp.int32), M((4, 128, 512), f32), M((2, 512, 512), bf16), M((512, 512), bf16)]


def attn_fwd(nz, blk, x, wqkv, bq, bkv):
    V = pl.BlockSpec(memory_space=pltpu.VMEM)
    return pl.pallas_call(
        functools.partial(fwd_local, nz), out_shape=fwd_outs(nz),
        in_specs=[pl.BlockSpec(memory_space=pltpu.SMEM)] + [V] * 5, out_specs=(V,) * 8, scratch_shapes=fwd_scratch(nz),
        compiler_params=pltpu.CompilerParams(vmem_limit_bytes=58 << 20), name="attn_fwd")(blk, x, wqkv, bq, bkv, bkv.reshape(256, 1))


def bwd_query(pairs, i, do_ref, ot, qn, qt, qs, dos, qns, dons, dl):
    for u, do in enumerate(pairs.ordered(i, do_ref[i])):
        dot_t = do.astype(f32).T
        prod = dot_t * ot[i, u]
        low = dot_t.astype(bf16)
        q, t = qn[i, u], qt[i, u]
        for hs, cs in head_slices():
            qs[i, u, hs, cs] = t[hs]
            dos[i, u, hs, cs] = low[hs]
            qns[i, u, cs, hs] = q[:, hs]
            dons[i, u, cs, hs] = do[:, hs]
            dl[i, u, :, cs] = jnp.sum(prod[hs], axis=0, keepdims=True)


def bwd_step(pairs, r, i, own, first, K, V, KT, qs, dos, qns, dons, lse, dl, dk, dv, dq, d_s, gb, js=(0, 1, 2, 3)):
    lo_i = pairs.lo(i)
    pick = {j: lo_i > pairs.lo(r * 4 + j) for j in js}
    part = slice(js[0] * BLOCK, js[-1] * BLOCK + BLOCK)

    def pieces(k, v, u, mask):
        s = dot(k, qs[i, u]) - lse[i, u]
        if mask is not None:
            s = jnp.where(d_s[...] <= mask, s, FAR)
        p = jnp.exp2(s)
        g = p * (dot(v, dos[i, u]) - dl[i, u])
        return p.astype(bf16), g.astype(bf16)

    p, g = pieces(K[r][0, part, :], V[r][0, part, :], 1, None)
    dv[0, part, :] += dot(p, dons[i, 1])
    dk[0, part, :] += dot(g, qns[i, 1])
    q_hi = by_pair(KT[r][0, :, part], g)
    for j in js:
        u = jnp.where(pick[j], 0, 1)
        rows = slice(j * BLOCK, (j + 1) * BLOCK)
        p, g = pieces(K[r][u, rows, :], V[r][u, rows, :], u, jnp.where(i == j, 0, 2 * BLOCK) if own else None)
        gv, gk = dot(p, dons[i, u]), dot(g, qns[i, u])
        dv[0, rows, :] += jnp.where(pick[j], gv, 0.0)
        dv[1, rows, :] += jnp.where(pick[j], 0.0, gv)
        dk[0, rows, :] += jnp.where(pick[j], gk, 0.0)
        dk[1, rows, :] += jnp.where(pick[j], 0.0, gk)
        zero = jnp.zeros_like(g)
        gb[0, rows, :] = jnp.where(pick[j], g, zero)
        gb[1, rows, :] = jnp.where(pick[j], zero, g)
    q_hi = q_hi + by_pair(KT[r][1, :, part], gb[1, part, :])
    q_lo = by_pair(KT[r][0, :, part], gb[0, part, :])
    if own:
        rows = pl.ds(pl.multiple_of(i * BLOCK, BLOCK), BLOCK)
        p, g = pieces(K[r][0, rows, :], V[r][0, rows, :], 0, 0)
        dv[0, rows, :] += dot(p, dons[i, 0])
        dk[0, rows, :] += dot(g, qns[i, 0])
        q_lo = q_lo + by_pair(KT[r][0, :, rows], g)
    if first:
        dq[i, 1], dq[i, 0] = q_hi, q_lo
    else:
        dq[i, 1] += q_hi
        dq[i, 0] += q_lo


def bwd_chunk_weights(pairs, r, x_ref, dk, dv, dw, db, gp, js=(0, 1, 2, 3)):
    total = jnp.zeros((1, 256), f32)
    for p in js:
        at = slice(p * BLOCK, (p + 1) * BLOCK)
        g = [jnp.concatenate([(dk[u, at, :] * (1.0 / LOG2E)).astype(bf16), dv[u, at, :].astype(bf16)], axis=1) for u in range(2)]
        total = total + jnp.sum(g[0][:, 256:].astype(f32), axis=0, keepdims=True) + jnp.sum(g[1][:, 256:].astype(f32), axis=0, keepdims=True)
        first = pairs.first_lo(r * 4 + p)
        gp[p * 256:p * 256 + BLOCK, :] = jnp.where(first, g[0], g[1])
        gp[p * 256 + BLOCK:p * 256 + 256, :] = jnp.where(first, g[1], g[0])
    db[1:2, :] += total
    n = len(js)
    dw[:, 256:768] += dot(x_ref[r, js[0]:js[0] + n].reshape(n * 256, 512), gp[js[0] * 256:(js[0] + n) * 256, :], TN)


def bwd_chunk_rows(r, last, wqkv_ref, dxq, dx, gp, js=(1, 3, 0, 2)):
    for p in js:
        rows = slice(p * 256, p * 256 + 256)
        d = dot(gp[rows, :], wqkv_ref[:, 256:768], NT)
        if last:
            d = d + dxq[p]
        dx[r, rows, :] = d.astype(bf16)


def bwd_query_out(pairs, x_ref, wqkv_ref, dq, dxq, dw, db):
    def piece(i, _):
        t = [(unpair(dq[i, u]) * 0.125).T.astype(bf16) for u in range(2)]
        first = pairs.first_lo(i)
        g = jnp.concatenate([jnp.where(first, t[0], t[1]), jnp.where(first, t[1], t[0])], axis=0)
        dxq[i] = dot(g, wqkv_ref[:, 0:256], NT)
        dw[:, 0:256] += dot(x_ref[0, i], g, TN)
        db[0:1, :] += jnp.sum(g.astype(f32), axis=0, keepdims=True)
        return 0
    lax.fori_loop(0, 4, piece, 0)


def weight_rows(dw, gq):
    for k in range(2):
        for m in range(3):
            gq[k, m * 256:m * 256 + 256, :] = dw[k * 256:k * 256 + 256, m * 256:m * 256 + 256].astype(bf16)


def bwd_local(nz, blk_ref, x_ref, wqkv_ref, K, V, KT, qn, qt, ot, lse, do_ref, dx, gq, db, qs, dos, qns, dons, dl, dk, dv, dq, d_s, gb, dxq, dw, gp):
    pairs = Pairs(nz * 8, lambda n: blk_ref[2 * n])
    kv = [[a.at[r] for r in range(nz)] for a in (K, V, KT)]
    diagonal(d_s)
    dw[...] = jnp.zeros_like(dw)
    db[...] = jnp.zeros_like(db)
    for s in (qs, dos, qns, dons):
        s[...] = jnp.zeros_like(s)
    for i in range(4):
        bwd_query(pairs, i, do_ref, ot, qn, qt, qs, dos, qns, dons, dl)
    for r in list(range(1, nz)) + [0]:
        dk[...] = jnp.zeros_like(dk)
        dv[...] = jnp.zeros_like(dv)
        def step(i, _):
            bwd_step(pairs, r, i, r == 0, r == 1, *kv, qs, dos, qns, dons, lse, dl, dk, dv, dq, d_s, gb)
            return 0
        lax.fori_loop(0, 4, step, 0)
        if r == 0:
            bwd_query_out(pairs, x_ref, wqkv_ref, dq, dxq, dw, db)
        bwd_chunk_weights(pairs, r, x_ref, dk, dv, dw, db, gp)
        bwd_chunk_rows(r, r == 0, wqkv_ref, dxq, dx, gp)
    weight_rows(dw, gq)


def bwd_scratch():
    M = pltpu.VMEM
    return [M((4, 2, 256, 512), bf16), M((4, 2, 256, 512), bf16), M((4, 2, 512, 256), bf16), M((4, 2, 512, 256), bf16), M((4, 2, 1, 512), f32),
            M((2, 512, 256), f32), M((2, 512, 256), f32), M((4, 2, 128, 512), f32), M((128, 512), jnp.int32), M((2, 512, 512), bf16),
            M((4, 256, 512), f32), M((512, 768), f32)]


def attn_bwd(nz, blk, x, wqkv, K, V, KT, qn, qt, ot, lse, do):
    S = pl.BlockSpec(memory_space=pltpu.VMEM)
    sds = jax.ShapeDtypeStruct
    return pl.pallas_call(
        functools.partial(bwd_local, nz), out_shape=(sds((nz, 1024, 512), bf16), sds((2, 768, 256), bf16), sds((8, 256), f32)),
        in_specs=[pl.BlockSpec(memory_space=pltpu.SMEM)] + [S] * 10, out_specs=(S,) * 3, scratch_shapes=bwd_scratch() + [pltpu.VMEM((1024, 512), bf16)],
        compiler_params=pltpu.CompilerParams(vmem_limit_bytes=58 << 20), name="attn_bwd")(blk, x, wqkv, K, V, KT, qn, qt, ot, lse, do)


def dense_kernel(x_ref, cot_ref, att_ref, wo_ref, wu_ref, wd_ref, sm_ref,
                 out_ref, dsm_ref, do_ref, gw_ref, gv_ref, act_s, gp_s, norm_s, dpre_s):
    ff = wu_ref.shape[1]
    chunk = 512
    x = x_ref[...].astype(f32)
    vec = lambda i: jnp.concatenate([sm_ref[0, i:i + 1, :], sm_ref[1, i:i + 1, :]], axis=1)
    b_out, g1, s1, b_down, g2, s2 = (vec(i) for i in range(2, 8))
    mean = lambda v: jnp.mean(v, axis=-1, keepdims=True)
    col = lambda v: jnp.sum(v, axis=0, keepdims=True)
    mix = x + dot(att_ref[...], wo_ref[...]) + b_out
    cen = mix - mean(mix)
    r1 = lax.rsqrt(mean(cen * cen) + norm_eps)
    n1 = cen * r1
    normed = n1 * g1 + s1
    nlow = normed.astype(bf16)
    norm_s[...] = nlow
    ffn = None
    for f in range(0, ff, chunk):
        fs = slice(f, f + chunk)
        at = 8 + f % (ff // 2) // 256
        b_up = jnp.concatenate([sm_ref[2 * f // ff, at + k:at + k + 1, :] for k in range(chunk // 256)], axis=1)
        pre = dot(nlow, wu_ref[:, fs]) + b_up
        c0 = math.sqrt(2.0 / math.pi)
        sq = pre * pre
        th = jnp.tanh(c0 * pre * (1.0 + 0.044715 * sq))
        half = 0.5 * (1.0 + th)
        act = (pre * half).astype(bf16)
        act_s[:, fs] = act
        gp_s[:, fs] = half + 0.5 * pre * (1.0 - th * th) * (c0 * (1.0 + 3 * 0.044715 * sq))
        part = dot(act, wd_ref[fs, :])
        ffn = part if ffn is None else ffn + part
    summed = ffn + b_down + normed + x
    cen = summed - mean(summed)
    r2 = lax.rsqrt(mean(cen * cen) + norm_eps)
    n2 = cen * r2
    out_ref[...] = (n2 * g2 + s2).astype(bf16)
    up = cot_ref[...].astype(f32)
    gv_ref[4:5, :] = col(up * n2)
    gv_ref[5:6, :] = col(up)
    dn = up * g2
    dsum = r2 * (dn - mean(dn) - n2 * mean(dn * n2))
    dffn = dsum.astype(bf16)
    gv_ref[3:4, :] = col(dffn.astype(f32))
    dnorm = dsum
    half_rows = wo_ref.shape[0] // 2
    half_ff = ff // 2
    def put(g, at, rows):
        gw_ref[0, at:at + rows, :] = g[:rows].astype(bf16)
        gw_ref[1, at:at + rows, :] = g[rows:].astype(bf16)
    for f in range(0, ff, chunk):
        fs = slice(f, f + chunk)
        dact = dot(dffn, wd_ref[fs, :], NT)
        dpre = (dact * gp_s[:, fs]).astype(bf16)
        gv_ref[8 + f // chunk:9 + f // chunk, :] = col(dpre.astype(f32))
        dnorm = dnorm + dot(dpre, wu_ref[:, fs], NT)
        put(dot(norm_s[...], dpre, TN), half_rows + (f // chunk) * half_rows, half_rows)
        gd = dot(act_s[:, fs], dffn, TN).astype(bf16)
        base = half_rows * (1 + ff // chunk)
        which, off = f // half_ff, f % half_ff
        gw_ref[which, base + off:base + off + chunk, :] = gd
    gv_ref[1:2, :] = col(dnorm * n1)
    gv_ref[2:3, :] = col(dnorm)
    dn = dnorm * g1
    dmix = r1 * (dn - mean(dn) - n1 * mean(dn * n1))
    dsm_ref[...] = dsum + dmix
    dbr = dmix.astype(bf16)
    gv_ref[0:1, :] = col(dbr.astype(f32))
    do_ref[...] = dot(dbr, wo_ref[...], NT).astype(bf16)
    put(dot(att_ref[...], dbr, TN), 0, half_rows)


def dense(x, cot, att, wo, wu, wd, sm):
    V = pl.BlockSpec(memory_space=pltpu.VMEM)
    tok, dim = x.shape
    ff = wu.shape[1]
    rows = (2 * dim * ff + dim * dim) // 2 // dim
    return pl.pallas_call(
        dense_kernel,
        out_shape=(jax.ShapeDtypeStruct((tok, dim), bf16), jax.ShapeDtypeStruct((tok, dim), f32),
                   jax.ShapeDtypeStruct((tok, dim), bf16), jax.ShapeDtypeStruct((2, rows, dim), bf16),
                   jax.ShapeDtypeStruct((16, dim), f32)),
        in_specs=[V] * 7, out_specs=(V,) * 5,
        scratch_shapes=[pltpu.VMEM((tok, ff), bf16), pltpu.VMEM((tok, ff), f32), pltpu.VMEM((tok, dim), bf16),
                        pltpu.VMEM((8, 128), f32)],
        compiler_params=pltpu.CompilerParams(vmem_limit_bytes=56 << 20),
        name="dense")(x, cot, att, wo, wu, wd, sm)


MESH = pl.DeviceIdType.MESH


def places(nz):
    me, wi = lax.axis_index("ctx"), lax.axis_index("wt")
    z, y, c = me // 4, lax.rem(me // 2, 2), lax.rem(me, 2)
    low = lax.rem(me, 4)
    at = lambda zz, ll: (zz * 4 + ll, wi)
    to = dict(up=at(lax.rem(z + 1, nz), low), down=at(lax.rem(z + nz - 1, nz), low), core=at(z, low + 1 - 2 * c), y=at(z, low + 2 - 4 * y),
              x=(me, 1 - wi))
    return me, wi, z, y, c, low, to


def meet(targets):
    bar = pltpu.get_barrier_semaphore()
    for t in targets:
        pl.semaphore_signal(bar, inc=1, device_id=t, device_id_type=MESH)
    pl.semaphore_wait(bar, len(targets))


class Wires:
    def __init__(self, send, recv):
        self.send, self.recv, self.n, self.live = send, recv, 0, []

    def make(self, src, dst, to):
        cp = pltpu.make_async_remote_copy(src, dst, self.send.at[self.n], self.recv.at[self.n], device_id=to, device_id_type=MESH)
        self.n += 1
        self.live.append(cp)
        return cp

    def go(self, src, dst, to):
        cp = self.make(src, dst, to)
        cp.start()
        return cp

    def drain(self):
        for cp in self.live:
            cp.wait_send()


def rows_of(start, size, mult=16):
    return pl.ds(pl.multiple_of(start, mult), size)


def gather_kernel(nz, with_w, *refs):
    if with_w:
        (x_ref, wq_ref, wk_ref, wv_ref, wo_ref, wu_ref, wd_ref, sm_ref,
         xall, wqkv, wo, wu, wd, sm, send, recv, lsem) = refs
    else:
        x_ref, xall, send, recv, lsem = refs
    me, wi, z, y, c, low, to = places(nz)
    rows = x_ref.shape[1]
    local = []

    def copy(src, dst):
        cp = pltpu.make_async_copy(src, dst, lsem.at[len(local)])
        cp.start()
        local.append(cp)

    copy(x_ref.at[y], xall.at[0, 0])
    if with_w:
        R, half = wq_ref.shape[0], wq_ref.shape[1] // 2
        for i, w in enumerate((wq_ref, wk_ref, wv_ref)):
            copy(w.at[:, rows_of(c * half, half, 128)], wqkv.at[rows_of(wi * R, R), pl.ds(i * half, half)])
        for w, full in ((wo_ref, wo), (wu_ref, wu), (wd_ref, wd)):
            n = w.shape[0]
            copy(w, full.at[rows_of(wi * n, n)])
        copy(sm_ref, sm.at[wi])
    near = [to["up"], to["down"], to["core"], to["y"]] + ([to["x"]] if with_w else [])
    meet(near)
    wires = Wires(send, recv)
    yx = wires.go(x_ref.at[1 - y], xall.at[0, 2], to["y"])
    ring = {(1, 0): wires.go(x_ref.at[y], xall.at[1, 0], to["up"])}
    core = {(0, 0): wires.go(x_ref.at[y], xall.at[0, 1], to["core"])}
    if with_w:
        xs = []
        for i, w in enumerate((wq_ref, wk_ref, wv_ref)):
            xs.append(wires.go(w.at[:, rows_of(c * half, half, 128)], wqkv.at[rows_of(wi * R, R), pl.ds(i * half, half)], to["x"]))
        xs.append(wires.go(sm_ref, sm.at[wi], to["x"]))
        big = []
        for w, full in ((wo_ref, wo), (wu_ref, wu), (wd_ref, wd)):
            n = w.shape[0]
            h = n // 2
            cp = wires.go(w.at[rows_of(c * h, h)], full.at[rows_of(wi * n + c * h, h)], to["x"])
            big.append((cp, full, rows_of((1 - wi) * n + c * h, h)))
    yx.wait_recv()
    ring[1, 1] = wires.go(xall.at[0, 2], xall.at[1, 2], to["up"])
    core[0, 1] = wires.go(xall.at[0, 2], xall.at[0, 3], to["core"])
    shared = []
    for r in range(1, nz):
        for s in range(2):
            ring[r, s].wait_recv()
            if r < nz - 1:
                ring[r + 1, s] = wires.go(xall.at[r, 2 * s], xall.at[r + 1, 2 * s], to["up"])
            core[r, s] = wires.go(xall.at[r, 2 * s], xall.at[r, 2 * s + 1], to["core"])
        if with_w and r - 1 < len(big):
            cp, full, where = big[r - 1]
            cp.wait_recv()
            shared.append(wires.go(full.at[where], full.at[where], to["core"]))
    if with_w:
        for cp, full, where in big[nz - 1:]:
            cp.wait_recv()
            shared.append(wires.go(full.at[where], full.at[where], to["core"]))
        for cp in xs + shared:
            cp.wait_recv()
    for cp in core.values():
        cp.wait_recv()
    wires.drain()
    for cp in local:
        cp.wait()


def gather_all(nz, x, weights=None, small=None):
    A = pl.BlockSpec(memory_space=pl.ANY)
    sds = jax.ShapeDtypeStruct
    rows, dim = x.shape[1:]
    outs = [sds((nz, 4, rows, dim), bf16)]
    ins = [x]
    ncopy = 1 + 2 * (nz - 1) + 2 * nz
    if weights is not None:
        wq, wk, wv, wo, wu, wd = weights
        ins += list(weights) + [small]
        outs += [sds((dim, 3 * dim // 2), bf16)] + [sds((2 * w.shape[0], w.shape[1]), bf16) for w in (wo, wu, wd)] + [sds((2,) + small.shape, bf16)]
        ncopy += 10
    return pl.pallas_call(
        functools.partial(gather_kernel, nz, weights is not None),
        out_shape=tuple(outs), in_specs=[A] * len(ins), out_specs=(A,) * len(outs),
        scratch_shapes=[pltpu.SemaphoreType.DMA((ncopy,)), pltpu.SemaphoreType.DMA((ncopy,)), pltpu.SemaphoreType.DMA((8,))],
        compiler_params=pltpu.CompilerParams(collective_id=1, has_side_effects=True, vmem_limit_bytes=16 << 20),
        name="gather_all")(*ins)


def add_into(dst, parts, rows, step=64):
    def body(i, _):
        r = rows_of(i * step, step)
        total = parts[0](r)[...].astype(f32)
        for p in parts[1:]:
            total = total + p(r)[...].astype(f32)
        d = dst(r)
        d[...] = total.astype(bf16)
        return 0
    lax.fori_loop(0, rows // step, body, 0)


def offset(ref, lead, start):
    def view(r):
        at = pl.ds(pl.multiple_of(start + r.start, 16), r.size)
        return ref.at[lead + (at,)]
    return view


def chip_pairs(nz, order_ref):
    me = lax.axis_index("ctx")
    z, y, c = me // 4, lax.rem(me // 2, 2), lax.rem(me, 2)

    def first(n):
        r, p = n // 4, n % 4
        a, b = p // 2, p % 2
        yy, cc = y + a - 2 * y * a, c + b - 2 * c * b
        return order_ref[y, 2 * (lax.rem(z - r + nz, nz) * 4 + yy * 2 + cc)]
    return Pairs(nz * 8, first)


def front_kernel(nz, order_ref, bqr, bvr, bor, g1r, s1r, bdr, g2r, s2r, bur, x_ref, wq_ref, wk_ref, wv_ref, wo_ref, wu_ref, wd_ref,
                 att, wo, wu, wd, sm, xall, wqkv, ot_o, lse_o, K_o, V_o, KT_o, qn_o, qt_o,
                 xs, ws, sms, wos, wus, wds, K, V, KT, VT, qn, qt, qs, m_s, l_s, acc, d_s, sb, pb, wkvt, bkvt, ot, lse, o_s, send, recv, lsem):
    me, wi, z, y, c, low, to = places(nz)
    to["yc"] = (z * 4 + 3 - low, wi)
    half, R = 256, wq_ref.shape[0]
    local = []

    def copy(src, dst):
        cp = pltpu.make_async_copy(src, dst, lsem.at[len(local)])
        cp.start()
        local.append(cp)
        return cp

    own_x = copy(x_ref.at[y], xs.at[0, 0])
    own_w = [copy(w.at[:, rows_of(c * half, half, 128)], ws.at[rows_of(wi * R, R), pl.ds(i * half, half)]) for i, w in enumerate((wq_ref, wk_ref, wv_ref))]
    for i, v in enumerate((bqr, bvr, bor, g1r, s1r, bdr, g2r, s2r)):
        sms[wi, i:i + 1, :] = v[...].astype(f32).reshape(1, half)
    up_b = bur[...].astype(f32).reshape(1, 1024)
    for i in range(4):
        sms[wi, 8 + i:9 + i, :] = up_b[:, i * half:(i + 1) * half]
    sms[wi, 12:16, :] = jnp.zeros((4, half), f32)
    meet([to[k] for k in ("up", "down", "core", "y", "yc", "x")])
    w = Wires(send, recv)
    yx = w.go(x_ref.at[1 - y], xs.at[0, 2], to["y"])
    ring, core = {}, {}
    ring[1, 0] = w.go(x_ref.at[y], xs.at[1, 0], to["up"])
    core[0, 0] = w.go(x_ref.at[y], xs.at[0, 1], to["core"])
    wx = []
    for i, m in enumerate((wq_ref, wk_ref, wv_ref)):
        wx.append(w.go(m.at[:, rows_of(c * half, half, 128)], ws.at[rows_of(wi * R, R), pl.ds(i * half, half)], to["x"]))
    wx.append(w.go(sms.at[wi], sms.at[wi], to["x"]))
    big = []
    for m, full in ((wo_ref, wos), (wu_ref, wus), (wd_ref, wds)):
        n = m.shape[0]
        h = n // 2
        copy(m, full.at[rows_of(wi * n, n)])
        big.append((m.at[rows_of(c * h, h)], full.at[rows_of(wi * n + c * h, h)], full, rows_of((1 - wi) * n + c * h, h)))

    pairs = chip_pairs(nz, order_ref)
    diagonal(d_s)
    yx.wait_recv()
    ring[1, 1] = w.go(xs.at[0, 2], xs.at[1, 2], to["up"])
    core[0, 1] = w.go(xs.at[0, 2], xs.at[0, 3], to["core"])

    def pump(r, s):
        ring[r, s].wait_recv()
        if r < nz - 1:
            ring[r + 1, s] = w.go(xs.at[r, 2 * s], xs.at[r + 1, 2 * s], to["up"])
        core[r, s] = w.go(xs.at[r, 2 * s], xs.at[r, 2 * s + 1], to["core"])

    shared = []

    def share(k):
        cp, full, where = sent[k]
        cp.wait_recv()
        shared.append(w.go(full.at[where], (wo, wu, wd)[k].at[where], to["core"]))

    pump(1, 0)
    for cp in own_w:
        cp.wait()
    for cp in wx:
        cp.wait_recv()
    sent = [(w.go(src, dst, to["x"]), full, where) for src, dst, full, where in big]
    copy(sms, sm)
    copy(ws, wqkv)
    wkvt[...] = turned(ws[:, 256:])
    bv = sms[c, 1:2, :]
    bkvt[...] = jnp.broadcast_to(bv, (8, half)).T[:, 0:1]
    own_x.wait()
    core[0, 0].wait_recv()
    core[0, 1].wait_recv()
    project_queries(pairs, xs, ws.at[:, 0:256], sms.at[c, 0:1], qn, qt, qs)
    copy(qn, qn_o)
    copy(qt, qt_o)

    def bring(r, s):
        if r:
            core[r, s].wait_recv()
        project_chunk(pairs, r, xs, ws.at[:, 256:768], wkvt, sms.at[c, 1:2], bkvt, K, V, KT, VT, 2 * s, 2 * s + 2)
        for a, b in ((xs, xall), (K, K_o), (V, V_o), (KT, KT_o)):
            if s:
                copy(a.at[r], b.at[r])

    def attend(r, js, last=False):
        def step(n, _):
            i = lax.rem(n + 2, 4) if last else n
            fwd_step(pairs, r, i, r == 0, K, VT, qs, m_s, l_s, acc, d_s, sb, pb, js)
            if last:
                fwd_finish(pairs, i, m_s, l_s, acc, lse, ot, o_s)
                for p in outs:
                    pl.when(i == p)(outs[p].start)
            return 0
        lax.fori_loop(0, 4, step, 0)

    def half_chunk(r, s, last=False):
        bring(r, s)
        attend(r, (2 * s, 2 * s + 1), last)

    cols = pl.ds(pl.multiple_of(c * half, half), half)
    outs = {p: w.make(o_s.at[p], att.at[y, :, cols], to[k]) for p, k in ((2, "y"), (3, "yc"), (1, "core"))}
    bring(0, 0)
    bring(0, 1)
    pump(1, 1)
    attend(0, (0, 1, 2, 3))
    for k, (a, b) in enumerate(((wos, wo), (wus, wu), (wds, wd))):
        local[4 + k].wait()
        n = a.shape[0] // 2
        copy(a.at[rows_of(wi * n, n)], b.at[rows_of(wi * n, n)])
    pump(2, 0)
    for r in range(1, nz - 1):
        half_chunk(r, 0)
        if r > 1:
            pump(r + 1, 0)
        half_chunk(r, 1)
        if r < nz - 2:
            pump(r + 1, 1)
    half_chunk(nz - 1, 0)
    pump(nz - 1, 1)
    half_chunk(nz - 1, 1, True)
    copy(o_s.at[0], att.at[y, :, cols])
    copy(ot, ot_o)
    copy(lse, lse_o)
    for k, (a, b) in enumerate(((wos, wo), (wus, wu), (wds, wd))):
        share(k)
        copy(a.at[sent[k][2]], b.at[sent[k][2]])
    for cp in shared:
        cp.wait_recv()
    for cp in outs.values():
        cp.wait_recv()
    w.drain()
    for cp in local[7:]:
        cp.wait()


def front(nz, order, vectors, x, weights):
    A = pl.BlockSpec(memory_space=pltpu.HBM)
    V = pl.BlockSpec(memory_space=pltpu.VMEM)
    sds = jax.ShapeDtypeStruct
    M = pltpu.VMEM
    rows, dim = x.shape[1:]
    wq, wk, wv, wo, wu, wd = weights
    outs = [sds((2, rows, dim), bf16)] + [sds((2 * w.shape[0], w.shape[1]), bf16) for w in (wo, wu, wd)]
    outs += [sds((2, 16, 256), f32), sds((nz, 4, rows, dim), bf16), sds((dim, 768), bf16)] + list(fwd_outs(nz)[1:])
    scratch = [M((nz, 4, rows, dim), bf16), M((dim, 768), bf16), M((2, 16, 256), f32)] + [M(o.shape, bf16) for o in outs[1:4]]
    scratch += [M((nz, 2, 512, 256), bf16)] * 2 + [M((nz, 2, 256, 512), bf16)] * 2 + [M((4, 2, 128, 256), bf16), M((4, 2, 256, 128), bf16)]
    scratch += fwd_scratch(nz)[1:] + [M((256, 1), f32), M((4, 2, 256, 128), f32), M((4, 2, 1, 512), f32), M((4, 256, 256), bf16)]
    scratch += [pltpu.SemaphoreType.DMA((40,)), pltpu.SemaphoreType.DMA((40,)), pltpu.SemaphoreType.DMA((40,))]
    return pl.pallas_call(
        functools.partial(front_kernel, nz), out_shape=tuple(outs),
        in_specs=[pl.BlockSpec(memory_space=pltpu.SMEM)] + [V] * 9 + [A] * 7, out_specs=(A,) * len(outs), scratch_shapes=scratch,
        compiler_params=pltpu.CompilerParams(collective_id=1, has_side_effects=True, vmem_limit_bytes=58 << 20), name="front")(
            order, *vectors, x, *weights)


def back_kernel(nz, order_ref, gv_ref, do_ref, x_hbm, w_hbm, K_h, V_h, KT_h, qn_h, qt_h, ot_h, lse_h, gw_ref,
                dxo, go, gqo, gvo,
                xs, wqkv, K, V, KT, qn, qt, ot, lse, do, qs, dos, qns, dons, dl, dk, dv, dq, d_s, gb, dxq, dw, dx, gp, gq, db, outdx,
                dx_core, dx_in, cr, cs, xr, xs_, yr, ys_, za, zs, zb, xrq, xsq, yrq, ysq, zrq, gsum, gqsum, gvs, gvr, send, recv, lsem):
    me, wi, z, y, c, low, to = places(nz)
    to["yc"] = (z * 4 + 3 - low, wi)
    zto = [(lax.rem(z + d, nz) * 4 + low, wi) for d in range(1, nz)]
    half, hrow = 256, 256
    w = Wires(send, recv)
    local = []

    def copy(src, dst):
        cp = pltpu.make_async_copy(src, dst, lsem.at[len(local)])
        cp.start()
        local.append(cp)
        return cp

    cols = pl.ds(pl.multiple_of(c * half, half), half)
    other = pl.ds(pl.multiple_of((1 - c) * half, half), half)
    meet([to[k] for k in ("core", "y", "yc", "x")] + zto)
    dos_in = [w.go(do_ref.at[1 - y, :, cols], do.at[2], to["y"]), w.go(do_ref.at[1 - y, :, other], do.at[3], to["yc"]),
              w.go(do_ref.at[y, :, other], do.at[1], to["core"])]
    got = {}
    for s in range(3):
        got["c", s] = w.go(gw_ref.at[:, rows_of(s * 768 + (1 - c) * 384, 384)], cr.at[s], to["core"])
    mine_gw = [copy(gw_ref.at[:, rows_of(s * 768 + c * 384, 384)], cs.at[s]) for s in range(3)]
    first_in = [copy(do_ref.at[y, :, cols], do.at[0])] + [copy(a, b) for a, b in ((qn_h, qn), (qt_h, qt), (ot_h, ot), (lse_h, lse))]
    kv_in = {}
    for r in list(range(1, nz)) + [0]:
        kv_in[r] = [copy(a.at[r], b[r]) for a, b in ((K_h, K), (V_h, V), (KT_h, KT))]
    for r in kv_in:
        kv_in[r].append(copy(x_hbm.at[r], xs.at[r]))
    w_in = copy(w_hbm, wqkv)

    n = range(5)
    wide = [384, 192, 48]
    zp = (z + 1 - 2 * lax.rem(z, 2)) * 4 + low, wi
    zq = (z + 2 - 4 * (z // 2)) * 4 + low, wi
    odd, far = lax.rem(z, 2), z // 2
    X_in = [xr.at[s] for s in range(3)] + [xrq.at[s] for s in range(2)]
    X_sum = [xs_.at[s] for s in range(3)] + [xsq.at[s] for s in range(2)]
    Y_in = [yr.at[s] for s in range(3)] + [yrq.at[s] for s in range(2)]
    Y_sum = [ys_.at[s] for s in range(3)] + [ysq.at[s] for s in range(2)]
    Z_in = [zrq.at[s] for s in range(2)]
    out = [gsum.at[s] for s in range(3)] + [gqsum.at[s] for s in range(2)]
    done = [go.at[s] for s in range(3)] + [gqo.at[s] for s in range(2)]
    start_c, start_y = c * 384, c * 384 + y * 192
    at_c, at_y = rows_of(start_c, 384), rows_of(start_y, 192)
    pos = odd * 2 + far
    start_p, start_h = start_y + pos * 48, start_y + odd * 96
    at_p, at_h = rows_of(start_p, 48), rows_of(start_h, 96)
    start_z = start_y + z * 48
    at_z = rows_of(start_z, 48)
    theirs = rows_of((1 - y) * 192, 192)
    for s in n:
        got["x", s] = w.make(cs.at[s, 1 - wi] if s < 3 else gq.at[1 - wi, pl.ds((s - 3) * 384, 384)], X_in[s], to["x"])
        got["y", s] = w.make(X_sum[s].at[theirs], Y_in[s], to["y"])
        got["ys", s] = w.make(out[s].at[at_y], out[s].at[at_y], to["y"])
        got["cs", s] = w.make(out[s].at[at_c], done[s].at[at_c], to["core"])
        if s < 3:
            got["za", s] = w.make(ys_.at[s, rows_of((1 - odd) * 96, 96)], za.at[s], zp)
            got["zb", s] = w.make(zs.at[s, rows_of((1 - far) * 48, 48)], zb.at[s], zq)
            got["zc", s] = w.make(out[s].at[at_p], out[s].at[at_p], zq)
            got["zd", s] = w.make(out[s].at[at_h], out[s].at[at_h], zp)
        else:
            for d in range(1, nz):
                got["z", s, d] = w.make(Y_sum[s].at[rows_of(lax.rem(z + d, nz) * 48, 48)], Z_in[s - 3].at[d - 1], zto[d - 1])
                got["zs", s, d] = w.make(out[s].at[at_z], out[s].at[at_z], zto[d - 1])

    def x_send(s):
        if s < 3:
            mine_gw[s].wait()
            got["c", s].wait_recv()
            add_into(offset(cs, (s, 1 - wi), 0), [offset(cs, (s, 1 - wi), 0), offset(cr, (s, 1 - wi), 0)], 384, 128)
            got["x", s].start()
            add_into(offset(cs, (s, wi), 0), [offset(cs, (s, wi), 0), offset(cr, (s, wi), 0)], 384, 128)
        else:
            got["x", s].start()

    def y_send(s):
        got["x", s].wait_recv()
        mine = lambda lo: offset(cs, (s, wi), lo) if s < 3 else offset(gq, (wi,), (s - 3) * 384 + lo)
        for half_y in (1 - y, y):
            lo = half_y * 192
            add_into(offset(X_sum[s], (), lo), [mine(lo), offset(X_in[s], (), lo)], 192, 96)
            if half_y is not y:
                got["y", s].start()

    def z_a(s):
        got["y", s].wait_recv()
        add_into(offset(ys_, (s,), 0), [offset(xs_, (s,), y * 192), offset(yr, (s,), 0)], 192, 96)
        got["za", s].start()

    def z_b(s):
        got["za", s].wait_recv()
        add_into(offset(zs, (s,), 0), [offset(ys_, (s,), odd * 96), offset(za, (s,), 0)], 96, 96)
        got["zb", s].start()

    def z_c(s):
        got["zb", s].wait_recv()
        add_into(offset(out[s], (), start_p), [offset(zs, (s,), far * 48), offset(zb, (s,), 0)], 48, 48)
        got["zc", s].start()

    def z_d(s):
        got["zc", s].wait_recv()
        got["zd", s].start()

    def z_send(s):
        got["y", s].wait_recv()
        add_into(offset(Y_sum[s], (), 0), [offset(X_sum[s], (), y * 192), offset(Y_in[s], (), 0)], 192, 192)
        for d in range(1, nz):
            got["z", s, d].start()

    def z_share(s):
        for d in range(1, nz):
            got["z", s, d].wait_recv()
        add_into(offset(out[s], (), start_z), [offset(Y_sum[s], (), z * 48)] + [offset(Z_in[s - 3], (d,), 0) for d in range(nz - 1)], 48, 48)
        for d in range(1, nz):
            got["zs", s, d].start()

    def y_share(s):
        for k in (["zd"] if s < 3 else [("zs", d) for d in range(1, nz)]):
            got[(k, s) if s < 3 else (k[0], s, k[1])].wait_recv()
        got["ys", s].start()

    def c_share(s):
        got["ys", s].wait_recv()
        got["cs", s].start()
        copy(out[s].at[at_c], done[s].at[at_c])

    for r in range(nz):
        for h in range(2):
            at = pl.ds(h * 512, hrow)
            got["d", r, h] = w.make(dx.at[r, pl.ds(h * 512 + hrow, hrow)], dx_core.at[r, h], to["core"])
            if r:
                got["r", (r + 1) % nz, h] = w.make(dx.at[r, at], dx_in.at[(r + 1) % nz, h], to["up"])
    got["dy"] = w.make(dx.at[0, pl.ds(512, hrow)], dxo.at[1], to["y"])

    def give(r, h):
        got["d", r, h].start()

    def fold(r, h):
        got["d", r, h].wait_recv()
        add_into(offset(dx, (r,), h * 512), [offset(dx, (r,), h * 512), offset(dx_core, (r, h), 0)], hrow, 128)
        if r == 1:
            got["r", 2, h].start()

    def hop(r, h):
        got["r", r, h].wait_recv()
        dst = offset(dx, (r,), h * 512) if r or h else offset(outdx, (0,), 0)
        add_into(dst, [offset(dx, (r,), h * 512), offset(dx_in, (r, h), 0)], hrow, 128)
        if r:
            got["r", (r + 1) % nz, h].start()
        elif h:
            got["dy"].start()
        else:
            copy(outdx.at[0], dxo.at[0])

    vec_to = [to["core"], to["y"], to["x"]] + [(zz * 4 + low, wi) for zz in (z + 1 - 2 * lax.rem(z, 2), z + 2 - 4 * (z // 2))]

    def vec_send(k):
        if k == 0:
            gvs[0] = jnp.zeros_like(gvs[0])
            gvs[0, 0:16, :] = gv_ref[...]
            zero = jnp.zeros((1, half), f32)
            for i in range(2):
                v = db[i:i + 1, :]
                gvs[0, 16 + i:17 + i, :] = jnp.concatenate([jnp.where(c == 0, v, zero), jnp.where(c == 0, zero, v)], axis=1)
        else:
            got["v", k - 1].wait_recv()
            gvs[k] = gvs[k - 1] + gvr[k - 1]
        if k < 5:
            got["v", k].start()
        else:
            gvo[...] = gvs[5]

    pairs = chip_pairs(nz, order_ref)
    for k in range(5):
        got["v", k] = w.make(gvs.at[k], gvr.at[k], vec_to[k])
    diagonal(d_s)
    dw[...] = jnp.zeros_like(dw)
    db[...] = jnp.zeros_like(db)
    for s in (qs, dos, qns, dons):
        s[...] = jnp.zeros_like(s)
    x_send(0)
    for cp in first_in:
        cp.wait()
    dos_in[2].wait_recv()
    hooks = plan(dict(x=x_send, y=y_send, za=z_a, zb=z_b, zc=z_c, zd=z_d, ys=y_share, cs=c_share, fold=fold, hop=hop, z=z_send, zs=z_share, vec=vec_send))
    hook = lambda *k: hooks[k]() if k in hooks else None
    hook("pre")
    for r in list(range(1, nz)) + [0]:
        dk[...] = jnp.zeros_like(dk)
        dv[...] = jnp.zeros_like(dv)
        for cp in kv_in[r][:3]:
            cp.wait()
        for n, js in enumerate(((2, 3), (0, 1)) if r == 1 else ((0, 1, 2, 3),)):
            def step(i, _):
                if r == 1 and n == 0:
                    for k in range(2):
                        pl.when(i == 2)(dos_in[k].wait_recv)
                    bwd_query(pairs, i, do, ot, qn, qt, qs, dos, qns, dons, dl)
                bwd_step(pairs, r, i, r == 0, r == 1 and n == 0, K, V, KT, qs, dos, qns, dons, lse, dl, dk, dv, dq, d_s, gb, js)
                for k in range(4):
                    if (r, n, k) in hooks:
                        pl.when(i == k)(hooks[r, n, k])
                return 0
            lax.fori_loop(0, 4, step, 0)
            if r == 1 and n == 0:
                for q in kv_in:
                    kv_in[q][3].wait()
                w_in.wait()
            if r == 0:
                bwd_query_out(pairs, xs, wqkv, dq, dxq, dw, db)
                hook(0, 0, "q")
            bwd_chunk_weights(pairs, r, xs, dk, dv, dw, db, gp, js)
            if r == 0:
                weight_rows(dw, gq)
                x_send(3)
            hook(r, n, "w")
            bwd_chunk_rows(r, r == 0, wqkv, dxq, dx, gp, [p for p in (3, 1, 2, 0) if p in js])
            for h in (1, 0):
                if 2 * h in js:
                    give(r, h)
            hook(r, n, "r")
    hook("tail")
    for s in range(5):
        got["cs", s].wait_recv()
    got["dy"].wait_recv()
    w.drain()
    for cp in local[-6:]:
        cp.wait()


PLAN = {
    (1, 0, "r"): (("x", 2),),
    (1, 1, 1): (("fold", 1, 1),),
    (1, 1, 2): (("y", 0),),
    (2, 0, 1): (("fold", 1, 0),),
    (2, 0, 2): (("x", 1), ("za", 0),),
    (2, 0, "r"): (("y", 2),),
    (3, 0, 2): (("zb", 0),),
    (3, 0, 3): (("za", 2), ("fold", 2, 0), ("y", 1),),
    (3, 0, "r"): (("zc", 0), ("hop", 2, 0),),
    (0, 0, 0): (("fold", 2, 1), ("hop", 2, 1),),
    (0, 0, 2): (("za", 1),),
    (0, 0, "q"): (("zb", 2), ("zd", 0), ),
    (0, 0, "w"): (("zc", 2), ("vec", 0), ("zb", 1), ("fold", 3, 1), ("fold", 3, 0), ("y", 3), ("x", 4), ("zd", 2), ("zc", 1), ("ys",
        0), ("z", 3), ("y", 4),),
    (0, 0, "r"): (("zd", 1), ("fold", 0, 1), ("hop", 3, 1), ("zs", 3), ("ys", 2), ("z", 4),),
    "tail": (("fold", 0, 0), ("vec", 1), ("ys", 1), ("ys", 3), ("vec", 2), ("cs", 0), ("zs", 4), ("vec", 3), ("hop", 3, 0), ("cs", 2), ("hop", 0, 1),
        ("cs", 1), ("ys", 4), ("cs", 3), ("vec", 4), ("cs", 4), ("vec", 5), ("hop", 0, 0),),
}


def plan(ops):
    def run(items):
        def go():
            for name, *a in items:
                ops[name](*a)
        return go
    return {k if isinstance(k, tuple) else (k,): run(v) for k, v in PLAN.items()}


def back(nz, order, gv, do, x_all, wqkv, k, v, kt, qn, qt, ot, lse, gw):
    A = pl.BlockSpec(memory_space=pltpu.HBM)
    V = pl.BlockSpec(memory_space=pltpu.VMEM)
    sds = jax.ShapeDtypeStruct
    B = lambda *s: pltpu.VMEM(s, bf16)
    F = lambda *s: pltpu.VMEM(s, f32)
    ins = (x_all, wqkv, k, v, kt, qn, qt, ot, lse)
    scratch = [[pltpu.VMEM(a.shape[1:], a.dtype)] * nz if any(a is b for b in (k, v, kt)) else pltpu.VMEM(a.shape, a.dtype) for a in ins] + [B(4, 256, 256)] + bwd_scratch()
    scratch += [B(nz, 1024, 512), B(1024, 512), B(2, 768, 256), F(8, 256), B(1, 256, 512)]
    scratch += [B(nz, 2, 256, 512), B(nz, 2, 256, 512), B(3, 2, 384, 512), B(3, 2, 384, 512), B(3, 384, 512), B(3, 384, 512), B(3, 192, 512), B(3, 192, 512),
                B(3, 96, 512), B(3, 96, 512), B(3, 48, 512), B(2, 384, 256), B(2, 384, 256), B(2, 192, 256), B(2, 192, 256), B(2, nz - 1, 48, 256),
                B(3, 768, 512), B(2, 768, 256),
                F(6, 24, 512), F(5, 24, 512)]
    scratch += [pltpu.SemaphoreType.DMA((80,)), pltpu.SemaphoreType.DMA((80,)), pltpu.SemaphoreType.DMA((40,))]
    return pl.pallas_call(
        functools.partial(back_kernel, nz),
        out_shape=(sds((2, 256, 512), bf16), sds((3, 768, 512), bf16), sds((2, 768, 256), bf16), sds((24, 512), f32)),
        in_specs=[pl.BlockSpec(memory_space=pltpu.SMEM), V] + [A] * 11, out_specs=(A, A, A, V), scratch_shapes=scratch,
        compiler_params=pltpu.CompilerParams(collective_id=2, has_side_effects=True, vmem_limit_bytes=62 << 20), name="back")(order, gv, do, *ins, gw)


def last_kernel(nu, go_ref, gq_ref, gv_ref, dx_ref, dsm_ref, gin, dwq, dbq, dwk, dwv, dbv, dwo, dbo, dg1, ds1, dwu, dbu, dwd, dbd, dg2, ds2):
    wi, y = lax.axis_index("wt"), lax.rem(lax.axis_index("ctx") // 2, 2)
    for s in range(2):
        seq = jnp.where(y == 0, s, 1 - s)
        gin[s] = (dsm_ref[s] + dx_ref[seq].astype(f32)).astype(bf16)
    hr = dwq.shape[0]
    for k in range(2):
        at, low = slice(k * 256, k * 256 + 256), k * 384
        dwq[:, at] = gq_ref[0, low:low + 256, :].astype(f32)
        dwk[0:128, at] = gq_ref[0, low + 256:low + 384, :].astype(f32)
        dwk[128:256, at] = gq_ref[1, low:low + 128, :].astype(f32)
        dwv[:, at] = gq_ref[1, low + 128:low + 384, :].astype(f32)
    dwo[...] = go_ref[0:hr, :].astype(f32)
    for k in range(nu):
        dwu[:, k * 512:k * 512 + 512] = go_ref[hr + k * hr:2 * hr + k * hr, :].astype(f32)
    dwd[...] = go_ref[hr + nu * hr:, :].astype(f32)

    def row(i):
        v = gv_ref[i:i + 1, :]
        return jnp.where(wi == 0, v[:, :256], v[:, 256:])

    for o, i in ((dbo, 0), (dg1, 1), (ds1, 2), (dbd, 3), (dg2, 4), (ds2, 5), (dbq, 16), (dbv, 17)):
        o[...] = row(i).reshape(256)
    h = nu // 2
    a, b = [jnp.concatenate([gv_ref[8 + k * h + i:9 + k * h + i, :] for i in range(h)], axis=1) for k in range(2)]
    dbu[...] = jnp.where(wi == 0, a, b).reshape(a.shape[1])


def last(nu, go, gqo, gv, dxo, dsm):
    V = pl.BlockSpec(memory_space=pltpu.VMEM)
    f = lambda *s: jax.ShapeDtypeStruct(s, f32)
    ff = nu * 512
    outs = (jax.ShapeDtypeStruct((2, 256, 512), bf16), f(256, 512), f(256), f(256, 512), f(256, 512), f(256), f(256, 512), f(256), f(256), f(256),
            f(256, ff), f(ff // 2), f(ff // 2, 512), f(256), f(256), f(256))
    return pl.pallas_call(functools.partial(last_kernel, nu), out_shape=outs, in_specs=[V] * 5, out_specs=(V,) * 16,
                          compiler_params=pltpu.CompilerParams(vmem_limit_bytes=56 << 20), name="last")(go, gqo, gv, dxo, dsm)


def body(block_in, block_order, w_query, b_query, w_key, w_value, b_value, w_out, b_out, gain_one, shift_one,
         w_up, b_up, w_down, b_down, gain_two, shift_two, cotangent, *, nc, nw):
    seqs, rows, dim = block_in.shape
    nz = nc // 4
    hb = rows // BLOCK
    half = dim // 2
    me = lax.axis_index("ctx")
    yy = (me // 2) % 2
    cc = me % 2
    zz = me // 4
    xor = lambda v: [(i, i ^ v) for i in range(nc)]
    ring = [(i, ((i // 4 + 1) % nz) * 4 + i % 4) for i in range(nc)]
    perm = lambda v, p: lax.ppermute(v, "ctx", p)
    gather = lambda v: lax.all_gather(v, "wt", axis=0, tiled=True)
    pick = lambda v, i: lax.dynamic_index_in_dim(v, i, 0, keepdims=False)

    ours = nw == 2 and nz == 4
    small = (b_query, b_value, b_out, gain_one, shift_one, b_down, gain_two, shift_two, b_up)
    by_seq = lambda a, b: jnp.where(yy == 0, jnp.concatenate([a, b], 0), jnp.concatenate([b, a], 0))
    r_ids = (zz - jnp.arange(nz, dtype=jnp.int32)) % nz
    quad = (me % 4) ^ jnp.array([0, 1, 2, 3], jnp.int32)
    order_row = pick(block_order, yy)
    slots = (r_ids[:, None, None] * 4 + quad[None, :, None]) * hb + jnp.arange(hb, dtype=jnp.int32)
    blk = order_row[slots.reshape(-1)]

    if ours:
        att, wo, wu, wd, sm, x_all, wqkv, ot, lse, k, v, kt, qn, qt = front(nz, block_order, small, block_in, (w_query, w_key, w_value, w_out, w_up, w_down))
        att = att.reshape(-1, dim)
    else:
        cols = lambda w: lax.dynamic_slice_in_dim(w, cc * half, half, 1)
        wqkv = gather(jnp.concatenate([cols(w_query), cols(w_key), cols(w_value)], axis=1))
        small = lax.all_gather(jnp.concatenate(small), "wt", axis=0)
        vec8 = jnp.transpose(small[:, :8 * dim // nw].reshape(nw, 8, dim // nw), (1, 0, 2)).reshape(8, 2, half)
        upb = small[:, 8 * dim // nw:].reshape(2, 4, half)
        sm = jnp.pad(jnp.concatenate([jnp.transpose(vec8, (1, 0, 2)), upb], axis=1).astype(f32), ((0, 0), (0, 4), (0, 0)))
        wo, wu, wd = gather(w_out), gather(w_up), gather(w_down)
        x_all = gather_all(nz, block_in)[0]
        o, ot, lse, k, v, kt, qn, qt = attn_fwd(nz, blk, x_all, wqkv, pick(sm, cc)[0:1], pick(sm, cc)[1:2])
        o_self, o_c, o_y, o_yc = o[0], perm(o[1], xor(1)), perm(o[2], xor(2)), perm(o[3], xor(3))
        mine, other = by_seq(o_self, o_y), by_seq(o_c, o_yc)
        att = jnp.where(cc == 0, jnp.concatenate([mine, other], 1), jnp.concatenate([other, mine], 1))

    out, dsm, d_o, gw, gv = dense(block_in.reshape(-1, dim), cotangent.reshape(-1, dim), att, wo, wu, wd, sm)

    if ours:
        dxo, go, gqo, gvec = back(nz, block_order, gv, d_o.reshape(seqs, rows, dim), x_all, wqkv, k, v, kt, qn, qt, ot, lse, gw)
        return (out.reshape(seqs, rows, dim),) + tuple(last(w_up.shape[1] // dim, go.reshape(-1, dim), gqo, gvec, dxo, dsm.reshape(seqs, rows, dim)))
    d_o = d_o.reshape(seqs, rows, dim)
    d_own, d_oth = pick(d_o, yy), pick(d_o, 1 - yy)
    fh = lambda v, c: lax.dynamic_slice_in_dim(v, c * half, half, 1)
    do_all = jnp.concatenate([fh(d_own, cc), perm(fh(d_own, 1 - cc), xor(1)), perm(fh(d_oth, cc), xor(2)), perm(fh(d_oth, 1 - cc), xor(3))], axis=0)
    dx, gq, gb = attn_bwd(nz, blk, x_all, wqkv, k, v, kt, qn, qt, ot, lse, do_all.reshape(4, rows, half))
    gvec = jnp.zeros((24, dim), f32).at[:16].set(gv)
    gvec = lax.dynamic_update_slice(gvec, gb[0:1], (16, cc * half))
    gvec = lax.dynamic_update_slice(gvec, gb[1:2], (17, cc * half))
    wi = lax.axis_index("wt")
    ff, hr = w_up.shape[1], dim // 2
    nu = ff // dim
    dx = jnp.transpose(dx.reshape(nz, 2, 2, rows, dim), (0, 2, 1, 3, 4)).reshape(nz, 2, 2 * rows, dim)
    part = lambda r: dx[r, 0].astype(f32) + perm(dx[r, 1], xor(1)).astype(f32)
    acc = None
    for r in list(range(1, nz)) + [0]:
        acc = part(r) if acc is None else perm(acc.astype(bf16), ring).astype(f32) + part(r)
    from_y = perm(acc[rows:].astype(bf16), xor(2)).astype(f32)
    dkv_sum = by_seq(acc[:rows], from_y)
    gvec = lax.psum(gvec, ("ctx", "wt"))
    g_out = gw[:, :hr].reshape(dim, dim)
    g_up = gw[:, hr:hr + nu * hr].reshape(2, nu, hr, dim).transpose(0, 2, 1, 3).reshape(dim, ff)
    g_down = gw[:, hr + nu * hr:].reshape(ff, dim)
    gq3 = gq.reshape(2, 3, hr, half).transpose(1, 0, 2, 3).reshape(3, dim, half)
    g_qkv = lax.dynamic_update_slice(jnp.zeros((3, dim, dim), bf16), gq3, (0, 0, cc * half))
    total = lambda g: lax.psum(lax.psum_scatter(g, "wt", scatter_dimension=0, tiled=True), "ctx").astype(f32)
    t_out, t_up, t_down = total(g_out), total(g_up), total(g_down)
    t_qkv = [total(g_qkv[i]) for i in range(3)]
    grad_in = (dsm + dkv_sum).astype(bf16).reshape(seqs, rows, dim)

    def share(vv):
        n = vv.size // nw
        return lax.dynamic_slice_in_dim(vv.reshape(-1), wi * n, n, 0)
    return (out.reshape(seqs, rows, dim), grad_in, t_qkv[0], share(gvec[16]), t_qkv[1], t_qkv[2], share(gvec[17]), t_out, share(gvec[0]),
            share(gvec[1]), share(gvec[2]), t_up, share(gvec[8:8 + nu]), t_down, share(gvec[3]), share(gvec[4]), share(gvec[5]))


def solution(mesh):
    seq, mat, vec = P("wt", "ctx", None), P("wt", None), P("wt")
    ins = (seq, mat, mat, vec, mat, mat, vec, mat, vec, vec, vec, mat, vec, mat, vec, vec, vec, seq)
    outs = (seq, seq, mat, vec, mat, mat, vec, mat, vec, vec, vec, mat, vec, mat, vec, vec, vec)
    run = functools.partial(body, nc=mesh.shape["ctx"], nw=mesh.shape["wt"])
    return jax.shard_map(run, mesh=mesh, in_specs=ins, out_specs=outs, check_vma=False)
```
